32 devices in a mesh: seq: 4 (over y, x), grp: 8 (over z, core).
Axes of the slice: x: 2, y: 2, z: 4, core: 2. Of those that a mesh axis runs over, the one named last changes fastest.
Arguments:
- tokens: bfloat16 [16384, 768], P(('grp', 'seq')), may hold values from -6 to 6
- cotangent: bfloat16 [16384, 768], P(('grp', 'seq')), may hold values from -6 to 6
- seq_len: int32 [8], P('grp'), may hold values from 1024 to 2048, as said below
- weight_mats: bfloat16 [768, 9280], replicated
- weight_vecs: bfloat16 [768, 13], replicated
- master_mats: float32 [768, 9280], P('grp'), may hold values from -0.21875 to 0.21875
- master_vecs: float32 [768, 13], P('grp'), may hold values from -3 to 3
- moment_mats: float32 [768, 9280], P('grp'), may hold values from -384 to 384
- moment_vecs: float32 [768, 13], P('grp'), may hold values from -384 to 384
- square_mats: float32 [768, 9280], P('grp'), may hold values from 819.2 to 32768
- square_vecs: float32 [768, 13], P('grp'), may hold values from 819.2 to 32768
- average_mats: float32 [768, 9280], P('grp'), may hold values from -0.21875 to 0.21875
- average_vecs: float32 [768, 13], P('grp'), may hold values from -3 to 3
Outputs:
- block_output: bfloat16 [16384, 768], P(('grp', 'seq'))
- input_grad: bfloat16 [16384, 768], P(('grp', 'seq'))
- grad_mats: float32 [768, 9280], P('grp')
- grad_vecs: float32 [768, 13], P('grp')
- master_mats_new: float32 [768, 9280], P('grp')
- master_vecs_new: float32 [768, 13], P('grp')
- moment_mats_new: float32 [768, 9280], P('grp')
- moment_vecs_new: float32 [768, 13], P('grp')
- square_mats_new: float32 [768, 9280], P('grp')
- square_vecs_new: float32 [768, 13], P('grp')
- average_mats_new: float32 [768, 9280], P('grp')
- average_vecs_new: float32 [768, 13], P('grp')
- copy_mats: bfloat16 [768, 9280], P('grp')
- copy_vecs: bfloat16 [768, 13], P('grp')
The draws below stay inside these ranges and needn't reach their ends.
Inputs may be any that keep to these rules, and one draw needn't show every extreme that they name: Each group's sequences all have the length seq_len of that group; both values 2 * 512 and 2048 occur in every draw.
All inputs are finite; a program needn't handle non-finite values.
Results may differ from the reference program's by a relative error of at most 0.018.
Values may be sent and summed in bfloat16 or wider, within the bound.
No kernel may reach another device: no remote copies, remote signals or barrier semaphores. Data moves between devices by JAX's collectives and lax.ppermute only.
A program may use at most 192 MiB of HBM per device.

```python
import math
from functools import partial
import jax
import jax.numpy as jnp
from jax import lax

D = 768
HEADS = 12
HD = 64
FF = 3072
TOK_DEV = 512
TOKENS = 16384
MW = 9280
VR = 13
N_SEQ = 4
N_GRP = 8


def draw_seq_len(key, part):
    choose = jax.random.randint(jax.random.fold_in(key, 3), (N_GRP,), 0, 2)
    choose = choose.at[0].set(0).at[1].set(1)
    return (2 * TOK_DEV * (1 + choose)).astype(jnp.int32)


def draw_weight_mats(key, part):
    noise = jax.random.normal(jax.random.fold_in(key, 11), (D, 4 * D + 2 * FF + HD), jnp.float32)
    scales = jnp.concatenate([jnp.full((3 * D,), D ** (-0.5), jnp.float32), jnp.full((D,), 0.5 * (TOK_DEV / D) ** 0.5, jnp.float32), jnp.full((FF,), D ** (-0.5), jnp.float32), jnp.full((FF,), FF ** (-0.5), jnp.float32), jnp.full((HD,), 1.5 * HD ** (-0.5), jnp.float32)])
    return (noise * scales[None, :]).astype(jnp.bfloat16)


def draw_weight_vecs(key, part):
    noise = jax.random.normal(jax.random.fold_in(key, 23), (D, 9 + FF // D), jnp.float32)
    offsets = jnp.zeros((9 + FF // D,), jnp.float32).at[0].set(1.0).at[2].set(1.0)
    return (offsets[None, :] + 0.1 * noise).astype(jnp.bfloat16)


def block_levels(own_key, shape, split, least, largest):
    level = 1.0
    for axis_at, shards_of in split:
        heights = jax.random.uniform(jax.random.fold_in(jax.random.fold_in(own_key, 6), axis_at), (shards_of,), jnp.float32, least / len(split), largest / len(split))
        level = level * jnp.repeat(jnp.exp(heights), shape[axis_at] // shards_of).reshape((-1,) + (1,) * (len(shape) - 1 - axis_at))
    return level


def bell_draw(own_key, shape, scale, limit, shards=(), held_as=jnp.bfloat16):
    values = jax.random.normal(own_key, shape, jnp.float32) * scale
    if len(shards) > 0:
        values = block_levels(own_key, shape, shards, -0.22, 0.18) * values
    return jnp.clip(values, min=-limit, max=limit).astype(held_as)


def setup_inputs(seed: int = 0) -> dict:
    streams_of = jax.random.split(jax.random.key(seed), 14)
    return {
        "tokens": bell_draw(streams_of[0], (TOKENS, D), 1.0, 6.0, ((0, 32),)),
        "cotangent": bell_draw(streams_of[1], (TOKENS, D), 1.0, 6.0, ((0, 32),)),
        "seq_len": draw_seq_len(jax.random.fold_in(streams_of[13], 71), 0),
        "weight_mats": draw_weight_mats(jax.random.fold_in(streams_of[13], 71), 0),
        "weight_vecs": draw_weight_vecs(jax.random.fold_in(streams_of[13], 71), 0),
        "master_mats": bell_draw(streams_of[5], (D, MW), D ** -0.5, 0.21875, ((0, 8),), jnp.float32),
        "master_vecs": bell_draw(streams_of[6], (D, VR), 0.2, 3.0, ((0, 8),), jnp.float32),
        "moment_mats": bell_draw(streams_of[7], (D, MW), (0.5 * TOKENS ** 0.5), 384.0, ((0, 8),), jnp.float32),
        "moment_vecs": bell_draw(streams_of[8], (D, VR), (0.5 * TOKENS ** 0.5), 384.0, ((0, 8),), jnp.float32),
        "square_mats": jnp.clip(jnp.exp(math.log(32768.0) - 3.6888794 * jax.random.uniform(streams_of[9], (D, MW), jnp.float32) ** block_levels(streams_of[9], (D, MW), ((0, 8),), -0.2, 0.2)), 819.2, 32768.0),
        "square_vecs": jnp.clip(jnp.exp(math.log(32768.0) - 3.6888794 * jax.random.uniform(streams_of[10], (D, VR), jnp.float32) ** block_levels(streams_of[10], (D, VR), ((0, 8),), -0.2, 0.2)), 819.2, 32768.0),
        "average_mats": bell_draw(streams_of[11], (D, MW), D ** -0.5, 0.21875, ((0, 8),), jnp.float32),
        "average_vecs": bell_draw(streams_of[12], (D, VR), 0.2, 3.0, ((0, 8),), jnp.float32),
    }


norm_eps = 1e-05
adam_eps = 1e-08
beta_first = 0.5
beta_second = 0.5
learn_rate = 0.01
vector_rate = 0.06
decay_rate = 0.1
average_keep = 0.9
highest = lax.Precision.HIGHEST

@jax.custom_vjp
def low(v):
    return lax.optimization_barrier(v.astype(jnp.bfloat16)).astype(jnp.float32)

@jax.custom_vjp
def low_back(v):
    return v

def low_keep(v):
    return (low(v), None)

def low_pass(kept, grad):
    return (grad,)

def back_keep(v):
    return (v, None)

def back_low(kept, grad):
    return (low(grad),)
low.defvjp(low_keep, low_pass)
low_back.defvjp(back_keep, back_low)

def matmul(left, right):
    return jnp.dot(left, right, preferred_element_type=jnp.float32, precision=highest)

def norm_rows(values, gain, shift):
    average = lax.optimization_barrier(jnp.mean(values, axis=1, keepdims=True))
    centered = values - average
    variance = lax.optimization_barrier(jnp.mean(centered * centered, axis=1, keepdims=True))
    return centered * lax.rsqrt(variance + norm_eps) * gain + shift

def feature_map(values, hedge_map):
    count = values.shape[0]
    per_head = values.reshape(count, HEADS, HD)
    scores = jnp.einsum('nhi,hij->nhj', per_head, hedge_map, precision=highest)
    return jnp.concatenate([jax.nn.softmax(scores, axis=-1), jax.nn.softmax(-scores, axis=-1)], axis=-1)

def attention(query_feat, key_feat, value_heads, seq_length):
    count = query_feat.shape[0]
    block = min(512, TOK_DEV)
    blocks = count // block
    kind = query_feat.dtype
    causal = jnp.tril(jnp.ones((block, block), kind))
    query_blocks = query_feat.reshape(blocks, block, HEADS, 2 * HD)
    key_blocks = key_feat.reshape(blocks, block, HEADS, 2 * HD)
    value_blocks = value_heads.reshape(blocks, block, HEADS, HD)
    firsts = jnp.arange(blocks, dtype=jnp.int32) * block

    def block_step(carry, parts):
        state, total = carry
        query_part, key_part, value_part, first = parts
        fresh = 1.0 - (first % seq_length == 0).astype(kind)
        state = state * fresh
        total = total * fresh
        weights = jnp.einsum('thf,shf->hts', query_part, key_part, precision=highest) * causal
        numer = jnp.einsum('hts,shd->thd', weights, value_part, precision=highest)
        numer = numer + jnp.einsum('thf,hfd->thd', query_part, state, precision=highest)
        denom = lax.optimization_barrier(jnp.sum(weights, axis=2)).T + jnp.einsum('thf,hf->th', query_part, total, precision=highest)
        outs = numer / denom[:, :, None]
        state = state + jnp.einsum('shf,shd->hfd', key_part, value_part, precision=highest)
        total = total + lax.optimization_barrier(jnp.sum(key_part, axis=0))
        return ((state, total), outs)
    start_state = (jnp.zeros((HEADS, 2 * HD, HD), kind), jnp.zeros((HEADS, 2 * HD), kind))
    ignored, outs = lax.scan(jax.checkpoint(block_step), start_state, (query_blocks, key_blocks, value_blocks, firsts))
    return outs.reshape(count, HEADS * HD)

def forward(inputs, mats, vecs, seq_length):
    w_qkv = mats[:, :3 * D]
    w_proj = mats[:, 3 * D:4 * D]
    w_fc = mats[:, 4 * D:4 * D + FF]
    w_down = mats[:, 4 * D + FF:4 * D + 2 * FF]
    hedge_map = mats[:, 4 * D + 2 * FF:].reshape(HEADS, HD, HD)
    bias_qkv = vecs[:, 6:9].T.reshape(3 * D)
    bias_fc = vecs[:, 9:].T.reshape(FF)
    count = inputs.shape[0]
    normed_one = low(norm_rows(inputs, vecs[:, 0], vecs[:, 1]))
    projected = low_back(matmul(normed_one, w_qkv) + bias_qkv)
    queries = projected[:, :D]
    keys = projected[:, D:2 * D]
    values = low(projected[:, 2 * D:])
    query_feat = low(feature_map(queries, hedge_map))
    key_feat = low(feature_map(keys, hedge_map))
    mixed = attention(query_feat, key_feat, values.reshape(count, HEADS, HD), seq_length)
    mixed = low_back(low(mixed))
    attn_out = low_back(matmul(mixed, w_proj) + vecs[:, 4])
    resid = inputs + attn_out
    normed_two = low(norm_rows(resid, vecs[:, 2], vecs[:, 3]))
    hidden_pre = low_back(matmul(normed_two, w_fc) + bias_fc)
    hidden = low(jax.nn.gelu(hidden_pre, approximate=True))
    return resid + matmul(hidden, w_down.T) + vecs[:, 5]

def adam_step(grad, master, first, second, rate):
    new_first = beta_first * first + (1.0 - beta_first) * grad
    new_second = beta_second * second + (1.0 - beta_second) * grad * grad
    new_master = master - rate * (new_first / (jnp.sqrt(new_second) + adam_eps) + decay_rate * master)
    return (new_master, new_first, new_second)

def reference(tokens, cotangent, seq_len, weight_mats, weight_vecs, master_mats, master_vecs, moment_mats, moment_vecs, square_mats, square_vecs, average_mats, average_vecs):
    mats_full = weight_mats.astype(jnp.float32)
    vecs_full = weight_vecs.astype(jnp.float32)
    group_tokens = N_SEQ * TOK_DEV
    token_groups = tokens.reshape(N_GRP, group_tokens, D)
    cot_groups = cotangent.reshape(N_GRP, group_tokens, D)

    def group_step(carry, parts):
        grad_m, grad_v = carry
        stretch_rows, cot_rows, length = parts
        result, pullback = jax.vjp(partial(forward, seq_length=length), stretch_rows.astype(jnp.float32), mats_full, vecs_full)
        d_inputs, d_mats, d_vecs = pullback(cot_rows.astype(jnp.float32))
        return ((grad_m + d_mats, grad_v + d_vecs), (result.astype(jnp.bfloat16), d_inputs.astype(jnp.bfloat16)))
    start_grads = (jnp.zeros_like(mats_full), jnp.zeros_like(vecs_full))
    (grad_mats, grad_vecs), (outputs, input_grads) = lax.scan(group_step, start_grads, (token_groups, cot_groups, seq_len))
    new_mats, new_first_m, new_second_m = adam_step(grad_mats, master_mats, moment_mats, square_mats, learn_rate)
    new_vecs, new_first_v, new_second_v = adam_step(grad_vecs, master_vecs, moment_vecs, square_vecs, vector_rate)
    new_avg_m = average_keep * average_mats + (1.0 - average_keep) * new_mats
    new_avg_v = average_keep * average_vecs + (1.0 - average_keep) * new_vecs
    return (outputs.reshape(N_GRP * group_tokens, D), input_grads.reshape(N_GRP * group_tokens, D), grad_mats, grad_vecs, new_mats, new_vecs, new_first_m, new_first_v, new_second_m, new_second_v, new_avg_m, new_avg_v, new_mats.astype(jnp.bfloat16), new_vecs.astype(jnp.bfloat16))
```

```python
from functools import partial

import jax
import jax.numpy as jnp
from jax import lax
from jax.experimental import pallas as pl
from jax.experimental.pallas import tpu as pltpu
from jax.sharding import PartitionSpec as P

D = 768
HEADS = 12
HD = 64
FF = 3072
QUAD = 4
N_QUAD = HEADS // QUAD
AUG = 80

norm_eps = 1e-05
adam_eps = 1e-08
beta_first = 0.5
beta_second = 0.5
learn_rate = 0.01
vector_rate = 0.06
decay_rate = 0.1
average_keep = 0.9

f32 = jnp.float32
bf16 = jnp.bfloat16

S_SEQ, S_GRP, S_MASK, S_BACK = 0, 1, 4, 8

VMEM_BYTES = 56 * 1024 * 1024


def dot_nn(a, b):
    return lax.dot_general(a, b, (((1,), (0,)), ((), ())), preferred_element_type=f32)


def dot_nt(a, b):
    return lax.dot_general(a, b, (((1,), (1,)), ((), ())), preferred_element_type=f32)


def dot_tn(a, b):
    return lax.dot_general(a, b, (((0,), (0,)), ((), ())), preferred_element_type=f32)


def whole(shape):
    return pl.BlockSpec(tuple(shape), lambda *_: (0,) * len(shape))


def sds(shape, dtype):
    return jax.ShapeDtypeStruct(tuple(shape), dtype)


def kernel_call(body, scal, args, in_specs, outs, out_specs, grid=(1,), scratch=(), flops=0,
                aliases=None, name=None):
    moved = sum(o.size * o.dtype.itemsize for o in outs)
    moved += sum(a.size * a.dtype.itemsize for a in args if a.size < 4 * D * D)
    return pl.pallas_call(
        body,
        out_shape=tuple(outs),
        grid_spec=pltpu.PrefetchScalarGridSpec(
            num_scalar_prefetch=1,
            grid=grid,
            in_specs=list(in_specs),
            out_specs=tuple(out_specs),
            scratch_shapes=list(scratch),
        ),
        compiler_params=pltpu.CompilerParams(
            dimension_semantics=("arbitrary",) * len(grid), vmem_limit_bytes=VMEM_BYTES
        ),
        cost_estimate=pl.CostEstimate(flops=int(flops), bytes_accessed=int(moved), transcendentals=0),
        input_output_aliases=aliases or {},
        name=name,
    )(scal, *args)


def row_place(scal, j, fast):
    if not fast:
        return j
    rel = jnp.bitwise_xor(scal[S_GRP], j)
    return (1 - jnp.bitwise_and(rel, 1)) * 4 + jnp.right_shift(rel, 1)


def store_rows(ref, values, scal, fast):
    if not fast:
        ref[...] = values
        return
    block = D // 8
    for j in range(8):
        at = pl.multiple_of(row_place(scal, j, fast) * block, block)
        ref[pl.ds(at, block), :] = values[j * block : (j + 1) * block, :]


def normalize(values):
    average = jnp.mean(values, axis=1, keepdims=True)
    centered = values - average
    variance = jnp.mean(centered * centered, axis=1, keepdims=True)
    inverse = lax.rsqrt(variance + norm_eps)
    return centered * inverse, inverse


def quad_maps(hedge_quad):
    wide = QUAD * HD
    col = lax.broadcasted_iota(jnp.int32, (HD, wide), 1)
    row = lax.broadcasted_iota(jnp.int32, (HD, wide), 0)
    spread = (jnp.bitwise_and(col, HD - 1) == row).astype(bf16)
    tiled = dot_nn(hedge_quad, spread)
    big_r = lax.broadcasted_iota(jnp.int32, (wide, wide), 0)
    big_c = lax.broadcasted_iota(jnp.int32, (wide, wide), 1)
    same = jnp.right_shift(big_r, 6) == jnp.right_shift(big_c, 6)
    return jnp.where(same, tiled, 0.0)


def ones_rows(count):
    return (lax.broadcasted_iota(jnp.int32, (AUG - HD, count), 0) == 0).astype(f32).astype(bf16)


def pre_body(fast, scal, x_ref, w_ref, hedge_ref, vt_ref, h1t_ref, qt_ref, kt_ref, fq_ref, fk_ref,
             vt_out, s_ref):
    rows = x_ref.shape[0]
    vt = vt_ref[...]
    normed, _ = normalize(x_ref[...].astype(f32))
    h1 = (normed * vt[0:1] + vt[1:2]).astype(bf16)
    store_rows(h1t_ref, h1.T, scal, fast)
    v_row = (dot_nn(h1, w_ref[:, 2 * D : 3 * D]) + vt[8:9]).astype(bf16)
    vt_out[...] = v_row.T
    wide = QUAD * HD
    for quad in range(N_QUAD):
        lo, hi = quad * wide, (quad + 1) * wide
        maps = quad_maps(hedge_ref[lo:hi, :]).T.astype(bf16)
        maps2 = jnp.concatenate([maps, maps], axis=1)
        for which, (save, feat) in enumerate(((qt_ref, fq_ref), (kt_ref, fk_ref))):
            base = which * D
            p = dot_nn(h1, w_ref[:, base + lo : base + hi]) + vt[6 + which : 7 + which, lo:hi]
            pt = p.T
            high = pt.astype(bf16)
            save[lo:hi, :] = high
            rest = (pt - high.astype(f32)).astype(bf16)
            scores = dot_nn(maps2, jnp.concatenate([high, rest], axis=0))
            for h in range(QUAD):
                s = scores[h * HD : (h + 1) * HD, :]
                top = jnp.max(s, axis=0, keepdims=True)
                bottom = jnp.min(s, axis=0, keepdims=True)
                pos = jnp.exp(s - top)
                neg = jnp.exp(bottom - s)
                pos = pos / jnp.sum(pos, axis=0, keepdims=True)
                neg = neg / jnp.sum(neg, axis=0, keepdims=True)
                at = (quad * QUAD + h) * 2 * HD
                feat[at : at + HD, :] = pos.astype(bf16)
                feat[at + HD : at + 2 * HD, :] = neg.astype(bf16)
    extra = ones_rows(rows)
    for h in range(HEADS):
        va = jnp.concatenate([vt_out[h * HD : (h + 1) * HD, :], extra], axis=0)
        s_ref[h * AUG : (h + 1) * AUG, :] = dot_nt(va, fk_ref[h * 2 * HD : (h + 1) * 2 * HD, :]).astype(bf16)


def tri_mask(half):
    return lax.broadcasted_iota(jnp.int32, (half, half), 0) <= lax.broadcasted_iota(
        jnp.int32, (half, half), 1
    )


def masked_pair(left0, left1, right, keep):
    half = right.shape[1] // 2
    full = dot_tn(left0, right)
    low = dot_tn(left1, right[:, half:])
    diag0 = jnp.where(keep, full[:, :half], 0.0).astype(bf16)
    above = full[:, half:].astype(bf16)
    diag1 = jnp.where(keep, low, 0.0).astype(bf16)
    return diag0, above, diag1


def local_body(scal, fq_ref, fk_ref, vt_ref, num_ref):
    rows = fq_ref.shape[1]
    half = rows // 2
    keep = tri_mask(half)
    extra = ones_rows(rows)
    for h in range(QUAD):
        fq = fq_ref[h * 2 * HD : (h + 1) * 2 * HD, :]
        fk = fk_ref[h * 2 * HD : (h + 1) * 2 * HD, :]
        va = jnp.concatenate([vt_ref[h * HD : (h + 1) * HD, :], extra], axis=0)
        a00, a01, a11 = masked_pair(fk[:, :half], fk[:, half:], fq, keep)
        num_ref[h * AUG : (h + 1) * AUG, :half] = dot_nn(va[:, :half], a00)
        num_ref[h * AUG : (h + 1) * AUG, half:] = dot_nn(va[:, :half], a01) + dot_nn(va[:, half:], a11)


def weighted_state(scal, slot, parts):
    total = None
    for k, part in enumerate(parts):
        term = scal[slot + k].astype(f32) * part.astype(f32)
        total = term if total is None else total + term
    return total.astype(bf16)


def after_body(fast, n_parts, scal, *refs):
    parts = refs[:n_parts]
    (num_ref, fq_ref, x_ref, w_ref, vt_ref, o_ref, den_ref, obs_ref, r_ref, h2_ref, h2t_ref, sin_ref,
     ob_ref) = refs[n_parts:]
    vt = vt_ref[...]
    state = weighted_state(scal, S_MASK, [p[...] for p in parts])
    sin_ref[...] = state
    for h in range(HEADS):
        num = num_ref[h * AUG : (h + 1) * AUG, :] + dot_nn(
            state[h * AUG : (h + 1) * AUG, :], fq_ref[h * 2 * HD : (h + 1) * 2 * HD, :]
        )
        den = num[HD : HD + 1, :]
        out = num[:HD, :] / den
        o_ref[h * HD : (h + 1) * HD, :] = out
        den_ref[h : h + 1, :] = den
        ob_ref[h * HD : (h + 1) * HD, :] = out.astype(bf16)
    obt = ob_ref[...]
    store_rows(obs_ref, obt, scal, fast)
    r = x_ref[...].astype(f32) + dot_tn(obt, w_ref[...]) + vt[4:5]
    r_ref[...] = r
    normed, _ = normalize(r)
    h2 = (normed * vt[2:3] + vt[3:4]).astype(bf16)
    h2_ref[...] = h2
    store_rows(h2t_ref, h2.T, scal, fast)


gelu_c = 0.7978845608028654
gelu_k = 0.044715


def mlp_body(first, scal, h2_ref, g_ref, wf_ref, wd_ref, bias_ref, *refs):
    if first:
        out_ref, dh_ref, e_ref, du_ref, db_ref = refs
    else:
        out_in, dh_in, out_ref, dh_ref, e_ref, du_ref, db_ref = refs
    u = dot_nn(h2_ref[...], wf_ref[...]) + bias_ref[...]
    de = dot_nn(g_ref[...], wd_ref[...])
    uu = u * u
    t = jnp.tanh(gelu_c * u * (1.0 + gelu_k * uu))
    half_t = 0.5 * (1.0 + t)
    e = (u * half_t).astype(bf16)
    slope = half_t + 0.5 * u * (1.0 - t * t) * (gelu_c * (1.0 + 3.0 * gelu_k * uu))
    du = (de * slope).astype(bf16)
    e_ref[...] = e[None]
    du_ref[...] = du[None]
    db_ref[...] = jnp.sum(du.astype(f32), axis=0, keepdims=True)
    add_out = dot_nt(e, wd_ref[...])
    add_dh = dot_nt(du, wf_ref[...])
    step = pl.program_id(0)

    @pl.when(step == 0)
    def _():
        if first:
            out_ref[...] = add_out
            dh_ref[...] = add_dh
        else:
            out_ref[...] = out_in[...] + add_out
            dh_ref[...] = dh_in[...] + add_dh

    @pl.when(step > 0)
    def _():
        out_ref[...] += add_out
        dh_ref[...] += add_dh


def back_body(scal, out_ref, dh_ref, r_ref, g_ref, w_ref, vt_ref, o_ref, den_ref, fq_ref, y_ref, dr_ref,
              da_ref, rho_ref, ds_ref, sums_ref, do_ref):
    vt = vt_ref[...]
    r = r_ref[...]
    y_ref[...] = (r + out_ref[...] + vt[5:6]).astype(bf16)
    grad_out = g_ref[...].astype(f32)
    normed, inverse = normalize(r)
    up = dh_ref[...]
    dn = up * vt[2:3]
    dr = grad_out + inverse * (
        dn - jnp.mean(dn, axis=1, keepdims=True) - normed * jnp.mean(dn * normed, axis=1, keepdims=True)
    )
    dr_ref[...] = dr
    da = dr.astype(bf16)
    da_ref[...] = da
    sums_ref[...] = jnp.concatenate(
        [
            jnp.sum(up * normed, axis=0, keepdims=True),
            jnp.sum(up, axis=0, keepdims=True),
            jnp.sum(da.astype(f32), axis=0, keepdims=True),
            jnp.sum(grad_out, axis=0, keepdims=True),
        ],
        axis=0,
    )
    do_ref[...] = dot_nt(w_ref[...], da).astype(bf16)
    rows = r.shape[0]
    zero_row = lax.broadcasted_iota(jnp.int32, (AUG - HD, rows), 0) == 0
    for h in range(HEADS):
        dout = do_ref[h * HD : (h + 1) * HD, :].astype(f32)
        inv = 1.0 / den_ref[h : h + 1, :]
        rho = (dout * inv).astype(bf16)
        c = -jnp.sum(dout * o_ref[h * HD : (h + 1) * HD, :], axis=0, keepdims=True) * inv
        extra = jnp.where(zero_row, jnp.broadcast_to(c, (AUG - HD, rows)), 0.0).astype(bf16)
        ra = jnp.concatenate([rho, extra], axis=0)
        rho_ref[h * AUG : (h + 1) * AUG, :] = ra
        ds_ref[h * AUG : (h + 1) * AUG, :] = dot_nt(ra, fq_ref[h * 2 * HD : (h + 1) * 2 * HD, :]).astype(bf16)


def feature_back(feat, upstream):
    pos, neg = feat[:HD].astype(f32), feat[HD:].astype(f32)
    up_pos, up_neg = upstream[:HD], upstream[HD:]
    return pos * (up_pos - jnp.sum(pos * up_pos, axis=0, keepdims=True)) - neg * (
        up_neg - jnp.sum(neg * up_neg, axis=0, keepdims=True)
    )


def attend_back_body(scal, fq_ref, fk_ref, vt_ref, rho_ref, sin_ref, qt_ref, hedge_ref, dq_ref, dfk_ref,
                     dv_ref, dm_ref, dbq_ref):
    rows = fq_ref.shape[1]
    half = rows // 2
    keep = tri_mask(half)
    extra = ones_rows(rows)
    parts = []
    for h in range(QUAD):
        fq = fq_ref[h * 2 * HD : (h + 1) * 2 * HD, :]
        fk = fk_ref[h * 2 * HD : (h + 1) * 2 * HD, :]
        va = jnp.concatenate([vt_ref[h * HD : (h + 1) * HD, :], extra], axis=0)
        ra = rho_ref[h * AUG : (h + 1) * AUG, :]
        state = sin_ref[h * AUG : (h + 1) * AUG, :]
        a00, a01, a11 = masked_pair(fk[:, :half], fk[:, half:], fq, keep)
        g00, g01, g11 = masked_pair(va[:, :half], va[:, half:], ra, keep)
        far = dot_tn(state, ra)
        left = far[:, :half] + dot_nn(fk[:, :half], g00)
        right = far[:, half:] + dot_nn(fk[:, :half], g01) + dot_nn(fk[:, half:], g11)
        dfq = jnp.concatenate([left, right], axis=1)
        at = h * 2 * HD
        dfk_ref[at : at + 2 * HD, :half] = dot_nt(fq[:, :half], g00) + dot_nt(fq[:, half:], g01)
        dfk_ref[at : at + 2 * HD, half:] = dot_nt(fq[:, half:], g11)
        rv = ra[:HD]
        dv_ref[h * HD : (h + 1) * HD, :half] = dot_nt(rv[:, :half], a00) + dot_nt(rv[:, half:], a01)
        dv_ref[h * HD : (h + 1) * HD, half:] = dot_nt(rv[:, half:], a11)
        ds = feature_back(fq, dfq).astype(bf16)
        parts.append(ds)
        dm_ref[h * HD : (h + 1) * HD, :] = dot_nt(qt_ref[h * HD : (h + 1) * HD, :], ds)
    maps = quad_maps(hedge_ref[...]).astype(bf16)
    dq = dot_nn(maps, jnp.concatenate(parts, axis=0)).astype(bf16)
    dq_ref[...] = dq
    dbq_ref[...] = jnp.sum(dq.astype(f32), axis=1, keepdims=True)


def key_back_body(n_parts, scal, *refs):
    parts = refs[:n_parts]
    (dfk_ref, dv_ref, fk_ref, vt_ref, kt_ref, hedge_ref, dmq_ref, dk_ref, dvo_ref, dm_ref,
     db_ref) = refs[n_parts:]
    rows = fk_ref.shape[1]
    extra = ones_rows(rows)
    state = weighted_state(scal, S_BACK, [p[...] for p in parts])
    grads = []
    for h in range(QUAD):
        fk = fk_ref[h * 2 * HD : (h + 1) * 2 * HD, :]
        va = jnp.concatenate([vt_ref[h * HD : (h + 1) * HD, :], extra], axis=0)
        st = state[h * AUG : (h + 1) * AUG, :]
        dfk = dfk_ref[h * 2 * HD : (h + 1) * 2 * HD, :] + dot_tn(st, va)
        dv = dv_ref[h * HD : (h + 1) * HD, :] + dot_nn(st, fk)[:HD]
        dvo_ref[h * HD : (h + 1) * HD, :] = dv.astype(bf16)
        ds = feature_back(fk, dfk).astype(bf16)
        grads.append(ds)
        dm_ref[h * HD : (h + 1) * HD, :] = dmq_ref[h * HD : (h + 1) * HD, :] + dot_nt(
            kt_ref[h * HD : (h + 1) * HD, :], ds
        )
    maps = quad_maps(hedge_ref[...]).astype(bf16)
    dk = dot_nn(maps, jnp.concatenate(grads, axis=0)).astype(bf16)
    dk_ref[...] = dk
    db_ref[...] = jnp.concatenate(
        [
            jnp.sum(dk.astype(f32), axis=1, keepdims=True),
            jnp.sum(dvo_ref[...].astype(f32), axis=1, keepdims=True),
        ],
        axis=1,
    )


def input_body(fast, scal, dq_ref, dk_ref, dv_ref, w_ref, x_ref, dr_ref, vt_ref, sums_ref, dbfc_ref,
               dbq_ref, dbkv_ref, dm_ref, gin_ref, small_ref):
    vt = vt_ref[...]
    dh1t = (
        dot_nn(w_ref[:, :D], dq_ref[...])
        + dot_nn(w_ref[:, D : 2 * D], dk_ref[...])
        + dot_nn(w_ref[:, 2 * D : 3 * D], dv_ref[...])
    )
    up = dh1t.T
    normed, inverse = normalize(x_ref[...].astype(f32))
    dn = up * vt[0:1]
    gin = dr_ref[...] + inverse * (
        dn - jnp.mean(dn, axis=1, keepdims=True) - normed * jnp.mean(dn * normed, axis=1, keepdims=True)
    )
    gin_ref[...] = gin.astype(bf16)
    rows16 = jnp.concatenate(
        [
            jnp.sum(up * normed, axis=0, keepdims=True),
            jnp.sum(up, axis=0, keepdims=True),
            sums_ref[...],
            jnp.zeros((3, D), f32),
            dbfc_ref[...],
            jnp.zeros((3, D), f32),
        ],
        axis=0,
    )
    cols = rows16.T
    lane = lax.broadcasted_iota(jnp.int32, (D, HD), 1)
    tail = jnp.concatenate([cols, jnp.zeros((D, HD - 16), f32)], axis=1)
    tail = jnp.where(lane == 6, dbq_ref[...], tail)
    tail = jnp.where(lane == 7, dbkv_ref[:, 0:1], tail)
    tail = jnp.where(lane == 8, dbkv_ref[:, 1:2], tail)
    small = jnp.concatenate([dm_ref[...], tail], axis=1)
    store_rows(small_ref, small, scal, fast)


def mlp_grads_body(n_src, scal, *refs):
    lefts_a, lefts_b = refs[:n_src], refs[n_src : 2 * n_src]
    rights_a, rights_b = refs[2 * n_src : 3 * n_src], refs[3 * n_src : 4 * n_src]
    send_a, keep_a, send_b, keep_b = refs[4 * n_src :]
    step = pl.program_id(0)

    def total(lefts, rights):
        acc = dot_nn(lefts[0][...], rights[0][0])
        for left, right in zip(lefts[1:], rights[1:]):
            acc += dot_nn(left[...], right[0])
        return acc.astype(bf16)[None]

    a, b = total(lefts_a, rights_a), total(lefts_b, rights_b)

    @pl.when(step < 2)
    def _():
        send_a[...] = a
        send_b[...] = b

    @pl.when(step >= 2)
    def _():
        keep_a[...] = a
        keep_b[...] = b


def order_a(i):
    return jnp.where(i < 2, 2 * i + 1, 2 * i - 4)


def order_b(i):
    return jnp.where(i < 2, i + 2, i - 2)


def mlp_grads(scal, lefts_a, lefts_b, rights_a, rights_b):
    n_src = len(lefts_a)
    depth = lefts_a[0].shape[0]
    rows = lefts_a[0].shape[1]
    wq = rights_a[0].shape[2]
    left = pl.BlockSpec((depth, rows), lambda i, s: (0, 0))
    right_a = pl.BlockSpec((1, rows, wq), lambda i, s: (order_a(i), 0, 0))
    right_b = pl.BlockSpec((1, rows, wq), lambda i, s: (order_b(i), 0, 0))
    send = pl.BlockSpec((1, depth, wq), lambda i, s: (jnp.minimum(i, 1), 0, 0))
    keep = pl.BlockSpec((1, depth, wq), lambda i, s: (jnp.maximum(i - 2, 0), 0, 0))
    out = sds((2, depth, wq), bf16)
    return kernel_call(
        partial(mlp_grads_body, n_src),
        scal,
        [*lefts_a, *lefts_b, *rights_a, *rights_b],
        [left] * (2 * n_src) + [right_a] * n_src + [right_b] * n_src,
        [out] * 4,
        [send, keep, send, keep],
        grid=(4,),
        flops=2 * 2 * n_src * depth * rows * wq * 4,
        name="mlp_grads",
    )


def tail_grads_body(n_src, scal, *refs):
    it = iter(refs)

    def take():
        return [next(it) for _ in range(n_src)]

    h1, ob, dq, dk, dv, da = take(), take(), take(), take(), take(), take()
    send_a, keep_a, send_b, keep_b = it
    step = pl.program_id(0)
    seq = scal[S_SEQ]
    qa = jnp.bitwise_xor(order_a(step), seq)
    qb = jnp.bitwise_xor(order_b(step), seq)

    def total(dot, lefts, rights):
        acc = dot(lefts[0][...], rights[0][...])
        for left, right in zip(lefts[1:], rights[1:]):
            acc += dot(left[...], right[...])
        return acc.astype(bf16)[None]

    def put(send, keep, value):
        @pl.when(step < 2)
        def _():
            send[...] = value

        @pl.when(step >= 2)
        def _():
            keep[...] = value

    @pl.when(qa < 2)
    def _():
        put(send_a, keep_a, total(dot_nt, h1, dq))

    @pl.when(qa >= 2)
    def _():
        put(send_a, keep_a, total(dot_nt, h1, dk))

    @pl.when(qb < 2)
    def _():
        put(send_b, keep_b, total(dot_nt, h1, dv))

    @pl.when(qb >= 2)
    def _():
        put(send_b, keep_b, total(dot_nn, ob, da))


def tail_grads(scal, h1, ob, dq, dk, dv, da):
    n_src = len(h1)
    depth, rows = h1[0].shape
    wq = D // 2
    left = pl.BlockSpec((depth, rows), lambda i, s: (0, 0))

    def low(order):
        return lambda i, s: (jnp.minimum(jnp.bitwise_xor(order(i), s[S_SEQ]), 1), 0)

    def high(order):
        return lambda i, s: (jnp.maximum(jnp.bitwise_xor(order(i), s[S_SEQ]) - 2, 0), 0)

    def high_col(order):
        return lambda i, s: (0, jnp.maximum(jnp.bitwise_xor(order(i), s[S_SEQ]) - 2, 0))

    send = pl.BlockSpec((1, depth, wq), lambda i, s: (jnp.minimum(i, 1), 0, 0))
    keep = pl.BlockSpec((1, depth, wq), lambda i, s: (jnp.maximum(i - 2, 0), 0, 0))
    out = sds((2, depth, wq), bf16)
    return kernel_call(
        partial(tail_grads_body, n_src),
        scal,
        [*h1, *ob, *dq, *dk, *dv, *da],
        [left] * (2 * n_src)
        + [pl.BlockSpec((wq, rows), low(order_a))] * n_src
        + [pl.BlockSpec((wq, rows), high(order_a))] * n_src
        + [pl.BlockSpec((wq, rows), low(order_b))] * n_src
        + [pl.BlockSpec((rows, wq), high_col(order_b))] * n_src,
        [out] * 4,
        [send, keep, send, keep],
        grid=(4,),
        flops=2 * 2 * n_src * depth * rows * wq * 4,
        name="tail_grads",
    )


def swap(value, axis, size, bit):
    return lax.ppermute(value, axis, [(i, i ^ bit) for i in range(size)])


def add_one_body(scal, keep_a, recv_a, keep_b, recv_b, send_a, send_b):
    send_a[...] = (keep_a[0].astype(f32) + recv_a[0].astype(f32)).astype(bf16)
    send_b[...] = (keep_b[0].astype(f32) + recv_b[0].astype(f32)).astype(bf16)


def add_two_body(scal, keep_a, recv_a, keep_b, recv_b, far_a, far_b, own_ref, *out_refs):
    block = own_ref.shape[1]
    for path, (keep, recv, far) in enumerate(((keep_a, recv_a, far_a), (keep_b, recv_b, far_b))):
        total = keep[0].astype(f32) + recv[0].astype(f32) + far[...].astype(f32)
        own_ref[path] = total[:block]
        for k, ref in enumerate(out_refs):
            ref[path] = total[(k + 1) * block : (k + 2) * block].astype(bf16)


def add_three_body(scal, own, *refs):
    total = own[...]
    for ref in refs[:-1]:
        total = total + ref[...].astype(f32)
    refs[-1][...] = total.astype(refs[-1].dtype)


def reduce_piece(scal, send_a, keep_a, send_b, keep_b):
    two, depth, wq = keep_a.shape
    recv_a, recv_b = swap(send_a, "seq", 4, 1), swap(send_b, "seq", 4, 2)
    one = pl.BlockSpec((1, depth, wq), lambda i, s: (1, 0, 0))
    zero = pl.BlockSpec((1, depth, wq), lambda i, s: (0, 0, 0))
    flat = whole((depth, wq))
    next_a, next_b = kernel_call(
        add_one_body, scal, [keep_a, recv_a, keep_b, recv_b], [one] * 4,
        [sds((depth, wq), bf16)] * 2, [flat] * 2, flops=2 * depth * wq, name="add_one",
    )
    far_a, far_b = swap(next_a, "seq", 4, 2), swap(next_b, "seq", 4, 1)
    block = depth // 4
    shard = (2, block, wq)
    own, *sends = kernel_call(
        add_two_body, scal, [keep_a, recv_a, keep_b, recv_b, far_a, far_b], [zero] * 4 + [flat] * 2,
        [sds(shard, f32)] + [sds(shard, bf16)] * 3, [whole(shard)] * 4, flops=4 * depth * wq,
        name="add_two",
    )
    got = [swap(v, "grp", 8, 2 * (k + 1)) for k, v in enumerate(sends)]
    (mine,) = kernel_call(
        add_three_body, scal, [own, *got], [whole(shard)] * 4, [sds(shard, bf16)], [whole(shard)],
        flops=6 * block * wq, name="add_three",
    )
    return [mine] + [swap(mine, "seq", 4, k) for k in (1, 2, 3)]


def adam_math(grad, master, first, second, average, rate):
    new_first = beta_first * first + (1.0 - beta_first) * grad
    new_second = beta_second * second + (1.0 - beta_second) * grad * grad
    new_master = master - rate * (
        new_first / (jnp.sqrt(new_second) + adam_eps) + decay_rate * master
    )
    new_average = average_keep * average + (1.0 - average_keep) * new_master
    return new_master, new_first, new_second, new_average


def adam_body(n_alias, scal, p0, p1, p2, p3, master, first, second, average, *refs):
    outs = refs[n_alias:]
    part = pl.program_id(1)
    path = pl.program_id(0)
    grad_ref = outs[0]
    for k, ref in enumerate((p0, p1, p2, p3)):

        @pl.when(part == k)
        def _(ref=ref):
            grad_ref[...] = ref[path].astype(f32)

    results = adam_math(grad_ref[...], master[...], first[...], second[...], average[...], learn_rate)
    for ref, value in zip(outs[1:5], results):
        ref[...] = value
    outs[5][...] = results[0].astype(bf16)


def adam_piece(scal, parts, states, outs, block_of):
    _, block, wq = parts[0].shape
    rows, wide = states[0].shape

    def at(path, part, s):
        return (0, block_of(path, jnp.bitwise_xor(part, s[S_SEQ])))

    spec = pl.BlockSpec((block, wq), at)
    anywhere = pl.BlockSpec(memory_space=pl.ANY)
    n_alias = 0 if outs is None else 6
    shapes = [sds((rows, wide), f32)] * 5 + [sds((rows, wide), bf16)]
    return kernel_call(
        partial(adam_body, n_alias),
        scal,
        [*parts, *states, *(outs or [])],
        [whole(parts[0].shape)] * 4 + [spec] * 4 + [anywhere] * n_alias,
        shapes,
        [spec] * 6,
        grid=(2, 4),
        flops=20 * 8 * block * wq,
        aliases={9 + i: i for i in range(n_alias)},
        name="adam",
    )


def small_core_body(scal, mine, recv, out):
    out[...] = mine[...] + recv[...]


def on_device(
    n_seq,
    n_grp,
    tokens,
    cotangent,
    seq_len,
    weight_mats,
    weight_vecs,
    master_mats,
    master_vecs,
    moment_mats,
    moment_vecs,
    square_mats,
    square_vecs,
    average_mats,
    average_vecs,
):
    rows = tokens.shape[0]
    fast = n_seq == 4 and n_grp == 8
    seq_at = lax.axis_index("seq")
    grp_at = lax.axis_index("grp")
    slot = jnp.arange(16, dtype=jnp.int32)
    seq_length = seq_len[0]
    peer = jnp.bitwise_xor(seq_at, jnp.bitwise_and(slot, 3) + 1)
    same = (peer * rows) // seq_length == (seq_at * rows) // seq_length
    before = (same & (peer < seq_at)).astype(jnp.int32)
    after = (same & (peer > seq_at)).astype(jnp.int32)
    scal = jnp.where(slot < 8, before, after)
    scal = jnp.where(slot == S_SEQ, seq_at if fast else 0, scal)
    scal = jnp.where(slot == S_GRP, grp_at, scal)

    vec_all = weight_vecs.astype(f32)
    vt = vec_all.T
    bias_fc = vt[9:].reshape(1, FF)
    hedge = weight_mats[:, 4 * D + 2 * FF :]
    wide = QUAD * HD

    def cols(width, index):
        return pl.BlockSpec((D, width), lambda *_: (0, index))

    tr = (rows,)
    h1t, qt, kt, fq, fk, v_t, s_own = kernel_call(
        partial(pre_body, fast),
        scal,
        [tokens, weight_mats, hedge, vt],
        [whole((rows, D)), cols(3 * D, 0), whole((D, HD)), whole(vt.shape)],
        [
            sds((D, rows), bf16),
            sds((D, rows), bf16),
            sds((D, rows), bf16),
            sds((2 * D, rows), bf16),
            sds((2 * D, rows), bf16),
            sds((D, rows), bf16),
            sds((HEADS * AUG, 2 * HD), bf16),
        ],
        [whole((D, rows))] * 3 + [whole((2 * D, rows))] * 2 + [whole((D, rows)), whole((HEADS * AUG, 2 * HD))],
        flops=2 * rows * D * 3 * D,
        name="pre",
    )
    n_peer = n_seq - 1
    states = [swap(s_own, "seq", n_seq, k + 1) for k in range(n_peer)]

    feat_spec = pl.BlockSpec((2 * wide, rows), lambda i, s: (i, 0))
    head_spec = pl.BlockSpec((wide, rows), lambda i, s: (i, 0))
    aug_spec = pl.BlockSpec((QUAD * AUG, rows), lambda i, s: (i, 0))
    (num,) = kernel_call(
        local_body,
        scal,
        [fq, fk, v_t],
        [feat_spec, feat_spec, head_spec],
        [sds((HEADS * AUG, rows), f32)],
        [aug_spec],
        grid=(N_QUAD,),
        flops=HEADS * 2 * rows * rows * 256,
        name="local",
    )
    st_shape = (HEADS * AUG, 2 * HD)
    o_t, den, obs, resid, h2, h2t, s_in = kernel_call(
        partial(after_body, fast, n_peer),
        scal,
        [*states, num, fq, tokens, weight_mats, vt],
        [whole(st_shape)] * n_peer
        + [whole(num.shape), whole(fq.shape), whole((rows, D)), cols(D, 3), whole(vt.shape)],
        [
            sds((D, rows), f32),
            sds((16, rows), f32),
            sds((D, rows), bf16),
            sds((rows, D), f32),
            sds((rows, D), bf16),
            sds((D, rows), bf16),
            sds(st_shape, bf16),
        ],
        [whole((D, rows)), whole((16, rows)), whole((D, rows)), whole((rows, D)), whole((rows, D)),
         whole((D, rows)), whole(st_shape)],
        scratch=[pltpu.VMEM((D, rows), bf16)],
        flops=2 * rows * D * D,
        name="after",
    )

    def theirs_mine(value):
        half = value.shape[0] // 2
        return value[:half], value[half:]

    if fast:
        g_t = cotangent.T.reshape(8, D // 8, rows)
        place = jnp.bitwise_xor(jnp.array([2 * z + c for c in (1, 0) for z in range(4)], jnp.int32), grp_at)
        g_sel = jnp.take(g_t, place, axis=0).reshape(D, rows)

        def pair(value):
            other, mine = theirs_mine(value)
            return [mine, swap(other, "grp", 8, 1)]

        def both(value):
            return [value, swap(value, "grp", 8, 1)]
    else:
        g_sel = cotangent.T

        def pair(value):
            return [value]

        both = pair

    g_pair, h1_pair, ob_pair, h2_pair = pair(g_sel), pair(h1t), pair(obs), pair(h2t)

    n_piece = 3
    piece = FF // n_piece
    wq = piece // 4
    acc = []
    pieces, db_fc = [], []
    for j in range(n_piece):

        def quarter(base, j=j):
            return pl.BlockSpec((D, wq), lambda i, s: (0, base // wq + 4 * j + jnp.bitwise_xor(i, s[S_SEQ])))

        act = pl.BlockSpec((1, rows, wq), lambda i, s: (i, 0, 0))
        out_y, out_dh, e, du, db = kernel_call(
            partial(mlp_body, j == 0),
            scal,
            [h2, cotangent, weight_mats, weight_mats, bias_fc, *acc],
            [
                whole((rows, D)),
                whole((rows, D)),
                quarter(4 * D),
                quarter(4 * D + FF),
                pl.BlockSpec((1, wq), lambda i, s, j=j: (0, 4 * j + jnp.bitwise_xor(i, s[S_SEQ]))),
            ]
            + [whole((rows, D))] * len(acc),
            [sds((rows, D), f32), sds((rows, D), f32), sds((4, rows, wq), bf16), sds((4, rows, wq), bf16),
             sds((1, piece), f32)],
            [whole((rows, D)), whole((rows, D)), act, act,
             pl.BlockSpec((1, wq), lambda i, s: (0, jnp.bitwise_xor(i, s[S_SEQ])))],
            grid=(4,),
            flops=4 * 2 * rows * D * piece,
            name="mlp",
        )
        acc = [out_y, out_dh]
        db_fc.append(db)
        pieces.append(mlp_grads(scal, g_pair, h2_pair, both(e), both(du)))

    block_output, d_resid, d_attn, rho, ds_own, sums = kernel_call(
        back_body,
        scal,
        [*acc, resid, cotangent, weight_mats, vt, o_t, den, fq],
        [whole((rows, D))] * 4 + [cols(D, 3), whole(vt.shape), whole((D, rows)), whole((16, rows)),
                                  whole((2 * D, rows))],
        [
            sds((rows, D), bf16),
            sds((rows, D), f32),
            sds((rows, D), bf16),
            sds((HEADS * AUG, rows), bf16),
            sds(st_shape, bf16),
            sds((4, D), f32),
        ],
        [whole((rows, D))] * 3 + [whole((HEADS * AUG, rows)), whole(st_shape), whole((4, D))],
        scratch=[pltpu.VMEM((D, rows), bf16)],
        flops=2 * rows * D * D,
        name="back",
    )
    back_states = [swap(ds_own, "seq", n_seq, k + 1) for k in range(n_peer)]
    da_pair = both(d_attn)

    quad_state = pl.BlockSpec((QUAD * AUG, 2 * HD), lambda i, s: (i, 0))
    quad_map = pl.BlockSpec((wide, HD), lambda i, s: (i, 0))
    quad_col = pl.BlockSpec((wide, 1), lambda i, s: (i, 0))
    dq_t, dfk, dv_local, dm_q, dbq = kernel_call(
        attend_back_body,
        scal,
        [fq, fk, v_t, rho, s_in, qt, hedge],
        [feat_spec, feat_spec, head_spec, aug_spec, quad_state, head_spec, quad_map],
        [sds((D, rows), bf16), sds((2 * D, rows), f32), sds((D, rows), f32), sds((D, HD), f32), sds((D, 1), f32)],
        [head_spec, feat_spec, head_spec, quad_map, quad_col],
        grid=(N_QUAD,),
        flops=HEADS * 2 * rows * rows * 768,
        name="attend_back",
    )
    dq_pair = both(dq_t)
    dk_t, dv_t, dm, dbkv = kernel_call(
        partial(key_back_body, n_peer),
        scal,
        [*back_states, dfk, dv_local, fk, v_t, kt, hedge, dm_q],
        [quad_state] * n_peer + [feat_spec, head_spec, feat_spec, head_spec, head_spec, quad_map, quad_map],
        [sds((D, rows), bf16), sds((D, rows), bf16), sds((D, HD), f32), sds((D, 2), f32)],
        [head_spec, head_spec, quad_map, pl.BlockSpec((wide, 2), lambda i, s: (i, 0))],
        grid=(N_QUAD,),
        flops=HEADS * 2 * rows * 256 * 128,
        name="key_back",
    )
    dk_pair, dv_pair = both(dk_t), both(dv_t)
    db_fc_rows = jnp.concatenate(db_fc, axis=1).reshape(FF // D, D)
    input_grad, small = kernel_call(
        partial(input_body, fast),
        scal,
        [dq_t, dk_t, dv_t, weight_mats, tokens, d_resid, vt, sums, db_fc_rows, dbq, dbkv, dm],
        [whole((D, rows))] * 3
        + [cols(3 * D, 0), whole((rows, D)), whole((rows, D)), whole(vt.shape), whole((4, D)),
           whole((FF // D, D)), whole((D, 1)), whole((D, 2)), whole((D, HD))],
        [sds((rows, D), bf16), sds((D, 2 * HD), f32)],
        [whole((rows, D)), whole((D, 2 * HD))],
        flops=2 * rows * D * 3 * D,
        name="input",
    )
    tail = tail_grads(scal, h1_pair, ob_pair, dq_pair, dk_pair, dv_pair, da_pair)

    states_m = [master_mats, moment_mats, square_mats, average_mats]
    if fast:
        outs = None
        for j in range(n_piece):
            parts = reduce_piece(scal, *pieces[j])
            outs = adam_piece(
                scal, parts, states_m, outs,
                lambda path, q, j=j: jnp.where(path == 0, (4 * D + FF) // wq, 4 * D // wq) + 4 * j + q,
            )
        parts = reduce_piece(scal, *tail)
        outs = adam_piece(scal, parts, states_m, outs, lambda path, q: 4 * path + q)
        other, mine = theirs_mine(small)
        small_sum = mine + swap(other.astype(bf16), "grp", 8, 1).astype(f32)
        for bit in (1, 2):
            small_sum = small_sum + swap(small_sum.astype(bf16), "seq", 4, bit).astype(f32)
        small_sum = small_sum.reshape(4, D // 8, 2 * HD)
        small_low = small_sum.astype(bf16)
        small_own = small_sum[0]
        for k in (1, 2, 3):
            small_own = small_own + swap(small_low[k], "grp", 8, 2 * k).astype(f32)
    else:
        def joined(send, keep, order):
            parts = {**dict(zip(order[:2], send)), **dict(zip(order[2:], keep))}
            return [parts[q] for q in range(4)]

        fc, dn = [], []
        for send_a, keep_a, send_b, keep_b in pieces:
            dn += joined(send_a, keep_a, (1, 3, 0, 2))
            fc += joined(send_b, keep_b, (2, 3, 0, 1))
        send_a, keep_a, send_b, keep_b = tail
        first = joined(send_a, keep_a, (1, 3, 0, 2)) + joined(send_b, keep_b, (2, 3, 0, 1))
        mats = jnp.concatenate([*first, *fc, *dn], axis=1)
        own = lax.psum_scatter(mats, "grp", scatter_dimension=0, tiled=True)
        own = lax.psum(own, "seq").astype(f32)
        small_own = lax.psum(lax.psum_scatter(small, "grp", scatter_dimension=0, tiled=True), "seq")
        main = 4 * D + 2 * FF
        results = adam_math(own, *[v[:, :main] for v in states_m], learn_rate)
        outs = [own, *results, results[0].astype(bf16)]
        outs = [jnp.pad(v, ((0, 0), (0, HD))) for v in outs]

    start = 4 * D + 2 * FF
    grad_m = small_own[:, :HD]
    extra = adam_math(grad_m, *[v[:, start:] for v in states_m], learn_rate)
    extra = [grad_m, *extra, extra[0].astype(bf16)]
    outs = [lax.dynamic_update_slice(v, e, (0, start)) for v, e in zip(outs, extra)]
    grad_v = small_own[:, HD : HD + master_vecs.shape[1]]
    vec = adam_math(grad_v, master_vecs, moment_vecs, square_vecs, average_vecs, vector_rate)
    vec = [grad_v, *vec, vec[0].astype(bf16)]
    flat = [x for both_ in zip(outs, vec) for x in both_]
    return (block_output, input_grad, *flat)


def solution(mesh):
    tok = P(("grp", "seq"), None)
    own = P("grp", None)
    in_specs = (tok, tok, P("grp"), P(), P()) + (own,) * 8
    out_specs = (tok, tok) + (own,) * 12
    body = partial(on_device, mesh.shape["seq"], mesh.shape["grp"])
    return jax.shard_map(body, mesh=mesh, in_specs=in_specs, out_specs=out_specs, check_vma=False)
```

```python
from functools import partial

import jax
import jax.numpy as jnp
from jax import lax
from jax.experimental import pallas as pl
from jax.experimental.pallas import tpu as pltpu
from jax.sharding import PartitionSpec as P

D = 768
HEADS = 12
HD = 64
FF = 3072
QUAD = 4
N_QUAD = HEADS // QUAD
AUG = 80

norm_eps = 1e-05
adam_eps = 1e-08
beta_first = 0.5
beta_second = 0.5
learn_rate = 0.01
vector_rate = 0.06
decay_rate = 0.1
average_keep = 0.9

f32 = jnp.float32
bf16 = jnp.bfloat16

S_SEQ, S_GRP, S_MASK, S_BACK = 0, 1, 4, 8

MIB = 1024 * 1024


def dot_nn(a, b):
    return lax.dot_general(a, b, (((1,), (0,)), ((), ())), preferred_element_type=f32)


def dot_nt(a, b):
    return lax.dot_general(a, b, (((1,), (1,)), ((), ())), preferred_element_type=f32)


def dot_tn(a, b):
    return lax.dot_general(a, b, (((0,), (0,)), ((), ())), preferred_element_type=f32)


def whole(shape):
    return pl.BlockSpec(tuple(shape), lambda *_: (0,) * len(shape))


def along(block, axis=0):
    return pl.BlockSpec(tuple(block), lambda i, s: tuple(i if d == axis else 0 for d in range(len(block))))


def sds(shape, dtype):
    return jax.ShapeDtypeStruct(tuple(shape), dtype)


class Line:
    def __init__(self, scal):
        self.scal = scal

    def call(self, body, args, in_specs, outs, out_specs, grid=(1,), scratch=(), flops=0, vmem=32,
             aliases=None, name=None):
        moved = sum(o.size * o.dtype.itemsize for o in outs)
        moved += sum(a.size * a.dtype.itemsize for a in args if a.size < 4 * D * D)
        got = pl.pallas_call(
            body,
            out_shape=tuple(outs),
            grid_spec=pltpu.PrefetchScalarGridSpec(
                num_scalar_prefetch=1,
                grid=grid,
                in_specs=list(in_specs),
                out_specs=tuple(out_specs),
                scratch_shapes=list(scratch),
            ),
            compiler_params=pltpu.CompilerParams(
                dimension_semantics=("arbitrary",) * len(grid), vmem_limit_bytes=vmem * MIB
            ),
            cost_estimate=pl.CostEstimate(
                flops=int(flops), bytes_accessed=int(moved), transcendentals=0
            ),
            input_output_aliases=aliases or {},
            name=name,
        )(self.scal, *args)
        self.scal, got = lax.optimization_barrier((self.scal, got))
        return got


def store_sel(refs, at, values, scal):
    if len(refs) == 1:
        refs[0][at] = values
        return
    block = D // 8
    for j in range(8):
        rel = jnp.bitwise_xor(scal[S_GRP], j)
        place = pl.multiple_of(jnp.right_shift(rel, 1) * block, block)
        odd = jnp.bitwise_and(rel, 1)
        part = values[j * block : (j + 1) * block, :]

        @pl.when(odd == 1)
        def _(part=part, place=place):
            refs[0][at, pl.ds(place, block), :] = part

        @pl.when(odd == 0)
        def _(part=part, place=place):
            refs[1][at, pl.ds(place, block), :] = part


def normalize(values):
    average = jnp.mean(values, axis=1, keepdims=True)
    centered = values - average
    variance = jnp.mean(centered * centered, axis=1, keepdims=True)
    inverse = lax.rsqrt(variance + norm_eps)
    return centered * inverse, inverse


def quad_maps(hedge_t):
    wide = QUAD * HD
    row = lax.broadcasted_iota(jnp.int32, (wide, HD), 0)
    col = lax.broadcasted_iota(jnp.int32, (wide, HD), 1)
    spread = (jnp.bitwise_and(row, HD - 1) == col).astype(bf16)
    tiled = dot_nn(spread, hedge_t)
    big_r = lax.broadcasted_iota(jnp.int32, (wide, wide), 0)
    big_c = lax.broadcasted_iota(jnp.int32, (wide, wide), 1)
    same = jnp.right_shift(big_r, 6) == jnp.right_shift(big_c, 6)
    return jnp.where(same, tiled, 0.0)


def ones_rows(count):
    return (lax.broadcasted_iota(jnp.int32, (AUG - HD, count), 0) == 0).astype(f32).astype(bf16)


def rows_up(values):
    return jnp.concatenate([values, jnp.zeros((3, values.shape[1]), f32)], axis=0).T


def pre_body(n_sel, scal, x_ref, g_ref, wq_ref, wk_ref, wv_ref, hedge_ref, vt_ref, vq_ref, *refs):
    sel = refs[:n_sel]
    qt_ref, kt_ref, fq_ref, fk_ref, vt_out, s_ref, h1_ref = refs[n_sel:]
    rows = x_ref.shape[0]

    @pl.when(pl.program_id(0) == 0)
    def _():
        normed, _ = normalize(x_ref[...].astype(f32))
        vt = vt_ref[...].astype(f32)
        h1 = (normed * vt[0:1] + vt[1:2]).astype(bf16)
        h1_ref[...] = h1
        store_sel(sel, 0, g_ref[...].T, scal)
        store_sel(sel, 1, h1.T, scal)

    h1 = h1_ref[...]
    bias = rows_up(vq_ref[...].astype(f32))
    v_t = (dot_nt(wv_ref[...], h1) + bias[:, 8:9]).astype(bf16)
    vt_out[...] = v_t
    maps = quad_maps(hedge_ref[...]).astype(bf16)
    maps2 = jnp.concatenate([maps, maps], axis=1)
    extra = ones_rows(rows)
    for which, (w_ref, save, feat) in enumerate(((wk_ref, kt_ref, fk_ref), (wq_ref, qt_ref, fq_ref))):
        pt = dot_nt(w_ref[...], h1) + bias[:, 7 - which : 8 - which]
        high = pt.astype(bf16)
        save[...] = high
        rest = (pt - high.astype(f32)).astype(bf16)
        scores = dot_nn(maps2, jnp.concatenate([high, rest], axis=0))
        for h in range(QUAD):
            s = scores[h * HD : (h + 1) * HD, :]
            top = jnp.max(s, axis=0, keepdims=True)
            bottom = jnp.min(s, axis=0, keepdims=True)
            pos = jnp.exp(s - top)
            neg = jnp.exp(bottom - s)
            pos = pos * (1.0 / jnp.sum(pos, axis=0, keepdims=True))
            neg = neg * (1.0 / jnp.sum(neg, axis=0, keepdims=True))
            both = jnp.concatenate([pos, neg], axis=0).astype(bf16)
            feat[h * 2 * HD : (h + 1) * 2 * HD, :] = both
            if which == 0:
                va = jnp.concatenate([v_t[h * HD : (h + 1) * HD, :], extra], axis=0)
                s_ref[h * AUG : (h + 1) * AUG, :] = dot_nt(va, both).astype(bf16)


def tri_mask(half):
    return lax.broadcasted_iota(jnp.int32, (half, half), 0) <= lax.broadcasted_iota(
        jnp.int32, (half, half), 1
    )


def masked_pair(left0, left1, right, keep):
    half = right.shape[1] // 2
    full = dot_tn(left0, right)
    low = dot_tn(left1, right[:, half:])
    diag0 = jnp.where(keep, full[:, :half], 0.0).astype(bf16)
    above = full[:, half:].astype(bf16)
    diag1 = jnp.where(keep, low, 0.0).astype(bf16)
    return diag0, above, diag1


def local_body(scal, fq_ref, fk_ref, vt_ref, num_ref):
    rows = fq_ref.shape[1]
    half = rows // 2
    keep = tri_mask(half)
    extra = ones_rows(rows)
    for h in range(QUAD):
        fq = fq_ref[h * 2 * HD : (h + 1) * 2 * HD, :]
        fk = fk_ref[h * 2 * HD : (h + 1) * 2 * HD, :]
        va = jnp.concatenate([vt_ref[h * HD : (h + 1) * HD, :], extra], axis=0)
        a00, a01, a11 = masked_pair(fk[:, :half], fk[:, half:], fq, keep)
        num_ref[h * AUG : (h + 1) * AUG, :half] = dot_nn(va[:, :half], a00)
        num_ref[h * AUG : (h + 1) * AUG, half:] = dot_nn(va[:, :half], a01) + dot_nn(va[:, half:], a11)


def weighted_state(scal, slot, parts):
    total = None
    for k, part in enumerate(parts):
        term = scal[slot + k].astype(f32) * part.astype(f32)
        total = term if total is None else total + term
    return total.astype(bf16)


def after_body(n_sel, n_parts, scal, *refs):
    parts = refs[:n_parts]
    num_ref, fq_ref, x_ref, w_ref, vt_ref, o_ref, den_ref, r_ref, h2_ref, sin_ref = refs[n_parts : n_parts + 10]
    sel = refs[n_parts + 10 : n_parts + 10 + n_sel]
    ob_ref = refs[-1]
    vt = vt_ref[...].astype(f32)
    state = weighted_state(scal, S_MASK, [p[...] for p in parts])
    sin_ref[...] = state
    for h in range(HEADS):
        num = num_ref[h * AUG : (h + 1) * AUG, :] + dot_nn(
            state[h * AUG : (h + 1) * AUG, :], fq_ref[h * 2 * HD : (h + 1) * 2 * HD, :]
        )
        den = num[HD : HD + 1, :]
        out = num[:HD, :] * (1.0 / den)
        o_ref[h * HD : (h + 1) * HD, :] = out
        den_ref[h : h + 1, :] = den
        ob_ref[h * HD : (h + 1) * HD, :] = out.astype(bf16)
    obt = ob_ref[...]
    store_sel(sel, 0, obt, scal)
    r = x_ref[...].astype(f32) + dot_nt(obt.T, w_ref[...]) + vt[4:5]
    r_ref[...] = r
    normed, _ = normalize(r)
    h2 = (normed * vt[2:3] + vt[3:4]).astype(bf16)
    h2_ref[...] = h2
    store_sel(sel, 1, h2.T, scal)


gelu_c = 0.7978845608028654
gelu_k = 0.044715


def mlp_body(first, scal, h2_ref, g_ref, wf_ref, wd_ref, bias_ref, *refs):
    if first:
        out_ref, dh_ref, act_ref, db_ref = refs
    else:
        out_in, dh_in, out_ref, dh_ref, act_ref, db_ref = refs
    u = dot_nt(h2_ref[...], wf_ref[...]) + bias_ref[...].astype(f32)
    de = dot_nt(g_ref[...], wd_ref[...])
    uu = u * u
    t = jnp.tanh(gelu_c * u * (1.0 + gelu_k * uu))
    half_t = 0.5 * (1.0 + t)
    e = (u * half_t).astype(bf16)
    slope = half_t + 0.5 * u * (1.0 - t * t) * (gelu_c * (1.0 + 3.0 * gelu_k * uu))
    du = (de * slope).astype(bf16)
    act_ref[0, 0] = e
    act_ref[1, 0] = du
    db_ref[...] = jnp.sum(du.astype(f32), axis=0, keepdims=True)
    add_out = dot_nn(e, wd_ref[...])
    add_dh = dot_nn(du, wf_ref[...])
    step = pl.program_id(0)

    @pl.when(step == 0)
    def _():
        if first:
            out_ref[...] = add_out
            dh_ref[...] = add_dh
        else:
            out_ref[...] = out_in[...] + add_out
            dh_ref[...] = dh_in[...] + add_dh

    @pl.when(step > 0)
    def _():
        out_ref[...] += add_out
        dh_ref[...] += add_dh


def back_body(scal, out_ref, dh_ref, r_ref, g_ref, w_ref, vt_ref, o_ref, den_ref, fq_ref, y_ref, dr_ref,
              da_ref, rho_ref, ds_ref, sums_ref, do_ref):
    vt = vt_ref[...].astype(f32)
    r = r_ref[...]
    y_ref[...] = (r + out_ref[...] + vt[5:6]).astype(bf16)
    grad_out = g_ref[...].astype(f32)
    normed, inverse = normalize(r)
    up = dh_ref[...]
    dn = up * vt[2:3]
    dr = grad_out + inverse * (
        dn - jnp.mean(dn, axis=1, keepdims=True) - normed * jnp.mean(dn * normed, axis=1, keepdims=True)
    )
    dr_ref[...] = dr
    da = dr.astype(bf16)
    da_ref[...] = da
    sums_ref[...] = jnp.concatenate(
        [
            jnp.sum(up * normed, axis=0, keepdims=True),
            jnp.sum(up, axis=0, keepdims=True),
            jnp.sum(da.astype(f32), axis=0, keepdims=True),
            jnp.sum(grad_out, axis=0, keepdims=True),
        ],
        axis=0,
    )
    do_ref[...] = dot_nn(da, w_ref[...]).astype(bf16).T
    rows = r.shape[0]
    zero_row = lax.broadcasted_iota(jnp.int32, (AUG - HD, rows), 0) == 0
    for h in range(HEADS):
        dout = do_ref[h * HD : (h + 1) * HD, :].astype(f32)
        inv = 1.0 / den_ref[h : h + 1, :]
        rho = (dout * inv).astype(bf16)
        c = -jnp.sum(dout * o_ref[h * HD : (h + 1) * HD, :], axis=0, keepdims=True) * inv
        extra = jnp.where(zero_row, jnp.broadcast_to(c, (AUG - HD, rows)), 0.0).astype(bf16)
        ra = jnp.concatenate([rho, extra], axis=0)
        rho_ref[h * AUG : (h + 1) * AUG, :] = ra
        ds_ref[h * AUG : (h + 1) * AUG, :] = dot_nt(ra, fq_ref[h * 2 * HD : (h + 1) * 2 * HD, :]).astype(bf16)


def feature_back(feat, upstream):
    pos, neg = feat[:HD].astype(f32), feat[HD:].astype(f32)
    up_pos, up_neg = upstream[:HD], upstream[HD:]
    return pos * (up_pos - jnp.sum(pos * up_pos, axis=0, keepdims=True)) - neg * (
        up_neg - jnp.sum(neg * up_neg, axis=0, keepdims=True)
    )


def attend_back_body(n_parts, scal, *refs):
    parts = refs[:n_parts]
    (fq_ref, fk_ref, vt_ref, rho_ref, sin_ref, qt_ref, kt_ref, hedge_ref, dp_ref, dm_ref,
     db_ref) = refs[n_parts:]
    rows = fq_ref.shape[1]
    half = rows // 2
    keep = tri_mask(half)
    extra = ones_rows(rows)
    back_state = weighted_state(scal, S_BACK, [p[...] for p in parts])
    ds_q, ds_k = [], []
    for h in range(QUAD):
        fq = fq_ref[h * 2 * HD : (h + 1) * 2 * HD, :]
        fk = fk_ref[h * 2 * HD : (h + 1) * 2 * HD, :]
        head = slice(h * HD, (h + 1) * HD)
        aug = slice(h * AUG, (h + 1) * AUG)
        va = jnp.concatenate([vt_ref[head, :], extra], axis=0)
        ra = rho_ref[aug, :]
        state, back = sin_ref[aug, :], back_state[aug, :]
        a00, a01, a11 = masked_pair(fk[:, :half], fk[:, half:], fq, keep)
        g00, g01, g11 = masked_pair(va[:, :half], va[:, half:], ra, keep)
        far = dot_tn(state, ra)
        left = far[:, :half] + dot_nn(fk[:, :half], g00)
        right = far[:, half:] + dot_nn(fk[:, :half], g01) + dot_nn(fk[:, half:], g11)
        dfq = jnp.concatenate([left, right], axis=1)
        far_k = dot_tn(back, va)
        left = far_k[:, :half] + dot_nt(fq[:, :half], g00) + dot_nt(fq[:, half:], g01)
        right = far_k[:, half:] + dot_nt(fq[:, half:], g11)
        dfk = jnp.concatenate([left, right], axis=1)
        far_v = dot_nn(back, fk)[:HD]
        rv = ra[:HD]
        left = far_v[:, :half] + dot_nt(rv[:, :half], a00) + dot_nt(rv[:, half:], a01)
        right = far_v[:, half:] + dot_nt(rv[:, half:], a11)
        dp_ref[2, head, :] = jnp.concatenate([left, right], axis=1).astype(bf16)
        dsq = feature_back(fq, dfq).astype(bf16)
        dsk = feature_back(fk, dfk).astype(bf16)
        ds_q.append(dsq)
        ds_k.append(dsk)
        dm_ref[head, :] = dot_nt(qt_ref[head, :], dsq) + dot_nt(kt_ref[head, :], dsk)
    maps = quad_maps(hedge_ref[...]).T.astype(bf16)
    dq = dot_nn(maps, jnp.concatenate(ds_q, axis=0)).astype(bf16)
    dk = dot_nn(maps, jnp.concatenate(ds_k, axis=0)).astype(bf16)
    dp_ref[0] = dq
    dp_ref[1] = dk
    db_ref[...] = jnp.concatenate(
        [jnp.sum(v.astype(f32), axis=1, keepdims=True) for v in (dq, dk, dp_ref[2])], axis=1
    )


def input_body(fast, scal, dp_ref, w_ref, x_ref, dr_ref, vt_ref, sums_ref, dbfc_ref, db_ref, dm_ref, *refs):
    gin_ref, *small_refs, acc_ref = refs
    step = pl.program_id(0)
    part = dot_tn(dp_ref[0], w_ref[...])

    @pl.when(step == 0)
    def _():
        acc_ref[...] = part

    @pl.when(step == 1)
    def _():
        acc_ref[...] += part

    @pl.when(step == 2)
    def _():
        vt = vt_ref[...].astype(f32)
        up = acc_ref[...] + part
        normed, inverse = normalize(x_ref[...].astype(f32))
        dn = up * vt[0:1]
        gin = dr_ref[...] + inverse * (
            dn - jnp.mean(dn, axis=1, keepdims=True) - normed * jnp.mean(dn * normed, axis=1, keepdims=True)
        )
        gin_ref[...] = gin.astype(bf16)
        rows16 = jnp.concatenate(
            [
                jnp.sum(up * normed, axis=0, keepdims=True),
                jnp.sum(up, axis=0, keepdims=True),
                sums_ref[...],
                jnp.zeros((3, D), f32),
                dbfc_ref[...],
                jnp.zeros((3, D), f32),
            ],
            axis=0,
        )
        cols = rows16.T
        lane = lax.broadcasted_iota(jnp.int32, (D, HD), 1)
        tail = jnp.concatenate([cols, jnp.zeros((D, HD - 16), f32)], axis=1)
        for k in range(3):
            tail = jnp.where(lane == 6 + k, db_ref[:, k : k + 1], tail)
        small = jnp.concatenate([dm_ref[...], tail], axis=1)
        store_sel(small_refs, 0, small, scal)


def order_a(i):
    return jnp.where(i < 2, 2 * i + 1, 2 * i - 4)


def order_b(i):
    return jnp.where(i < 2, i + 2, i - 2)


def put(send, keep, value):
    step = pl.program_id(0)

    @pl.when(step < 2)
    def _():
        send[...] = value[None]

    @pl.when(step >= 2)
    def _():
        keep[...] = value[None]


def mlp_grads_body(n_src, scal, *refs):
    sels, acts_a, acts_b = refs[:n_src], refs[n_src : 2 * n_src], refs[2 * n_src : 3 * n_src]
    sels_h = refs[3 * n_src : 4 * n_src]
    send_a, keep_a, send_b, keep_b = refs[4 * n_src :]

    def total(lefts, rights):
        acc = dot_nn(lefts[0][0], rights[0][0, 0])
        for left, right in zip(lefts[1:], rights[1:]):
            acc += dot_nn(left[0], right[0, 0])
        return acc.astype(bf16)

    put(send_a, keep_a, total(sels, acts_a))
    put(send_b, keep_b, total(sels_h, acts_b))


def split_specs(depth, wq):
    send = pl.BlockSpec((1, depth, wq), lambda i, s: (jnp.minimum(i, 1), 0, 0))
    keep = pl.BlockSpec((1, depth, wq), lambda i, s: (jnp.maximum(i - 2, 0), 0, 0))
    return [sds((2, depth, wq), bf16)] * 4, [send, keep, send, keep]


def mlp_grads(line, sel_first, sel_second, acts):
    n_src = len(acts)
    _, depth, rows = sel_first[0].shape
    wq = acts[0].shape[3]
    outs, out_specs = split_specs(depth, wq)
    return line.call(
        partial(mlp_grads_body, n_src),
        [*sel_first, *acts, *acts, *sel_second],
        [pl.BlockSpec((1, depth, rows), lambda i, s: (0, 0, 0))] * n_src
        + [pl.BlockSpec((1, 1, rows, wq), lambda i, s: (0, order_a(i), 0, 0))] * n_src
        + [pl.BlockSpec((1, 1, rows, wq), lambda i, s: (1, order_b(i), 0, 0))] * n_src
        + [pl.BlockSpec((1, depth, rows), lambda i, s: (1, 0, 0))] * n_src,
        outs,
        out_specs,
        grid=(4,),
        flops=2 * 2 * n_src * depth * rows * wq * 4,
        vmem=24,
        name="mlp_grads",
    )


def tail_grads_body(n_src, scal, *refs):
    it = iter(refs)

    def take():
        return [next(it) for _ in range(n_src)]

    h1, ob, dqk, dv, da = take(), take(), take(), take(), take()
    send_a, keep_a, send_b, keep_b = it
    qb = jnp.bitwise_xor(order_b(pl.program_id(0)), scal[S_SEQ])

    def total(lefts, rights):
        acc = dot_nt(lefts[0][0], rights[0][0])
        for left, right in zip(lefts[1:], rights[1:]):
            acc += dot_nt(left[0], right[0])
        return acc.astype(bf16)

    put(send_a, keep_a, total(h1, dqk))

    @pl.when(qb < 2)
    def _():
        put(send_b, keep_b, total(h1, dv))

    @pl.when(qb >= 2)
    def _():
        acc = dot_nn(ob[0][0], da[0][...])
        for left, right in zip(ob[1:], da[1:]):
            acc += dot_nn(left[0], right[...])
        put(send_b, keep_b, acc.astype(bf16))


def tail_grads(line, sel_first, sel_second, dp, da):
    n_src = len(dp)
    _, depth, rows = sel_first[0].shape
    wq = D // 2
    dp = [v.reshape(6, wq, rows) for v in dp]
    outs, out_specs = split_specs(depth, wq)
    return line.call(
        partial(tail_grads_body, n_src),
        [*sel_first, *sel_second, *dp, *dp, *da],
        [pl.BlockSpec((1, depth, rows), lambda i, s: (1, 0, 0))] * n_src
        + [pl.BlockSpec((1, depth, rows), lambda i, s: (0, 0, 0))] * n_src
        + [pl.BlockSpec((1, wq, rows), lambda i, s: (jnp.bitwise_xor(order_a(i), s[S_SEQ]), 0, 0))] * n_src
        + [pl.BlockSpec((1, wq, rows), lambda i, s: (
            4 + jnp.minimum(jnp.bitwise_xor(order_b(i), s[S_SEQ]), 1), 0, 0))] * n_src
        + [pl.BlockSpec((rows, wq), lambda i, s: (
            0, jnp.maximum(jnp.bitwise_xor(order_b(i), s[S_SEQ]) - 2, 0)))] * n_src,
        outs,
        out_specs,
        grid=(4,),
        flops=2 * 2 * n_src * depth * rows * wq * 4,
        vmem=24,
        name="tail_grads",
    )


def swap(value, axis, size, bit):
    return lax.ppermute(value, axis, [(i, i ^ bit) for i in range(size)])


def add_one_body(scal, keep_a, recv_a, keep_b, recv_b, send_a, send_b):
    send_a[...] = (keep_a[0].astype(f32) + recv_a[0].astype(f32)).astype(bf16)
    send_b[...] = (keep_b[0].astype(f32) + recv_b[0].astype(f32)).astype(bf16)


def add_two_body(scal, keep_a, recv_a, keep_b, recv_b, far_a, far_b, own_ref, *out_refs):
    block = own_ref.shape[1]
    for path, (keep, recv, far) in enumerate(((keep_a, recv_a, far_a), (keep_b, recv_b, far_b))):
        total = keep[0].astype(f32) + recv[0].astype(f32) + far[...].astype(f32)
        own_ref[path] = total[:block]
        for k, ref in enumerate(out_refs):
            ref[path] = total[(k + 1) * block : (k + 2) * block].astype(bf16)


def add_three_body(scal, own, *refs):
    total = own[...]
    for ref in refs[:-1]:
        total = total + ref[...].astype(f32)
    refs[-1][...] = total.astype(refs[-1].dtype)


class Piece:
    def __init__(self, line, send_a, keep_a, send_b, keep_b):
        self.line = line
        self.keep_a, self.keep_b = keep_a, keep_b
        self.recv_a, self.recv_b = swap(send_a, "seq", 4, 1), swap(send_b, "seq", 4, 2)

    def one(self):
        _, depth, wq = self.keep_a.shape
        second = pl.BlockSpec((1, depth, wq), lambda i, s: (1, 0, 0))
        next_a, next_b = self.line.call(
            add_one_body, [self.keep_a, self.recv_a, self.keep_b, self.recv_b], [second] * 4,
            [sds((depth, wq), bf16)] * 2, [whole((depth, wq))] * 2, flops=2 * depth * wq, vmem=8,
            name="add_one",
        )
        self.far_a, self.far_b = swap(next_a, "seq", 4, 2), swap(next_b, "seq", 4, 1)

    def two(self):
        _, depth, wq = self.keep_a.shape
        zero = pl.BlockSpec((1, depth, wq), lambda i, s: (0, 0, 0))
        shard = (2, depth // 4, wq)
        self.own, *sends = self.line.call(
            add_two_body,
            [self.keep_a, self.recv_a, self.keep_b, self.recv_b, self.far_a, self.far_b],
            [zero] * 4 + [whole((depth, wq))] * 2,
            [sds(shard, f32)] + [sds(shard, bf16)] * 3, [whole(shard)] * 4, flops=4 * depth * wq, vmem=10,
            name="add_two",
        )
        self.got = [swap(v, "grp", 8, 2 * (k + 1)) for k, v in enumerate(sends)]

    def three(self):
        shard = self.own.shape
        (mine,) = self.line.call(
            add_three_body, [self.own, *self.got], [whole(shard)] * 4, [sds(shard, bf16)], [whole(shard)],
            flops=6 * shard[1] * shard[2], vmem=6, name="add_three",
        )
        self.parts = [mine] + [swap(mine, "seq", 4, k) for k in (1, 2, 3)]


def adam_math(grad, master, first, second, average, rate):
    new_first = beta_first * first + (1.0 - beta_first) * grad
    new_second = beta_second * second + (1.0 - beta_second) * grad * grad
    new_master = master - rate * (
        new_first / (jnp.sqrt(new_second) + adam_eps) + decay_rate * master
    )
    new_average = average_keep * average + (1.0 - average_keep) * new_master
    return new_master, new_first, new_second, new_average


def adam_body(n_alias, has_small, scal, *refs):
    parts, refs = refs[:4], refs[4:]
    if has_small:
        small, vec_in, refs = refs[0], refs[1:5], refs[5:]
    states, refs = refs[:4], refs[4 + n_alias :]
    outs, vec_outs = refs[:6], refs[6:]
    grad_ref = outs[0]
    wq = parts[0].shape[2]
    step = pl.program_id(0)
    path, half = jnp.right_shift(step, 1), jnp.bitwise_and(step, 1)
    for k, ref in enumerate(parts):
        quarter = jnp.bitwise_xor(scal[S_SEQ], k)

        @pl.when((jnp.right_shift(quarter, 1) == half) & (step < 4))
        def _(ref=ref, quarter=quarter):
            at = pl.multiple_of(jnp.bitwise_and(quarter, 1) * wq, 128)
            grad_ref[:, pl.ds(at, wq)] = ref[jnp.minimum(path, 1)].astype(f32)

    if has_small:

        @pl.when(step == 4)
        def _():
            grad_ref[...] = jnp.zeros_like(grad_ref)
            grad_ref[:, : 2 * HD] = small[...]
            grad = small[...].T[HD : HD + vec_in[0].shape[0]]
            results = adam_math(grad, *[v[...] for v in vec_in], vector_rate)
            for ref, value in zip(vec_outs, (grad, *results, results[0])):
                ref[...] = value.astype(ref.dtype)

    results = adam_math(grad_ref[...], *[v[...] for v in states], learn_rate)
    for ref, value in zip(outs[1:], (*results, results[0])):
        ref[...] = value.astype(ref.dtype)


def adam_piece(line, parts, states, outs, block_of, small=(), vecs=()):
    _, block, _ = parts[0].shape
    rows, wide = states[0].shape
    spec = pl.BlockSpec((block, D), lambda i, s: (0, block_of(i)))
    anywhere = pl.BlockSpec(memory_space=pl.ANY)
    n_alias = 0 if outs is None else 6
    shapes = [sds((rows, wide), f32)] * 5 + [sds((rows, wide), bf16)]
    args = [*parts, *small, *vecs, *states]
    n_before = len(args)
    out_specs = [spec] * 6
    if vecs:
        shapes += [sds(vecs[0].shape, f32)] * 5 + [sds(vecs[0].shape, bf16)]
        out_specs += [whole(vecs[0].shape)] * 6
    return line.call(
        partial(adam_body, n_alias, bool(vecs)),
        [*args, *(outs or [])],
        [whole(v.shape) for v in [*parts, *small, *vecs]] + [spec] * 4 + [anywhere] * n_alias,
        shapes,
        out_specs,
        grid=(5,) if vecs else (4,),
        flops=20 * 4 * block * D,
        aliases={1 + n_before + i: i for i in range(n_alias)},
        vmem=16,
        name="adam",
    )


def on_device(
    n_seq,
    n_grp,
    tokens,
    cotangent,
    seq_len,
    weight_mats,
    weight_vecs,
    master_mats,
    master_vecs,
    moment_mats,
    moment_vecs,
    square_mats,
    square_vecs,
    average_mats,
    average_vecs,
):
    rows = tokens.shape[0]
    fast = n_seq == 4 and n_grp == 8
    seq_at = lax.axis_index("seq")
    grp_at = lax.axis_index("grp")
    slot = jnp.arange(16, dtype=jnp.int32)
    seq_length = seq_len[0]
    peer = jnp.bitwise_xor(seq_at, jnp.bitwise_and(slot, 3) + 1)
    same = (peer * rows) // seq_length == (seq_at * rows) // seq_length
    before = (same & (peer < seq_at)).astype(jnp.int32)
    after = (same & (peer > seq_at)).astype(jnp.int32)
    scal = jnp.where(slot < 8, before, after)
    scal = jnp.where(slot == S_SEQ, seq_at if fast else 0, scal)
    scal = jnp.where(slot == S_GRP, grp_at, scal)
    line = Line(scal)

    w_t = weight_mats.T
    v_t13 = weight_vecs.T
    n_vec = v_t13.shape[0]
    bias_fc = v_t13[9:].reshape(1, FF)
    wide = QUAD * HD
    n_peer = n_seq - 1
    sel_rows = [D // 2, D // 2] if fast else [D]
    n_sel = len(sel_rows)
    sel_shapes = [sds((2, r, rows), bf16) for r in sel_rows]
    sel_specs = [whole(s.shape) for s in sel_shapes]

    def both(value):
        return [value, swap(value, "grp", 8, 1)] if fast else [value]

    def pair(sel):
        return [sel[1], swap(sel[0], "grp", 8, 1)] if fast else list(sel)

    def w_rows(count, at):
        return pl.BlockSpec((count, D), lambda i, s: (at(i, s), 0))

    hedge_spec = pl.BlockSpec((HD, wide), lambda i, s: ((4 * D + 2 * FF) // HD, i))
    vec_whole = whole(v_t13.shape)
    head_spec, feat_spec = along((wide, rows)), along((2 * wide, rows))
    aug_spec, quad_state = along((QUAD * AUG, rows)), along((QUAD * AUG, 2 * HD))
    st_shape = (HEADS * AUG, 2 * HD)
    got = line.call(
        partial(pre_body, n_sel),
        [tokens, cotangent, w_t, w_t, w_t, w_t, v_t13, v_t13],
        [
            whole((rows, D)),
            whole((rows, D)),
            w_rows(wide, lambda i, s: i),
            w_rows(wide, lambda i, s: N_QUAD + i),
            w_rows(wide, lambda i, s: 2 * N_QUAD + i),
            hedge_spec,
            vec_whole,
            pl.BlockSpec((n_vec, wide), lambda i, s: (0, i)),
        ],
        sel_shapes
        + [
            sds((D, rows), bf16),
            sds((D, rows), bf16),
            sds((2 * D, rows), bf16),
            sds((2 * D, rows), bf16),
            sds((D, rows), bf16),
            sds(st_shape, bf16),
        ],
        sel_specs + [head_spec, head_spec, feat_spec, feat_spec, head_spec, quad_state],
        grid=(N_QUAD,),
        scratch=[pltpu.VMEM((rows, D), bf16)],
        flops=2 * rows * D * 3 * D,
        vmem=32,
        name="pre",
    )
    sel_first = got[:n_sel]
    qt, kt, fq, fk, v_t, s_own = got[n_sel:]
    states = [swap(s_own, "seq", n_seq, k + 1) for k in range(n_peer)]
    sel_first = pair(sel_first)

    (num,) = line.call(
        local_body,
        [fq, fk, v_t],
        [feat_spec, feat_spec, head_spec],
        [sds((HEADS * AUG, rows), f32)],
        [aug_spec],
        grid=(N_QUAD,),
        flops=HEADS * 2 * rows * rows * 256,
        vmem=24,
        name="local",
    )
    got = line.call(
        partial(after_body, n_sel, n_peer),
        [*states, num, fq, tokens, w_t, v_t13],
        [whole(st_shape)] * n_peer
        + [whole(num.shape), whole(fq.shape), whole((rows, D)), w_rows(D, lambda i, s: 3), vec_whole],
        [
            sds((D, rows), f32),
            sds((16, rows), f32),
            sds((rows, D), f32),
            sds((rows, D), bf16),
            sds(st_shape, bf16),
        ]
        + sel_shapes,
        [whole((D, rows)), whole((16, rows)), whole((rows, D)), whole((rows, D)), whole(st_shape)] + sel_specs,
        scratch=[pltpu.VMEM((D, rows), bf16)],
        flops=2 * rows * D * D,
        vmem=32,
        name="after",
    )
    o_t, den, resid, h2, s_in = got[:5]
    sel_second = pair(got[5:])

    n_piece = 2
    piece = FF // n_piece
    wq = piece // 4
    acc, acts, db_fc = [], [], []
    for j in range(n_piece):
        q_of = lambda i, s, j=j: 4 * j + jnp.bitwise_xor(i, s[S_SEQ])
        out_y, out_dh, act, db = line.call(
            partial(mlp_body, j == 0),
            [h2, cotangent, w_t, w_t, bias_fc, *acc],
            [
                whole((rows, D)),
                whole((rows, D)),
                w_rows(wq, lambda i, s: 4 * D // wq + q_of(i, s)),
                w_rows(wq, lambda i, s: (4 * D + FF) // wq + q_of(i, s)),
                pl.BlockSpec((1, wq), lambda i, s: (0, q_of(i, s))),
            ]
            + [whole((rows, D))] * len(acc),
            [sds((rows, D), f32), sds((rows, D), f32), sds((2, 4, rows, wq), bf16), sds((1, piece), f32)],
            [
                whole((rows, D)),
                whole((rows, D)),
                pl.BlockSpec((2, 1, rows, wq), lambda i, s: (0, i, 0, 0)),
                pl.BlockSpec((1, wq), lambda i, s: (0, jnp.bitwise_xor(i, s[S_SEQ]))),
            ],
            grid=(4,),
            flops=4 * 2 * rows * D * piece,
            vmem=32,
            name="mlp",
        )
        acc = [out_y, out_dh]
        db_fc.append(db)
        acts.append(both(act))

    grads = [mlp_grads(line, sel_first, sel_second, acts[0])]
    if fast:
        first = Piece(line, *grads[0])
    block_output, d_resid, d_attn, rho, ds_own, sums = line.call(
        back_body,
        [*acc, resid, cotangent, w_t, v_t13, o_t, den, fq],
        [whole((rows, D))] * 4
        + [w_rows(D, lambda i, s: 3), vec_whole, whole((D, rows)), whole((16, rows)), whole((2 * D, rows))],
        [
            sds((rows, D), bf16),
            sds((rows, D), f32),
            sds((rows, D), bf16),
            sds((HEADS * AUG, rows), bf16),
            sds(st_shape, bf16),
            sds((4, D), f32),
        ],
        [whole((rows, D))] * 3 + [whole((HEADS * AUG, rows)), whole(st_shape), whole((4, D))],
        scratch=[pltpu.VMEM((D, rows), bf16)],
        flops=2 * rows * D * D,
        vmem=32,
        name="back",
    )
    back_states = [swap(ds_own, "seq", n_seq, k + 1) for k in range(n_peer)]
    da = both(d_attn)
    grads.append(mlp_grads(line, sel_first, sel_second, acts[1]))
    if fast:
        second = Piece(line, *grads[1])
        first.one()

    dp, dm, db_qkv = line.call(
        partial(attend_back_body, n_peer),
        [*back_states, fq, fk, v_t, rho, s_in, qt, kt, w_t],
        [quad_state] * n_peer
        + [feat_spec, feat_spec, head_spec, aug_spec, quad_state, head_spec, head_spec, hedge_spec],
        [sds((3, D, rows), bf16), sds((D, HD), f32), sds((D, 3), f32)],
        [along((3, wide, rows), 1), along((wide, HD)), along((wide, 3))],
        grid=(N_QUAD,),
        flops=HEADS * 2 * rows * rows * 768,
        vmem=32,
        name="attend_back",
    )
    dp_both = both(dp)
    if fast:
        second.one()
        first.two()
    db_fc_rows = jnp.concatenate(db_fc, axis=1).reshape(FF // D, D)
    input_grad, *small = line.call(
        partial(input_body, fast),
        [dp, w_t, tokens, d_resid, v_t13, sums, db_fc_rows, db_qkv, dm],
        [
            along((1, D, rows)),
            w_rows(D, lambda i, s: i),
            whole((rows, D)),
            whole((rows, D)),
            vec_whole,
            whole((4, D)),
            whole((FF // D, D)),
            whole((D, 3)),
            whole((D, HD)),
        ],
        [sds((rows, D), bf16)] + [sds((1, r, 2 * HD), f32) for r in sel_rows],
        [whole((rows, D))] + [whole((1, r, 2 * HD)) for r in sel_rows],
        grid=(3,),
        scratch=[pltpu.VMEM((rows, D), f32)],
        flops=2 * rows * D * 3 * D,
        vmem=32,
        name="input",
    )
    tail = tail_grads(line, sel_first, sel_second, dp_both, da)

    states_m = [master_mats, moment_mats, square_mats, average_mats]
    states_v = [v.T for v in (master_vecs, moment_vecs, square_vecs, average_vecs)]
    if fast:
        last = Piece(line, *tail)
        theirs, mine = small
        total = mine[0] + swap(theirs[0].astype(bf16), "grp", 8, 1).astype(f32)
        for bit in (1, 2):
            total = total + swap(total.astype(bf16), "seq", 4, bit).astype(f32)
        total = total.reshape(4, D // 8, 2 * HD)
        low = total.astype(bf16)
        small_own = total[0]
        for k in (1, 2, 3):
            small_own = small_own + swap(low[k], "grp", 8, 2 * k).astype(f32)

        def at_piece(j):
            return lambda i: jnp.where(i < 2, (4 * D + FF) // D + 2 * j + i, 4 + 2 * j + i - 2)

        second.two()
        first.three()
        last.one()
        second.three()
        outs = adam_piece(line, first.parts, states_m, None, at_piece(0))
        last.two()
        outs = adam_piece(line, second.parts, states_m, outs, at_piece(1))
        last.three()
        outs = adam_piece(
            line, last.parts, states_m, outs, lambda i: jnp.where(i < 4, i, (4 * D + 2 * FF) // D),
            small=[small_own], vecs=states_v,
        )
        mats, vecs = outs[:6], [v.T for v in outs[6:]]
    else:

        def joined(send, keep, order):
            parts = {**dict(zip(order[:2], send)), **dict(zip(order[2:], keep))}
            return [parts[q] for q in range(4)]

        fc, dn = [], []
        for send_a, keep_a, send_b, keep_b in grads:
            dn += joined(send_a, keep_a, (1, 3, 0, 2))
            fc += joined(send_b, keep_b, (2, 3, 0, 1))
        send_a, keep_a, send_b, keep_b = tail
        qkvo = joined(send_a, keep_a, (1, 3, 0, 2)) + joined(send_b, keep_b, (2, 3, 0, 1))
        small = small[0][0]
        grad = jnp.concatenate([*qkvo, *fc, *dn, small[:, :HD].astype(bf16)], axis=1)
        own = lax.psum_scatter(grad, "grp", scatter_dimension=0, tiled=True)
        own = lax.psum(own, "seq").astype(f32)
        own_v = lax.psum(lax.psum_scatter(small, "grp", scatter_dimension=0, tiled=True), "seq")
        own_v = own_v[:, HD : HD + n_vec]
        results = adam_math(own, *states_m, learn_rate)
        mats = [own, *results, results[0].astype(bf16)]
        results = adam_math(own_v.T, *states_v, vector_rate)
        vecs = [own_v, *[v.T for v in (*results, results[0].astype(bf16))]]
    flat = [x for pair_ in zip(mats, vecs) for x in pair_]
    return (block_output, input_grad, *flat)


def solution(mesh):
    tok = P(("grp", "seq"), None)
    own = P("grp", None)
    in_specs = (tok, tok, P("grp"), P(), P()) + (own,) * 8
    out_specs = (tok, tok) + (own,) * 12
    body = partial(on_device, mesh.shape["seq"], mesh.shape["grp"])
    return jax.shard_map(body, mesh=mesh, in_specs=in_specs, out_specs=out_specs, check_vma=False)
```

```python
from functools import partial

import jax
import jax.numpy as jnp
from jax import lax
from jax.experimental import pallas as pl
from jax.experimental.pallas import tpu as pltpu
from jax.sharding import PartitionSpec as P

D = 768
HEADS = 12
HD = 64
FF = 3072
QUAD = 4
N_QUAD = HEADS // QUAD
AUG = 80

norm_eps = 1e-05
adam_eps = 1e-08
beta_first = 0.5
beta_second = 0.5
learn_rate = 0.01
vector_rate = 0.06
decay_rate = 0.1
average_keep = 0.9

f32 = jnp.float32
bf16 = jnp.bfloat16

S_SEQ, S_GRP, S_MASK, S_BACK = 0, 1, 4, 8

MIB = 1024 * 1024


def dot_nn(a, b):
    return lax.dot_general(a, b, (((1,), (0,)), ((), ())), preferred_element_type=f32)


def dot_nt(a, b):
    return lax.dot_general(a, b, (((1,), (1,)), ((), ())), preferred_element_type=f32)


def dot_tn(a, b):
    return lax.dot_general(a, b, (((0,), (0,)), ((), ())), preferred_element_type=f32)


def whole(shape):
    return pl.BlockSpec(tuple(shape), lambda *_: (0,) * len(shape))


def along(block, axis=0):
    return pl.BlockSpec(tuple(block), lambda i, s: tuple(i if d == axis else 0 for d in range(len(block))))


def sds(shape, dtype):
    return jax.ShapeDtypeStruct(tuple(shape), dtype)


class Line:
    def __init__(self, scal):
        self.scal = scal
        self.stay = set()

    def wait(self, *values):
        self.scal, values = lax.optimization_barrier((self.scal, values))
        return values

    def call(self, body, args, in_specs, outs, out_specs, grid=(1,), scratch=(), vmem=32,
             hold=0, aliases=None, name=None):
        args = [pltpu.with_memory_space_constraint(a, pltpu.HBM) if id(a) in self.stay else a for a in args]
        got = pl.pallas_call(
            body,
            out_shape=tuple(outs),
            grid_spec=pltpu.PrefetchScalarGridSpec(
                num_scalar_prefetch=1,
                grid=grid,
                in_specs=list(in_specs),
                out_specs=tuple(out_specs),
                scratch_shapes=list(scratch),
            ),
            compiler_params=pltpu.CompilerParams(
                dimension_semantics=("arbitrary",) * len(grid), vmem_limit_bytes=vmem * MIB
            ),
            cost_estimate=pl.CostEstimate(
                flops=hold * 10**9, bytes_accessed=1024, transcendentals=0
            ),
            input_output_aliases=aliases or {},
            name=name,
        )(self.scal, *args)
        self.scal, got = lax.optimization_barrier((self.scal, got))
        return got


def store_sel(refs, at, values, scal):
    if len(refs) == 1:
        refs[0][at] = values
        return
    block = D // 8
    for j in range(8):
        rel = jnp.bitwise_xor(scal[S_GRP], j)
        place = pl.multiple_of(jnp.right_shift(rel, 1) * block, block)
        odd = jnp.bitwise_and(rel, 1)
        part = values[j * block : (j + 1) * block, :]

        @pl.when(odd == 1)
        def _(part=part, place=place):
            refs[0][at, pl.ds(place, block), :] = part

        @pl.when(odd == 0)
        def _(part=part, place=place):
            refs[1][at, pl.ds(place, block), :] = part


def normalize(values):
    average = jnp.mean(values, axis=1, keepdims=True)
    centered = values - average
    variance = jnp.mean(centered * centered, axis=1, keepdims=True)
    inverse = lax.rsqrt(variance + norm_eps)
    return centered * inverse, inverse


def quad_maps(hedge_t):
    wide = QUAD * HD
    row = lax.broadcasted_iota(jnp.int32, (wide, HD), 0)
    col = lax.broadcasted_iota(jnp.int32, (wide, HD), 1)
    spread = (jnp.bitwise_and(row, HD - 1) == col).astype(bf16)
    tiled = dot_nn(spread, hedge_t)
    big_r = lax.broadcasted_iota(jnp.int32, (wide, wide), 0)
    big_c = lax.broadcasted_iota(jnp.int32, (wide, wide), 1)
    same = jnp.right_shift(big_r, 6) == jnp.right_shift(big_c, 6)
    return jnp.where(same, tiled, 0.0)


def ones_rows(count):
    return (lax.broadcasted_iota(jnp.int32, (AUG - HD, count), 0) == 0).astype(f32).astype(bf16)


def rows_up(values):
    return jnp.concatenate([values, jnp.zeros((3, values.shape[1]), f32)], axis=0).T


def pre_body(n_sel, scal, x_ref, g_ref, wq_ref, wk_ref, wv_ref, hedge_ref, vt_ref, vq_ref, *refs):
    sel = refs[:n_sel]
    qt_ref, kt_ref, fq_ref, fk_ref, vt_out, s_ref, h1_ref = refs[n_sel:]
    rows = x_ref.shape[0]

    @pl.when(pl.program_id(0) == 0)
    def _():
        normed, _ = normalize(x_ref[...].astype(f32))
        vt = vt_ref[...].astype(f32)
        h1 = (normed * vt[0:1] + vt[1:2]).astype(bf16)
        h1_ref[...] = h1
        store_sel(sel, 0, g_ref[...].T, scal)
        store_sel(sel, 1, h1.T, scal)

    h1 = h1_ref[...]
    bias = rows_up(vq_ref[...].astype(f32))
    v_t = (dot_nt(wv_ref[...], h1) + bias[:, 8:9]).astype(bf16)
    vt_out[...] = v_t
    maps = quad_maps(hedge_ref[...]).astype(bf16)
    maps2 = jnp.concatenate([maps, maps], axis=1)
    extra = ones_rows(rows)
    for which, (w_ref, save, feat) in enumerate(((wk_ref, kt_ref, fk_ref), (wq_ref, qt_ref, fq_ref))):
        pt = dot_nt(w_ref[...], h1) + bias[:, 7 - which : 8 - which]
        high = pt.astype(bf16)
        save[...] = high
        rest = (pt - high.astype(f32)).astype(bf16)
        scores = dot_nn(maps2, jnp.concatenate([high, rest], axis=0))
        for h in range(QUAD):
            s = scores[h * HD : (h + 1) * HD, :]
            top = jnp.max(s, axis=0, keepdims=True)
            bottom = jnp.min(s, axis=0, keepdims=True)
            pos = jnp.exp(s - top)
            neg = jnp.exp(bottom - s)
            pos = pos * (1.0 / jnp.sum(pos, axis=0, keepdims=True))
            neg = neg * (1.0 / jnp.sum(neg, axis=0, keepdims=True))
            both = jnp.concatenate([pos, neg], axis=0).astype(bf16)
            feat[h * 2 * HD : (h + 1) * 2 * HD, :] = both
            if which == 0:
                va = jnp.concatenate([v_t[h * HD : (h + 1) * HD, :], extra], axis=0)
                s_ref[h * AUG : (h + 1) * AUG, :] = dot_nt(va, both).astype(bf16)


def tri_mask(half):
    return lax.broadcasted_iota(jnp.int32, (half, half), 0) <= lax.broadcasted_iota(
        jnp.int32, (half, half), 1
    )


def masked_pair(left0, left1, right, keep):
    half = right.shape[1] // 2
    full = dot_tn(left0, right)
    low = dot_tn(left1, right[:, half:])
    diag0 = jnp.where(keep, full[:, :half], 0.0).astype(bf16)
    above = full[:, half:].astype(bf16)
    diag1 = jnp.where(keep, low, 0.0).astype(bf16)
    return diag0, above, diag1


def local_body(scal, fq_ref, fk_ref, vt_ref, num_ref):
    rows = fq_ref.shape[1]
    half = rows // 2
    keep = tri_mask(half)
    extra = ones_rows(rows)
    for h in range(QUAD):
        fq = fq_ref[h * 2 * HD : (h + 1) * 2 * HD, :]
        fk = fk_ref[h * 2 * HD : (h + 1) * 2 * HD, :]
        va = jnp.concatenate([vt_ref[h * HD : (h + 1) * HD, :], extra], axis=0)
        a00, a01, a11 = masked_pair(fk[:, :half], fk[:, half:], fq, keep)
        num_ref[h * AUG : (h + 1) * AUG, :half] = dot_nn(va[:, :half], a00)
        num_ref[h * AUG : (h + 1) * AUG, half:] = dot_nn(va[:, :half], a01) + dot_nn(va[:, half:], a11)


def weighted_state(scal, slot, parts):
    total = None
    for k, part in enumerate(parts):
        term = scal[slot + k].astype(f32) * part.astype(f32)
        total = term if total is None else total + term
    return total.astype(bf16)


def after_body(n_sel, n_parts, scal, *refs):
    parts = refs[:n_parts]
    num_ref, fq_ref, x_ref, w_ref, vt_ref = refs[n_parts : n_parts + 5]
    o_ref, den_ref, r_ref, h2_ref, sin_ref = refs[n_parts + 5 + n_sel : n_parts + 10 + n_sel]
    sel = refs[-1 - n_sel : -1]
    ob_ref = refs[-1]
    vt = vt_ref[...].astype(f32)
    state = weighted_state(scal, S_MASK, [p[...] for p in parts])
    sin_ref[...] = state
    for h in range(HEADS):
        num = num_ref[h * AUG : (h + 1) * AUG, :] + dot_nn(
            state[h * AUG : (h + 1) * AUG, :], fq_ref[h * 2 * HD : (h + 1) * 2 * HD, :]
        )
        den = num[HD : HD + 1, :]
        out = num[:HD, :] * (1.0 / den)
        o_ref[h * HD : (h + 1) * HD, :] = out
        den_ref[h : h + 1, :] = den
        ob_ref[h * HD : (h + 1) * HD, :] = out.astype(bf16)
    obt = ob_ref[...]
    store_sel(sel, 0, obt, scal)
    r = x_ref[...].astype(f32) + dot_nt(obt.T, w_ref[...]) + vt[4:5]
    r_ref[...] = r
    normed, _ = normalize(r)
    h2 = (normed * vt[2:3] + vt[3:4]).astype(bf16)
    h2_ref[...] = h2
    store_sel(sel, 1, h2.T, scal)


gelu_c = 0.7978845608028654
gelu_k = 0.044715


def mlp_body(first, scal, h2_ref, g_ref, wf_ref, wd_ref, bias_ref, *refs):
    if first:
        out_ref, dh_ref, act_ref, db_ref = refs
    else:
        out_in, dh_in, out_ref, dh_ref, act_ref, db_ref = refs
    u = dot_nt(h2_ref[...], wf_ref[...]) + bias_ref[...].astype(f32)
    de = dot_nt(g_ref[...], wd_ref[...])
    uu = u * u
    t = jnp.tanh(gelu_c * u * (1.0 + gelu_k * uu))
    half_t = 0.5 * (1.0 + t)
    e = (u * half_t).astype(bf16)
    slope = half_t + 0.5 * u * (1.0 - t * t) * (gelu_c * (1.0 + 3.0 * gelu_k * uu))
    du = (de * slope).astype(bf16)
    act_ref[0, 0] = e
    act_ref[1, 0] = du
    db_ref[...] = jnp.sum(du.astype(f32), axis=0, keepdims=True)
    add_out = dot_nn(e, wd_ref[...])
    add_dh = dot_nn(du, wf_ref[...])
    step = pl.program_id(0)

    @pl.when(step == 0)
    def _():
        if first:
            out_ref[...] = add_out
            dh_ref[...] = add_dh
        else:
            out_ref[...] = out_in[...] + add_out
            dh_ref[...] = dh_in[...] + add_dh

    @pl.when(step > 0)
    def _():
        out_ref[...] += add_out
        dh_ref[...] += add_dh


def back_body(scal, out_ref, dh_ref, r_ref, g_ref, w_ref, vt_ref, o_ref, den_ref, fq_ref, y_ref, dr_ref,
              da_ref, rho_ref, ds_ref, sums_ref, do_ref):
    vt = vt_ref[...].astype(f32)
    r = r_ref[...]
    y_ref[...] = (r + out_ref[...] + vt[5:6]).astype(bf16)
    grad_out = g_ref[...].astype(f32)
    normed, inverse = normalize(r)
    up = dh_ref[...]
    dn = up * vt[2:3]
    dr = grad_out + inverse * (
        dn - jnp.mean(dn, axis=1, keepdims=True) - normed * jnp.mean(dn * normed, axis=1, keepdims=True)
    )
    dr_ref[...] = dr
    da = dr.astype(bf16)
    da_ref[...] = da.T
    sums_ref[...] = jnp.concatenate(
        [
            jnp.sum(up * normed, axis=0, keepdims=True),
            jnp.sum(up, axis=0, keepdims=True),
            jnp.sum(da.astype(f32), axis=0, keepdims=True),
            jnp.sum(grad_out, axis=0, keepdims=True),
        ],
        axis=0,
    )
    do_ref[...] = dot_nn(da, w_ref[...]).astype(bf16).T
    rows = r.shape[0]
    zero_row = lax.broadcasted_iota(jnp.int32, (AUG - HD, rows), 0) == 0
    for h in range(HEADS):
        dout = do_ref[h * HD : (h + 1) * HD, :].astype(f32)
        inv = 1.0 / den_ref[h : h + 1, :]
        rho = (dout * inv).astype(bf16)
        c = -jnp.sum(dout * o_ref[h * HD : (h + 1) * HD, :], axis=0, keepdims=True) * inv
        extra = jnp.where(zero_row, jnp.broadcast_to(c, (AUG - HD, rows)), 0.0).astype(bf16)
        ra = jnp.concatenate([rho, extra], axis=0)
        rho_ref[h * AUG : (h + 1) * AUG, :] = ra
        ds_ref[h * AUG : (h + 1) * AUG, :] = dot_nt(ra, fq_ref[h * 2 * HD : (h + 1) * 2 * HD, :]).astype(bf16)


def feature_back(feat, upstream):
    pos, neg = feat[:HD].astype(f32), feat[HD:].astype(f32)
    up_pos, up_neg = upstream[:HD], upstream[HD:]
    return pos * (up_pos - jnp.sum(pos * up_pos, axis=0, keepdims=True)) - neg * (
        up_neg - jnp.sum(neg * up_neg, axis=0, keepdims=True)
    )


def attend_back_body(n_parts, scal, *refs):
    parts = refs[:n_parts]
    (fq_ref, fk_ref, vt_ref, rho_ref, sin_ref, qt_ref, kt_ref, hedge_ref, da_ref, dp_ref, dm_ref,
     db_ref) = refs[n_parts:]
    dp_ref[3] = da_ref[...]
    rows = fq_ref.shape[1]
    half = rows // 2
    keep = tri_mask(half)
    extra = ones_rows(rows)
    back_state = weighted_state(scal, S_BACK, [p[...] for p in parts])
    ds_q, ds_k = [], []
    for h in range(QUAD):
        fq = fq_ref[h * 2 * HD : (h + 1) * 2 * HD, :]
        fk = fk_ref[h * 2 * HD : (h + 1) * 2 * HD, :]
        head = slice(h * HD, (h + 1) * HD)
        aug = slice(h * AUG, (h + 1) * AUG)
        va = jnp.concatenate([vt_ref[head, :], extra], axis=0)
        ra = rho_ref[aug, :]
        state, back = sin_ref[aug, :], back_state[aug, :]
        a00, a01, a11 = masked_pair(fk[:, :half], fk[:, half:], fq, keep)
        g00, g01, g11 = masked_pair(va[:, :half], va[:, half:], ra, keep)
        far = dot_tn(state, ra)
        left = far[:, :half] + dot_nn(fk[:, :half], g00)
        right = far[:, half:] + dot_nn(fk[:, :half], g01) + dot_nn(fk[:, half:], g11)
        dfq = jnp.concatenate([left, right], axis=1)
        far_k = dot_tn(back, va)
        left = far_k[:, :half] + dot_nt(fq[:, :half], g00) + dot_nt(fq[:, half:], g01)
        right = far_k[:, half:] + dot_nt(fq[:, half:], g11)
        dfk = jnp.concatenate([left, right], axis=1)
        far_v = dot_nn(back, fk)[:HD]
        rv = ra[:HD]
        left = far_v[:, :half] + dot_nt(rv[:, :half], a00) + dot_nt(rv[:, half:], a01)
        right = far_v[:, half:] + dot_nt(rv[:, half:], a11)
        dp_ref[2, head, :] = jnp.concatenate([left, right], axis=1).astype(bf16)
        dsq = feature_back(fq, dfq).astype(bf16)
        dsk = feature_back(fk, dfk).astype(bf16)
        ds_q.append(dsq)
        ds_k.append(dsk)
        dm_ref[head, :] = dot_nt(qt_ref[head, :], dsq) + dot_nt(kt_ref[head, :], dsk)
    maps = quad_maps(hedge_ref[...]).T.astype(bf16)
    dq = dot_nn(maps, jnp.concatenate(ds_q, axis=0)).astype(bf16)
    dk = dot_nn(maps, jnp.concatenate(ds_k, axis=0)).astype(bf16)
    dp_ref[0] = dq
    dp_ref[1] = dk
    db_ref[...] = jnp.concatenate(
        [jnp.sum(v.astype(f32), axis=1, keepdims=True) for v in (dq, dk, dp_ref[2])], axis=1
    )


def input_body(fast, scal, dp_ref, w_ref, x_ref, dr_ref, vt_ref, sums_ref, dbfc_ref, db_ref, dm_ref, *refs):
    gin_ref, *small_refs, acc_ref = refs
    step = pl.program_id(0)
    part = dot_tn(dp_ref[0], w_ref[...])

    @pl.when(step == 0)
    def _():
        acc_ref[...] = part

    @pl.when(step == 1)
    def _():
        acc_ref[...] += part

    @pl.when(step == 2)
    def _():
        vt = vt_ref[...].astype(f32)
        up = acc_ref[...] + part
        normed, inverse = normalize(x_ref[...].astype(f32))
        dn = up * vt[0:1]
        gin = dr_ref[...] + inverse * (
            dn - jnp.mean(dn, axis=1, keepdims=True) - normed * jnp.mean(dn * normed, axis=1, keepdims=True)
        )
        gin_ref[...] = gin.astype(bf16)
        rows16 = jnp.concatenate(
            [
                jnp.sum(up * normed, axis=0, keepdims=True),
                jnp.sum(up, axis=0, keepdims=True),
                sums_ref[...],
                jnp.zeros((3, D), f32),
                dbfc_ref[...],
                jnp.zeros((3, D), f32),
            ],
            axis=0,
        )
        cols = rows16.T
        lane = lax.broadcasted_iota(jnp.int32, (D, HD), 1)
        tail = jnp.concatenate([cols, jnp.zeros((D, HD - 16), f32)], axis=1)
        for k in range(3):
            tail = jnp.where(lane == 6 + k, db_ref[:, k : k + 1], tail)
        small = jnp.concatenate([dm_ref[...], tail], axis=1)
        store_sel(small_refs, 0, small, scal)


def mlp_grads_body(by_z, scal, *refs):
    sels, acts_a, acts_b, sels_h = refs[0:2], refs[2:4], refs[4:6], refs[6:8]
    send, keep = refs[8:]
    block = D // 8

    def total(lefts, rights):
        return (dot_nn(lefts[0][0], rights[0][0, 0]) + dot_nn(lefts[1][0], rights[1][0, 0])).astype(bf16)

    for path, value in enumerate((total(sels, acts_a), total(sels_h, acts_b))):
        rows = slice(path * block, (path + 1) * block)

        def part(z, value=value):
            return value[z * block : (z + 1) * block]

        if by_z:
            for at, z in enumerate((3, 1)):
                send[at, rows, :] = part(z)
            for at, z in enumerate((2, 0)):
                keep[at, rows, :] = part(z)
        else:

            @pl.when(pl.program_id(0) < 2)
            def _(part=part, rows=rows):
                for at, z in enumerate((3, 1, 2, 0)):
                    send[at, rows, :] = part(z)

            @pl.when(pl.program_id(0) >= 2)
            def _(part=part, rows=rows):
                for at, z in enumerate((3, 1, 2, 0)):
                    keep[at, rows, :] = part(z)


def mlp_grads(line, by_z, sels, acts):
    _, depth, rows = sels[0].shape
    wq = acts[0].shape[3]
    half = sds((8, 2 * (D // 8), wq), bf16)

    def quarter(i):
        high, low = 1 - i // 2, 1 - lax.rem(i, 2)
        return high + 2 * low if by_z else 2 * high + low

    def act(path):
        return pl.BlockSpec((1, 1, rows, wq), lambda i, s: (path, quarter(i), 0, 0))

    def sel(slot):
        return pl.BlockSpec((1, depth, rows), lambda i, s: (slot, 0, 0))

    if by_z:
        out_specs = [along((2,) + half.shape[1:])] * 2
    else:
        out_specs = [
            pl.BlockSpec((4,) + half.shape[1:], lambda i, s: (jnp.minimum(i, 1), 0, 0)),
            pl.BlockSpec((4,) + half.shape[1:], lambda i, s: (jnp.maximum(i - 2, 0), 0, 0)),
        ]
    return line.call(
        partial(mlp_grads_body, by_z),
        [*sels, *acts, *acts, *sels],
        [sel(0)] * 2 + [act(0)] * 2 + [act(1)] * 2 + [sel(3)] * 2,
        [half] * 2,
        out_specs,
        grid=(4,),
        vmem=20,
        name="mlp_grads",
    )


def pack_rows(values, count):
    return jnp.concatenate([values[b * count : (b + 1) * count] for b in range(3)], axis=1)


def unpack_rows(values):
    return jnp.concatenate([values[:, b * 128 : (b + 1) * 128] for b in range(3)], axis=0)


def order_a(i):
    return jnp.where(i < 2, 2 * i + 1, 2 * i - 4)


def order_b(i):
    return jnp.where(i < 2, i + 2, i - 2)


def tail_grads_body(scal, *refs):
    h1, ob, dqk, dvo = refs[0:2], refs[2:4], refs[4:6], refs[6:8]
    small_own, small_other, send_a, keep_a, send_b, keep_b, small_ref = refs[8:]
    step = pl.program_id(0)
    wq = send_a.shape[1]
    qb = jnp.bitwise_xor(order_b(step), scal[S_SEQ])
    at = pl.multiple_of(jnp.bitwise_and(step, 1) * wq, wq)

    def total(lefts, rights):
        return (dot_nt(lefts[0][0], rights[0][0]) + dot_nt(lefts[1][0], rights[1][0])).astype(bf16)

    def put(send, keep, value):
        @pl.when(step < 2)
        def _():
            send[pl.ds(at, wq), :] = value

        @pl.when(step >= 2)
        def _():
            keep[pl.ds(at, wq), :] = value

    put(send_a, keep_a, total(h1, dqk))

    @pl.when(qb < 2)
    def _():
        put(send_b, keep_b, total(h1, dvo))

    @pl.when(qb >= 2)
    def _():
        put(send_b, keep_b, total(ob, dvo))

    @pl.when(step == 0)
    def _():
        small = pack_rows(small_own[0] + small_other[0].astype(f32), 128)
        small_ref[...] = small
        send_a[2 * wq :, :] = small.astype(bf16)


def tail_grads(line, sels, dp, small):
    _, depth, rows = sels[0].shape
    wq = D // 2
    dp = [v.reshape(8, wq, rows) for v in dp]

    def sel(slot):
        return pl.BlockSpec((1, depth, rows), lambda i, s: (slot, 0, 0))

    outs = [
        sds((2 * wq + 128, wq), bf16), sds((2 * wq, wq), bf16),
        sds((2 * wq, wq), bf16), sds((2 * wq, wq), bf16), sds((128, wq), f32),
    ]
    return line.call(
        tail_grads_body,
        [*sels, *sels, *dp, *dp, *small],
        [sel(1)] * 2
        + [sel(2)] * 2
        + [pl.BlockSpec((1, wq, rows), lambda i, s: (jnp.bitwise_xor(order_a(i), s[S_SEQ]), 0, 0))] * 2
        + [pl.BlockSpec((1, wq, rows), lambda i, s: (4 + jnp.bitwise_xor(order_b(i), s[S_SEQ]), 0, 0))] * 2
        + [whole(small[0].shape)] * 2,
        outs,
        [whole(o.shape) for o in outs],
        grid=(4,),
        vmem=20,
        name="tail_grads",
    )


def swap(value, axis, size, bit):
    return lax.ppermute(value, axis, [(i, i ^ bit) for i in range(size)])


def halve_body(scal, keep_ref, recv_ref, send_ref, left_ref):
    half = send_ref.shape[0]
    send_ref[...] = (keep_ref[:half].astype(f32) + recv_ref[:half].astype(f32)).astype(bf16)
    left_ref[...] = (keep_ref[half:].astype(f32) + recv_ref[half:].astype(f32)).astype(left_ref.dtype)


class Halves:
    def __init__(self, line, send, keep, stages):
        self.line, self.keep, self.stages = line, keep, list(stages)
        self.recv = swap(send, *self.stages.pop(0))

    def step(self, hold=0):
        count, rows, wq = self.keep.shape
        shape = (count // 2, rows, wq)
        send, self.keep = self.line.call(
            halve_body, [self.keep, self.recv], [whole(self.keep.shape)] * 2,
            [sds(shape, bf16), sds(shape, self.keep.dtype)], [whole(shape)] * 2,
            vmem=2 + count * rows * wq * 12 // MIB, hold=hold, name="halve",
        )
        self.recv = swap(send, *self.stages.pop(0))


def final_body(scal, *refs):
    out = refs[-1]
    for j in range(2):
        out[j] = (refs[2 * j][0].astype(f32) + refs[2 * j + 1][0].astype(f32)).astype(bf16)


def final_both(line, pieces):
    shape = (2,) + pieces[0].keep.shape[1:]
    (mine,) = line.call(
        final_body, [v for p in pieces for v in (p.keep, p.recv)], [whole((1,) + shape[1:])] * 4,
        [sds(shape, bf16)], [whole(shape)], vmem=4, name="final",
    )
    return mine.reshape(4, D // 8, shape[2])


def tail_one_body(scal, keep_a, recv_a, keep_b, recv_b, small_ref, send_a, send_b):
    wq = send_b.shape[0]
    send_a[:wq, :] = (keep_a[wq : 2 * wq].astype(f32) + recv_a[wq : 2 * wq].astype(f32)).astype(bf16)
    send_a[wq:, :] = (small_ref[...] + recv_a[2 * wq :].astype(f32)).astype(bf16)
    send_b[...] = (keep_b[wq:].astype(f32) + recv_b[wq:].astype(f32)).astype(bf16)


def tail_two_body(scal, keep_a, recv_a, keep_b, recv_b, small_ref, far_a, far_b, send_ref, left_ref):
    wq = far_b.shape[0]
    block = D // 8
    small = small_ref[...] + recv_a[2 * wq :].astype(f32) + far_a[wq:].astype(f32)
    small = unpack_rows(small)
    first = keep_a[:wq].astype(f32) + recv_a[:wq].astype(f32) + far_a[:wq].astype(f32)
    second = keep_b[:wq].astype(f32) + recv_b[:wq].astype(f32) + far_b[...].astype(f32)
    for ref, order in ((send_ref, (3, 1)), (left_ref, (2, 0))):
        for at, z in enumerate(order):
            rows = slice(z * block, (z + 1) * block)
            ref[at, :block, :] = first[rows].astype(ref.dtype)
            ref[at, block : 2 * block, :] = second[rows].astype(ref.dtype)
            ref[at, 2 * block :, :] = pack_rows(small[rows], block // 3).astype(ref.dtype)


def tail_final_body(scal, keep_ref, recv_ref, mine_ref, small_ref):
    block = mine_ref.shape[1]
    total = keep_ref[0] + recv_ref[0].astype(f32)
    mine_ref[0] = total[:block].astype(bf16)
    mine_ref[1] = total[block : 2 * block].astype(bf16)
    small_ref[...] = unpack_rows(total[2 * block :])


def tail_one(line, tail):
    send_a, keep_a, send_b, keep_b, small = tail
    wq = D // 2
    recv_a, recv_b = swap(send_a, "seq", 4, 1), swap(send_b, "seq", 4, 2)
    shapes = [sds((wq + 128, wq), bf16), sds((wq, wq), bf16)]

    def first():
        args = [keep_a, recv_a, keep_b, recv_b, small]
        next_a, next_b = line.call(
            tail_one_body, args, [whole(v.shape) for v in args], shapes, [whole(v.shape) for v in shapes],            vmem=12, name="tail_one",
        )
        return swap(next_a, "seq", 4, 2), swap(next_b, "seq", 4, 1)

    def second(far_a, far_b):
        args = [keep_a, recv_a, keep_b, recv_b, small, far_a, far_b]
        shape = (2, 2 * (D // 8) + D // 24, wq)
        send, keep = line.call(
            tail_two_body, args, [whole(v.shape) for v in args], [sds(shape, bf16), sds(shape, f32)],
            [whole(shape)] * 2, vmem=16, name="tail_two",
        )
        return Halves(line, send, keep, [("grp", 8, 2), ("grp", 8, 4)])

    return first, second


def tail_final(line, piece):
    wq = piece.keep.shape[2]
    shapes = [sds((2, D // 8, wq), bf16), sds((D // 8, 2 * HD), f32)]
    return line.call(
        tail_final_body, [piece.keep, piece.recv], [whole(piece.keep.shape)] * 2, shapes,
        [whole(v.shape) for v in shapes], vmem=4, name="tail_final",
    )


def gather_parts(mine):
    return [mine] + [swap(mine, "seq", 4, k) for k in (1, 2, 3)]


def adam_math(grad, master, first, second, average, rate):
    new_first = beta_first * first + (1.0 - beta_first) * grad
    new_second = beta_second * second + (1.0 - beta_second) * grad * grad
    new_master = master - rate * (
        new_first / (jnp.sqrt(new_second) + adam_eps) + decay_rate * master
    )
    new_average = average_keep * average + (1.0 - average_keep) * new_master
    return new_master, new_first, new_second, new_average


def adam_body(n_alias, has_small, scal, *refs):
    parts, refs = refs[:4], refs[4:]
    if has_small:
        small, vec_in, refs = refs[0], refs[1:5], refs[5:]
    states, refs = refs[:4], refs[4 + n_alias :]
    outs, vec_outs = refs[:6], refs[6:]
    grad_ref = outs[0]
    count, _, wq = parts[0].shape
    step = pl.program_id(0)
    path, half = jnp.right_shift(step, 1), jnp.bitwise_and(step, 1)
    for k, ref in enumerate(parts):
        quarter = jnp.bitwise_xor(scal[S_SEQ], k)

        @pl.when((jnp.right_shift(quarter, 1) == half) & (step < 2 * count))
        def _(ref=ref, quarter=quarter):
            at = pl.multiple_of(jnp.bitwise_and(quarter, 1) * wq, 128)
            grad_ref[:, pl.ds(at, wq)] = ref[jnp.minimum(path, count - 1)].astype(f32)

    if has_small:

        @pl.when(step == 2 * count)
        def _():
            grad_ref[...] = jnp.zeros_like(grad_ref)
            grad_ref[:, : 2 * HD] = small[...]
            grad = small[...].T[HD : HD + vec_in[0].shape[0]]
            results = adam_math(grad, *[v[...] for v in vec_in], vector_rate)
            for ref, value in zip(vec_outs, (grad, *results, results[0])):
                ref[...] = value.astype(ref.dtype)

    results = adam_math(grad_ref[...], *[v[...] for v in states], learn_rate)
    for ref, value in zip(outs[1:], (*results, results[0])):
        ref[...] = value.astype(ref.dtype)


def adam_piece(line, parts, states, outs, block_of, small=(), vecs=()):
    count, block, _ = parts[0].shape
    rows, wide = states[0].shape
    spec = pl.BlockSpec((block, D), lambda i, s: (0, block_of(i)))
    anywhere = pl.BlockSpec(memory_space=pl.ANY)
    n_alias = 0 if outs is None else 6
    shapes = [sds((rows, wide), f32)] * 5 + [sds((rows, wide), bf16)]
    args = [*parts, *small, *vecs, *states]
    n_before = len(args)
    out_specs = [spec] * 6
    if vecs:
        shapes += [sds(vecs[0].shape, f32)] * 5 + [sds(vecs[0].shape, bf16)]
        out_specs += [whole(vecs[0].shape)] * 6
    return line.call(
        partial(adam_body, n_alias, bool(vecs)),
        [*args, *(outs or [])],
        [whole(v.shape) for v in [*parts, *small, *vecs]] + [spec] * 4 + [anywhere] * n_alias,
        shapes,
        out_specs,
        grid=(2 * count + (1 if vecs else 0),),
        aliases={1 + n_before + i: i for i in range(n_alias)},
        vmem=16,
        name="adam",
    )


def on_device(
    n_seq,
    n_grp,
    tokens,
    cotangent,
    seq_len,
    weight_mats,
    weight_vecs,
    master_mats,
    master_vecs,
    moment_mats,
    moment_vecs,
    square_mats,
    square_vecs,
    average_mats,
    average_vecs,
):
    rows = tokens.shape[0]
    fast = n_seq == 4 and n_grp == 8
    seq_at = lax.axis_index("seq")
    grp_at = lax.axis_index("grp")
    slot = jnp.arange(16, dtype=jnp.int32)
    seq_length = seq_len[0]
    peer = jnp.bitwise_xor(seq_at, jnp.bitwise_and(slot, 3) + 1)
    same = (peer * rows) // seq_length == (seq_at * rows) // seq_length
    before = (same & (peer < seq_at)).astype(jnp.int32)
    after = (same & (peer > seq_at)).astype(jnp.int32)
    scal = jnp.where(slot < 8, before, after)
    scal = jnp.where(slot == S_SEQ, seq_at if fast else 0, scal)
    scal = jnp.where(slot == S_GRP, grp_at, scal)
    line = Line(scal)

    w_t = weight_mats.T
    line.stay = {id(w_t), id(tokens), id(cotangent)}
    v_t13 = weight_vecs.T
    n_vec = v_t13.shape[0]
    bias_fc = v_t13[9:].reshape(1, FF)
    wide = QUAD * HD
    n_peer = n_seq - 1
    sel_rows = [D // 2, D // 2] if fast else [D]
    n_sel = len(sel_rows)
    sel_shapes = [sds((4, r, rows), bf16) for r in sel_rows]
    sel_low = [whole((2, r, rows)) for r in sel_rows]
    sel_high = [pl.BlockSpec((2, r, rows), lambda i, s: (1, 0, 0)) for r in sel_rows]

    def both(value):
        return [value, swap(value, "grp", 8, 1)] if fast else [value]

    def w_rows(count, at):
        return pl.BlockSpec((count, D), lambda i, s: (at(i, s), 0))

    hedge_spec = pl.BlockSpec((HD, wide), lambda i, s: ((4 * D + 2 * FF) // HD, i))
    vec_whole = whole(v_t13.shape)
    head_spec, feat_spec = along((wide, rows)), along((2 * wide, rows))
    aug_spec, quad_state = along((QUAD * AUG, rows)), along((QUAD * AUG, 2 * HD))
    st_shape = (HEADS * AUG, 2 * HD)
    got = line.call(
        partial(pre_body, n_sel),
        [tokens, cotangent, w_t, w_t, w_t, w_t, v_t13, v_t13],
        [
            whole((rows, D)),
            whole((rows, D)),
            w_rows(wide, lambda i, s: i),
            w_rows(wide, lambda i, s: N_QUAD + i),
            w_rows(wide, lambda i, s: 2 * N_QUAD + i),
            hedge_spec,
            vec_whole,
            pl.BlockSpec((n_vec, wide), lambda i, s: (0, i)),
        ],
        sel_shapes
        + [
            sds((D, rows), bf16),
            sds((D, rows), bf16),
            sds((2 * D, rows), bf16),
            sds((2 * D, rows), bf16),
            sds((D, rows), bf16),
            sds(st_shape, bf16),
        ],
        sel_low + [head_spec, head_spec, feat_spec, feat_spec, head_spec, quad_state],
        grid=(N_QUAD,),
        scratch=[pltpu.VMEM((rows, D), bf16)],
        vmem=32,
        name="pre",
    )
    sels = got[:n_sel]
    qt, kt, fq, fk, v_t, s_own = got[n_sel:]
    states = [swap(s_own, "seq", n_seq, k + 1) for k in range(n_peer)]

    (num,) = line.call(
        local_body,
        [fq, fk, v_t],
        [feat_spec, feat_spec, head_spec],
        [sds((HEADS * AUG, rows), f32)],
        [aug_spec],
        grid=(N_QUAD,),
        vmem=24,
        name="local",
    )
    got = line.call(
        partial(after_body, n_sel, n_peer),
        [*states, num, fq, tokens, w_t, v_t13, *sels],
        [whole(st_shape)] * n_peer
        + [whole(num.shape), whole(fq.shape), whole((rows, D)), w_rows(D, lambda i, s: 3), vec_whole]
        + [pl.BlockSpec(memory_space=pl.ANY)] * n_sel,
        [
            sds((D, rows), f32),
            sds((16, rows), f32),
            sds((rows, D), f32),
            sds((rows, D), bf16),
            sds(st_shape, bf16),
        ]
        + sel_shapes,
        [whole((D, rows)), whole((16, rows)), whole((rows, D)), whole((rows, D)), whole(st_shape)] + sel_high,
        aliases={n_peer + 6 + i: 5 + i for i in range(n_sel)},
        scratch=[pltpu.VMEM((D, rows), bf16)],
        vmem=32,
        name="after",
    )
    o_t, den, resid, h2, s_in = got[:5]
    sels = got[5:]
    if fast:
        sels = [sels[1], swap(sels[0], "grp", 8, 1)]

    n_piece = 2
    piece = FF // n_piece
    wq = piece // 4
    acc, acts, db_fc = [], [], []
    for j in range(n_piece):
        if j == 1:
            (sels,) = line.wait(sels)
        q_of = lambda i, s, j=j: 4 * j + jnp.bitwise_xor(i, s[S_SEQ])
        out_y, out_dh, act, db = line.call(
            partial(mlp_body, j == 0),
            [h2, cotangent, w_t, w_t, bias_fc, *acc],
            [
                whole((rows, D)),
                whole((rows, D)),
                w_rows(wq, lambda i, s: 4 * D // wq + q_of(i, s)),
                w_rows(wq, lambda i, s: (4 * D + FF) // wq + q_of(i, s)),
                pl.BlockSpec((1, wq), lambda i, s: (0, q_of(i, s))),
            ]
            + [whole((rows, D))] * len(acc),
            [sds((rows, D), f32), sds((rows, D), f32), sds((2, 4, rows, wq), bf16), sds((1, piece), f32)],
            [
                whole((rows, D)),
                whole((rows, D)),
                pl.BlockSpec((2, 1, rows, wq), lambda i, s: (0, i, 0, 0)),
                pl.BlockSpec((1, wq), lambda i, s: (0, jnp.bitwise_xor(i, s[S_SEQ]))),
            ],
            grid=(4,),
            vmem=32,
            name="mlp",
        )
        acc = [out_y, out_dh]
        db_fc.append(db)
        acts.append(both(act))

    if fast:
        (acts[0],) = line.wait(acts[0])
    block_output, d_resid, d_attn, rho, ds_own, sums = line.call(
        back_body,
        [*acc, resid, cotangent, w_t, v_t13, o_t, den, fq],
        [whole((rows, D))] * 4
        + [w_rows(D, lambda i, s: 3), vec_whole, whole((D, rows)), whole((16, rows)), whole((2 * D, rows))],
        [
            sds((rows, D), bf16),
            sds((rows, D), f32),
            sds((D, rows), bf16),
            sds((HEADS * AUG, rows), bf16),
            sds(st_shape, bf16),
            sds((4, D), f32),
        ],
        [whole((rows, D))] * 2
        + [whole((D, rows)), whole((HEADS * AUG, rows)), whole(st_shape), whole((4, D))],
        scratch=[pltpu.VMEM((D, rows), bf16)],
        vmem=32,
        name="back",
    )
    back_states = [swap(ds_own, "seq", n_seq, k + 1) for k in range(n_peer)]
    if fast:
        first = Halves(
            line, *mlp_grads(line, True, sels, acts[0]),
            [("grp", 8, 2), ("seq", 4, 1), ("seq", 4, 2), ("grp", 8, 4)],
        )
        (acts[1],) = line.wait(acts[1])
        second = mlp_grads(line, False, sels, acts[1])
        (back_states,) = line.wait(back_states)
        second = Halves(
            line, *second, [("seq", 4, 2), ("seq", 4, 1), ("grp", 8, 2), ("grp", 8, 4)]
        )

    dp, dm, db_qkv = line.call(
        partial(attend_back_body, n_peer),
        [*back_states, fq, fk, v_t, rho, s_in, qt, kt, w_t, d_attn],
        [quad_state] * n_peer
        + [feat_spec, feat_spec, head_spec, aug_spec, quad_state, head_spec, head_spec, hedge_spec, head_spec],
        [sds((4, D, rows), bf16), sds((D, HD), f32), sds((D, 3), f32)],
        [along((4, wide, rows), 1), along((wide, HD)), along((wide, 3))],
        grid=(N_QUAD,),
        vmem=32,
        hold=12,
        name="attend_back",
    )
    dp_both = both(dp)
    if fast:
        first.step()
    db_fc_rows = jnp.concatenate(db_fc, axis=1).reshape(FF // D, D)
    input_grad, *small = line.call(
        partial(input_body, fast),
        [dp, w_t, tokens, d_resid, v_t13, sums, db_fc_rows, db_qkv, dm],
        [
            along((1, D, rows)),
            w_rows(D, lambda i, s: i),
            whole((rows, D)),
            whole((rows, D)),
            vec_whole,
            whole((4, D)),
            whole((FF // D, D)),
            whole((D, 3)),
            whole((D, HD)),
        ],
        [sds((rows, D), bf16)] + [sds((1, r, 2 * HD), f32) for r in sel_rows],
        [whole((rows, D))] + [whole((1, r, 2 * HD)) for r in sel_rows],
        grid=(3,),
        scratch=[pltpu.VMEM((rows, D), f32)],
        vmem=32,
        hold=12,
        name="input",
    )
    states_m = [master_mats, moment_mats, square_mats, average_mats]
    states_v = [v.T for v in (master_vecs, moment_vecs, square_vecs, average_vecs)]
    if fast:
        theirs, mine = small
        small = [mine, swap(theirs, "grp", 8, 1)]
        second.step(hold=60)
        tail = tail_grads(line, sels, dp_both, small)
        tail_first, tail_second = tail_one(line, tail)
        first.step()
        far = tail_first()
        first.step()
        second.step()
        last = tail_second(*far)
        second.step()
        both_mine = gather_parts(final_both(line, [first, second]))
        last.step()
        last_mine, small_own = tail_final(line, last)
        outs = adam_piece(
            line, both_mine, states_m, None,
            lambda i: jnp.where(jnp.bitwise_and(i, 2) == 0, 8, 4) + 2 * (i // 4) + jnp.bitwise_and(i, 1),
        )
        last_parts = gather_parts(last_mine)
        outs = adam_piece(
            line, last_parts, states_m, outs, lambda i: jnp.where(i < 4, i, (4 * D + 2 * FF) // D),
            small=[small_own], vecs=states_v,
        )
        mats, vecs = outs[:6], [v.T for v in outs[6:]]
    else:
        h1t, obt, h2t = sels[0][1], sels[0][2], sels[0][3]
        joined = [jnp.transpose(a[0], (0, 2, 1, 3)).reshape(2, rows, piece) for a in acts]
        dn = [dot_tn(cotangent, v[0]) for v in joined]
        fc = [dot_nn(h2t, v[1]) for v in joined]
        qkvo = [dot_nt(h1t, dp[k]) for k in range(3)] + [dot_nt(obt, dp[3])]
        small = small[0][0]
        grad = jnp.concatenate([*qkvo, *fc, *dn, small[:, :HD]], axis=1).astype(bf16)
        own = lax.psum_scatter(grad, "grp", scatter_dimension=0, tiled=True)
        own = lax.psum(own, "seq").astype(f32)
        own_v = lax.psum(lax.psum_scatter(small, "grp", scatter_dimension=0, tiled=True), "seq")
        own_v = own_v[:, HD : HD + n_vec]
        results = adam_math(own, *states_m, learn_rate)
        mats = [own, *results, results[0].astype(bf16)]
        results = adam_math(own_v.T, *states_v, vector_rate)
        vecs = [own_v, *[v.T for v in (*results, results[0].astype(bf16))]]
    flat = [x for pair_ in zip(mats, vecs) for x in pair_]
    return (block_output, input_grad, *flat)


def solution(mesh):
    tok = P(("grp", "seq"), None)
    own = P("grp", None)
    in_specs = (tok, tok, P("grp"), P(), P()) + (own,) * 8
    out_specs = (tok, tok) + (own,) * 12
    body = partial(on_device, mesh.shape["seq"], mesh.shape["grp"])
    return jax.shard_map(body, mesh=mesh, in_specs=in_specs, out_specs=out_specs, check_vma=False)
```

```python
from functools import partial

import jax
import jax.numpy as jnp
from jax import lax
from jax.experimental import pallas as pl
from jax.experimental.pallas import tpu as pltpu
from jax.sharding import PartitionSpec as P

D = 768
HEADS = 12
HD = 64
FF = 3072
QUAD = 4
N_QUAD = HEADS // QUAD
AUG = 80

norm_eps = 1e-05
adam_eps = 1e-08
beta_first = 0.5
beta_second = 0.5
learn_rate = 0.01
vector_rate = 0.06
decay_rate = 0.1
average_keep = 0.9

f32 = jnp.float32
bf16 = jnp.bfloat16

S_SEQ, S_GRP, S_MASK, S_BACK = 0, 1, 4, 8

MIB = 1024 * 1024


def dot_nn(a, b):
    return lax.dot_general(a, b, (((1,), (0,)), ((), ())), preferred_element_type=f32)


def dot_nt(a, b):
    return lax.dot_general(a, b, (((1,), (1,)), ((), ())), preferred_element_type=f32)


def dot_tn(a, b):
    return lax.dot_general(a, b, (((0,), (0,)), ((), ())), preferred_element_type=f32)


def whole(shape):
    return pl.BlockSpec(tuple(shape), lambda *_: (0,) * len(shape))


def along(block, axis=0):
    return pl.BlockSpec(tuple(block), lambda i, s: tuple(i if d == axis else 0 for d in range(len(block))))


def sds(shape, dtype):
    return jax.ShapeDtypeStruct(tuple(shape), dtype)


class Line:
    def __init__(self, scal):
        self.scal = scal
        self.stay = set()

    def wait(self, *values):
        self.scal, values = lax.optimization_barrier((self.scal, values))
        return values

    def call(self, body, args, in_specs, outs, out_specs, grid=(1,), scratch=(), vmem=32,
             hold=0, far=(), aliases=None, name=None):
        args = [
            pltpu.with_memory_space_constraint(a, pltpu.HBM) if id(a) in self.stay or k in far else a
            for k, a in enumerate(args)
        ]
        got = pl.pallas_call(
            body,
            out_shape=tuple(outs),
            grid_spec=pltpu.PrefetchScalarGridSpec(
                num_scalar_prefetch=1,
                grid=grid,
                in_specs=list(in_specs),
                out_specs=tuple(out_specs),
                scratch_shapes=list(scratch),
            ),
            compiler_params=pltpu.CompilerParams(
                dimension_semantics=("arbitrary",) * len(grid), vmem_limit_bytes=vmem * MIB
            ),
            cost_estimate=pl.CostEstimate(
                flops=hold * 10**9, bytes_accessed=1024, transcendentals=0
            ),
            input_output_aliases=aliases or {},
            name=name,
        )(self.scal, *args)
        self.scal, got = lax.optimization_barrier((self.scal, got))
        return got


def store_sel(refs, at, values, scal):
    if len(refs) == 1:
        refs[0][at] = values
        return
    block = D // 8
    for j in range(8):
        rel = jnp.bitwise_xor(scal[S_GRP], j)
        place = pl.multiple_of(jnp.right_shift(rel, 1) * block, block)
        odd = jnp.bitwise_and(rel, 1)
        part = values[j * block : (j + 1) * block, :]

        @pl.when(odd == 1)
        def _(part=part, place=place):
            refs[0][at, pl.ds(place, block), :] = part

        @pl.when(odd == 0)
        def _(part=part, place=place):
            refs[1][at, pl.ds(place, block), :] = part


def normalize(values):
    average = jnp.mean(values, axis=1, keepdims=True)
    centered = values - average
    variance = jnp.mean(centered * centered, axis=1, keepdims=True)
    inverse = lax.rsqrt(variance + norm_eps)
    return centered * inverse, inverse


def quad_maps(hedge_t):
    wide = QUAD * HD
    row = lax.broadcasted_iota(jnp.int32, (wide, HD), 0)
    col = lax.broadcasted_iota(jnp.int32, (wide, HD), 1)
    spread = (jnp.bitwise_and(row, HD - 1) == col).astype(bf16)
    tiled = dot_nn(spread, hedge_t)
    big_r = lax.broadcasted_iota(jnp.int32, (wide, wide), 0)
    big_c = lax.broadcasted_iota(jnp.int32, (wide, wide), 1)
    same = jnp.right_shift(big_r, 6) == jnp.right_shift(big_c, 6)
    return jnp.where(same, tiled, 0.0)


def ones_rows(count):
    return (lax.broadcasted_iota(jnp.int32, (AUG - HD, count), 0) == 0).astype(f32).astype(bf16)


def rows_up(values):
    return jnp.concatenate([values, jnp.zeros((3, values.shape[1]), f32)], axis=0).T


def features(pt, maps):
    high = pt.astype(bf16)
    rest = (pt - high.astype(f32)).astype(bf16)
    scores = dot_nn(jnp.concatenate([maps, maps], axis=1), jnp.concatenate([high, rest], axis=0))
    heads = []
    for h in range(QUAD):
        s = scores[h * HD : (h + 1) * HD, :]
        top = jnp.max(s, axis=0, keepdims=True)
        bottom = jnp.min(s, axis=0, keepdims=True)
        pos = jnp.exp(s - top)
        neg = jnp.exp(bottom - s)
        pos = pos * (1.0 / jnp.sum(pos, axis=0, keepdims=True))
        neg = neg * (1.0 / jnp.sum(neg, axis=0, keepdims=True))
        heads.append(jnp.concatenate([pos, neg], axis=0).astype(bf16))
    return high, heads


def keys_body(scal, x_ref, wk_ref, wv_ref, hedge_ref, vt_ref, vq_ref, h1_ref, kt_ref, fk_ref, vt_out, s_ref):
    rows = x_ref.shape[0]

    @pl.when(pl.program_id(0) == 0)
    def _():
        normed, _ = normalize(x_ref[...].astype(f32))
        vt = vt_ref[...].astype(f32)
        h1_ref[...] = (normed * vt[0:1] + vt[1:2]).astype(bf16)

    h1 = h1_ref[...]
    bias = rows_up(vq_ref[...].astype(f32))
    v_t = (dot_nt(wv_ref[...], h1) + bias[:, 8:9]).astype(bf16)
    vt_out[...] = v_t
    pt = dot_nt(wk_ref[...], h1) + bias[:, 7:8]
    kt_ref[...], heads = features(pt, quad_maps(hedge_ref[...]).astype(bf16))
    extra = ones_rows(rows)
    for h, both in enumerate(heads):
        fk_ref[h * 2 * HD : (h + 1) * 2 * HD, :] = both
        va = jnp.concatenate([v_t[h * HD : (h + 1) * HD, :], extra], axis=0)
        s_ref[h * AUG : (h + 1) * AUG, :] = dot_nt(va, both).astype(bf16)


def queries_body(n_sel, scal, h1_ref, g_ref, wq_ref, hedge_ref, vq_ref, *refs):
    sel = refs[:n_sel]
    qt_ref, fq_ref = refs[n_sel:]
    h1 = h1_ref[...]

    @pl.when(pl.program_id(0) == 0)
    def _():
        store_sel(sel, 0, g_ref[...].T, scal)
        store_sel(sel, 1, h1.T, scal)

    bias = rows_up(vq_ref[...].astype(f32))
    pt = dot_nt(wq_ref[...], h1) + bias[:, 6:7]
    qt_ref[...], heads = features(pt, quad_maps(hedge_ref[...]).astype(bf16))
    for h, both in enumerate(heads):
        fq_ref[h * 2 * HD : (h + 1) * 2 * HD, :] = both


def tri_mask(half):
    return lax.broadcasted_iota(jnp.int32, (half, half), 0) <= lax.broadcasted_iota(
        jnp.int32, (half, half), 1
    )


def masked_pair(left0, left1, right, keep):
    half = right.shape[1] // 2
    full = dot_tn(left0, right)
    low = dot_tn(left1, right[:, half:])
    diag0 = jnp.where(keep, full[:, :half], 0.0).astype(bf16)
    above = full[:, half:].astype(bf16)
    diag1 = jnp.where(keep, low, 0.0).astype(bf16)
    return diag0, above, diag1


def local_body(scal, fq_ref, fk_ref, vt_ref, num_ref):
    rows = fq_ref.shape[1]
    half = rows // 2
    keep = tri_mask(half)
    extra = ones_rows(rows)
    for h in range(QUAD):
        fq = fq_ref[h * 2 * HD : (h + 1) * 2 * HD, :]
        fk = fk_ref[h * 2 * HD : (h + 1) * 2 * HD, :]
        va = jnp.concatenate([vt_ref[h * HD : (h + 1) * HD, :], extra], axis=0)
        a00, a01, a11 = masked_pair(fk[:, :half], fk[:, half:], fq, keep)
        num_ref[h * AUG : (h + 1) * AUG, :half] = dot_nn(va[:, :half], a00)
        num_ref[h * AUG : (h + 1) * AUG, half:] = dot_nn(va[:, :half], a01) + dot_nn(va[:, half:], a11)


def weighted_state(scal, slot, parts):
    total = None
    for k, part in enumerate(parts):
        term = scal[slot + k].astype(f32) * part.astype(f32)
        total = term if total is None else total + term
    return total.astype(bf16)


def after_body(n_sel, n_parts, scal, *refs):
    parts = refs[:n_parts]
    num_ref, fq_ref, x_ref, w_ref, vt_ref = refs[n_parts : n_parts + 5]
    o_ref, den_ref, r_ref, h2_ref, sin_ref = refs[n_parts + 5 + n_sel : n_parts + 10 + n_sel]
    sel = refs[-1 - n_sel : -1]
    ob_ref = refs[-1]
    vt = vt_ref[...].astype(f32)
    state = weighted_state(scal, S_MASK, [p[...] for p in parts])
    sin_ref[...] = state
    for h in range(HEADS):
        num = num_ref[h * AUG : (h + 1) * AUG, :] + dot_nn(
            state[h * AUG : (h + 1) * AUG, :], fq_ref[h * 2 * HD : (h + 1) * 2 * HD, :]
        )
        den = num[HD : HD + 1, :]
        out = num[:HD, :] * (1.0 / den)
        o_ref[h * HD : (h + 1) * HD, :] = out
        den_ref[h : h + 1, :] = den
        ob_ref[h * HD : (h + 1) * HD, :] = out.astype(bf16)
    obt = ob_ref[...]
    store_sel(sel, 0, obt, scal)
    r = x_ref[...].astype(f32) + dot_nt(obt.T, w_ref[...]) + vt[4:5]
    r_ref[...] = r
    normed, _ = normalize(r)
    h2 = (normed * vt[2:3] + vt[3:4]).astype(bf16)
    h2_ref[...] = h2
    store_sel(sel, 1, h2.T, scal)


gelu_c = 0.7978845608028654
gelu_k = 0.044715


def mlp_body(first, scal, h2_ref, g_ref, wf_ref, wd_ref, bias_ref, *refs):
    if first:
        out_ref, dh_ref, act_ref, db_ref = refs
    else:
        out_in, dh_in, out_ref, dh_ref, act_ref, db_ref = refs
    u = dot_nt(h2_ref[...], wf_ref[...]) + bias_ref[...].astype(f32)
    de = dot_nt(g_ref[...], wd_ref[...])
    uu = u * u
    t = jnp.tanh(gelu_c * u * (1.0 + gelu_k * uu))
    half_t = 0.5 * (1.0 + t)
    e = (u * half_t).astype(bf16)
    slope = half_t + 0.5 * u * (1.0 - t * t) * (gelu_c * (1.0 + 3.0 * gelu_k * uu))
    du = (de * slope).astype(bf16)
    act_ref[0, 0] = e
    act_ref[1, 0] = du
    db_ref[...] = jnp.sum(du.astype(f32), axis=0, keepdims=True)
    add_out = dot_nn(e, wd_ref[...])
    add_dh = dot_nn(du, wf_ref[...])
    step = pl.program_id(0)

    @pl.when(step == 0)
    def _():
        if first:
            out_ref[...] = add_out
            dh_ref[...] = add_dh
        else:
            out_ref[...] = out_in[...] + add_out
            dh_ref[...] = dh_in[...] + add_dh

    @pl.when(step > 0)
    def _():
        out_ref[...] += add_out
        dh_ref[...] += add_dh


def back_body(scal, out_ref, dh_ref, r_ref, g_ref, w_ref, vt_ref, o_ref, den_ref, fq_ref, y_ref, dr_ref,
              da_ref, rho_ref, ds_ref, sums_ref, do_ref):
    vt = vt_ref[...].astype(f32)
    r = r_ref[...]
    y_ref[...] = (r + out_ref[...] + vt[5:6]).astype(bf16)
    grad_out = g_ref[...].astype(f32)
    normed, inverse = normalize(r)
    up = dh_ref[...]
    dn = up * vt[2:3]
    dr = grad_out + inverse * (
        dn - jnp.mean(dn, axis=1, keepdims=True) - normed * jnp.mean(dn * normed, axis=1, keepdims=True)
    )
    dr_ref[...] = dr
    da = dr.astype(bf16)
    da_ref[...] = da.T
    sums_ref[...] = jnp.concatenate(
        [
            jnp.sum(up * normed, axis=0, keepdims=True),
            jnp.sum(up, axis=0, keepdims=True),
            jnp.sum(da.astype(f32), axis=0, keepdims=True),
            jnp.sum(grad_out, axis=0, keepdims=True),
        ],
        axis=0,
    )
    do_ref[...] = dot_nn(da, w_ref[...]).astype(bf16).T
    rows = r.shape[0]
    zero_row = lax.broadcasted_iota(jnp.int32, (AUG - HD, rows), 0) == 0
    for h in range(HEADS):
        dout = do_ref[h * HD : (h + 1) * HD, :].astype(f32)
        inv = 1.0 / den_ref[h : h + 1, :]
        rho = (dout * inv).astype(bf16)
        c = -jnp.sum(dout * o_ref[h * HD : (h + 1) * HD, :], axis=0, keepdims=True) * inv
        extra = jnp.where(zero_row, jnp.broadcast_to(c, (AUG - HD, rows)), 0.0).astype(bf16)
        ra = jnp.concatenate([rho, extra], axis=0)
        rho_ref[h * AUG : (h + 1) * AUG, :] = ra
        ds_ref[h * AUG : (h + 1) * AUG, :] = dot_nt(ra, fq_ref[h * 2 * HD : (h + 1) * 2 * HD, :]).astype(bf16)


def feature_back(feat, upstream):
    pos, neg = feat[:HD].astype(f32), feat[HD:].astype(f32)
    up_pos, up_neg = upstream[:HD], upstream[HD:]
    return pos * (up_pos - jnp.sum(pos * up_pos, axis=0, keepdims=True)) - neg * (
        up_neg - jnp.sum(neg * up_neg, axis=0, keepdims=True)
    )


def attend_back_body(n_parts, scal, *refs):
    parts = refs[:n_parts]
    (fq_ref, fk_ref, vt_ref, rho_ref, sin_ref, qt_ref, kt_ref, hedge_ref, da_ref) = refs[n_parts : n_parts + 9]
    dp_ref, dm_ref, db_ref = refs[-3:]
    dp_ref[3] = da_ref[...]
    rows = fq_ref.shape[1]
    half = rows // 2
    keep = tri_mask(half)
    extra = ones_rows(rows)
    back_state = weighted_state(scal, S_BACK, [p[...] for p in parts])
    ds_q, ds_k = [], []
    for h in range(QUAD):
        fq = fq_ref[h * 2 * HD : (h + 1) * 2 * HD, :]
        fk = fk_ref[h * 2 * HD : (h + 1) * 2 * HD, :]
        head = slice(h * HD, (h + 1) * HD)
        aug = slice(h * AUG, (h + 1) * AUG)
        va = jnp.concatenate([vt_ref[head, :], extra], axis=0)
        ra = rho_ref[aug, :]
        state, back = sin_ref[aug, :], back_state[aug, :]
        a00, a01, a11 = masked_pair(fk[:, :half], fk[:, half:], fq, keep)
        g00, g01, g11 = masked_pair(va[:, :half], va[:, half:], ra, keep)
        far = dot_tn(state, ra)
        left = far[:, :half] + dot_nn(fk[:, :half], g00)
        right = far[:, half:] + dot_nn(fk[:, :half], g01) + dot_nn(fk[:, half:], g11)
        dfq = jnp.concatenate([left, right], axis=1)
        far_k = dot_tn(back, va)
        left = far_k[:, :half] + dot_nt(fq[:, :half], g00) + dot_nt(fq[:, half:], g01)
        right = far_k[:, half:] + dot_nt(fq[:, half:], g11)
        dfk = jnp.concatenate([left, right], axis=1)
        far_v = dot_nn(back, fk)[:HD]
        rv = ra[:HD]
        left = far_v[:, :half] + dot_nt(rv[:, :half], a00) + dot_nt(rv[:, half:], a01)
        right = far_v[:, half:] + dot_nt(rv[:, half:], a11)
        dp_ref[2, head, :] = jnp.concatenate([left, right], axis=1).astype(bf16)
        dsq = feature_back(fq, dfq).astype(bf16)
        dsk = feature_back(fk, dfk).astype(bf16)
        ds_q.append(dsq)
        ds_k.append(dsk)
        dm_ref[head, :] = dot_nt(qt_ref[head, :], dsq) + dot_nt(kt_ref[head, :], dsk)
    maps = quad_maps(hedge_ref[...]).T.astype(bf16)
    dq = dot_nn(maps, jnp.concatenate(ds_q, axis=0)).astype(bf16)
    dk = dot_nn(maps, jnp.concatenate(ds_k, axis=0)).astype(bf16)
    dp_ref[0] = dq
    dp_ref[1] = dk
    db_ref[...] = jnp.concatenate(
        [jnp.sum(v.astype(f32), axis=1, keepdims=True) for v in (dq, dk, dp_ref[2])], axis=1
    )


def input_body(fast, scal, dp_ref, w_ref, x_ref, dr_ref, vt_ref, sums_ref, dbfc_ref, db_ref, dm_ref, *refs):
    gin_ref, *small_refs, acc_ref = refs
    step = pl.program_id(0)
    part = dot_tn(dp_ref[0], w_ref[...])

    @pl.when(step == 0)
    def _():
        acc_ref[...] = part

    @pl.when(step == 1)
    def _():
        acc_ref[...] += part

    @pl.when(step == 2)
    def _():
        vt = vt_ref[...].astype(f32)
        up = acc_ref[...] + part
        normed, inverse = normalize(x_ref[...].astype(f32))
        dn = up * vt[0:1]
        gin = dr_ref[...] + inverse * (
            dn - jnp.mean(dn, axis=1, keepdims=True) - normed * jnp.mean(dn * normed, axis=1, keepdims=True)
        )
        gin_ref[...] = gin.astype(bf16)
        rows16 = jnp.concatenate(
            [
                jnp.sum(up * normed, axis=0, keepdims=True),
                jnp.sum(up, axis=0, keepdims=True),
                sums_ref[...],
                jnp.zeros((3, D), f32),
                dbfc_ref[...],
                jnp.zeros((3, D), f32),
            ],
            axis=0,
        )
        cols = rows16.T
        lane = lax.broadcasted_iota(jnp.int32, (D, HD), 1)
        tail = jnp.concatenate([cols, jnp.zeros((D, HD - 16), f32)], axis=1)
        for k in range(3):
            tail = jnp.where(lane == 6 + k, db_ref[:, k : k + 1], tail)
        small = jnp.concatenate([dm_ref[...], tail], axis=1)
        store_sel(small_refs, 0, small, scal)


def mlp_grads_body(by_y, scal, *refs):
    sels, acts_a, acts_b, sels_h = refs[0:2], refs[2:4], refs[4:6], refs[6:8]
    send, keep = refs[8:]
    block = D // 8
    wq = send.shape[2]
    y_last = 1 - pl.program_id(0)

    def total(lefts, rights):
        return (dot_nn(lefts[0][0], rights[0][0, 0]) + dot_nn(lefts[1][0], rights[1][0, 0])).astype(bf16)

    for path, value in enumerate((total(sels, acts_a), total(sels_h, acts_b))):
        rows = slice(path * block, (path + 1) * block)
        for half in range(2):
            x_last = 1 - jnp.bitwise_xor(half, jnp.bitwise_and(scal[S_SEQ], 1))
            cols = slice(half * wq, (half + 1) * wq)

            def part(z, value=value, cols=cols):
                return value[z * block : (z + 1) * block, cols]

            if by_y:
                for bit, ref in ((0, send), (1, keep)):

                    @pl.when(y_last == bit)
                    def _(ref=ref, part=part, rows=rows, x_last=x_last):
                        for at, z in enumerate((3, 1, 2, 0)):
                            ref[4 * (at // 2) + 2 * x_last + at % 2, rows, :] = part(z)
            else:
                base = y_last + 4 * x_last
                for ref, order in ((send, (3, 1)), (keep, (2, 0))):
                    for at, z in enumerate(order):
                        ref[2 * at + base, rows, :] = part(z)


def mlp_grads(line, by_y, sels, acts):
    _, depth, rows = sels[0].shape
    half = sds((8, 2 * (D // 8), D // 2), bf16)

    def act(path):
        return pl.BlockSpec((1, 1, rows, D), lambda i, s: (path, i, 0, 0))

    def sel(slot):
        return pl.BlockSpec((1, depth, rows), lambda i, s: (slot, 0, 0))

    return line.call(
        partial(mlp_grads_body, by_y),
        [*sels, *acts, *acts, *sels],
        [sel(0)] * 2 + [act(0)] * 2 + [act(1)] * 2 + [sel(3)] * 2,
        [half] * 2,
        [whole(half.shape)] * 2,
        grid=(2,),
        vmem=10,
        name="mlp_grads",
    )


def pack_rows(values, count):
    return jnp.concatenate([values[b * count : (b + 1) * count] for b in range(3)], axis=1)


def unpack_rows(values):
    return jnp.concatenate([values[:, b * 128 : (b + 1) * 128] for b in range(3)], axis=0)


def order_a(i):
    return jnp.where(i < 2, 2 * i + 1, 2 * i - 4)


def order_b(i):
    return jnp.where(i < 2, i + 2, i - 2)


def tail_grads_body(scal, *refs):
    h1, ob, dqk, dvo = refs[0:2], refs[2:4], refs[4:6], refs[6:8]
    small_own, small_other, send_a, keep_a, send_b, keep_b, small_ref = refs[8:]
    step = pl.program_id(0)
    wq = send_a.shape[1]
    qb = jnp.bitwise_xor(order_b(step), scal[S_SEQ])
    at = pl.multiple_of(jnp.bitwise_and(step, 1) * wq, wq)

    def total(lefts, rights):
        return (dot_nt(lefts[0][0], rights[0][0]) + dot_nt(lefts[1][0], rights[1][0])).astype(bf16)

    def put(send, keep, value):
        @pl.when(step < 2)
        def _():
            send[pl.ds(at, wq), :] = value

        @pl.when(step >= 2)
        def _():
            keep[pl.ds(at, wq), :] = value

    put(send_a, keep_a, total(h1, dqk))

    @pl.when(qb < 2)
    def _():
        put(send_b, keep_b, total(h1, dvo))

    @pl.when(qb >= 2)
    def _():
        put(send_b, keep_b, total(ob, dvo))

    @pl.when(step == 0)
    def _():
        small = pack_rows(small_own[0] + small_other[0].astype(f32), 128)
        small_ref[...] = small
        send_a[2 * wq :, :] = small.astype(bf16)


def tail_grads(line, sels, dp, small):
    _, depth, rows = sels[0].shape
    wq = D // 2
    dp = [v.reshape(8, wq, rows) for v in dp]

    def sel(slot):
        return pl.BlockSpec((1, depth, rows), lambda i, s: (slot, 0, 0))

    outs = [
        sds((2 * wq + 128, wq), bf16), sds((2 * wq, wq), bf16),
        sds((2 * wq, wq), bf16), sds((2 * wq, wq), bf16), sds((128, wq), f32),
    ]
    return line.call(
        tail_grads_body,
        [*sels, *sels, *dp, *dp, *small],
        [sel(1)] * 2
        + [sel(2)] * 2
        + [pl.BlockSpec((1, wq, rows), lambda i, s: (jnp.bitwise_xor(order_a(i), s[S_SEQ]), 0, 0))] * 2
        + [pl.BlockSpec((1, wq, rows), lambda i, s: (4 + jnp.bitwise_xor(order_b(i), s[S_SEQ]), 0, 0))] * 2
        + [whole(small[0].shape)] * 2,
        outs,
        [whole(o.shape) for o in outs],
        grid=(4,),
        vmem=10,
        name="tail_grads",
    )


def swap(value, axis, size, bit):
    return lax.ppermute(value, axis, [(i, i ^ bit) for i in range(size)])


def halve_body(scal, keep_ref, recv_ref, send_ref, left_ref):
    half = send_ref.shape[0]
    send_ref[...] = (keep_ref[:half].astype(f32) + recv_ref[:half].astype(f32)).astype(bf16)
    left_ref[...] = (keep_ref[half:].astype(f32) + recv_ref[half:].astype(f32)).astype(left_ref.dtype)


class Halves:
    def __init__(self, line, send, keep, stages):
        self.line, self.keep, self.stages = line, keep, list(stages)
        self.recv = swap(send, *self.stages.pop(0))

    def step(self, hold=0):
        count, rows, wq = self.keep.shape
        shape = (count // 2, rows, wq)
        send, self.keep = self.line.call(
            halve_body, [self.keep, self.recv], [whole(self.keep.shape)] * 2,
            [sds(shape, bf16), sds(shape, self.keep.dtype)], [whole(shape)] * 2,
            vmem=8, hold=hold, name="halve",
        )
        self.recv = swap(send, *self.stages.pop(0))


def final_body(scal, *refs):
    out = refs[-1]
    for j in range(2):
        out[j] = (refs[2 * j][0].astype(f32) + refs[2 * j + 1][0].astype(f32)).astype(bf16)


def final_both(line, pieces):
    shape = (2,) + pieces[0].keep.shape[1:]
    (mine,) = line.call(
        final_body, [v for p in pieces for v in (p.keep, p.recv)], [whole((1,) + shape[1:])] * 4,
        [sds(shape, bf16)], [whole(shape)], vmem=4, name="final",
    )
    return mine.reshape(4, D // 8, shape[2])


def tail_one_body(scal, keep_a, recv_a, keep_b, recv_b, small_ref, send_a, send_b):
    wq = send_b.shape[0]
    send_a[:wq, :] = (keep_a[wq : 2 * wq].astype(f32) + recv_a[wq : 2 * wq].astype(f32)).astype(bf16)
    send_a[wq:, :] = (small_ref[...] + recv_a[2 * wq :].astype(f32)).astype(bf16)
    send_b[...] = (keep_b[wq:].astype(f32) + recv_b[wq:].astype(f32)).astype(bf16)


def tail_two_body(scal, keep_a, recv_a, keep_b, recv_b, small_ref, far_a, far_b, own_ref, *out_refs):
    wq = far_b.shape[0]
    block = D // 8
    small = small_ref[...] + recv_a[2 * wq :].astype(f32) + far_a[wq:].astype(f32)
    small = unpack_rows(small)
    first = keep_a[:wq].astype(f32) + recv_a[:wq].astype(f32) + far_a[:wq].astype(f32)
    second = keep_b[:wq].astype(f32) + recv_b[:wq].astype(f32) + far_b[...].astype(f32)
    for z, ref in enumerate((own_ref, *out_refs)):
        rows = slice(z * block, (z + 1) * block)
        ref[:block, :] = first[rows].astype(ref.dtype)
        ref[block : 2 * block, :] = second[rows].astype(ref.dtype)
        ref[2 * block :, :] = pack_rows(small[rows], block // 3).astype(ref.dtype)


def tail_final_body(scal, *refs):
    mine_ref, small_ref = refs[-2:]
    block = mine_ref.shape[1]
    total = refs[0][...]
    for ref in refs[1:-2]:
        total = total + ref[...].astype(f32)
    mine_ref[0] = total[:block].astype(bf16)
    mine_ref[1] = total[block : 2 * block].astype(bf16)
    small_ref[...] = unpack_rows(total[2 * block :])


def tail_one(line, tail):
    send_a, keep_a, send_b, keep_b, small = tail
    wq = D // 2
    recv_a, recv_b = swap(send_a, "seq", 4, 1), swap(send_b, "seq", 4, 2)
    shapes = [sds((wq + 128, wq), bf16), sds((wq, wq), bf16)]

    def first():
        args = [keep_a, recv_a, keep_b, recv_b, small]
        next_a, next_b = line.call(
            tail_one_body, args, [whole(v.shape) for v in args], shapes, [whole(v.shape) for v in shapes],
            vmem=12, name="tail_one",
        )
        return swap(next_a, "seq", 4, 2), swap(next_b, "seq", 4, 1)

    def second(far_a, far_b):
        args = [keep_a, recv_a, keep_b, recv_b, small, far_a, far_b]
        shape = (2 * (D // 8) + D // 24, wq)
        own, *sends = line.call(
            tail_two_body, args, [whole(v.shape) for v in args], [sds(shape, f32)] + [sds(shape, bf16)] * 3,
            [whole(shape)] * 4, vmem=10, hold=5, name="tail_two",
        )
        return [own, *(swap(v, "grp", 8, 2 * (k + 1)) for k, v in enumerate(sends))]

    return first, second


def tail_final(line, args):
    wq = D // 2
    shapes = [sds((2, D // 8, wq), bf16), sds((D // 8, 2 * HD), f32)]
    return line.call(
        tail_final_body, args, [whole(v.shape) for v in args], shapes, [whole(v.shape) for v in shapes],
        vmem=6, hold=5, name="tail_final",
    )


def gather_parts(mine):
    return [mine] + [swap(mine, "seq", 4, k) for k in (1, 2, 3)]


def adam_math(grad, master, first, second, average, rate):
    new_first = beta_first * first + (1.0 - beta_first) * grad
    new_second = beta_second * second + (1.0 - beta_second) * grad * grad
    new_master = master - rate * (
        new_first / (jnp.sqrt(new_second) + adam_eps) + decay_rate * master
    )
    new_average = average_keep * average + (1.0 - average_keep) * new_master
    return new_master, new_first, new_second, new_average


def adam_body(n_alias, has_small, scal, *refs):
    parts, refs = refs[:4], refs[4:]
    if has_small:
        small, vec_in, refs = refs[0], refs[1:5], refs[5:]
    states, refs = refs[:4], refs[4 + n_alias :]
    outs, vec_outs = refs[:6], refs[6:]
    grad_ref = outs[0]
    count, _, wq = parts[0].shape
    step = pl.program_id(0)
    path, half = jnp.right_shift(step, 1), jnp.bitwise_and(step, 1)
    for k, ref in enumerate(parts):
        quarter = jnp.bitwise_xor(scal[S_SEQ], k)

        @pl.when((jnp.right_shift(quarter, 1) == half) & (step < 2 * count))
        def _(ref=ref, quarter=quarter):
            at = pl.multiple_of(jnp.bitwise_and(quarter, 1) * wq, 128)
            grad_ref[:, pl.ds(at, wq)] = ref[jnp.minimum(path, count - 1)].astype(f32)

    if has_small:

        @pl.when(step == 2 * count)
        def _():
            grad_ref[...] = jnp.zeros_like(grad_ref)
            grad_ref[:, : 2 * HD] = small[...]
            grad = small[...].T[HD : HD + vec_in[0].shape[0]]
            results = adam_math(grad, *[v[...] for v in vec_in], vector_rate)
            for ref, value in zip(vec_outs, (grad, *results, results[0])):
                ref[...] = value.astype(ref.dtype)

    results = adam_math(grad_ref[...], *[v[...] for v in states], learn_rate)
    for ref, value in zip(outs[1:], (*results, results[0])):
        ref[...] = value.astype(ref.dtype)


def adam_piece(line, parts, states, outs, block_of, small=(), vecs=()):
    count, block, _ = parts[0].shape
    rows, wide = states[0].shape
    spec = pl.BlockSpec((block, D), lambda i, s: (0, block_of(i)))
    anywhere = pl.BlockSpec(memory_space=pl.ANY)
    n_alias = 0 if outs is None else 6
    shapes = [sds((rows, wide), f32)] * 5 + [sds((rows, wide), bf16)]
    args = [*parts, *small, *vecs, *states]
    n_before = len(args)
    out_specs = [spec] * 6
    if vecs:
        shapes += [sds(vecs[0].shape, f32)] * 5 + [sds(vecs[0].shape, bf16)]
        out_specs += [whole(vecs[0].shape)] * 6
    return line.call(
        partial(adam_body, n_alias, bool(vecs)),
        [*args, *(outs or [])],
        [whole(v.shape) for v in [*parts, *small, *vecs]] + [spec] * 4 + [anywhere] * n_alias,
        shapes,
        out_specs,
        grid=(2 * count + (1 if vecs else 0),),
        aliases={1 + n_before + i: i for i in range(n_alias)},
        vmem=16,
        name="adam",
    )


def on_device(
    n_seq,
    n_grp,
    tokens,
    cotangent,
    seq_len,
    weight_mats,
    weight_vecs,
    master_mats,
    master_vecs,
    moment_mats,
    moment_vecs,
    square_mats,
    square_vecs,
    average_mats,
    average_vecs,
):
    rows = tokens.shape[0]
    fast = n_seq == 4 and n_grp == 8
    seq_at = lax.axis_index("seq")
    grp_at = lax.axis_index("grp")
    slot = jnp.arange(16, dtype=jnp.int32)
    seq_length = seq_len[0]
    peer = jnp.bitwise_xor(seq_at, jnp.bitwise_and(slot, 3) + 1)
    same = (peer * rows) // seq_length == (seq_at * rows) // seq_length
    before = (same & (peer < seq_at)).astype(jnp.int32)
    after = (same & (peer > seq_at)).astype(jnp.int32)
    scal = jnp.where(slot < 8, before, after)
    scal = jnp.where(slot == S_SEQ, seq_at if fast else 0, scal)
    scal = jnp.where(slot == S_GRP, grp_at, scal)
    line = Line(scal)

    w_t = weight_mats.T
    states_m = [master_mats, moment_mats, square_mats, average_mats]
    line.stay = {id(v) for v in (w_t, tokens, cotangent)}
    v_t13 = weight_vecs.T
    n_vec = v_t13.shape[0]
    bias_fc = v_t13[9:].reshape(1, FF)
    wide = QUAD * HD
    n_peer = n_seq - 1
    sel_rows = [D // 2, D // 2] if fast else [D]
    n_sel = len(sel_rows)
    sel_shapes = [sds((4, r, rows), bf16) for r in sel_rows]
    sel_low = [whole((2, r, rows)) for r in sel_rows]
    sel_high = [pl.BlockSpec((2, r, rows), lambda i, s: (1, 0, 0)) for r in sel_rows]

    def both(value):
        return [value, swap(value, "grp", 8, 1)] if fast else [value]

    def w_rows(count, at):
        return pl.BlockSpec((count, D), lambda i, s: (at(i, s), 0))

    hedge_spec = pl.BlockSpec((HD, wide), lambda i, s: ((4 * D + 2 * FF) // HD, i))
    vec_whole = whole(v_t13.shape)
    head_spec, feat_spec = along((wide, rows)), along((2 * wide, rows))
    aug_spec, quad_state = along((QUAD * AUG, rows)), along((QUAD * AUG, 2 * HD))
    st_shape = (HEADS * AUG, 2 * HD)
    vec_quad = pl.BlockSpec((n_vec, wide), lambda i, s: (0, i))
    h1, kt, fk, v_t, s_own = line.call(
        keys_body,
        [tokens, w_t, w_t, w_t, v_t13, v_t13],
        [
            whole((rows, D)),
            w_rows(wide, lambda i, s: N_QUAD + i),
            w_rows(wide, lambda i, s: 2 * N_QUAD + i),
            hedge_spec,
            vec_whole,
            vec_quad,
        ],
        [
            sds((rows, D), bf16),
            sds((D, rows), bf16),
            sds((2 * D, rows), bf16),
            sds((D, rows), bf16),
            sds(st_shape, bf16),
        ],
        [whole((rows, D)), head_spec, feat_spec, head_spec, quad_state],
        grid=(N_QUAD,),
        vmem=12,
        name="keys",
    )
    n_peer = n_seq - 1
    states = [swap(s_own, "seq", n_seq, k + 1) for k in range(n_peer)]
    got = line.call(
        partial(queries_body, n_sel),
        [h1, cotangent, w_t, w_t, v_t13],
        [whole((rows, D)), whole((rows, D)), w_rows(wide, lambda i, s: i), hedge_spec, vec_quad],
        sel_shapes + [sds((D, rows), bf16), sds((2 * D, rows), bf16)],
        sel_low + [head_spec, feat_spec],
        grid=(N_QUAD,),
        vmem=12,
        name="queries",
    )
    sels, (qt, fq) = got[:n_sel], got[n_sel:]

    (num,) = line.call(
        local_body,
        [fq, fk, v_t],
        [feat_spec, feat_spec, head_spec],
        [sds((HEADS * AUG, rows), f32)],
        [aug_spec],
        grid=(N_QUAD,),
        vmem=10,
        name="local",
    )
    got = line.call(
        partial(after_body, n_sel, n_peer),
        [*states, num, fq, tokens, w_t, v_t13, *sels],
        [whole(st_shape)] * n_peer
        + [whole(num.shape), whole(fq.shape), whole((rows, D)), w_rows(D, lambda i, s: 3), vec_whole]
        + [pl.BlockSpec(memory_space=pl.ANY)] * n_sel,
        [
            sds((D, rows), f32),
            sds((16, rows), f32),
            sds((rows, D), f32),
            sds((rows, D), bf16),
            sds(st_shape, bf16),
        ]
        + sel_shapes,
        [whole((D, rows)), whole((16, rows)), whole((rows, D)), whole((rows, D)), whole(st_shape)] + sel_high,
        aliases={n_peer + 6 + i: 5 + i for i in range(n_sel)},
        scratch=[pltpu.VMEM((D, rows), bf16)],
        vmem=10,
        name="after",
    )
    o_t, den, resid, h2, s_in = got[:5]
    sels = got[5:]
    if fast:
        sels = [sels[1], swap(sels[0], "grp", 8, 1)]

    n_piece = 2
    piece = FF // n_piece
    acc, acts, db_fc = [], [], []
    for j in range(n_piece):
        if j == 1:
            (sels,) = line.wait(sels)
        pair_of = lambda i, s, j=j: 2 * j + jnp.bitwise_xor(i, jnp.right_shift(s[S_SEQ], 1))
        out_y, out_dh, act, db = line.call(
            partial(mlp_body, j == 0),
            [h2, cotangent, w_t, w_t, bias_fc, *acc],
            [
                whole((rows, D)),
                whole((rows, D)),
                w_rows(D, lambda i, s: 4 + pair_of(i, s)),
                w_rows(D, lambda i, s: 8 + pair_of(i, s)),
                pl.BlockSpec((1, D), lambda i, s: (0, pair_of(i, s))),
            ]
            + [whole((rows, D))] * len(acc),
            [sds((rows, D), f32), sds((rows, D), f32), sds((2, 2, rows, D), bf16), sds((1, piece), f32)],
            [
                whole((rows, D)),
                whole((rows, D)),
                pl.BlockSpec((2, 1, rows, D), lambda i, s: (0, i, 0, 0)),
                pl.BlockSpec((1, D), lambda i, s: (0, jnp.bitwise_xor(i, jnp.right_shift(s[S_SEQ], 1)))),
            ],
            grid=(2,),
            vmem=14,
            name="mlp",
        )
        acc = [out_y, out_dh]
        db_fc.append(db)
        acts.append(both(act))

    if fast:
        first = Halves(
            line, *mlp_grads(line, False, sels, acts[0]),
            [("grp", 8, 2), ("seq", 4, 1), ("grp", 8, 4), ("seq", 4, 2)],
        )
        (acts[1],) = line.wait(acts[1])
    block_output, d_resid, d_attn, rho, ds_own, sums = line.call(
        back_body,
        [*acc, resid, cotangent, w_t, v_t13, o_t, den, fq],
        [whole((rows, D))] * 4
        + [w_rows(D, lambda i, s: 3), vec_whole, whole((D, rows)), whole((16, rows)), whole((2 * D, rows))],
        [
            sds((rows, D), bf16),
            sds((rows, D), f32),
            sds((D, rows), bf16),
            sds((HEADS * AUG, rows), bf16),
            sds(st_shape, bf16),
            sds((4, D), f32),
        ],
        [whole((rows, D))] * 2
        + [whole((D, rows)), whole((HEADS * AUG, rows)), whole(st_shape), whole((4, D))],
        scratch=[pltpu.VMEM((D, rows), bf16)],
        vmem=10,
        name="back",
    )
    back_states = [swap(ds_own, "seq", n_seq, k + 1) for k in range(n_peer)]
    if fast:
        second = mlp_grads(line, True, sels, acts[1])
        (back_states,) = line.wait(back_states)
        second = Halves(
            line, *second, [("seq", 4, 2), ("grp", 8, 2), ("seq", 4, 1), ("grp", 8, 4)]
        )

    grads = [sds((4, D, rows), bf16), sds((D, HD), f32), sds((D, 3), f32)]
    got = []
    for start, count in ((0, N_QUAD),):

        def at(block, axis=0, start=start):
            return pl.BlockSpec(
                tuple(block), lambda i, s: tuple(start + i if d == axis else 0 for d in range(len(block)))
            )

        feat, head = at((2 * wide, rows)), at((wide, rows))
        state = at((QUAD * AUG, 2 * HD))
        args = [*back_states, fq, fk, v_t, rho, s_in, qt, kt, w_t, d_attn]
        got = line.call(
            partial(attend_back_body, n_peer),
            [*args, *got],
            [state] * n_peer
            + [feat, feat, head, at((QUAD * AUG, rows)), state, head, head]
            + [pl.BlockSpec((HD, wide), lambda i, s, start=start: ((4 * D + 2 * FF) // HD, start + i)), head]
            + [pl.BlockSpec(memory_space=pl.ANY)] * len(got),
            grads,
            [at((4, wide, rows), 1), at((wide, HD)), at((wide, 3))],
            grid=(count,),
            aliases={1 + len(args) + k: k for k in range(len(got))},
            hold=1,
            vmem=12,
            name="attend_back",
        )
    dp, dm, db_qkv = got
    dp_both = both(dp)
    db_fc_rows = jnp.concatenate(db_fc, axis=1).reshape(FF // D, D)
    input_grad, *small = line.call(
        partial(input_body, fast),
        [dp, w_t, tokens, d_resid, v_t13, sums, db_fc_rows, db_qkv, dm],
        [
            along((1, D, rows)),
            w_rows(D, lambda i, s: i),
            whole((rows, D)),
            whole((rows, D)),
            vec_whole,
            whole((4, D)),
            whole((FF // D, D)),
            whole((D, 3)),
            whole((D, HD)),
        ],
        [sds((rows, D), bf16)] + [sds((1, r, 2 * HD), f32) for r in sel_rows],
        [whole((rows, D))] + [whole((1, r, 2 * HD)) for r in sel_rows],
        grid=(3,),
        scratch=[pltpu.VMEM((rows, D), f32)],
        vmem=14,
        name="input",
    )
    states_v = [v.T for v in (master_vecs, moment_vecs, square_vecs, average_vecs)]
    if fast:
        theirs, mine = small
        small = [mine, swap(theirs, "grp", 8, 1)]
        first.step(hold=14)
        second.step(hold=60)
        tail = tail_grads(line, sels, dp_both, small)
        tail_first, tail_second = tail_one(line, tail)
        first.step()
        second.step(hold=4)
        far = tail_first()
        first.step()
        second.step()
        mine = final_both(line, [first, second])
        part_x, part_y = swap(mine, "seq", 4, 1), swap(mine, "seq", 4, 2)
        both_mine = [mine, part_x, part_y, swap(part_x, "seq", 4, 2)]
        last = tail_second(*far)
        last_mine, small_own = tail_final(line, last)
        outs = adam_piece(
            line, both_mine, states_m, None,
            lambda i: jnp.where(jnp.bitwise_and(i, 2) == 0, 8, 4) + 2 * (i // 4) + jnp.bitwise_and(i, 1),
        )
        last_parts = gather_parts(last_mine)
        outs = adam_piece(
            line, last_parts, states_m, outs, lambda i: jnp.where(i < 4, i, (4 * D + 2 * FF) // D),
            small=[small_own], vecs=states_v,
        )
        mats, vecs = outs[:6], [v.T for v in outs[6:]]
    else:
        h1t, obt, h2t = sels[0][1], sels[0][2], sels[0][3]
        joined = [jnp.transpose(a[0], (0, 2, 1, 3)).reshape(2, rows, piece) for a in acts]
        dn = [dot_tn(cotangent, v[0]) for v in joined]
        fc = [dot_nn(h2t, v[1]) for v in joined]
        qkvo = [dot_nt(h1t, dp[k]) for k in range(3)] + [dot_nt(obt, dp[3])]
        small = small[0][0]
        grad = jnp.concatenate([*qkvo, *fc, *dn, small[:, :HD]], axis=1).astype(bf16)
        own = lax.psum_scatter(grad, "grp", scatter_dimension=0, tiled=True)
        own = lax.psum(own, "seq").astype(f32)
        own_v = lax.psum(lax.psum_scatter(small, "grp", scatter_dimension=0, tiled=True), "seq")
        own_v = own_v[:, HD : HD + n_vec]
        results = adam_math(own, *states_m, learn_rate)
        mats = [own, *results, results[0].astype(bf16)]
        results = adam_math(own_v.T, *states_v, vector_rate)
        vecs = [own_v, *[v.T for v in (*results, results[0].astype(bf16))]]
    flat = [x for pair_ in zip(mats, vecs) for x in pair_]
    return (block_output, input_grad, *flat)


def solution(mesh):
    tok = P(("grp", "seq"), None)
    own = P("grp", None)
    in_specs = (tok, tok, P("grp"), P(), P()) + (own,) * 8
    out_specs = (tok, tok) + (own,) * 12
    body = partial(on_device, mesh.shape["seq"], mesh.shape["grp"])
    return jax.shard_map(body, mesh=mesh, in_specs=in_specs, out_specs=out_specs, check_vma=False)
```

```python
from functools import partial

import jax
import jax.numpy as jnp
from jax import lax
from jax.experimental import pallas as pl
from jax.experimental.pallas import tpu as pltpu
from jax.sharding import PartitionSpec as P

D = 768
HEADS = 12
HD = 64
FF = 3072
QUAD = 4
N_QUAD = HEADS // QUAD
AUG = 80

norm_eps = 1e-05
adam_eps = 1e-08
beta_first = 0.5
beta_second = 0.5
learn_rate = 0.01
vector_rate = 0.06
decay_rate = 0.1
average_keep = 0.9

f32 = jnp.float32
bf16 = jnp.bfloat16

S_SEQ, S_GRP, S_MASK, S_BACK = 0, 1, 4, 8

MIB = 1024 * 1024


def dot_nn(a, b):
    return lax.dot_general(a, b, (((1,), (0,)), ((), ())), preferred_element_type=f32)


def dot_nt(a, b):
    return lax.dot_general(a, b, (((1,), (1,)), ((), ())), preferred_element_type=f32)


def dot_tn(a, b):
    return lax.dot_general(a, b, (((0,), (0,)), ((), ())), preferred_element_type=f32)


def whole(shape):
    return pl.BlockSpec(tuple(shape), lambda *_: (0,) * len(shape))


def along(block, axis=0):
    return pl.BlockSpec(tuple(block), lambda i, s: tuple(i if d == axis else 0 for d in range(len(block))))


def sds(shape, dtype):
    return jax.ShapeDtypeStruct(tuple(shape), dtype)


class Line:
    def __init__(self, scal):
        self.scal = scal
        self.stay = set()

    def wait(self, *values):
        self.scal, values = lax.optimization_barrier((self.scal, values))
        return values

    def call(self, body, args, in_specs, outs, out_specs, grid=(1,), scratch=(), vmem=32,
             hold=0, far=(), out_far=(), aliases=None, name=None):
        args = [
            pltpu.with_memory_space_constraint(a, pltpu.HBM) if id(a) in self.stay or k in far else a
            for k, a in enumerate(args)
        ]
        got = pl.pallas_call(
            body,
            out_shape=tuple(pltpu.HBM(o.shape, o.dtype) if k in out_far else o for k, o in enumerate(outs)),
            grid_spec=pltpu.PrefetchScalarGridSpec(
                num_scalar_prefetch=1,
                grid=grid,
                in_specs=list(in_specs),
                out_specs=tuple(out_specs),
                scratch_shapes=list(scratch),
            ),
            compiler_params=pltpu.CompilerParams(
                dimension_semantics=("arbitrary",) * len(grid), vmem_limit_bytes=vmem * MIB
            ),
            cost_estimate=pl.CostEstimate(
                flops=hold * 10**9, bytes_accessed=1024, transcendentals=0
            ),
            input_output_aliases=aliases or {},
            name=name,
        )(self.scal, *args)
        self.scal, got = lax.optimization_barrier((self.scal, got))
        return got


def store_sel(refs, at, values, scal):
    if len(refs) == 1:
        refs[0][at] = values
        return
    block = D // 8
    for j in range(8):
        rel = jnp.bitwise_xor(scal[S_GRP], j)
        place = pl.multiple_of(jnp.right_shift(rel, 1) * block, block)
        odd = jnp.bitwise_and(rel, 1)
        part = values[j * block : (j + 1) * block, :]

        @pl.when(odd == 1)
        def _(part=part, place=place):
            refs[0][at, pl.ds(place, block), :] = part

        @pl.when(odd == 0)
        def _(part=part, place=place):
            refs[1][at, pl.ds(place, block), :] = part


def normalize(values):
    average = jnp.mean(values, axis=1, keepdims=True)
    centered = values - average
    variance = jnp.mean(centered * centered, axis=1, keepdims=True)
    inverse = lax.rsqrt(variance + norm_eps)
    return centered * inverse, inverse


def quad_maps(hedge_t):
    wide = QUAD * HD
    row = lax.broadcasted_iota(jnp.int32, (wide, HD), 0)
    col = lax.broadcasted_iota(jnp.int32, (wide, HD), 1)
    spread = (jnp.bitwise_and(row, HD - 1) == col).astype(bf16)
    tiled = dot_nn(spread, hedge_t)
    big_r = lax.broadcasted_iota(jnp.int32, (wide, wide), 0)
    big_c = lax.broadcasted_iota(jnp.int32, (wide, wide), 1)
    same = jnp.right_shift(big_r, 6) == jnp.right_shift(big_c, 6)
    return jnp.where(same, tiled, 0.0)


def ones_rows(count):
    return (lax.broadcasted_iota(jnp.int32, (AUG - HD, count), 0) == 0).astype(f32).astype(bf16)


def rows_up(values):
    return jnp.concatenate([values, jnp.zeros((3, values.shape[1]), f32)], axis=0).T


def features(pt, maps):
    high = pt.astype(bf16)
    rest = (pt - high.astype(f32)).astype(bf16)
    scores = dot_nn(jnp.concatenate([maps, maps], axis=1), jnp.concatenate([high, rest], axis=0))
    heads = []
    for h in range(QUAD):
        s = scores[h * HD : (h + 1) * HD, :]
        top = jnp.max(s, axis=0, keepdims=True)
        bottom = jnp.min(s, axis=0, keepdims=True)
        pos = jnp.exp(s - top)
        neg = jnp.exp(bottom - s)
        pos = pos * (1.0 / jnp.sum(pos, axis=0, keepdims=True))
        neg = neg * (1.0 / jnp.sum(neg, axis=0, keepdims=True))
        heads.append(jnp.concatenate([pos, neg], axis=0).astype(bf16))
    return high, heads


def keys_body(scal, x_ref, wk_ref, wv_ref, hedge_ref, vt_ref, vq_ref, h1_ref, kt_ref, fk_ref, vt_out, s_ref):
    rows = x_ref.shape[0]

    @pl.when(pl.program_id(0) == 0)
    def _():
        normed, _ = normalize(x_ref[...].astype(f32))
        vt = vt_ref[...].astype(f32)
        h1_ref[...] = (normed * vt[0:1] + vt[1:2]).astype(bf16)

    h1 = h1_ref[...]
    bias = rows_up(vq_ref[...].astype(f32))
    v_t = (dot_nt(wv_ref[...], h1) + bias[:, 8:9]).astype(bf16)
    vt_out[...] = v_t
    pt = dot_nt(wk_ref[...], h1) + bias[:, 7:8]
    kt_ref[...], heads = features(pt, quad_maps(hedge_ref[...]).astype(bf16))
    extra = ones_rows(rows)
    for h, both in enumerate(heads):
        fk_ref[h * 2 * HD : (h + 1) * 2 * HD, :] = both
        va = jnp.concatenate([v_t[h * HD : (h + 1) * HD, :], extra], axis=0)
        s_ref[h * AUG : (h + 1) * AUG, :] = dot_nt(va, both).astype(bf16)


def queries_body(n_sel, scal, h1_ref, g_ref, wq_ref, hedge_ref, vq_ref, *refs):
    sel = refs[:n_sel]
    qt_ref, fq_ref = refs[n_sel:]
    h1 = h1_ref[...]

    @pl.when(pl.program_id(0) == 0)
    def _():
        store_sel(sel, 0, g_ref[...].T, scal)
        store_sel(sel, 1, h1.T, scal)

    bias = rows_up(vq_ref[...].astype(f32))
    pt = dot_nt(wq_ref[...], h1) + bias[:, 6:7]
    qt_ref[...], heads = features(pt, quad_maps(hedge_ref[...]).astype(bf16))
    for h, both in enumerate(heads):
        fq_ref[h * 2 * HD : (h + 1) * 2 * HD, :] = both


def tri_mask(half):
    return lax.broadcasted_iota(jnp.int32, (half, half), 0) <= lax.broadcasted_iota(
        jnp.int32, (half, half), 1
    )


def masked_pair(left0, left1, right, keep):
    half = right.shape[1] // 2
    full = dot_tn(left0, right)
    low = dot_tn(left1, right[:, half:])
    diag0 = jnp.where(keep, full[:, :half], 0.0).astype(bf16)
    above = full[:, half:].astype(bf16)
    diag1 = jnp.where(keep, low, 0.0).astype(bf16)
    return diag0, above, diag1


def local_body(scal, fq_ref, fk_ref, vt_ref, num_ref):
    rows = fq_ref.shape[1]
    half = rows // 2
    keep = tri_mask(half)
    extra = ones_rows(rows)
    for h in range(QUAD):
        fq = fq_ref[h * 2 * HD : (h + 1) * 2 * HD, :]
        fk = fk_ref[h * 2 * HD : (h + 1) * 2 * HD, :]
        va = jnp.concatenate([vt_ref[h * HD : (h + 1) * HD, :], extra], axis=0)
        a00, a01, a11 = masked_pair(fk[:, :half], fk[:, half:], fq, keep)
        num_ref[h * AUG : (h + 1) * AUG, :half] = dot_nn(va[:, :half], a00)
        num_ref[h * AUG : (h + 1) * AUG, half:] = dot_nn(va[:, :half], a01) + dot_nn(va[:, half:], a11)


def weighted_state(scal, slot, parts):
    total = None
    for k, part in enumerate(parts):
        term = scal[slot + k].astype(f32) * part.astype(f32)
        total = term if total is None else total + term
    return total.astype(bf16)


def after_body(n_sel, n_parts, scal, *refs):
    parts = refs[:n_parts]
    num_ref, fq_ref, x_ref, w_ref, vt_ref = refs[n_parts : n_parts + 5]
    o_ref, den_ref, r_ref, h2_ref, sin_ref = refs[n_parts + 5 + n_sel : n_parts + 10 + n_sel]
    sel = refs[-1 - n_sel : -1]
    ob_ref = refs[-1]
    vt = vt_ref[...].astype(f32)
    state = weighted_state(scal, S_MASK, [p[...] for p in parts])
    sin_ref[...] = state
    for h in range(HEADS):
        num = num_ref[h * AUG : (h + 1) * AUG, :] + dot_nn(
            state[h * AUG : (h + 1) * AUG, :], fq_ref[h * 2 * HD : (h + 1) * 2 * HD, :]
        )
        den = num[HD : HD + 1, :]
        out = num[:HD, :] * (1.0 / den)
        o_ref[h * HD : (h + 1) * HD, :] = out
        den_ref[h : h + 1, :] = den
        ob_ref[h * HD : (h + 1) * HD, :] = out.astype(bf16)
    obt = ob_ref[...]
    store_sel(sel, 0, obt, scal)
    r = x_ref[...].astype(f32) + dot_nt(obt.T, w_ref[...]) + vt[4:5]
    r_ref[...] = r
    normed, _ = normalize(r)
    h2 = (normed * vt[2:3] + vt[3:4]).astype(bf16)
    h2_ref[...] = h2
    store_sel(sel, 1, h2.T, scal)


gelu_c = 0.7978845608028654
gelu_k = 0.044715


def mlp_body(first, scal, h2_ref, g_ref, wf_ref, wd_ref, bias_ref, *refs):
    if first:
        out_ref, dh_ref, act_ref, db_ref = refs
    else:
        out_in, dh_in, out_ref, dh_ref, act_ref, db_ref = refs
    u = dot_nt(h2_ref[...], wf_ref[...]) + bias_ref[...].astype(f32)
    de = dot_nt(g_ref[...], wd_ref[...])
    uu = u * u
    t = jnp.tanh(gelu_c * u * (1.0 + gelu_k * uu))
    half_t = 0.5 * (1.0 + t)
    e = (u * half_t).astype(bf16)
    slope = half_t + 0.5 * u * (1.0 - t * t) * (gelu_c * (1.0 + 3.0 * gelu_k * uu))
    du = (de * slope).astype(bf16)
    act_ref[0, 0] = e
    act_ref[1, 0] = du
    db_ref[...] = jnp.sum(du.astype(f32), axis=0, keepdims=True)
    add_out = dot_nn(e, wd_ref[...])
    add_dh = dot_nn(du, wf_ref[...])
    step = pl.program_id(0)

    @pl.when(step == 0)
    def _():
        if first:
            out_ref[...] = add_out
            dh_ref[...] = add_dh
        else:
            out_ref[...] = out_in[...] + add_out
            dh_ref[...] = dh_in[...] + add_dh

    @pl.when(step > 0)
    def _():
        out_ref[...] += add_out
        dh_ref[...] += add_dh


def back_body(scal, out_ref, dh_ref, r_ref, g_ref, w_ref, vt_ref, o_ref, den_ref, fq_ref, y_ref, dr_ref,
              da_ref, rho_ref, ds_ref, sums_ref, do_ref):
    vt = vt_ref[...].astype(f32)
    r = r_ref[...]
    y_ref[...] = (r + out_ref[...] + vt[5:6]).astype(bf16)
    grad_out = g_ref[...].astype(f32)
    normed, inverse = normalize(r)
    up = dh_ref[...]
    dn = up * vt[2:3]
    dr = grad_out + inverse * (
        dn - jnp.mean(dn, axis=1, keepdims=True) - normed * jnp.mean(dn * normed, axis=1, keepdims=True)
    )
    dr_ref[...] = dr
    da = dr.astype(bf16)
    da_ref[...] = da.T
    sums_ref[...] = jnp.concatenate(
        [
            jnp.sum(up * normed, axis=0, keepdims=True),
            jnp.sum(up, axis=0, keepdims=True),
            jnp.sum(da.astype(f32), axis=0, keepdims=True),
            jnp.sum(grad_out, axis=0, keepdims=True),
        ],
        axis=0,
    )
    do_ref[...] = dot_nn(da, w_ref[...]).astype(bf16).T
    rows = r.shape[0]
    zero_row = lax.broadcasted_iota(jnp.int32, (AUG - HD, rows), 0) == 0
    for h in range(HEADS):
        dout = do_ref[h * HD : (h + 1) * HD, :].astype(f32)
        inv = 1.0 / den_ref[h : h + 1, :]
        rho = (dout * inv).astype(bf16)
        c = -jnp.sum(dout * o_ref[h * HD : (h + 1) * HD, :], axis=0, keepdims=True) * inv
        extra = jnp.where(zero_row, jnp.broadcast_to(c, (AUG - HD, rows)), 0.0).astype(bf16)
        ra = jnp.concatenate([rho, extra], axis=0)
        rho_ref[h * AUG : (h + 1) * AUG, :] = ra
        ds_ref[h * AUG : (h + 1) * AUG, :] = dot_nt(ra, fq_ref[h * 2 * HD : (h + 1) * 2 * HD, :]).astype(bf16)


def feature_back(feat, upstream):
    pos, neg = feat[:HD].astype(f32), feat[HD:].astype(f32)
    up_pos, up_neg = upstream[:HD], upstream[HD:]
    return pos * (up_pos - jnp.sum(pos * up_pos, axis=0, keepdims=True)) - neg * (
        up_neg - jnp.sum(neg * up_neg, axis=0, keepdims=True)
    )


def attend_back_body(n_parts, scal, *refs):
    parts = refs[:n_parts]
    (fq_ref, fk_ref, vt_ref, rho_ref, sin_ref, qt_ref, kt_ref, hedge_ref, da_ref) = refs[n_parts : n_parts + 9]
    dp_ref, dm_ref, db_ref = refs[-3:]
    dp_ref[3] = da_ref[...]
    rows = fq_ref.shape[1]
    half = rows // 2
    keep = tri_mask(half)
    extra = ones_rows(rows)
    back_state = weighted_state(scal, S_BACK, [p[...] for p in parts])
    ds_q, ds_k = [], []
    for h in range(QUAD):
        fq = fq_ref[h * 2 * HD : (h + 1) * 2 * HD, :]
        fk = fk_ref[h * 2 * HD : (h + 1) * 2 * HD, :]
        head = slice(h * HD, (h + 1) * HD)
        aug = slice(h * AUG, (h + 1) * AUG)
        va = jnp.concatenate([vt_ref[head, :], extra], axis=0)
        ra = rho_ref[aug, :]
        state, back = sin_ref[aug, :], back_state[aug, :]
        a00, a01, a11 = masked_pair(fk[:, :half], fk[:, half:], fq, keep)
        g00, g01, g11 = masked_pair(va[:, :half], va[:, half:], ra, keep)
        far = dot_tn(state, ra)
        left = far[:, :half] + dot_nn(fk[:, :half], g00)
        right = far[:, half:] + dot_nn(fk[:, :half], g01) + dot_nn(fk[:, half:], g11)
        dfq = jnp.concatenate([left, right], axis=1)
        far_k = dot_tn(back, va)
        left = far_k[:, :half] + dot_nt(fq[:, :half], g00) + dot_nt(fq[:, half:], g01)
        right = far_k[:, half:] + dot_nt(fq[:, half:], g11)
        dfk = jnp.concatenate([left, right], axis=1)
        far_v = dot_nn(back, fk)[:HD]
        rv = ra[:HD]
        left = far_v[:, :half] + dot_nt(rv[:, :half], a00) + dot_nt(rv[:, half:], a01)
        right = far_v[:, half:] + dot_nt(rv[:, half:], a11)
        dp_ref[2, head, :] = jnp.concatenate([left, right], axis=1).astype(bf16)
        dsq = feature_back(fq, dfq).astype(bf16)
        dsk = feature_back(fk, dfk).astype(bf16)
        ds_q.append(dsq)
        ds_k.append(dsk)
        dm_ref[head, :] = dot_nt(qt_ref[head, :], dsq) + dot_nt(kt_ref[head, :], dsk)
    maps = quad_maps(hedge_ref[...]).T.astype(bf16)
    dq = dot_nn(maps, jnp.concatenate(ds_q, axis=0)).astype(bf16)
    dk = dot_nn(maps, jnp.concatenate(ds_k, axis=0)).astype(bf16)
    dp_ref[0] = dq
    dp_ref[1] = dk
    db_ref[...] = jnp.concatenate(
        [jnp.sum(v.astype(f32), axis=1, keepdims=True) for v in (dq, dk, dp_ref[2])], axis=1
    )


def input_body(fast, scal, dp_ref, w_ref, x_ref, dr_ref, vt_ref, sums_ref, dbfc_ref, db_ref, dm_ref, *refs):
    gin_ref, *small_refs, acc_ref = refs
    step = pl.program_id(0)
    part = dot_tn(dp_ref[0], w_ref[...])

    @pl.when(step == 0)
    def _():
        acc_ref[...] = part

    @pl.when(step == 1)
    def _():
        acc_ref[...] += part

    @pl.when(step == 2)
    def _():
        vt = vt_ref[...].astype(f32)
        up = acc_ref[...] + part
        normed, inverse = normalize(x_ref[...].astype(f32))
        dn = up * vt[0:1]
        gin = dr_ref[...] + inverse * (
            dn - jnp.mean(dn, axis=1, keepdims=True) - normed * jnp.mean(dn * normed, axis=1, keepdims=True)
        )
        gin_ref[...] = gin.astype(bf16)
        rows16 = jnp.concatenate(
            [
                jnp.sum(up * normed, axis=0, keepdims=True),
                jnp.sum(up, axis=0, keepdims=True),
                sums_ref[...],
                jnp.zeros((3, D), f32),
                dbfc_ref[...],
                jnp.zeros((3, D), f32),
            ],
            axis=0,
        )
        cols = rows16.T
        lane = lax.broadcasted_iota(jnp.int32, (D, HD), 1)
        tail = jnp.concatenate([cols, jnp.zeros((D, HD - 16), f32)], axis=1)
        for k in range(3):
            tail = jnp.where(lane == 6 + k, db_ref[:, k : k + 1], tail)
        small = jnp.concatenate([dm_ref[...], tail], axis=1)
        store_sel(small_refs, 0, small, scal)


def mlp_grads_body(by_y, scal, *refs):
    sels, acts_a, acts_b, sels_h = refs[0:2], refs[2:4], refs[4:6], refs[6:8]
    send, keep = refs[8:]
    block = D // 8
    wq = send.shape[2]
    y_last = 1 - pl.program_id(0)

    def total(lefts, rights):
        return (dot_nn(lefts[0][0], rights[0][0, 0]) + dot_nn(lefts[1][0], rights[1][0, 0])).astype(bf16)

    for path, value in enumerate((total(sels, acts_a), total(sels_h, acts_b))):
        rows = slice(path * block, (path + 1) * block)
        for half in range(2):
            x_last = 1 - jnp.bitwise_xor(half, jnp.bitwise_and(scal[S_SEQ], 1))
            cols = slice(half * wq, (half + 1) * wq)

            def part(z, value=value, cols=cols):
                return value[z * block : (z + 1) * block, cols]

            if by_y:
                for bit, ref in ((0, send), (1, keep)):

                    @pl.when(y_last == bit)
                    def _(ref=ref, part=part, rows=rows, x_last=x_last):
                        for at, z in enumerate((3, 1, 2, 0)):
                            ref[4 * (at // 2) + 2 * x_last + at % 2, rows, :] = part(z)
            else:
                base = y_last + 4 * x_last
                for ref, order in ((send, (3, 1)), (keep, (2, 0))):
                    for at, z in enumerate(order):
                        ref[2 * at + base, rows, :] = part(z)


def mlp_grads(line, by_y, sels, acts, far=(), out_far=()):
    _, depth, rows = sels[0].shape
    half = sds((8, 2 * (D // 8), D // 2), bf16)

    def act(path):
        return pl.BlockSpec((1, 1, rows, D), lambda i, s: (path, i, 0, 0))

    def sel(slot):
        return pl.BlockSpec((1, depth, rows), lambda i, s: (slot, 0, 0))

    return line.call(
        partial(mlp_grads_body, by_y),
        [*sels, *acts, *acts, *sels],
        [sel(0)] * 2 + [act(0)] * 2 + [act(1)] * 2 + [sel(3)] * 2,
        [half] * 2,
        [whole(half.shape)] * 2,
        grid=(2,),
        vmem=24,
        far=far,
        out_far=out_far,
        name="mlp_grads",
    )


def pack_rows(values, count):
    return jnp.concatenate([values[b * count : (b + 1) * count] for b in range(3)], axis=1)


def unpack_rows(values):
    return jnp.concatenate([values[:, b * 128 : (b + 1) * 128] for b in range(3)], axis=0)


def order_a(i):
    return jnp.where(i < 2, 2 * i + 1, 2 * i - 4)


def order_b(i):
    return jnp.where(i < 2, i + 2, i - 2)


def tail_grads_body(scal, *refs):
    h1, ob, dqk, dvo = refs[0:2], refs[2:4], refs[4:6], refs[6:8]
    small_own, small_other, send_a, keep_a, send_b, keep_b, small_ref = refs[8:]
    step = pl.program_id(0)
    wq = send_a.shape[1]
    qb = jnp.bitwise_xor(order_b(step), scal[S_SEQ])
    at = pl.multiple_of(jnp.bitwise_and(step, 1) * wq, wq)

    def total(lefts, rights):
        return (dot_nt(lefts[0][0], rights[0][0]) + dot_nt(lefts[1][0], rights[1][0])).astype(bf16)

    def put(send, keep, value):
        @pl.when(step < 2)
        def _():
            send[pl.ds(at, wq), :] = value

        @pl.when(step >= 2)
        def _():
            keep[pl.ds(at, wq), :] = value

    put(send_a, keep_a, total(h1, dqk))

    @pl.when(qb < 2)
    def _():
        put(send_b, keep_b, total(h1, dvo))

    @pl.when(qb >= 2)
    def _():
        put(send_b, keep_b, total(ob, dvo))

    @pl.when(step == 0)
    def _():
        small = pack_rows(small_own[0] + small_other[0].astype(f32), 128)
        small_ref[...] = small
        send_a[2 * wq :, :] = small.astype(bf16)


def tail_grads(line, sels, dp, small):
    _, depth, rows = sels[0].shape
    wq = D // 2
    dp = [v.reshape(8, wq, rows) for v in dp]

    def sel(slot):
        return pl.BlockSpec((1, depth, rows), lambda i, s: (slot, 0, 0))

    outs = [
        sds((2 * wq + 128, wq), bf16), sds((2 * wq, wq), bf16),
        sds((2 * wq, wq), bf16), sds((2 * wq, wq), bf16), sds((128, wq), f32),
    ]
    return line.call(
        tail_grads_body,
        [*sels, *sels, *dp, *dp, *small],
        [sel(1)] * 2
        + [sel(2)] * 2
        + [pl.BlockSpec((1, wq, rows), lambda i, s: (jnp.bitwise_xor(order_a(i), s[S_SEQ]), 0, 0))] * 2
        + [pl.BlockSpec((1, wq, rows), lambda i, s: (4 + jnp.bitwise_xor(order_b(i), s[S_SEQ]), 0, 0))] * 2
        + [whole(small[0].shape)] * 2,
        outs,
        [whole(o.shape) for o in outs],
        grid=(4,),
        vmem=10,
        hold=4,
        name="tail_grads",
    )


def swap(value, axis, size, bit):
    return lax.ppermute(value, axis, [(i, i ^ bit) for i in range(size)])


def halve_body(scal, keep_ref, recv_ref, send_ref, left_ref):
    half = send_ref.shape[0]
    send_ref[...] = (keep_ref[:half].astype(f32) + recv_ref[:half].astype(f32)).astype(bf16)
    left_ref[...] = (keep_ref[half:].astype(f32) + recv_ref[half:].astype(f32)).astype(left_ref.dtype)


class Halves:
    def __init__(self, line, send, keep, stages):
        self.line, self.keep, self.stages = line, keep, list(stages)
        self.recv = swap(send, *self.stages.pop(0))

    def step(self, hold=0):
        count, rows, wq = self.keep.shape
        shape = (count // 2, rows, wq)
        send, self.keep = self.line.call(
            halve_body, [self.keep, self.recv], [whole(self.keep.shape)] * 2,
            [sds(shape, bf16), sds(shape, self.keep.dtype)], [whole(shape)] * 2,
            vmem=8, hold=hold, name="halve",
        )
        self.recv = swap(send, *self.stages.pop(0))


def final_body(scal, *refs):
    out = refs[-1]
    for j in range(2):
        out[j] = (refs[2 * j][0].astype(f32) + refs[2 * j + 1][0].astype(f32)).astype(bf16)


def final_both(line, pieces):
    shape = (2,) + pieces[0].keep.shape[1:]
    (mine,) = line.call(
        final_body, [v for p in pieces for v in (p.keep, p.recv)], [whole((1,) + shape[1:])] * 4,
        [sds(shape, bf16)], [whole(shape)], vmem=4, name="final",
    )
    return mine.reshape(4, D // 8, shape[2])


def tail_one_body(scal, keep_a, recv_a, keep_b, recv_b, small_ref, send_a, send_b):
    wq = send_b.shape[0]
    send_a[:wq, :] = (keep_a[wq : 2 * wq].astype(f32) + recv_a[wq : 2 * wq].astype(f32)).astype(bf16)
    send_a[wq:, :] = (small_ref[...] + recv_a[2 * wq :].astype(f32)).astype(bf16)
    send_b[...] = (keep_b[wq:].astype(f32) + recv_b[wq:].astype(f32)).astype(bf16)


def tail_two_body(scal, keep_a, recv_a, keep_b, recv_b, small_ref, far_a, far_b, own_ref, *out_refs):
    wq = far_b.shape[0]
    block = D // 8
    small = small_ref[...] + recv_a[2 * wq :].astype(f32) + far_a[wq:].astype(f32)
    small = unpack_rows(small)
    first = keep_a[:wq].astype(f32) + recv_a[:wq].astype(f32) + far_a[:wq].astype(f32)
    second = keep_b[:wq].astype(f32) + recv_b[:wq].astype(f32) + far_b[...].astype(f32)
    for z, ref in enumerate((own_ref, *out_refs)):
        rows = slice(z * block, (z + 1) * block)
        ref[:block, :] = first[rows].astype(ref.dtype)
        ref[block : 2 * block, :] = second[rows].astype(ref.dtype)
        ref[2 * block :, :] = pack_rows(small[rows], block // 3).astype(ref.dtype)


def tail_final_body(scal, *refs):
    mine_ref, small_ref = refs[-2:]
    block = mine_ref.shape[1]
    total = refs[0][...]
    for ref in refs[1:-2]:
        total = total + ref[...].astype(f32)
    mine_ref[0] = total[:block].astype(bf16)
    mine_ref[1] = total[block : 2 * block].astype(bf16)
    small_ref[...] = unpack_rows(total[2 * block :])


def tail_one(line, tail):
    send_a, keep_a, send_b, keep_b, small = tail
    wq = D // 2
    recv_a, recv_b = swap(send_a, "seq", 4, 1), swap(send_b, "seq", 4, 2)
    shapes = [sds((wq + 128, wq), bf16), sds((wq, wq), bf16)]

    def first():
        args = [keep_a, recv_a, keep_b, recv_b, small]
        next_a, next_b = line.call(
            tail_one_body, args, [whole(v.shape) for v in args], shapes, [whole(v.shape) for v in shapes],
            vmem=12, name="tail_one",
        )
        return swap(next_a, "seq", 4, 2), swap(next_b, "seq", 4, 1)

    def second(far_a, far_b):
        args = [keep_a, recv_a, keep_b, recv_b, small, far_a, far_b]
        shape = (2 * (D // 8) + D // 24, wq)
        own, *sends = line.call(
            tail_two_body, args, [whole(v.shape) for v in args], [sds(shape, f32)] + [sds(shape, bf16)] * 3,
            [whole(shape)] * 4, vmem=10, hold=5, name="tail_two",
        )
        return [own, *(swap(v, "grp", 8, 2 * (k + 1)) for k, v in enumerate(sends))]

    return first, second


def tail_final(line, args):
    wq = D // 2
    shapes = [sds((2, D // 8, wq), bf16), sds((D // 8, 2 * HD), f32)]
    return line.call(
        tail_final_body, args, [whole(v.shape) for v in args], shapes, [whole(v.shape) for v in shapes],
        vmem=6, hold=5, name="tail_final",
    )


def gather_parts(mine):
    return [mine] + [swap(mine, "seq", 4, k) for k in (1, 2, 3)]


def adam_math(grad, master, first, second, average, rate):
    new_first = beta_first * first + (1.0 - beta_first) * grad
    new_second = beta_second * second + (1.0 - beta_second) * grad * grad
    new_master = master - rate * (
        new_first / (jnp.sqrt(new_second) + adam_eps) + decay_rate * master
    )
    new_average = average_keep * average + (1.0 - average_keep) * new_master
    return new_master, new_first, new_second, new_average


def adam_body(n_alias, has_small, scal, *refs):
    parts, refs = refs[:4], refs[4:]
    if has_small:
        small, vec_in, refs = refs[0], refs[1:5], refs[5:]
    states, refs = refs[:4], refs[4 + n_alias :]
    outs, vec_outs = refs[:6], refs[6:]
    grad_ref = outs[0]
    count, _, wq = parts[0].shape
    step = pl.program_id(0)
    path, half = jnp.right_shift(step, 1), jnp.bitwise_and(step, 1)
    for k, ref in enumerate(parts):
        quarter = jnp.bitwise_xor(scal[S_SEQ], k)

        @pl.when((jnp.right_shift(quarter, 1) == half) & (step < 2 * count))
        def _(ref=ref, quarter=quarter):
            at = pl.multiple_of(jnp.bitwise_and(quarter, 1) * wq, 128)
            grad_ref[:, pl.ds(at, wq)] = ref[jnp.minimum(path, count - 1)].astype(f32)

    if has_small:

        @pl.when(step == 2 * count)
        def _():
            grad_ref[...] = jnp.zeros_like(grad_ref)
            grad_ref[:, : 2 * HD] = small[...]
            grad = small[...].T[HD : HD + vec_in[0].shape[0]]
            results = adam_math(grad, *[v[...] for v in vec_in], vector_rate)
            for ref, value in zip(vec_outs, (grad, *results, results[0])):
                ref[...] = value.astype(ref.dtype)

    results = adam_math(grad_ref[...], *[v[...] for v in states], learn_rate)
    for ref, value in zip(outs[1:], (*results, results[0])):
        ref[...] = value.astype(ref.dtype)


def adam_piece(line, parts, states, outs, block_of, small=(), vecs=()):
    count, block, _ = parts[0].shape
    rows, wide = states[0].shape
    spec = pl.BlockSpec((block, D), lambda i, s: (0, block_of(i)))
    anywhere = pl.BlockSpec(memory_space=pl.ANY)
    n_alias = 0 if outs is None else 6
    shapes = [sds((rows, wide), f32)] * 5 + [sds((rows, wide), bf16)]
    args = [*parts, *small, *vecs, *states]
    n_before = len(args)
    out_specs = [spec] * 6
    if vecs:
        shapes += [sds(vecs[0].shape, f32)] * 5 + [sds(vecs[0].shape, bf16)]
        out_specs += [whole(vecs[0].shape)] * 6
    return line.call(
        partial(adam_body, n_alias, bool(vecs)),
        [*args, *(outs or [])],
        [whole(v.shape) for v in [*parts, *small, *vecs]] + [spec] * 4 + [anywhere] * n_alias,
        shapes,
        out_specs,
        grid=(2 * count + (1 if vecs else 0),),
        aliases={1 + n_before + i: i for i in range(n_alias)},
        vmem=16,
        name="adam",
    )


def on_device(
    n_seq,
    n_grp,
    tokens,
    cotangent,
    seq_len,
    weight_mats,
    weight_vecs,
    master_mats,
    master_vecs,
    moment_mats,
    moment_vecs,
    square_mats,
    square_vecs,
    average_mats,
    average_vecs,
):
    rows = tokens.shape[0]
    fast = n_seq == 4 and n_grp == 8
    seq_at = lax.axis_index("seq")
    grp_at = lax.axis_index("grp")
    slot = jnp.arange(16, dtype=jnp.int32)
    seq_length = seq_len[0]
    peer = jnp.bitwise_xor(seq_at, jnp.bitwise_and(slot, 3) + 1)
    same = (peer * rows) // seq_length == (seq_at * rows) // seq_length
    before = (same & (peer < seq_at)).astype(jnp.int32)
    after = (same & (peer > seq_at)).astype(jnp.int32)
    scal = jnp.where(slot < 8, before, after)
    scal = jnp.where(slot == S_SEQ, seq_at if fast else 0, scal)
    scal = jnp.where(slot == S_GRP, grp_at, scal)
    line = Line(scal)

    w_t = weight_mats.T
    states_m = [master_mats, moment_mats, square_mats, average_mats]
    line.stay = {id(v) for v in (w_t, tokens, cotangent)}
    v_t13 = weight_vecs.T
    n_vec = v_t13.shape[0]
    bias_fc = v_t13[9:].reshape(1, FF)
    wide = QUAD * HD
    n_peer = n_seq - 1
    sel_rows = [D // 2, D // 2] if fast else [D]
    n_sel = len(sel_rows)
    sel_shapes = [sds((4, r, rows), bf16) for r in sel_rows]
    sel_low = [whole((2, r, rows)) for r in sel_rows]
    sel_high = [pl.BlockSpec((2, r, rows), lambda i, s: (1, 0, 0)) for r in sel_rows]

    def both(value):
        return [value, swap(value, "grp", 8, 1)] if fast else [value]

    def w_rows(count, at):
        return pl.BlockSpec((count, D), lambda i, s: (at(i, s), 0))

    hedge_spec = pl.BlockSpec((HD, wide), lambda i, s: ((4 * D + 2 * FF) // HD, i))
    vec_whole = whole(v_t13.shape)
    head_spec, feat_spec = along((wide, rows)), along((2 * wide, rows))
    aug_spec, quad_state = along((QUAD * AUG, rows)), along((QUAD * AUG, 2 * HD))
    st_shape = (HEADS * AUG, 2 * HD)
    vec_quad = pl.BlockSpec((n_vec, wide), lambda i, s: (0, i))
    h1, kt, fk, v_t, s_own = line.call(
        keys_body,
        [tokens, w_t, w_t, w_t, v_t13, v_t13],
        [
            whole((rows, D)),
            w_rows(wide, lambda i, s: N_QUAD + i),
            w_rows(wide, lambda i, s: 2 * N_QUAD + i),
            hedge_spec,
            vec_whole,
            vec_quad,
        ],
        [
            sds((rows, D), bf16),
            sds((D, rows), bf16),
            sds((2 * D, rows), bf16),
            sds((D, rows), bf16),
            sds(st_shape, bf16),
        ],
        [whole((rows, D)), head_spec, feat_spec, head_spec, quad_state],
        grid=(N_QUAD,),
        vmem=12,
        name="keys",
    )
    n_peer = n_seq - 1
    states = [swap(s_own, "seq", n_seq, k + 1) for k in range(n_peer)]
    got = line.call(
        partial(queries_body, n_sel),
        [h1, cotangent, w_t, w_t, v_t13],
        [whole((rows, D)), whole((rows, D)), w_rows(wide, lambda i, s: i), hedge_spec, vec_quad],
        sel_shapes + [sds((D, rows), bf16), sds((2 * D, rows), bf16)],
        sel_low + [head_spec, feat_spec],
        grid=(N_QUAD,),
        vmem=12,
        name="queries",
    )
    sels, (qt, fq) = got[:n_sel], got[n_sel:]

    (num,) = line.call(
        local_body,
        [fq, fk, v_t],
        [feat_spec, feat_spec, head_spec],
        [sds((HEADS * AUG, rows), f32)],
        [aug_spec],
        grid=(N_QUAD,),
        vmem=10,
        name="local",
    )
    got = line.call(
        partial(after_body, n_sel, n_peer),
        [*states, num, fq, tokens, w_t, v_t13, *sels],
        [whole(st_shape)] * n_peer
        + [whole(num.shape), whole(fq.shape), whole((rows, D)), w_rows(D, lambda i, s: 3), vec_whole]
        + [pl.BlockSpec(memory_space=pl.ANY)] * n_sel,
        [
            sds((D, rows), f32),
            sds((16, rows), f32),
            sds((rows, D), f32),
            sds((rows, D), bf16),
            sds(st_shape, bf16),
        ]
        + sel_shapes,
        [whole((D, rows)), whole((16, rows)), whole((rows, D)), whole((rows, D)), whole(st_shape)] + sel_high,
        aliases={n_peer + 6 + i: 5 + i for i in range(n_sel)},
        scratch=[pltpu.VMEM((D, rows), bf16)],
        vmem=10,
        name="after",
    )
    o_t, den, resid, h2, s_in = got[:5]
    sels = got[5:]
    if fast:
        sels = [sels[1], swap(sels[0], "grp", 8, 1)]

    n_piece = 2
    piece = FF // n_piece
    acc, acts, db_fc = [], [], []
    for j in range(n_piece):
        if j == 1:
            (sels,) = line.wait(sels)
        pair_of = lambda i, s, j=j: 2 * j + jnp.bitwise_xor(i, jnp.right_shift(s[S_SEQ], 1))
        out_y, out_dh, act, db = line.call(
            partial(mlp_body, j == 0),
            [h2, cotangent, w_t, w_t, bias_fc, *acc],
            [
                whole((rows, D)),
                whole((rows, D)),
                w_rows(D, lambda i, s: 4 + pair_of(i, s)),
                w_rows(D, lambda i, s: 8 + pair_of(i, s)),
                pl.BlockSpec((1, D), lambda i, s: (0, pair_of(i, s))),
            ]
            + [whole((rows, D))] * len(acc),
            [sds((rows, D), f32), sds((rows, D), f32), sds((2, 2, rows, D), bf16), sds((1, piece), f32)],
            [
                whole((rows, D)),
                whole((rows, D)),
                pl.BlockSpec((2, 1, rows, D), lambda i, s: (0, i, 0, 0)),
                pl.BlockSpec((1, D), lambda i, s: (0, jnp.bitwise_xor(i, jnp.right_shift(s[S_SEQ], 1)))),
            ],
            grid=(2,),
            vmem=14,
            name="mlp",
        )
        acc = [out_y, out_dh]
        db_fc.append(db)
        acts.append(both(act))

    if fast:
        first = Halves(
            line, *mlp_grads(line, False, sels, acts[0], out_far=(1,)),
            [("grp", 8, 2), ("seq", 4, 1), ("grp", 8, 4), ("seq", 4, 2)],
        )
        (acts[1],) = line.wait(acts[1])
    block_output, d_resid, d_attn, rho, ds_own, sums = line.call(
        back_body,
        [*acc, resid, cotangent, w_t, v_t13, o_t, den, fq],
        [whole((rows, D))] * 4
        + [w_rows(D, lambda i, s: 3), vec_whole, whole((D, rows)), whole((16, rows)), whole((2 * D, rows))],
        [
            sds((rows, D), bf16),
            sds((rows, D), f32),
            sds((D, rows), bf16),
            sds((HEADS * AUG, rows), bf16),
            sds(st_shape, bf16),
            sds((4, D), f32),
        ],
        [whole((rows, D))] * 2
        + [whole((D, rows)), whole((HEADS * AUG, rows)), whole(st_shape), whole((4, D))],
        scratch=[pltpu.VMEM((D, rows), bf16)],
        vmem=10,
        out_far=(1, 2, 3),
        name="back",
    )
    back_states = [swap(ds_own, "seq", n_seq, k + 1) for k in range(n_peer)]
    if fast:
        second = mlp_grads(line, True, sels, acts[1], far=range(2, 6))
        (back_states,) = line.wait(back_states)
        second = Halves(
            line, *second, [("seq", 4, 2), ("grp", 8, 2), ("seq", 4, 1), ("grp", 8, 4)]
        )

    grads = [sds((4, D, rows), bf16), sds((D, HD), f32), sds((D, 3), f32)]
    got = []
    for start, count in ((0, N_QUAD),):

        def at(block, axis=0, start=start):
            return pl.BlockSpec(
                tuple(block), lambda i, s: tuple(start + i if d == axis else 0 for d in range(len(block)))
            )

        feat, head = at((2 * wide, rows)), at((wide, rows))
        state = at((QUAD * AUG, 2 * HD))
        args = [*back_states, fq, fk, v_t, rho, s_in, qt, kt, w_t, d_attn]
        got = line.call(
            partial(attend_back_body, n_peer),
            [*args, *got],
            [state] * n_peer
            + [feat, feat, head, at((QUAD * AUG, rows)), state, head, head]
            + [pl.BlockSpec((HD, wide), lambda i, s, start=start: ((4 * D + 2 * FF) // HD, start + i)), head]
            + [pl.BlockSpec(memory_space=pl.ANY)] * len(got),
            grads,
            [at((4, wide, rows), 1), at((wide, HD)), at((wide, 3))],
            grid=(count,),
            aliases={1 + len(args) + k: k for k in range(len(got))},
            hold=1,
            far=(n_peer + 3, n_peer + 8),
            vmem=16,
            name="attend_back",
        )
    dp, dm, db_qkv = got
    dp_both = both(dp)
    db_fc_rows = jnp.concatenate(db_fc, axis=1).reshape(FF // D, D)
    input_grad, *small = line.call(
        partial(input_body, fast),
        [dp, w_t, tokens, d_resid, v_t13, sums, db_fc_rows, db_qkv, dm],
        [
            along((1, D, rows)),
            w_rows(D, lambda i, s: i),
            whole((rows, D)),
            whole((rows, D)),
            vec_whole,
            whole((4, D)),
            whole((FF // D, D)),
            whole((D, 3)),
            whole((D, HD)),
        ],
        [sds((rows, D), bf16)] + [sds((1, r, 2 * HD), f32) for r in sel_rows],
        [whole((rows, D))] + [whole((1, r, 2 * HD)) for r in sel_rows],
        grid=(3,),
        scratch=[pltpu.VMEM((rows, D), f32)],
        vmem=14,
        name="input",
    )
    states_v = [v.T for v in (master_vecs, moment_vecs, square_vecs, average_vecs)]
    if fast:
        theirs, mine = small
        small = [mine, swap(theirs, "grp", 8, 1)]
        first.step(hold=14)
        second.step(hold=60)
        tail = tail_grads(line, sels, dp_both, small)
        tail_first, tail_second = tail_one(line, tail)
        first.step()
        second.step(hold=4)
        far = tail_first()
        first.step()
        second.step()
        mine = final_both(line, [first, second])
        part_x, part_y = swap(mine, "seq", 4, 1), swap(mine, "seq", 4, 2)
        both_mine = [mine, part_x, part_y, swap(part_x, "seq", 4, 2)]
        last = tail_second(*far)
        last_mine, small_own = tail_final(line, last)
        outs = adam_piece(
            line, both_mine, states_m, None,
            lambda i: jnp.where(jnp.bitwise_and(i, 2) == 0, 8, 4) + 2 * (i // 4) + jnp.bitwise_and(i, 1),
        )
        last_parts = gather_parts(last_mine)
        outs = adam_piece(
            line, last_parts, states_m, outs, lambda i: jnp.where(i < 4, i, (4 * D + 2 * FF) // D),
            small=[small_own], vecs=states_v,
        )
        mats, vecs = outs[:6], [v.T for v in outs[6:]]
    else:
        h1t, obt, h2t = sels[0][1], sels[0][2], sels[0][3]
        joined = [jnp.transpose(a[0], (0, 2, 1, 3)).reshape(2, rows, piece) for a in acts]
        dn = [dot_tn(cotangent, v[0]) for v in joined]
        fc = [dot_nn(h2t, v[1]) for v in joined]
        qkvo = [dot_nt(h1t, dp[k]) for k in range(3)] + [dot_nt(obt, dp[3])]
        small = small[0][0]
        grad = jnp.concatenate([*qkvo, *fc, *dn, small[:, :HD]], axis=1).astype(bf16)
        own = lax.psum_scatter(grad, "grp", scatter_dimension=0, tiled=True)
        own = lax.psum(own, "seq").astype(f32)
        own_v = lax.psum(lax.psum_scatter(small, "grp", scatter_dimension=0, tiled=True), "seq")
        own_v = own_v[:, HD : HD + n_vec]
        results = adam_math(own, *states_m, learn_rate)
        mats = [own, *results, results[0].astype(bf16)]
        results = adam_math(own_v.T, *states_v, vector_rate)
        vecs = [own_v, *[v.T for v in (*results, results[0].astype(bf16))]]
    flat = [x for pair_ in zip(mats, vecs) for x in pair_]
    return (block_output, input_grad, *flat)


def solution(mesh):
    tok = P(("grp", "seq"), None)
    own = P("grp", None)
    in_specs = (tok, tok, P("grp"), P(), P()) + (own,) * 8
    out_specs = (tok, tok) + (own,) * 12
    body = partial(on_device, mesh.shape["seq"], mesh.shape["grp"])
    return jax.shard_map(body, mesh=mesh, in_specs=in_specs, out_specs=out_specs, check_vma=False)
```

```python
from functools import partial

import jax
import jax.numpy as jnp
from jax import lax
from jax.experimental import pallas as pl
from jax.experimental.pallas import tpu as pltpu
from jax.sharding import PartitionSpec as P

D = 768
HEADS = 12
HD = 64
FF = 3072
QUAD = 4
N_QUAD = HEADS // QUAD
AUG = 72

norm_eps = 1e-05
adam_eps = 1e-08
beta_first = 0.5
beta_second = 0.5
learn_rate = 0.01
vector_rate = 0.06
decay_rate = 0.1
average_keep = 0.9

f32 = jnp.float32
bf16 = jnp.bfloat16

S_SEQ, S_GRP, S_MASK, S_BACK = 0, 1, 4, 8

MIB = 1024 * 1024


def dot_nn(a, b):
    return lax.dot_general(a, b, (((1,), (0,)), ((), ())), preferred_element_type=f32)


def dot_nt(a, b):
    return lax.dot_general(a, b, (((1,), (1,)), ((), ())), preferred_element_type=f32)


def dot_tn(a, b):
    return lax.dot_general(a, b, (((0,), (0,)), ((), ())), preferred_element_type=f32)


def whole(shape):
    return pl.BlockSpec(tuple(shape), lambda *_: (0,) * len(shape))


def along(block, axis=0):
    return pl.BlockSpec(tuple(block), lambda i, s: tuple(i if d == axis else 0 for d in range(len(block))))


def sds(shape, dtype):
    return jax.ShapeDtypeStruct(tuple(shape), dtype)


class Line:
    def __init__(self, scal):
        self.scal = scal
        self.stay = set()

    def wait(self, *values):
        self.scal, values = lax.optimization_barrier((self.scal, values))
        return values

    def call(self, body, args, in_specs, outs, out_specs, grid=(1,), scratch=(), vmem=32,
             hold=0, far=(), out_far=(), aliases=None, name=None):
        args = [
            pltpu.with_memory_space_constraint(a, pltpu.HBM) if id(a) in self.stay or k in far else a
            for k, a in enumerate(args)
        ]
        got = pl.pallas_call(
            body,
            out_shape=tuple(pltpu.HBM(o.shape, o.dtype) if k in out_far else o for k, o in enumerate(outs)),
            grid_spec=pltpu.PrefetchScalarGridSpec(
                num_scalar_prefetch=1,
                grid=grid,
                in_specs=list(in_specs),
                out_specs=tuple(out_specs),
                scratch_shapes=list(scratch),
            ),
            compiler_params=pltpu.CompilerParams(
                dimension_semantics=("arbitrary",) * len(grid), vmem_limit_bytes=vmem * MIB
            ),
            cost_estimate=pl.CostEstimate(
                flops=hold * 10**9, bytes_accessed=1024, transcendentals=0
            ),
            input_output_aliases=aliases or {},
            name=name,
        )(self.scal, *args)
        self.scal, got = lax.optimization_barrier((self.scal, got))
        return got


def store_sel(refs, at, values, scal):
    if len(refs) == 1:
        refs[0][at] = values
        return
    block = D // 8
    for j in range(8):
        rel = jnp.bitwise_xor(scal[S_GRP], j)
        place = pl.multiple_of(jnp.right_shift(rel, 1) * block, block)
        odd = jnp.bitwise_and(rel, 1)
        part = values[j * block : (j + 1) * block, :]

        @pl.when(odd == 1)
        def _(part=part, place=place):
            refs[0][at, pl.ds(place, block), :] = part

        @pl.when(odd == 0)
        def _(part=part, place=place):
            refs[1][at, pl.ds(place, block), :] = part


def normalize(values):
    average = jnp.mean(values, axis=1, keepdims=True)
    centered = values - average
    variance = jnp.mean(centered * centered, axis=1, keepdims=True)
    inverse = lax.rsqrt(variance + norm_eps)
    return centered * inverse, inverse


def quad_maps(hedge_t):
    wide = QUAD * HD
    row = lax.broadcasted_iota(jnp.int32, (wide, HD), 0)
    col = lax.broadcasted_iota(jnp.int32, (wide, HD), 1)
    spread = (jnp.bitwise_and(row, HD - 1) == col).astype(bf16)
    tiled = dot_nn(spread, hedge_t)
    big_r = lax.broadcasted_iota(jnp.int32, (wide, wide), 0)
    big_c = lax.broadcasted_iota(jnp.int32, (wide, wide), 1)
    same = jnp.right_shift(big_r, 6) == jnp.right_shift(big_c, 6)
    return jnp.where(same, tiled, 0.0)


def ones_rows(count):
    return (lax.broadcasted_iota(jnp.int32, (AUG - HD, count), 0) == 0).astype(f32).astype(bf16)


def rows_up(values):
    return jnp.concatenate([values, jnp.zeros((3, values.shape[1]), f32)], axis=0).T


def features(pt, maps):
    high = pt.astype(bf16)
    rest = (pt - high.astype(f32)).astype(bf16)
    scores = dot_nn(jnp.concatenate([maps, maps], axis=1), jnp.concatenate([high, rest], axis=0))
    heads = []
    for h in range(QUAD):
        s = scores[h * HD : (h + 1) * HD, :]
        top = jnp.max(s, axis=0, keepdims=True)
        bottom = jnp.min(s, axis=0, keepdims=True)
        pos = jnp.exp(s - top)
        neg = jnp.exp(bottom - s)
        pos = pos * (1.0 / jnp.sum(pos, axis=0, keepdims=True))
        neg = neg * (1.0 / jnp.sum(neg, axis=0, keepdims=True))
        heads.append(jnp.concatenate([pos, neg], axis=0).astype(bf16))
    return high, heads


def keys_body(scal, x_ref, wk_ref, wv_ref, hedge_ref, vt_ref, vq_ref, h1_ref, kt_ref, fk_ref, vt_out, s_ref):
    rows = x_ref.shape[0]

    @pl.when(pl.program_id(0) == 0)
    def _():
        normed, _ = normalize(x_ref[...].astype(f32))
        vt = vt_ref[...].astype(f32)
        h1_ref[...] = (normed * vt[0:1] + vt[1:2]).astype(bf16)

    h1 = h1_ref[...]
    bias = rows_up(vq_ref[...].astype(f32))
    v_t = (dot_nt(wv_ref[...], h1) + bias[:, 8:9]).astype(bf16)
    vt_out[...] = v_t
    pt = dot_nt(wk_ref[...], h1) + bias[:, 7:8]
    kt_ref[...], heads = features(pt, quad_maps(hedge_ref[...]).astype(bf16))
    extra = ones_rows(rows)
    for h, both in enumerate(heads):
        fk_ref[h * 2 * HD : (h + 1) * 2 * HD, :] = both
        va = jnp.concatenate([v_t[h * HD : (h + 1) * HD, :], extra], axis=0)
        s_ref[h * AUG : (h + 1) * AUG, :] = dot_nt(va, both).astype(bf16)


def queries_body(n_sel, scal, h1_ref, g_ref, wq_ref, hedge_ref, vq_ref, *refs):
    sel = refs[:n_sel]
    qt_ref, fq_ref = refs[n_sel:]
    h1 = h1_ref[...]

    @pl.when(pl.program_id(0) == 0)
    def _():
        store_sel(sel, 0, g_ref[...].T, scal)
        store_sel(sel, 1, h1.T, scal)

    bias = rows_up(vq_ref[...].astype(f32))
    pt = dot_nt(wq_ref[...], h1) + bias[:, 6:7]
    qt_ref[...], heads = features(pt, quad_maps(hedge_ref[...]).astype(bf16))
    for h, both in enumerate(heads):
        fq_ref[h * 2 * HD : (h + 1) * 2 * HD, :] = both


def tri_mask(half):
    return lax.broadcasted_iota(jnp.int32, (half, half), 0) <= lax.broadcasted_iota(
        jnp.int32, (half, half), 1
    )


def masked_pair(left0, left1, right, keep):
    half = right.shape[1] // 2
    full = dot_tn(left0, right)
    low = dot_tn(left1, right[:, half:])
    diag0 = jnp.where(keep, full[:, :half], 0.0).astype(bf16)
    above = full[:, half:].astype(bf16)
    diag1 = jnp.where(keep, low, 0.0).astype(bf16)
    return diag0, above, diag1


def local_body(scal, fq_ref, fk_ref, vt_ref, num_ref):
    rows = fq_ref.shape[1]
    half = rows // 2
    keep = tri_mask(half)
    extra = ones_rows(rows)
    for h in range(QUAD):
        fq = fq_ref[h * 2 * HD : (h + 1) * 2 * HD, :]
        fk = fk_ref[h * 2 * HD : (h + 1) * 2 * HD, :]
        va = jnp.concatenate([vt_ref[h * HD : (h + 1) * HD, :], extra], axis=0)
        a00, a01, a11 = masked_pair(fk[:, :half], fk[:, half:], fq, keep)
        num_ref[h * AUG : (h + 1) * AUG, :half] = dot_nn(va[:, :half], a00)
        num_ref[h * AUG : (h + 1) * AUG, half:] = dot_nn(va[:, :half], a01) + dot_nn(va[:, half:], a11)


def weighted_state(scal, slot, parts):
    total = None
    for k, part in enumerate(parts):
        term = scal[slot + k].astype(f32) * part.astype(f32)
        total = term if total is None else total + term
    return total.astype(bf16)


def after_body(n_sel, n_parts, scal, *refs):
    parts = refs[:n_parts]
    num_ref, fq_ref, x_ref, w_ref, vt_ref = refs[n_parts : n_parts + 5]
    o_ref, den_ref, r_ref, h2_ref, sin_ref = refs[n_parts + 5 + n_sel : n_parts + 10 + n_sel]
    sel = refs[-1 - n_sel : -1]
    ob_ref = refs[-1]
    vt = vt_ref[...].astype(f32)
    state = weighted_state(scal, S_MASK, [p[...] for p in parts])
    sin_ref[...] = state
    for h in range(HEADS):
        num = num_ref[h * AUG : (h + 1) * AUG, :] + dot_nn(
            state[h * AUG : (h + 1) * AUG, :], fq_ref[h * 2 * HD : (h + 1) * 2 * HD, :]
        )
        den = num[HD : HD + 1, :]
        out = num[:HD, :] * (1.0 / den)
        o_ref[h * HD : (h + 1) * HD, :] = out
        den_ref[h : h + 1, :] = den
        ob_ref[h * HD : (h + 1) * HD, :] = out.astype(bf16)
    obt = ob_ref[...]
    store_sel(sel, 0, obt, scal)
    r = x_ref[...].astype(f32) + dot_nt(obt.T, w_ref[...]) + vt[4:5]
    r_ref[...] = r
    normed, _ = normalize(r)
    h2 = (normed * vt[2:3] + vt[3:4]).astype(bf16)
    h2_ref[...] = h2
    store_sel(sel, 1, h2.T, scal)


gelu_c = 0.7978845608028654
gelu_k = 0.044715


def mlp_body(first, scal, h2_ref, g_ref, wf_ref, wd_ref, bias_ref, *refs):
    if first:
        out_ref, dh_ref, act_ref, db_ref = refs
    else:
        out_in, dh_in, out_ref, dh_ref, act_ref, db_ref = refs
    u = dot_nt(h2_ref[...], wf_ref[...]) + bias_ref[...].astype(f32)
    de = dot_nt(g_ref[...], wd_ref[...])
    uu = u * u
    t = jnp.tanh(gelu_c * u * (1.0 + gelu_k * uu))
    half_t = 0.5 * (1.0 + t)
    e = (u * half_t).astype(bf16)
    slope = half_t + 0.5 * u * (1.0 - t * t) * (gelu_c * (1.0 + 3.0 * gelu_k * uu))
    du = (de * slope).astype(bf16)
    act_ref[0, 0] = e
    act_ref[1, 0] = du
    db_ref[...] = jnp.sum(du.astype(f32), axis=0, keepdims=True)
    add_out = dot_nn(e, wd_ref[...])
    add_dh = dot_nn(du, wf_ref[...])
    step = pl.program_id(0)

    @pl.when(step == 0)
    def _():
        if first:
            out_ref[...] = add_out
            dh_ref[...] = add_dh
        else:
            out_ref[...] = out_in[...] + add_out
            dh_ref[...] = dh_in[...] + add_dh

    @pl.when(step > 0)
    def _():
        out_ref[...] += add_out
        dh_ref[...] += add_dh


def back_body(scal, out_ref, dh_ref, r_ref, g_ref, w_ref, vt_ref, o_ref, den_ref, fq_ref, y_ref, dr_ref,
              da_ref, rho_ref, ds_ref, sums_ref, do_ref):
    vt = vt_ref[...].astype(f32)
    r = r_ref[...]
    y_ref[...] = (r + out_ref[...] + vt[5:6]).astype(bf16)
    grad_out = g_ref[...].astype(f32)
    normed, inverse = normalize(r)
    up = dh_ref[...]
    dn = up * vt[2:3]
    dr = grad_out + inverse * (
        dn - jnp.mean(dn, axis=1, keepdims=True) - normed * jnp.mean(dn * normed, axis=1, keepdims=True)
    )
    dr_ref[...] = dr
    da = dr.astype(bf16)
    da_ref[...] = da.T
    sums_ref[...] = jnp.concatenate(
        [
            jnp.sum(up * normed, axis=0, keepdims=True),
            jnp.sum(up, axis=0, keepdims=True),
            jnp.sum(da.astype(f32), axis=0, keepdims=True),
            jnp.sum(grad_out, axis=0, keepdims=True),
        ],
        axis=0,
    )
    do_ref[...] = dot_nn(da, w_ref[...]).astype(bf16).T
    rows = r.shape[0]
    zero_row = lax.broadcasted_iota(jnp.int32, (AUG - HD, rows), 0) == 0
    for h in range(HEADS):
        dout = do_ref[h * HD : (h + 1) * HD, :].astype(f32)
        inv = 1.0 / den_ref[h : h + 1, :]
        rho = (dout * inv).astype(bf16)
        c = -jnp.sum(dout * o_ref[h * HD : (h + 1) * HD, :], axis=0, keepdims=True) * inv
        extra = jnp.where(zero_row, jnp.broadcast_to(c, (AUG - HD, rows)), 0.0).astype(bf16)
        ra = jnp.concatenate([rho, extra], axis=0)
        rho_ref[h * AUG : (h + 1) * AUG, :] = ra
        ds_ref[h * AUG : (h + 1) * AUG, :] = dot_nt(ra, fq_ref[h * 2 * HD : (h + 1) * 2 * HD, :]).astype(bf16)


def feature_back(feat, upstream):
    pos, neg = feat[:HD].astype(f32), feat[HD:].astype(f32)
    up_pos, up_neg = upstream[:HD], upstream[HD:]
    return pos * (up_pos - jnp.sum(pos * up_pos, axis=0, keepdims=True)) - neg * (
        up_neg - jnp.sum(neg * up_neg, axis=0, keepdims=True)
    )


def attend_back_body(n_parts, scal, *refs):
    parts = refs[:n_parts]
    (fq_ref, fk_ref, vt_ref, rho_ref, sin_ref, qt_ref, kt_ref, hedge_ref, da_ref) = refs[n_parts : n_parts + 9]
    dp_ref, dm_ref, db_ref = refs[-3:]
    dp_ref[3] = da_ref[...]
    rows = fq_ref.shape[1]
    half = rows // 2
    keep = tri_mask(half)
    extra = ones_rows(rows)
    back_state = weighted_state(scal, S_BACK, [p[...] for p in parts])
    ds_q, ds_k = [], []
    for h in range(QUAD):
        fq = fq_ref[h * 2 * HD : (h + 1) * 2 * HD, :]
        fk = fk_ref[h * 2 * HD : (h + 1) * 2 * HD, :]
        head = slice(h * HD, (h + 1) * HD)
        aug = slice(h * AUG, (h + 1) * AUG)
        va = jnp.concatenate([vt_ref[head, :], extra], axis=0)
        ra = rho_ref[aug, :]
        state, back = sin_ref[aug, :], back_state[aug, :]
        a00, a01, a11 = masked_pair(fk[:, :half], fk[:, half:], fq, keep)
        g00, g01, g11 = masked_pair(va[:, :half], va[:, half:], ra, keep)
        far = dot_tn(state, ra)
        left = far[:, :half] + dot_nn(fk[:, :half], g00)
        right = far[:, half:] + dot_nn(fk[:, :half], g01) + dot_nn(fk[:, half:], g11)
        dfq = jnp.concatenate([left, right], axis=1)
        far_k = dot_tn(back, va)
        left = far_k[:, :half] + dot_nt(fq[:, :half], g00) + dot_nt(fq[:, half:], g01)
        right = far_k[:, half:] + dot_nt(fq[:, half:], g11)
        dfk = jnp.concatenate([left, right], axis=1)
        far_v = dot_nn(back, fk)[:HD]
        rv = ra[:HD]
        left = far_v[:, :half] + dot_nt(rv[:, :half], a00) + dot_nt(rv[:, half:], a01)
        right = far_v[:, half:] + dot_nt(rv[:, half:], a11)
        dp_ref[2, head, :] = jnp.concatenate([left, right], axis=1).astype(bf16)
        dsq = feature_back(fq, dfq).astype(bf16)
        dsk = feature_back(fk, dfk).astype(bf16)
        ds_q.append(dsq)
        ds_k.append(dsk)
        dm_ref[head, :] = dot_nt(qt_ref[head, :], dsq) + dot_nt(kt_ref[head, :], dsk)
    maps = quad_maps(hedge_ref[...]).T.astype(bf16)
    dq = dot_nn(maps, jnp.concatenate(ds_q, axis=0)).astype(bf16)
    dk = dot_nn(maps, jnp.concatenate(ds_k, axis=0)).astype(bf16)
    dp_ref[0] = dq
    dp_ref[1] = dk
    db_ref[...] = jnp.concatenate(
        [jnp.sum(v.astype(f32), axis=1, keepdims=True) for v in (dq, dk, dp_ref[2])], axis=1
    )


def input_body(fast, scal, dp_ref, w_ref, x_ref, dr_ref, vt_ref, sums_ref, dbfc_ref, db_ref, dm_ref, *refs):
    gin_ref, *small_refs, acc_ref = refs
    step = pl.program_id(0)
    part = dot_tn(dp_ref[0], w_ref[...])

    @pl.when(step == 0)
    def _():
        acc_ref[...] = part

    @pl.when(step == 1)
    def _():
        acc_ref[...] += part

    @pl.when(step == 2)
    def _():
        vt = vt_ref[...].astype(f32)
        up = acc_ref[...] + part
        normed, inverse = normalize(x_ref[...].astype(f32))
        dn = up * vt[0:1]
        gin = dr_ref[...] + inverse * (
            dn - jnp.mean(dn, axis=1, keepdims=True) - normed * jnp.mean(dn * normed, axis=1, keepdims=True)
        )
        gin_ref[...] = gin.astype(bf16)
        rows16 = jnp.concatenate(
            [
                jnp.sum(up * normed, axis=0, keepdims=True),
                jnp.sum(up, axis=0, keepdims=True),
                sums_ref[...],
                jnp.zeros((3, D), f32),
                dbfc_ref[...],
                jnp.zeros((3, D), f32),
            ],
            axis=0,
        )
        cols = rows16.T
        lane = lax.broadcasted_iota(jnp.int32, (D, HD), 1)
        tail = jnp.concatenate([cols, jnp.zeros((D, HD - 16), f32)], axis=1)
        for k in range(3):
            tail = jnp.where(lane == 6 + k, db_ref[:, k : k + 1], tail)
        small = jnp.concatenate([dm_ref[...], tail], axis=1)
        store_sel(small_refs, 0, small, scal)


def mlp_grads_body(by_y, scal, *refs):
    sels, acts_a, acts_b, sels_h = refs[0:2], refs[2:4], refs[4:6], refs[6:8]
    send, keep = refs[8:]
    block = D // 8
    wq = send.shape[2]
    y_last = 1 - pl.program_id(0)

    def total(lefts, rights):
        return (dot_nn(lefts[0][0], rights[0][0, 0]) + dot_nn(lefts[1][0], rights[1][0, 0])).astype(bf16)

    for path, value in enumerate((total(sels, acts_a), total(sels_h, acts_b))):
        rows = slice(path * block, (path + 1) * block)
        for half in range(2):
            x_last = 1 - jnp.bitwise_xor(half, jnp.bitwise_and(scal[S_SEQ], 1))
            cols = slice(half * wq, (half + 1) * wq)

            def part(z, value=value, cols=cols):
                return value[z * block : (z + 1) * block, cols]

            if by_y:
                for bit, ref in ((0, send), (1, keep)):

                    @pl.when(y_last == bit)
                    def _(ref=ref, part=part, rows=rows, x_last=x_last):
                        for at, z in enumerate((3, 1, 2, 0)):
                            ref[4 * (at // 2) + 2 * x_last + at % 2, rows, :] = part(z)
            else:
                base = 4 * y_last + 1 * x_last
                for ref, order in ((send, (3, 1)), (keep, (2, 0))):
                    for at, z in enumerate(order):
                        ref[2 * at + base, rows, :] = part(z)


def mlp_grads(line, by_y, sels, acts, far=(), out_far=()):
    _, depth, rows = sels[0].shape
    half = sds((8, 2 * (D // 8), D // 2), bf16)

    def act(path):
        return pl.BlockSpec((1, 1, rows, D), lambda i, s: (path, i, 0, 0))

    def sel(slot):
        return pl.BlockSpec((1, depth, rows), lambda i, s: (slot, 0, 0))

    return line.call(
        partial(mlp_grads_body, by_y),
        [*sels, *acts, *acts, *sels],
        [sel(0)] * 2 + [act(0)] * 2 + [act(1)] * 2 + [sel(3)] * 2,
        [half] * 2,
        [whole(half.shape)] * 2,
        grid=(2,),
        vmem=24,
        far=far,
        out_far=out_far,
        name="mlp_grads",
    )


def pack_rows(values, count):
    return jnp.concatenate([values[b * count : (b + 1) * count] for b in range(3)], axis=1)


def unpack_rows(values):
    return jnp.concatenate([values[:, b * 128 : (b + 1) * 128] for b in range(3)], axis=0)


def order_a(i):
    return jnp.where(i < 2, 2 * i + 1, 2 * i - 4)


def order_b(i):
    return jnp.where(i < 2, i + 2, i - 2)


def pick_rows(ref, half, count):
    rows = [ref[pl.ds(pl.multiple_of(z * 2 * count + half * count, 8), count), :] for z in range(4)]
    return jnp.concatenate(rows, axis=0)


def tail_grads_body(scal, *refs):
    h1, ob, dqk, dvo = refs[0:2], refs[2:4], refs[4:6], refs[6:8]
    small_own, small_other, send_a, keep_a, send_b, keep_b, small_ref, sum_ref = refs[8:]
    step = pl.program_id(0)
    wq = send_a.shape[1]
    qb = jnp.bitwise_xor(order_b(step), scal[S_SEQ])
    at = pl.multiple_of(jnp.bitwise_and(step, 1) * wq, wq)

    def total(lefts, rights):
        return (dot_nt(lefts[0][0], rights[0][0]) + dot_nt(lefts[1][0], rights[1][0])).astype(bf16)

    def put(send, keep, value):
        @pl.when(step < 2)
        def _():
            send[pl.ds(at, wq), :] = value

        @pl.when(step >= 2)
        def _():
            keep[pl.ds(at, wq), :] = value

    put(send_a, keep_a, total(h1, dqk))

    @pl.when(qb < 2)
    def _():
        put(send_b, keep_b, total(h1, dvo))

    @pl.when(qb >= 2)
    def _():
        put(send_b, keep_b, total(ob, dvo))

    @pl.when(step == 0)
    def _():
        sum_ref[...] = small_own[0] + small_other[0]
        x_abs = jnp.bitwise_and(scal[S_SEQ], 1)
        small_ref[...] = pack_rows(pick_rows(sum_ref, x_abs, 48), 64)
        send_a[2 * wq :, :] = pack_rows(pick_rows(sum_ref, 1 - x_abs, 48), 64).astype(bf16)


def tail_grads(line, sels, dp, small):
    _, depth, rows = sels[0].shape
    wq = D // 2
    dp = [v.reshape(8, wq, rows) for v in dp]

    def sel(slot):
        return pl.BlockSpec((1, depth, rows), lambda i, s: (slot, 0, 0))

    outs = [
        sds((2 * wq + 64, wq), bf16), sds((2 * wq, wq), bf16),
        sds((2 * wq, wq), bf16), sds((2 * wq, wq), bf16), sds((64, wq), f32),
    ]
    return line.call(
        tail_grads_body,
        [*sels, *sels, *dp, *dp, *small],
        [sel(1)] * 2
        + [sel(2)] * 2
        + [pl.BlockSpec((1, wq, rows), lambda i, s: (jnp.bitwise_xor(order_a(i), s[S_SEQ]), 0, 0))] * 2
        + [pl.BlockSpec((1, wq, rows), lambda i, s: (4 + jnp.bitwise_xor(order_b(i), s[S_SEQ]), 0, 0))] * 2
        + [whole(small[0].shape)] * 2,
        outs,
        [whole(o.shape) for o in outs],
        grid=(4,),
        scratch=[pltpu.VMEM((depth, 2 * HD), f32)],
        vmem=10,
        hold=4,
        name="tail_grads",
    )


def swap(value, axis, size, bit):
    return lax.ppermute(value, axis, [(i, i ^ bit) for i in range(size)])


def halve_body(scal, keep_ref, recv_ref, send_ref, left_ref):
    half = send_ref.shape[0]
    send_ref[...] = (keep_ref[:half].astype(f32) + recv_ref[:half].astype(f32)).astype(bf16)
    left_ref[...] = (keep_ref[half:].astype(f32) + recv_ref[half:].astype(f32)).astype(left_ref.dtype)


class Halves:
    def __init__(self, line, send, keep, stages):
        self.line, self.keep, self.stages = line, keep, list(stages)
        self.recv = swap(send, *self.stages.pop(0))

    def step(self, hold=0):
        count, rows, wq = self.keep.shape
        shape = (count // 2, rows, wq)
        send, self.keep = self.line.call(
            halve_body, [self.keep, self.recv], [whole(self.keep.shape)] * 2,
            [sds(shape, bf16), sds(shape, self.keep.dtype)], [whole(shape)] * 2,
            vmem=8, hold=hold, name="halve",
        )
        self.recv = swap(send, *self.stages.pop(0))


def final_body(scal, *refs):
    out = refs[-1]
    for j in range(2):
        out[j] = (refs[2 * j][0].astype(f32) + refs[2 * j + 1][0].astype(f32)).astype(bf16)


def final_both(line, pieces):
    shape = (2,) + pieces[0].keep.shape[1:]
    (mine,) = line.call(
        final_body, [v for p in pieces for v in (p.keep, p.recv)], [whole((1,) + shape[1:])] * 4,
        [sds(shape, bf16)], [whole(shape)], vmem=4, name="final",
    )
    return mine.reshape(4 * (D // 8), shape[2])


def tail_one_body(scal, keep_a, recv_a, keep_b, recv_b, small_ref, send_a, send_b, half_ref):
    wq = send_b.shape[0]
    send_a[:wq, :] = (keep_a[wq : 2 * wq].astype(f32) + recv_a[wq : 2 * wq].astype(f32)).astype(bf16)
    half_ref[...] = unpack_rows(small_ref[...] + recv_a[2 * wq :].astype(f32))
    y_abs = jnp.right_shift(scal[S_SEQ], 1)
    send_a[wq:, :] = pack_rows(pick_rows(half_ref, 1 - y_abs, 24), 32).astype(bf16)
    send_b[...] = (keep_b[wq:].astype(f32) + recv_b[wq:].astype(f32)).astype(bf16)


def tail_two_body(scal, keep_a, recv_a, keep_b, recv_b, small_ref, far_a, far_b, own_ref, *refs):
    out_refs, half_ref = refs[:-1], refs[-1]
    wq = far_b.shape[0]
    block = D // 8
    half_ref[...] = unpack_rows(small_ref[...] + recv_a[2 * wq :].astype(f32))
    small = pick_rows(half_ref, jnp.right_shift(scal[S_SEQ], 1), 24) + unpack_rows(far_a[wq:].astype(f32))
    first = keep_a[:wq].astype(f32) + recv_a[:wq].astype(f32) + far_a[:wq].astype(f32)
    second = keep_b[:wq].astype(f32) + recv_b[:wq].astype(f32) + far_b[...].astype(f32)
    for z, ref in enumerate((own_ref, *out_refs)):
        rows = slice(z * block, (z + 1) * block)
        ref[:block, :] = first[rows].astype(ref.dtype)
        ref[block : 2 * block, :] = second[rows].astype(ref.dtype)
        packed = pack_rows(small[z * 24 : (z + 1) * 24], 8)
        packed = jnp.concatenate([packed, jnp.zeros_like(packed)], axis=0)
        ref[2 * block :, :] = packed.astype(ref.dtype)


def tail_final_body(scal, *refs):
    total = refs[0][...]
    for ref in refs[1:-1]:
        total = total + ref[...].astype(f32)
    refs[-1][...] = total.astype(bf16)


def tail_one(line, tail):
    send_a, keep_a, send_b, keep_b, small = tail
    wq = D // 2
    recv_a, recv_b = swap(send_a, "seq", 4, 1), swap(send_b, "seq", 4, 2)
    shapes = [sds((wq + 32, wq), bf16), sds((wq, wq), bf16)]
    halves = [pltpu.VMEM((D // 4, 2 * HD), f32)]

    def first():
        args = [keep_a, recv_a, keep_b, recv_b, small]
        next_a, next_b = line.call(
            tail_one_body, args, [whole(v.shape) for v in args], shapes, [whole(v.shape) for v in shapes],
            scratch=halves, vmem=12, name="tail_one",
        )
        return swap(next_a, "seq", 4, 2), swap(next_b, "seq", 4, 1)

    def second(far_a, far_b):
        args = [keep_a, recv_a, keep_b, recv_b, small, far_a, far_b]
        shape = (2 * (D // 8) + 16, wq)
        own, *sends = line.call(
            tail_two_body, args, [whole(v.shape) for v in args], [sds(shape, f32)] + [sds(shape, bf16)] * 3,
            [whole(shape)] * 4, scratch=halves, vmem=10, hold=5, name="tail_two",
        )
        return [own, *(swap(v, "grp", 8, 2 * (k + 1)) for k, v in enumerate(sends))]

    return first, second


def tail_final(line, args):
    (mine,) = line.call(
        tail_final_body, args, [whole(v.shape) for v in args], [sds(args[0].shape, bf16)],
        [whole(args[0].shape)], vmem=6, hold=5, name="tail_final",
    )
    return mine


def gather_parts(mine):
    return [mine] + [swap(mine, "seq", 4, k) for k in (1, 2, 3)]


def adam_math(grad, master, first, second, average, rate):
    new_first = beta_first * first + (1.0 - beta_first) * grad
    new_second = beta_second * second + (1.0 - beta_second) * grad * grad
    new_master = master - rate * (
        new_first / (jnp.sqrt(new_second) + adam_eps) + decay_rate * master
    )
    new_average = average_keep * average + (1.0 - average_keep) * new_master
    return new_master, new_first, new_second, new_average


def adam_body(n_alias, has_small, scal, *refs):
    parts, refs = refs[:4], refs[4:]
    if has_small:
        vec_in, refs = refs[:4], refs[4:]
    states, refs = refs[:4], refs[4 + n_alias :]
    outs, refs = refs[:6], refs[6:]
    grad_ref = outs[0]
    block = D // 8
    count, wq = parts[0].shape[0] // block, parts[0].shape[1]
    step = pl.program_id(0)
    path, half = jnp.right_shift(step, 1), jnp.bitwise_and(step, 1)
    for k, ref in enumerate(parts):
        quarter = jnp.bitwise_xor(scal[S_SEQ], k)

        @pl.when((jnp.right_shift(quarter, 1) == half) & (step < 2 * count))
        def _(ref=ref, quarter=quarter):
            at = pl.multiple_of(jnp.bitwise_and(quarter, 1) * wq, 128)
            rows = pl.ds(pl.multiple_of(jnp.minimum(path, count - 1) * block, block), block)
            grad_ref[:, pl.ds(at, wq)] = ref[rows, :].astype(f32)

    if has_small:
        vec_outs, small_ref = refs[:6], refs[6]

        @pl.when(step == 2 * count)
        def _():
            for k, ref in enumerate(parts):
                quarter = jnp.bitwise_xor(scal[S_SEQ], k)
                first = jnp.bitwise_and(quarter, 1) * 48 + jnp.right_shift(quarter, 1) * 24
                packed = ref[2 * block :].astype(f32)
                for b in range(3):
                    small_ref[pl.ds(pl.multiple_of(first + 8 * b, 8), 8), :] = packed[:8, b * 128 : (b + 1) * 128]
            small = small_ref[...]
            grad_ref[...] = jnp.zeros_like(grad_ref)
            grad_ref[:, : 2 * HD] = small
            grad = small.T[HD : HD + vec_in[0].shape[0]]
            results = adam_math(grad, *[v[...] for v in vec_in], vector_rate)
            for ref, value in zip(vec_outs, (grad, *results, results[0])):
                ref[...] = value.astype(ref.dtype)

    results = adam_math(grad_ref[...], *[v[...] for v in states], learn_rate)
    for ref, value in zip(outs[1:], (*results, results[0])):
        ref[...] = value.astype(ref.dtype)


def adam_piece(line, parts, states, outs, block_of, vecs=()):
    block = D // 8
    count = parts[0].shape[0] // block
    rows, wide = states[0].shape
    spec = pl.BlockSpec((block, D), lambda i, s: (0, block_of(i)))
    anywhere = pl.BlockSpec(memory_space=pl.ANY)
    n_alias = 0 if outs is None else 6
    shapes = [sds((rows, wide), f32)] * 5 + [sds((rows, wide), bf16)]
    args = [*parts, *vecs, *states]
    n_before = len(args)
    out_specs = [spec] * 6
    if vecs:
        shapes += [sds(vecs[0].shape, f32)] * 5 + [sds(vecs[0].shape, bf16)]
        out_specs += [whole(vecs[0].shape)] * 6
    return line.call(
        partial(adam_body, n_alias, bool(vecs)),
        [*args, *(outs or [])],
        [whole(v.shape) for v in [*parts, *vecs]] + [spec] * 4 + [anywhere] * n_alias,
        shapes,
        out_specs,
        grid=(2 * count + (1 if vecs else 0),),
        scratch=[pltpu.VMEM((rows, 2 * HD), f32)] if vecs else [],
        aliases={1 + n_before + i: i for i in range(n_alias)},
        vmem=16,
        name="adam",
    )


def on_device(
    n_seq,
    n_grp,
    tokens,
    cotangent,
    seq_len,
    weight_mats,
    weight_vecs,
    master_mats,
    master_vecs,
    moment_mats,
    moment_vecs,
    square_mats,
    square_vecs,
    average_mats,
    average_vecs,
):
    rows = tokens.shape[0]
    fast = n_seq == 4 and n_grp == 8
    seq_at = lax.axis_index("seq")
    grp_at = lax.axis_index("grp")
    slot = jnp.arange(16, dtype=jnp.int32)
    seq_length = seq_len[0]
    peer = jnp.bitwise_xor(seq_at, jnp.bitwise_and(slot, 3) + 1)
    same = (peer * rows) // seq_length == (seq_at * rows) // seq_length
    before = (same & (peer < seq_at)).astype(jnp.int32)
    after = (same & (peer > seq_at)).astype(jnp.int32)
    scal = jnp.where(slot < 8, before, after)
    scal = jnp.where(slot == S_SEQ, seq_at if fast else 0, scal)
    scal = jnp.where(slot == S_GRP, grp_at, scal)
    line = Line(scal)

    w_t = weight_mats.T
    states_m = [master_mats, moment_mats, square_mats, average_mats]
    line.stay = {id(v) for v in (w_t, tokens, cotangent)}
    v_t13 = weight_vecs.T
    n_vec = v_t13.shape[0]
    bias_fc = v_t13[9:].reshape(1, FF)
    wide = QUAD * HD
    n_peer = n_seq - 1
    sel_rows = [D // 2, D // 2] if fast else [D]
    n_sel = len(sel_rows)
    sel_shapes = [sds((4, r, rows), bf16) for r in sel_rows]
    sel_low = [whole((2, r, rows)) for r in sel_rows]
    sel_high = [pl.BlockSpec((2, r, rows), lambda i, s: (1, 0, 0)) for r in sel_rows]

    def both(value):
        return [value, swap(value, "grp", 8, 1)] if fast else [value]

    def w_rows(count, at):
        return pl.BlockSpec((count, D), lambda i, s: (at(i, s), 0))

    hedge_spec = pl.BlockSpec((HD, wide), lambda i, s: ((4 * D + 2 * FF) // HD, i))
    vec_whole = whole(v_t13.shape)
    head_spec, feat_spec = along((wide, rows)), along((2 * wide, rows))
    aug_spec, quad_state = along((QUAD * AUG, rows)), along((QUAD * AUG, 2 * HD))
    st_shape = (HEADS * AUG, 2 * HD)
    vec_quad = pl.BlockSpec((n_vec, wide), lambda i, s: (0, i))
    h1, kt, fk, v_t, s_own = line.call(
        keys_body,
        [tokens, w_t, w_t, w_t, v_t13, v_t13],
        [
            whole((rows, D)),
            w_rows(wide, lambda i, s: N_QUAD + i),
            w_rows(wide, lambda i, s: 2 * N_QUAD + i),
            hedge_spec,
            vec_whole,
            vec_quad,
        ],
        [
            sds((rows, D), bf16),
            sds((D, rows), bf16),
            sds((2 * D, rows), bf16),
            sds((D, rows), bf16),
            sds(st_shape, bf16),
        ],
        [whole((rows, D)), head_spec, feat_spec, head_spec, quad_state],
        grid=(N_QUAD,),
        vmem=12,
        name="keys",
    )
    n_peer = n_seq - 1
    states = [swap(s_own, "seq", n_seq, k + 1) for k in range(n_peer)]
    got = line.call(
        partial(queries_body, n_sel),
        [h1, cotangent, w_t, w_t, v_t13],
        [whole((rows, D)), whole((rows, D)), w_rows(wide, lambda i, s: i), hedge_spec, vec_quad],
        sel_shapes + [sds((D, rows), bf16), sds((2 * D, rows), bf16)],
        sel_low + [head_spec, feat_spec],
        grid=(N_QUAD,),
        vmem=12,
        name="queries",
    )
    sels, (qt, fq) = got[:n_sel], got[n_sel:]

    (num,) = line.call(
        local_body,
        [fq, fk, v_t],
        [feat_spec, feat_spec, head_spec],
        [sds((HEADS * AUG, rows), f32)],
        [aug_spec],
        grid=(N_QUAD,),
        vmem=10,
        name="local",
    )
    got = line.call(
        partial(after_body, n_sel, n_peer),
        [*states, num, fq, tokens, w_t, v_t13, *sels],
        [whole(st_shape)] * n_peer
        + [whole(num.shape), whole(fq.shape), whole((rows, D)), w_rows(D, lambda i, s: 3), vec_whole]
        + [pl.BlockSpec(memory_space=pl.ANY)] * n_sel,
        [
            sds((D, rows), f32),
            sds((16, rows), f32),
            sds((rows, D), f32),
            sds((rows, D), bf16),
            sds(st_shape, bf16),
        ]
        + sel_shapes,
        [whole((D, rows)), whole((16, rows)), whole((rows, D)), whole((rows, D)), whole(st_shape)] + sel_high,
        aliases={n_peer + 6 + i: 5 + i for i in range(n_sel)},
        scratch=[pltpu.VMEM((D, rows), bf16)],
        vmem=10,
        name="after",
    )
    o_t, den, resid, h2, s_in = got[:5]
    sels = got[5:]
    if fast:
        sels = [sels[1], swap(sels[0], "grp", 8, 1)]

    n_piece = 2
    piece = FF // n_piece
    acc, acts, db_fc = [], [], []
    for j in range(n_piece):
        if j == 1:
            (sels,) = line.wait(sels)
        pair_of = lambda i, s, j=j: 2 * j + jnp.bitwise_xor(i, jnp.right_shift(s[S_SEQ], 1))
        out_y, out_dh, act, db = line.call(
            partial(mlp_body, j == 0),
            [h2, cotangent, w_t, w_t, bias_fc, *acc],
            [
                whole((rows, D)),
                whole((rows, D)),
                w_rows(D, lambda i, s: 4 + pair_of(i, s)),
                w_rows(D, lambda i, s: 8 + pair_of(i, s)),
                pl.BlockSpec((1, D), lambda i, s: (0, pair_of(i, s))),
            ]
            + [whole((rows, D))] * len(acc),
            [sds((rows, D), f32), sds((rows, D), f32), sds((2, 2, rows, D), bf16), sds((1, piece), f32)],
            [
                whole((rows, D)),
                whole((rows, D)),
                pl.BlockSpec((2, 1, rows, D), lambda i, s: (0, i, 0, 0)),
                pl.BlockSpec((1, D), lambda i, s: (0, jnp.bitwise_xor(i, jnp.right_shift(s[S_SEQ], 1)))),
            ],
            grid=(2,),
            vmem=14,
            name="mlp",
        )
        acc = [out_y, out_dh]
        db_fc.append(db)
        acts.append(both(act))

    if fast:
        first = Halves(
            line, *mlp_grads(line, False, sels, acts[0], out_far=(1,)),
            [("grp", 8, 2), ("seq", 4, 2), ("grp", 8, 4), ("seq", 4, 1)],
        )
        (acts[1],) = line.wait(acts[1])
    block_output, d_resid, d_attn, rho, ds_own, sums = line.call(
        back_body,
        [*acc, resid, cotangent, w_t, v_t13, o_t, den, fq],
        [whole((rows, D))] * 4
        + [w_rows(D, lambda i, s: 3), vec_whole, whole((D, rows)), whole((16, rows)), whole((2 * D, rows))],
        [
            sds((rows, D), bf16),
            sds((rows, D), f32),
            sds((D, rows), bf16),
            sds((HEADS * AUG, rows), bf16),
            sds(st_shape, bf16),
            sds((4, D), f32),
        ],
        [whole((rows, D))] * 2
        + [whole((D, rows)), whole((HEADS * AUG, rows)), whole(st_shape), whole((4, D))],
        scratch=[pltpu.VMEM((D, rows), bf16)],
        vmem=10,
        out_far=(1, 2, 3),
        name="back",
    )
    back_states = [swap(ds_own, "seq", n_seq, k + 1) for k in range(n_peer)]
    if fast:
        second = mlp_grads(line, True, sels, acts[1], far=range(2, 6))
        (back_states,) = line.wait(back_states)
        second = Halves(
            line, *second, [("seq", 4, 2), ("grp", 8, 2), ("seq", 4, 1), ("grp", 8, 4)]
        )

    grads = [sds((4, D, rows), bf16), sds((D, HD), f32), sds((D, 3), f32)]
    got = []
    for start, count in ((0, N_QUAD),):

        def at(block, axis=0, start=start):
            return pl.BlockSpec(
                tuple(block), lambda i, s: tuple(start + i if d == axis else 0 for d in range(len(block)))
            )

        feat, head = at((2 * wide, rows)), at((wide, rows))
        state = at((QUAD * AUG, 2 * HD))
        args = [*back_states, fq, fk, v_t, rho, s_in, qt, kt, w_t, d_attn]
        got = line.call(
            partial(attend_back_body, n_peer),
            [*args, *got],
            [state] * n_peer
            + [feat, feat, head, at((QUAD * AUG, rows)), state, head, head]
            + [pl.BlockSpec((HD, wide), lambda i, s, start=start: ((4 * D + 2 * FF) // HD, start + i)), head]
            + [pl.BlockSpec(memory_space=pl.ANY)] * len(got),
            grads,
            [at((4, wide, rows), 1), at((wide, HD)), at((wide, 3))],
            grid=(count,),
            aliases={1 + len(args) + k: k for k in range(len(got))},
            hold=1,
            far=(n_peer + 3, n_peer + 8),
            vmem=16,
            name="attend_back",
        )
    dp, dm, db_qkv = got
    dp_both = both(dp)
    db_fc_rows = jnp.concatenate(db_fc, axis=1).reshape(FF // D, D)
    input_grad, *small = line.call(
        partial(input_body, fast),
        [dp, w_t, tokens, d_resid, v_t13, sums, db_fc_rows, db_qkv, dm],
        [
            along((1, D, rows)),
            w_rows(D, lambda i, s: i),
            whole((rows, D)),
            whole((rows, D)),
            vec_whole,
            whole((4, D)),
            whole((FF // D, D)),
            whole((D, 3)),
            whole((D, HD)),
        ],
        [sds((rows, D), bf16)] + [sds((1, r, 2 * HD), f32) for r in sel_rows],
        [whole((rows, D))] + [whole((1, r, 2 * HD)) for r in sel_rows],
        grid=(3,),
        scratch=[pltpu.VMEM((rows, D), f32)],
        vmem=14,
        name="input",
    )
    states_v = [v.T for v in (master_vecs, moment_vecs, square_vecs, average_vecs)]
    if fast:
        theirs, mine = small
        small = [mine, swap(theirs, "grp", 8, 1)]
        first.step(hold=14)
        second.step(hold=60)
        tail = tail_grads(line, sels, dp_both, small)
        tail_first, tail_second = tail_one(line, tail)
        first.step()
        second.step(hold=4)
        far = tail_first()
        first.step()
        second.step()
        mine = final_both(line, [first, second])
        part_x, part_y = swap(mine, "seq", 4, 1), swap(mine, "seq", 4, 2)
        last = tail_second(*far)
        (part_y,) = line.wait(part_y)
        both_mine = [mine, part_x, part_y, swap(part_x, "seq", 4, 2)]
        last_mine = tail_final(line, last)
        outs = adam_piece(
            line, both_mine, states_m, None,
            lambda i: jnp.where(jnp.bitwise_and(i, 2) == 0, 8, 4) + 2 * (i // 4) + jnp.bitwise_and(i, 1),
        )
        last_parts = gather_parts(last_mine)
        outs = adam_piece(
            line, last_parts, states_m, outs, lambda i: jnp.where(i < 4, i, (4 * D + 2 * FF) // D),
            vecs=states_v,
        )
        mats, vecs = outs[:6], [v.T for v in outs[6:]]
    else:
        h1t, obt, h2t = sels[0][1], sels[0][2], sels[0][3]
        joined = [jnp.transpose(a[0], (0, 2, 1, 3)).reshape(2, rows, piece) for a in acts]
        dn = [dot_tn(cotangent, v[0]) for v in joined]
        fc = [dot_nn(h2t, v[1]) for v in joined]
        qkvo = [dot_nt(h1t, dp[k]) for k in range(3)] + [dot_nt(obt, dp[3])]
        small = small[0][0]
        grad = jnp.concatenate([*qkvo, *fc, *dn, small[:, :HD]], axis=1).astype(bf16)
        own = lax.psum_scatter(grad, "grp", scatter_dimension=0, tiled=True)
        own = lax.psum(own, "seq").astype(f32)
        own_v = lax.psum(lax.psum_scatter(small, "grp", scatter_dimension=0, tiled=True), "seq")
        own_v = own_v[:, HD : HD + n_vec]
        results = adam_math(own, *states_m, learn_rate)
        mats = [own, *results, results[0].astype(bf16)]
        results = adam_math(own_v.T, *states_v, vector_rate)
        vecs = [own_v, *[v.T for v in (*results, results[0].astype(bf16))]]
    flat = [x for pair_ in zip(mats, vecs) for x in pair_]
    return (block_output, input_grad, *flat)


def solution(mesh):
    tok = P(("grp", "seq"), None)
    own = P("grp", None)
    in_specs = (tok, tok, P("grp"), P(), P()) + (own,) * 8
    out_specs = (tok, tok) + (own,) * 12
    body = partial(on_device, mesh.shape["seq"], mesh.shape["grp"])
    return jax.shard_map(body, mesh=mesh, in_specs=in_specs, out_specs=out_specs, check_vma=False)
```

```python
from functools import partial

import jax
import jax.numpy as jnp
from jax import lax
from jax.experimental import pallas as pl
from jax.experimental.pallas import tpu as pltpu
from jax.sharding import PartitionSpec as P

D = 768
HEADS = 12
HD = 64
FF = 3072
QUAD = 4
N_QUAD = HEADS // QUAD
AUG = 72

norm_eps = 1e-05
adam_eps = 1e-08
beta_first = 0.5
beta_second = 0.5
learn_rate = 0.01
vector_rate = 0.06
decay_rate = 0.1
average_keep = 0.9

f32 = jnp.float32
bf16 = jnp.bfloat16

S_SEQ, S_GRP, S_MASK, S_BACK = 0, 1, 4, 8

MIB = 1024 * 1024


def dot_nn(a, b):
    return lax.dot_general(a, b, (((1,), (0,)), ((), ())), preferred_element_type=f32)


def dot_nt(a, b):
    return lax.dot_general(a, b, (((1,), (1,)), ((), ())), preferred_element_type=f32)


def dot_tn(a, b):
    return lax.dot_general(a, b, (((0,), (0,)), ((), ())), preferred_element_type=f32)


def whole(shape):
    return pl.BlockSpec(tuple(shape), lambda *_: (0,) * len(shape))


def along(block, axis=0):
    return pl.BlockSpec(tuple(block), lambda i, s: tuple(i if d == axis else 0 for d in range(len(block))))


def sds(shape, dtype):
    return jax.ShapeDtypeStruct(tuple(shape), dtype)


class Line:
    def __init__(self, scal):
        self.scal = scal
        self.stay = set()

    def wait(self, *values):
        self.scal, values = lax.optimization_barrier((self.scal, values))
        return values

    def call(self, body, args, in_specs, outs, out_specs, grid=(1,), scratch=(), vmem=32,
             hold=0, far=(), out_far=(), aliases=None, name=None):
        args = [
            pltpu.with_memory_space_constraint(a, pltpu.HBM) if id(a) in self.stay or k in far else a
            for k, a in enumerate(args)
        ]
        got = pl.pallas_call(
            body,
            out_shape=tuple(pltpu.HBM(o.shape, o.dtype) if k in out_far else o for k, o in enumerate(outs)),
            grid_spec=pltpu.PrefetchScalarGridSpec(
                num_scalar_prefetch=1,
                grid=grid,
                in_specs=list(in_specs),
                out_specs=tuple(out_specs),
                scratch_shapes=list(scratch),
            ),
            compiler_params=pltpu.CompilerParams(
                dimension_semantics=("arbitrary",) * len(grid), vmem_limit_bytes=vmem * MIB
            ),
            cost_estimate=pl.CostEstimate(
                flops=hold * 10**9, bytes_accessed=1024, transcendentals=0
            ),
            input_output_aliases=aliases or {},
            name=name,
        )(self.scal, *args)
        self.scal, got = lax.optimization_barrier((self.scal, got))
        return got


def store_sel(refs, at, values, scal):
    if len(refs) == 1:
        refs[0][at] = values
        return
    block = D // 8
    for j in range(8):
        rel = jnp.bitwise_xor(scal[S_GRP], j)
        place = pl.multiple_of(jnp.right_shift(rel, 1) * block, block)
        odd = jnp.bitwise_and(rel, 1)
        part = values[j * block : (j + 1) * block, :]

        @pl.when(odd == 1)
        def _(part=part, place=place):
            refs[0][at, pl.ds(place, block), :] = part

        @pl.when(odd == 0)
        def _(part=part, place=place):
            refs[1][at, pl.ds(place, block), :] = part


def normalize(values):
    average = jnp.mean(values, axis=1, keepdims=True)
    centered = values - average
    variance = jnp.mean(centered * centered, axis=1, keepdims=True)
    inverse = lax.rsqrt(variance + norm_eps)
    return centered * inverse, inverse


def quad_maps(hedge_t):
    wide = QUAD * HD
    row = lax.broadcasted_iota(jnp.int32, (wide, HD), 0)
    col = lax.broadcasted_iota(jnp.int32, (wide, HD), 1)
    spread = (jnp.bitwise_and(row, HD - 1) == col).astype(bf16)
    tiled = dot_nn(spread, hedge_t)
    big_r = lax.broadcasted_iota(jnp.int32, (wide, wide), 0)
    big_c = lax.broadcasted_iota(jnp.int32, (wide, wide), 1)
    same = jnp.right_shift(big_r, 6) == jnp.right_shift(big_c, 6)
    return jnp.where(same, tiled, 0.0)


def ones_rows(count):
    return (lax.broadcasted_iota(jnp.int32, (AUG - HD, count), 0) == 0).astype(f32).astype(bf16)


def rows_up(values):
    return jnp.concatenate([values, jnp.zeros((3, values.shape[1]), f32)], axis=0).T


def features(pt, maps):
    high = pt.astype(bf16)
    rest = (pt - high.astype(f32)).astype(bf16)
    scores = dot_nn(jnp.concatenate([maps, maps], axis=1), jnp.concatenate([high, rest], axis=0))
    heads = []
    for h in range(QUAD):
        s = scores[h * HD : (h + 1) * HD, :]
        top = jnp.max(s, axis=0, keepdims=True)
        bottom = jnp.min(s, axis=0, keepdims=True)
        pos = jnp.exp(s - top)
        neg = jnp.exp(bottom - s)
        pos = pos * (1.0 / jnp.sum(pos, axis=0, keepdims=True))
        neg = neg * (1.0 / jnp.sum(neg, axis=0, keepdims=True))
        heads.append(jnp.concatenate([pos, neg], axis=0).astype(bf16))
    return high, heads


def keys_body(scal, x_ref, wk_ref, wv_ref, hedge_ref, vt_ref, vq_ref, h1_ref, kt_ref, fk_ref, vt_out, s_ref):
    rows = x_ref.shape[0]

    @pl.when(pl.program_id(0) == 0)
    def _():
        normed, _ = normalize(x_ref[...].astype(f32))
        vt = vt_ref[...].astype(f32)
        h1_ref[...] = (normed * vt[0:1] + vt[1:2]).astype(bf16)

    h1 = h1_ref[...]
    bias = rows_up(vq_ref[...].astype(f32))
    v_t = (dot_nt(wv_ref[...], h1) + bias[:, 8:9]).astype(bf16)
    vt_out[...] = v_t
    pt = dot_nt(wk_ref[...], h1) + bias[:, 7:8]
    kt_ref[...], heads = features(pt, quad_maps(hedge_ref[...]).astype(bf16))
    extra = ones_rows(rows)
    for h, both in enumerate(heads):
        fk_ref[h * 2 * HD : (h + 1) * 2 * HD, :] = both
        va = jnp.concatenate([v_t[h * HD : (h + 1) * HD, :], extra], axis=0)
        s_ref[h * AUG : (h + 1) * AUG, :] = dot_nt(va, both).astype(bf16)


def queries_body(n_sel, scal, h1_ref, g_ref, wq_ref, hedge_ref, vq_ref, *refs):
    sel = refs[:n_sel]
    qt_ref, fq_ref = refs[n_sel:]
    h1 = h1_ref[...]

    @pl.when(pl.program_id(0) == 0)
    def _():
        store_sel(sel, 0, g_ref[...].T, scal)
        store_sel(sel, 1, h1.T, scal)

    bias = rows_up(vq_ref[...].astype(f32))
    pt = dot_nt(wq_ref[...], h1) + bias[:, 6:7]
    qt_ref[...], heads = features(pt, quad_maps(hedge_ref[...]).astype(bf16))
    for h, both in enumerate(heads):
        fq_ref[h * 2 * HD : (h + 1) * 2 * HD, :] = both


def tri_mask(half):
    return lax.broadcasted_iota(jnp.int32, (half, half), 0) <= lax.broadcasted_iota(
        jnp.int32, (half, half), 1
    )


def masked_pair(left0, left1, right, keep):
    half = right.shape[1] // 2
    full = dot_tn(left0, right)
    low = dot_tn(left1, right[:, half:])
    diag0 = jnp.where(keep, full[:, :half], 0.0).astype(bf16)
    above = full[:, half:].astype(bf16)
    diag1 = jnp.where(keep, low, 0.0).astype(bf16)
    return diag0, above, diag1


def local_body(scal, fq_ref, fk_ref, vt_ref, num_ref):
    rows = fq_ref.shape[1]
    half = rows // 2
    keep = tri_mask(half)
    extra = ones_rows(rows)
    for h in range(QUAD):
        fq = fq_ref[h * 2 * HD : (h + 1) * 2 * HD, :]
        fk = fk_ref[h * 2 * HD : (h + 1) * 2 * HD, :]
        va = jnp.concatenate([vt_ref[h * HD : (h + 1) * HD, :], extra], axis=0)
        a00, a01, a11 = masked_pair(fk[:, :half], fk[:, half:], fq, keep)
        num_ref[h * AUG : (h + 1) * AUG, :half] = dot_nn(va[:, :half], a00)
        num_ref[h * AUG : (h + 1) * AUG, half:] = dot_nn(va[:, :half], a01) + dot_nn(va[:, half:], a11)


def weighted_state(scal, slot, parts):
    total = None
    for k, part in enumerate(parts):
        term = scal[slot + k].astype(f32) * part.astype(f32)
        total = term if total is None else total + term
    return total.astype(bf16)


def after_body(n_sel, n_parts, scal, *refs):
    parts = refs[:n_parts]
    num_ref, fq_ref, x_ref, w_ref, vt_ref = refs[n_parts : n_parts + 5]
    o_ref, den_ref, r_ref, h2_ref, sin_ref = refs[n_parts + 5 + n_sel : n_parts + 10 + n_sel]
    sel = refs[-1 - n_sel : -1]
    ob_ref = refs[-1]
    vt = vt_ref[...].astype(f32)
    state = weighted_state(scal, S_MASK, [p[...] for p in parts])
    sin_ref[...] = state
    for h in range(HEADS):
        num = num_ref[h * AUG : (h + 1) * AUG, :] + dot_nn(
            state[h * AUG : (h + 1) * AUG, :], fq_ref[h * 2 * HD : (h + 1) * 2 * HD, :]
        )
        den = num[HD : HD + 1, :]
        out = num[:HD, :] * (1.0 / den)
        o_ref[h * HD : (h + 1) * HD, :] = out
        den_ref[h : h + 1, :] = den
        ob_ref[h * HD : (h + 1) * HD, :] = out.astype(bf16)
    obt = ob_ref[...]
    store_sel(sel, 0, obt, scal)
    r = x_ref[...].astype(f32) + dot_nt(obt.T, w_ref[...]) + vt[4:5]
    r_ref[...] = r
    normed, _ = normalize(r)
    h2 = (normed * vt[2:3] + vt[3:4]).astype(bf16)
    h2_ref[...] = h2
    store_sel(sel, 1, h2.T, scal)


gelu_c = 0.7978845608028654
gelu_k = 0.044715


def mlp_body(first, scal, h2_ref, g_ref, wf_ref, wd_ref, bias_ref, *refs):
    if first:
        out_ref, dh_ref, act_ref, db_ref = refs
    else:
        out_in, dh_in, out_ref, dh_ref, act_ref, db_ref = refs
    u = dot_nt(h2_ref[...], wf_ref[...]) + bias_ref[...].astype(f32)
    de = dot_nt(g_ref[...], wd_ref[...])
    uu = u * u
    t = jnp.tanh(gelu_c * u * (1.0 + gelu_k * uu))
    half_t = 0.5 * (1.0 + t)
    e = (u * half_t).astype(bf16)
    slope = half_t + 0.5 * u * (1.0 - t * t) * (gelu_c * (1.0 + 3.0 * gelu_k * uu))
    du = (de * slope).astype(bf16)
    act_ref[0, 0] = e
    act_ref[1, 0] = du
    db_ref[...] = jnp.sum(du.astype(f32), axis=0, keepdims=True)
    add_out = dot_nn(e, wd_ref[...])
    add_dh = dot_nn(du, wf_ref[...])
    step = pl.program_id(0)

    @pl.when(step == 0)
    def _():
        if first:
            out_ref[...] = add_out
            dh_ref[...] = add_dh
        else:
            out_ref[...] = out_in[...] + add_out
            dh_ref[...] = dh_in[...] + add_dh

    @pl.when(step > 0)
    def _():
        out_ref[...] += add_out
        dh_ref[...] += add_dh


def back_body(scal, out_ref, dh_ref, r_ref, g_ref, w_ref, vt_ref, o_ref, den_ref, fq_ref, y_ref, dr_ref,
              da_ref, rho_ref, ds_ref, sums_ref, do_ref):
    vt = vt_ref[...].astype(f32)
    r = r_ref[...]
    y_ref[...] = (r + out_ref[...] + vt[5:6]).astype(bf16)
    grad_out = g_ref[...].astype(f32)
    normed, inverse = normalize(r)
    up = dh_ref[...]
    dn = up * vt[2:3]
    dr = grad_out + inverse * (
        dn - jnp.mean(dn, axis=1, keepdims=True) - normed * jnp.mean(dn * normed, axis=1, keepdims=True)
    )
    dr_ref[...] = dr
    da = dr.astype(bf16)
    da_ref[...] = da.T
    sums_ref[...] = jnp.concatenate(
        [
            jnp.sum(up * normed, axis=0, keepdims=True),
            jnp.sum(up, axis=0, keepdims=True),
            jnp.sum(da.astype(f32), axis=0, keepdims=True),
            jnp.sum(grad_out, axis=0, keepdims=True),
        ],
        axis=0,
    )
    do_ref[...] = dot_nn(da, w_ref[...]).astype(bf16).T
    rows = r.shape[0]
    zero_row = lax.broadcasted_iota(jnp.int32, (AUG - HD, rows), 0) == 0
    for h in range(HEADS):
        dout = do_ref[h * HD : (h + 1) * HD, :].astype(f32)
        inv = 1.0 / den_ref[h : h + 1, :]
        rho = (dout * inv).astype(bf16)
        c = -jnp.sum(dout * o_ref[h * HD : (h + 1) * HD, :], axis=0, keepdims=True) * inv
        extra = jnp.where(zero_row, jnp.broadcast_to(c, (AUG - HD, rows)), 0.0).astype(bf16)
        ra = jnp.concatenate([rho, extra], axis=0)
        rho_ref[h * AUG : (h + 1) * AUG, :] = ra
        ds_ref[h * AUG : (h + 1) * AUG, :] = dot_nt(ra, fq_ref[h * 2 * HD : (h + 1) * 2 * HD, :]).astype(bf16)


def feature_back(feat, upstream):
    pos, neg = feat[:HD].astype(f32), feat[HD:].astype(f32)
    up_pos, up_neg = upstream[:HD], upstream[HD:]
    return pos * (up_pos - jnp.sum(pos * up_pos, axis=0, keepdims=True)) - neg * (
        up_neg - jnp.sum(neg * up_neg, axis=0, keepdims=True)
    )


def attend_back_body(n_parts, scal, *refs):
    parts = refs[:n_parts]
    (fq_ref, fk_ref, vt_ref, rho_ref, sin_ref, qt_ref, kt_ref, hedge_ref, da_ref) = refs[n_parts : n_parts + 9]
    dp_ref, dm_ref, db_ref = refs[-3:]
    dp_ref[3] = da_ref[...]
    rows = fq_ref.shape[1]
    half = rows // 2
    keep = tri_mask(half)
    extra = ones_rows(rows)
    back_state = weighted_state(scal, S_BACK, [p[...] for p in parts])
    ds_q, ds_k = [], []
    for h in range(QUAD):
        fq = fq_ref[h * 2 * HD : (h + 1) * 2 * HD, :]
        fk = fk_ref[h * 2 * HD : (h + 1) * 2 * HD, :]
        head = slice(h * HD, (h + 1) * HD)
        aug = slice(h * AUG, (h + 1) * AUG)
        va = jnp.concatenate([vt_ref[head, :], extra], axis=0)
        ra = rho_ref[aug, :]
        state, back = sin_ref[aug, :], back_state[aug, :]
        a00, a01, a11 = masked_pair(fk[:, :half], fk[:, half:], fq, keep)
        g00, g01, g11 = masked_pair(va[:, :half], va[:, half:], ra, keep)
        far = dot_tn(state, ra)
        left = far[:, :half] + dot_nn(fk[:, :half], g00)
        right = far[:, half:] + dot_nn(fk[:, :half], g01) + dot_nn(fk[:, half:], g11)
        dfq = jnp.concatenate([left, right], axis=1)
        far_k = dot_tn(back, va)
        left = far_k[:, :half] + dot_nt(fq[:, :half], g00) + dot_nt(fq[:, half:], g01)
        right = far_k[:, half:] + dot_nt(fq[:, half:], g11)
        dfk = jnp.concatenate([left, right], axis=1)
        far_v = dot_nn(back, fk)[:HD]
        rv = ra[:HD]
        left = far_v[:, :half] + dot_nt(rv[:, :half], a00) + dot_nt(rv[:, half:], a01)
        right = far_v[:, half:] + dot_nt(rv[:, half:], a11)
        dp_ref[2, head, :] = jnp.concatenate([left, right], axis=1).astype(bf16)
        dsq = feature_back(fq, dfq).astype(bf16)
        dsk = feature_back(fk, dfk).astype(bf16)
        ds_q.append(dsq)
        ds_k.append(dsk)
    maps = quad_maps(hedge_ref[...]).T.astype(bf16)
    ds_q, ds_k = jnp.concatenate(ds_q, axis=0), jnp.concatenate(ds_k, axis=0)
    dm = dot_nt(qt_ref[...], ds_q) + dot_nt(kt_ref[...], ds_k)
    for h in range(QUAD):
        head = slice(h * HD, (h + 1) * HD)
        dm_ref[head, :] = dm[head, head]
    dq = dot_nn(maps, ds_q).astype(bf16)
    dk = dot_nn(maps, ds_k).astype(bf16)
    dp_ref[0] = dq
    dp_ref[1] = dk
    db_ref[...] = jnp.concatenate(
        [jnp.sum(v.astype(f32), axis=1, keepdims=True) for v in (dq, dk, dp_ref[2])], axis=1
    )


def input_body(fast, scal, dp_ref, w_ref, x_ref, dr_ref, vt_ref, sums_ref, dbfc_ref, db_ref, dm_ref, *refs):
    gin_ref, *small_refs, acc_ref = refs
    step = pl.program_id(0)
    part = dot_tn(dp_ref[0], w_ref[...])

    @pl.when(step == 0)
    def _():
        acc_ref[...] = part

    @pl.when(step == 1)
    def _():
        acc_ref[...] += part

    @pl.when(step == 2)
    def _():
        vt = vt_ref[...].astype(f32)
        up = acc_ref[...] + part
        normed, inverse = normalize(x_ref[...].astype(f32))
        dn = up * vt[0:1]
        gin = dr_ref[...] + inverse * (
            dn - jnp.mean(dn, axis=1, keepdims=True) - normed * jnp.mean(dn * normed, axis=1, keepdims=True)
        )
        gin_ref[...] = gin.astype(bf16)
        rows16 = jnp.concatenate(
            [
                jnp.sum(up * normed, axis=0, keepdims=True),
                jnp.sum(up, axis=0, keepdims=True),
                sums_ref[...],
                jnp.zeros((3, D), f32),
                dbfc_ref[...],
                jnp.zeros((3, D), f32),
            ],
            axis=0,
        )
        cols = rows16.T
        lane = lax.broadcasted_iota(jnp.int32, (D, HD), 1)
        tail = jnp.concatenate([cols, jnp.zeros((D, HD - 16), f32)], axis=1)
        for k in range(3):
            tail = jnp.where(lane == 6 + k, db_ref[:, k : k + 1], tail)
        small = jnp.concatenate([dm_ref[...], tail], axis=1)
        store_sel(small_refs, 0, small, scal)


def mlp_grads_body(by_y, scal, *refs):
    sels, acts_a, acts_b, sels_h = refs[0:2], refs[2:4], refs[4:6], refs[6:8]
    send, keep = refs[8:]
    block = D // 8
    wq = send.shape[2]
    y_last = 1 - pl.program_id(0)

    def total(lefts, rights):
        return (dot_nn(lefts[0][0], rights[0][0, 0]) + dot_nn(lefts[1][0], rights[1][0, 0])).astype(bf16)

    for path, value in enumerate((total(sels, acts_a), total(sels_h, acts_b))):
        rows = slice(path * block, (path + 1) * block)
        for half in range(2):
            x_last = 1 - jnp.bitwise_xor(half, jnp.bitwise_and(scal[S_SEQ], 1))
            cols = slice(half * wq, (half + 1) * wq)

            def part(z, value=value, cols=cols):
                return value[z * block : (z + 1) * block, cols]

            if by_y:
                for bit, ref in ((0, send), (1, keep)):

                    @pl.when(y_last == bit)
                    def _(ref=ref, part=part, rows=rows, x_last=x_last):
                        for at, z in enumerate((3, 1, 2, 0)):
                            ref[4 * (at // 2) + 2 * x_last + at % 2, rows, :] = part(z)
            else:
                base = 4 * y_last + 1 * x_last
                for ref, order in ((send, (3, 1)), (keep, (2, 0))):
                    for at, z in enumerate(order):
                        ref[2 * at + base, rows, :] = part(z)


def mlp_grads(line, by_y, sels, acts, far=(), out_far=()):
    _, depth, rows = sels[0].shape
    half = sds((8, 2 * (D // 8), D // 2), bf16)

    def act(path):
        return pl.BlockSpec((1, 1, rows, D), lambda i, s: (path, i, 0, 0))

    def sel(slot):
        return pl.BlockSpec((1, depth, rows), lambda i, s: (slot, 0, 0))

    return line.call(
        partial(mlp_grads_body, by_y),
        [*sels, *acts, *acts, *sels],
        [sel(0)] * 2 + [act(0)] * 2 + [act(1)] * 2 + [sel(3)] * 2,
        [half] * 2,
        [whole(half.shape)] * 2,
        grid=(2,),
        vmem=24,
        far=far,
        out_far=out_far,
        name="mlp_grads",
    )


def pack_rows(values, count):
    return jnp.concatenate([values[b * count : (b + 1) * count] for b in range(3)], axis=1)


def unpack_rows(values):
    return jnp.concatenate([values[:, b * 128 : (b + 1) * 128] for b in range(3)], axis=0)


def order_a(i):
    return jnp.where(i < 2, 2 * i + 1, 2 * i - 4)


def order_b(i):
    return jnp.where(i < 2, i + 2, i - 2)


def pick_rows(ref, half, count):
    rows = [ref[pl.ds(pl.multiple_of(z * 2 * count + half * count, 8), count), :] for z in range(4)]
    return jnp.concatenate(rows, axis=0)


def tail_grads_body(scal, *refs):
    h1, ob, dqk, dvo = refs[0:2], refs[2:4], refs[4:6], refs[6:8]
    small_own, small_other, send_a, keep_a, send_b, keep_b, small_ref, sum_ref = refs[8:]
    step = pl.program_id(0)
    wq = send_a.shape[1]
    qb = jnp.bitwise_xor(order_b(step), scal[S_SEQ])
    at = pl.multiple_of(jnp.bitwise_and(step, 1) * wq, wq)

    def total(lefts, rights):
        return (dot_nt(lefts[0][0], rights[0][0]) + dot_nt(lefts[1][0], rights[1][0])).astype(bf16)

    def put(send, keep, value):
        @pl.when(step < 2)
        def _():
            send[pl.ds(at, wq), :] = value

        @pl.when(step >= 2)
        def _():
            keep[pl.ds(at, wq), :] = value

    put(send_a, keep_a, total(h1, dqk))

    @pl.when(qb < 2)
    def _():
        put(send_b, keep_b, total(h1, dvo))

    @pl.when(qb >= 2)
    def _():
        put(send_b, keep_b, total(ob, dvo))

    @pl.when(step == 0)
    def _():
        sum_ref[...] = small_own[0] + small_other[0]
        x_abs = jnp.bitwise_and(scal[S_SEQ], 1)
        small_ref[...] = pack_rows(pick_rows(sum_ref, x_abs, 48), 64)
        send_a[2 * wq :, :] = pack_rows(pick_rows(sum_ref, 1 - x_abs, 48), 64).astype(bf16)


def tail_grads(line, sels, dp, small):
    _, depth, rows = sels[0].shape
    wq = D // 2
    dp = [v.reshape(8, wq, rows) for v in dp]

    def sel(slot):
        return pl.BlockSpec((1, depth, rows), lambda i, s: (slot, 0, 0))

    outs = [
        sds((2 * wq + 64, wq), bf16), sds((2 * wq, wq), bf16),
        sds((2 * wq, wq), bf16), sds((2 * wq, wq), bf16), sds((64, wq), f32),
    ]
    return line.call(
        tail_grads_body,
        [*sels, *sels, *dp, *dp, *small],
        [sel(1)] * 2
        + [sel(2)] * 2
        + [pl.BlockSpec((1, wq, rows), lambda i, s: (jnp.bitwise_xor(order_a(i), s[S_SEQ]), 0, 0))] * 2
        + [pl.BlockSpec((1, wq, rows), lambda i, s: (4 + jnp.bitwise_xor(order_b(i), s[S_SEQ]), 0, 0))] * 2
        + [whole(small[0].shape)] * 2,
        outs,
        [whole(o.shape) for o in outs],
        grid=(4,),
        scratch=[pltpu.VMEM((depth, 2 * HD), f32)],
        vmem=10,
        hold=4,
        name="tail_grads",
    )


def swap(value, axis, size, bit):
    return lax.ppermute(value, axis, [(i, i ^ bit) for i in range(size)])


def halve_body(scal, keep_ref, recv_ref, send_ref, left_ref):
    half = send_ref.shape[0]
    send_ref[...] = (keep_ref[:half].astype(f32) + recv_ref[:half].astype(f32)).astype(bf16)
    left_ref[...] = (keep_ref[half:].astype(f32) + recv_ref[half:].astype(f32)).astype(left_ref.dtype)


class Halves:
    def __init__(self, line, send, keep, stages):
        self.line, self.keep, self.stages = line, keep, list(stages)
        self.recv = swap(send, *self.stages.pop(0))

    def step(self, hold=0):
        count, rows, wq = self.keep.shape
        shape = (count // 2, rows, wq)
        send, self.keep = self.line.call(
            halve_body, [self.keep, self.recv], [whole(self.keep.shape)] * 2,
            [sds(shape, bf16), sds(shape, self.keep.dtype)], [whole(shape)] * 2,
            vmem=8, hold=hold, name="halve",
        )
        self.recv = swap(send, *self.stages.pop(0))


def final_body(scal, *refs):
    out = refs[-1]
    for j in range(2):
        out[j] = (refs[2 * j][0].astype(f32) + refs[2 * j + 1][0].astype(f32)).astype(bf16)


def final_both(line, pieces):
    shape = (2,) + pieces[0].keep.shape[1:]
    (mine,) = line.call(
        final_body, [v for p in pieces for v in (p.keep, p.recv)], [whole((1,) + shape[1:])] * 4,
        [sds(shape, bf16)], [whole(shape)], vmem=4, name="final",
    )
    return mine.reshape(4 * (D // 8), shape[2])


def tail_one_body(scal, keep_a, recv_a, keep_b, recv_b, small_ref, send_a, send_b, half_ref):
    wq = send_b.shape[0]
    send_a[:wq, :] = (keep_a[wq : 2 * wq].astype(f32) + recv_a[wq : 2 * wq].astype(f32)).astype(bf16)
    half_ref[...] = unpack_rows(small_ref[...] + recv_a[2 * wq :].astype(f32))
    y_abs = jnp.right_shift(scal[S_SEQ], 1)
    send_a[wq:, :] = pack_rows(pick_rows(half_ref, 1 - y_abs, 24), 32).astype(bf16)
    send_b[...] = (keep_b[wq:].astype(f32) + recv_b[wq:].astype(f32)).astype(bf16)


def tail_two_body(scal, keep_a, recv_a, keep_b, recv_b, small_ref, far_a, far_b, own_ref, *refs):
    out_refs, half_ref = refs[:-1], refs[-1]
    wq = far_b.shape[0]
    block = D // 8
    half_ref[...] = unpack_rows(small_ref[...] + recv_a[2 * wq :].astype(f32))
    small = pick_rows(half_ref, jnp.right_shift(scal[S_SEQ], 1), 24) + unpack_rows(far_a[wq:].astype(f32))
    first = keep_a[:wq].astype(f32) + recv_a[:wq].astype(f32) + far_a[:wq].astype(f32)
    second = keep_b[:wq].astype(f32) + recv_b[:wq].astype(f32) + far_b[...].astype(f32)
    for z, ref in enumerate((own_ref, *out_refs)):
        rows = slice(z * block, (z + 1) * block)
        ref[:block, :] = first[rows].astype(ref.dtype)
        ref[block : 2 * block, :] = second[rows].astype(ref.dtype)
        packed = pack_rows(small[z * 24 : (z + 1) * 24], 8)
        packed = jnp.concatenate([packed, jnp.zeros_like(packed)], axis=0)
        ref[2 * block :, :] = packed.astype(ref.dtype)


def tail_final_body(scal, *refs):
    total = refs[0][...]
    for ref in refs[1:-1]:
        total = total + ref[...].astype(f32)
    refs[-1][...] = total.astype(bf16)


def tail_one(line, tail):
    send_a, keep_a, send_b, keep_b, small = tail
    wq = D // 2
    recv_a, recv_b = swap(send_a, "seq", 4, 1), swap(send_b, "seq", 4, 2)
    shapes = [sds((wq + 32, wq), bf16), sds((wq, wq), bf16)]
    halves = [pltpu.VMEM((D // 4, 2 * HD), f32)]

    def first():
        args = [keep_a, recv_a, keep_b, recv_b, small]
        next_a, next_b = line.call(
            tail_one_body, args, [whole(v.shape) for v in args], shapes, [whole(v.shape) for v in shapes],
            scratch=halves, vmem=12, name="tail_one",
        )
        return swap(next_a, "seq", 4, 2), swap(next_b, "seq", 4, 1)

    def second(far_a, far_b):
        args = [keep_a, recv_a, keep_b, recv_b, small, far_a, far_b]
        shape = (2 * (D // 8) + 16, wq)
        own, *sends = line.call(
            tail_two_body, args, [whole(v.shape) for v in args], [sds(shape, f32)] + [sds(shape, bf16)] * 3,
            [whole(shape)] * 4, scratch=halves, vmem=10, hold=5, name="tail_two",
        )
        return [own, *(swap(v, "grp", 8, 2 * (k + 1)) for k, v in enumerate(sends))]

    return first, second


def tail_final(line, args):
    (mine,) = line.call(
        tail_final_body, args, [whole(v.shape) for v in args], [sds(args[0].shape, bf16)],
        [whole(args[0].shape)], vmem=6, hold=5, name="tail_final",
    )
    return mine


def gather_parts(mine):
    return [mine] + [swap(mine, "seq", 4, k) for k in (1, 2, 3)]


def adam_math(grad, master, first, second, average, rate):
    new_first = beta_first * first + (1.0 - beta_first) * grad
    new_second = beta_second * second + (1.0 - beta_second) * grad * grad
    new_master = master - rate * (
        new_first / (jnp.sqrt(new_second) + adam_eps) + decay_rate * master
    )
    new_average = average_keep * average + (1.0 - average_keep) * new_master
    return new_master, new_first, new_second, new_average


def adam_body(n_alias, has_small, scal, *refs):
    parts, refs = refs[:4], refs[4:]
    if has_small:
        vec_in, refs = refs[:4], refs[4:]
    states, refs = refs[:4], refs[4 + n_alias :]
    outs, refs = refs[:6], refs[6:]
    grad_ref = outs[0]
    block = D // 8
    count, wq = parts[0].shape[0] // block, parts[0].shape[1]
    step = pl.program_id(0)
    path, half = jnp.right_shift(step, 1), jnp.bitwise_and(step, 1)
    for k, ref in enumerate(parts):
        quarter = jnp.bitwise_xor(scal[S_SEQ], k)

        @pl.when((jnp.right_shift(quarter, 1) == half) & (step < 2 * count))
        def _(ref=ref, quarter=quarter):
            at = pl.multiple_of(jnp.bitwise_and(quarter, 1) * wq, 128)
            rows = pl.ds(pl.multiple_of(jnp.minimum(path, count - 1) * block, block), block)
            grad_ref[:, pl.ds(at, wq)] = ref[rows, :].astype(f32)

    if has_small:
        vec_outs, small_ref = refs[:6], refs[6]

        @pl.when(step == 2 * count)
        def _():
            for k, ref in enumerate(parts):
                quarter = jnp.bitwise_xor(scal[S_SEQ], k)
                first = jnp.bitwise_and(quarter, 1) * 48 + jnp.right_shift(quarter, 1) * 24
                packed = ref[2 * block :].astype(f32)
                for b in range(3):
                    small_ref[pl.ds(pl.multiple_of(first + 8 * b, 8), 8), :] = packed[:8, b * 128 : (b + 1) * 128]
            small = small_ref[...]
            grad_ref[...] = jnp.zeros_like(grad_ref)
            grad_ref[:, : 2 * HD] = small
            grad = small.T[HD : HD + vec_in[0].shape[0]]
            results = adam_math(grad, *[v[...] for v in vec_in], vector_rate)
            for ref, value in zip(vec_outs, (grad, *results, results[0])):
                ref[...] = value.astype(ref.dtype)

    results = adam_math(grad_ref[...], *[v[...] for v in states], learn_rate)
    for ref, value in zip(outs[1:], (*results, results[0])):
        ref[...] = value.astype(ref.dtype)


def adam_piece(line, parts, states, outs, block_of, vecs=()):
    block = D // 8
    count = parts[0].shape[0] // block
    rows, wide = states[0].shape
    spec = pl.BlockSpec((block, D), lambda i, s: (0, block_of(i)))
    anywhere = pl.BlockSpec(memory_space=pl.ANY)
    n_alias = 0 if outs is None else 6
    shapes = [sds((rows, wide), f32)] * 5 + [sds((rows, wide), bf16)]
    args = [*parts, *vecs, *states]
    n_before = len(args)
    out_specs = [spec] * 6
    if vecs:
        shapes += [sds(vecs[0].shape, f32)] * 5 + [sds(vecs[0].shape, bf16)]
        out_specs += [whole(vecs[0].shape)] * 6
    return line.call(
        partial(adam_body, n_alias, bool(vecs)),
        [*args, *(outs or [])],
        [whole(v.shape) for v in [*parts, *vecs]] + [spec] * 4 + [anywhere] * n_alias,
        shapes,
        out_specs,
        grid=(2 * count + (1 if vecs else 0),),
        scratch=[pltpu.VMEM((rows, 2 * HD), f32)] if vecs else [],
        aliases={1 + n_before + i: i for i in range(n_alias)},
        vmem=16,
        name="adam",
    )


def on_device(
    n_seq,
    n_grp,
    tokens,
    cotangent,
    seq_len,
    weight_mats,
    weight_vecs,
    master_mats,
    master_vecs,
    moment_mats,
    moment_vecs,
    square_mats,
    square_vecs,
    average_mats,
    average_vecs,
):
    rows = tokens.shape[0]
    fast = n_seq == 4 and n_grp == 8
    seq_at = lax.axis_index("seq")
    grp_at = lax.axis_index("grp")
    slot = jnp.arange(16, dtype=jnp.int32)
    seq_length = seq_len[0]
    peer = jnp.bitwise_xor(seq_at, jnp.bitwise_and(slot, 3) + 1)
    same = (peer * rows) // seq_length == (seq_at * rows) // seq_length
    before = (same & (peer < seq_at)).astype(jnp.int32)
    after = (same & (peer > seq_at)).astype(jnp.int32)
    scal = jnp.where(slot < 8, before, after)
    scal = jnp.where(slot == S_SEQ, seq_at if fast else 0, scal)
    scal = jnp.where(slot == S_GRP, grp_at, scal)
    line = Line(scal)

    w_t = weight_mats.T
    states_m = [master_mats, moment_mats, square_mats, average_mats]
    line.stay = {id(v) for v in (w_t, tokens, cotangent)}
    v_t13 = weight_vecs.T
    n_vec = v_t13.shape[0]
    bias_fc = v_t13[9:].reshape(1, FF)
    wide = QUAD * HD
    n_peer = n_seq - 1
    sel_rows = [D // 2, D // 2] if fast else [D]
    n_sel = len(sel_rows)
    sel_shapes = [sds((4, r, rows), bf16) for r in sel_rows]
    sel_low = [whole((2, r, rows)) for r in sel_rows]
    sel_high = [pl.BlockSpec((2, r, rows), lambda i, s: (1, 0, 0)) for r in sel_rows]

    def both(value):
        return [value, swap(value, "grp", 8, 1)] if fast else [value]

    def w_rows(count, at):
        return pl.BlockSpec((count, D), lambda i, s: (at(i, s), 0))

    hedge_spec = pl.BlockSpec((HD, wide), lambda i, s: ((4 * D + 2 * FF) // HD, i))
    vec_whole = whole(v_t13.shape)
    head_spec, feat_spec = along((wide, rows)), along((2 * wide, rows))
    aug_spec, quad_state = along((QUAD * AUG, rows)), along((QUAD * AUG, 2 * HD))
    st_shape = (HEADS * AUG, 2 * HD)
    vec_quad = pl.BlockSpec((n_vec, wide), lambda i, s: (0, i))
    h1, kt, fk, v_t, s_own = line.call(
        keys_body,
        [tokens, w_t, w_t, w_t, v_t13, v_t13],
        [
            whole((rows, D)),
            w_rows(wide, lambda i, s: N_QUAD + i),
            w_rows(wide, lambda i, s: 2 * N_QUAD + i),
            hedge_spec,
            vec_whole,
            vec_quad,
        ],
        [
            sds((rows, D), bf16),
            sds((D, rows), bf16),
            sds((2 * D, rows), bf16),
            sds((D, rows), bf16),
            sds(st_shape, bf16),
        ],
        [whole((rows, D)), head_spec, feat_spec, head_spec, quad_state],
        grid=(N_QUAD,),
        vmem=12,
        name="keys",
    )
    n_peer = n_seq - 1
    states = [swap(s_own, "seq", n_seq, k + 1) for k in range(n_peer)]
    got = line.call(
        partial(queries_body, n_sel),
        [h1, cotangent, w_t, w_t, v_t13],
        [whole((rows, D)), whole((rows, D)), w_rows(wide, lambda i, s: i), hedge_spec, vec_quad],
        sel_shapes + [sds((D, rows), bf16), sds((2 * D, rows), bf16)],
        sel_low + [head_spec, feat_spec],
        grid=(N_QUAD,),
        vmem=12,
        name="queries",
    )
    sels, (qt, fq) = got[:n_sel], got[n_sel:]

    (num,) = line.call(
        local_body,
        [fq, fk, v_t],
        [feat_spec, feat_spec, head_spec],
        [sds((HEADS * AUG, rows), f32)],
        [aug_spec],
        grid=(N_QUAD,),
        vmem=10,
        name="local",
    )
    got = line.call(
        partial(after_body, n_sel, n_peer),
        [*states, num, fq, tokens, w_t, v_t13, *sels],
        [whole(st_shape)] * n_peer
        + [whole(num.shape), whole(fq.shape), whole((rows, D)), w_rows(D, lambda i, s: 3), vec_whole]
        + [pl.BlockSpec(memory_space=pl.ANY)] * n_sel,
        [
            sds((D, rows), f32),
            sds((16, rows), f32),
            sds((rows, D), f32),
            sds((rows, D), bf16),
            sds(st_shape, bf16),
        ]
        + sel_shapes,
        [whole((D, rows)), whole((16, rows)), whole((rows, D)), whole((rows, D)), whole(st_shape)] + sel_high,
        aliases={n_peer + 6 + i: 5 + i for i in range(n_sel)},
        scratch=[pltpu.VMEM((D, rows), bf16)],
        vmem=10,
        name="after",
    )
    o_t, den, resid, h2, s_in = got[:5]
    sels = got[5:]
    if fast:
        sels = [sels[1], swap(sels[0], "grp", 8, 1)]

    n_piece = 2
    piece = FF // n_piece
    acc, acts, db_fc = [], [], []
    for j in range(n_piece):
        if j == 1:
            (sels,) = line.wait(sels)
        pair_of = lambda i, s, j=j: 2 * j + jnp.bitwise_xor(i, jnp.right_shift(s[S_SEQ], 1))
        out_y, out_dh, act, db = line.call(
            partial(mlp_body, j == 0),
            [h2, cotangent, w_t, w_t, bias_fc, *acc],
            [
                whole((rows, D)),
                whole((rows, D)),
                w_rows(D, lambda i, s: 4 + pair_of(i, s)),
                w_rows(D, lambda i, s: 8 + pair_of(i, s)),
                pl.BlockSpec((1, D), lambda i, s: (0, pair_of(i, s))),
            ]
            + [whole((rows, D))] * len(acc),
            [sds((rows, D), f32), sds((rows, D), f32), sds((2, 2, rows, D), bf16), sds((1, piece), f32)],
            [
                whole((rows, D)),
                whole((rows, D)),
                pl.BlockSpec((2, 1, rows, D), lambda i, s: (0, i, 0, 0)),
                pl.BlockSpec((1, D), lambda i, s: (0, jnp.bitwise_xor(i, jnp.right_shift(s[S_SEQ], 1)))),
            ],
            grid=(2,),
            vmem=14,
            name="mlp",
        )
        acc = [out_y, out_dh]
        db_fc.append(db)
        acts.append(both(act))

    if fast:
        first = Halves(
            line, *mlp_grads(line, False, sels, acts[0], out_far=(1,)),
            [("grp", 8, 2), ("seq", 4, 2), ("grp", 8, 4), ("seq", 4, 1)],
        )
        (acts[1],) = line.wait(acts[1])
    block_output, d_resid, d_attn, rho, ds_own, sums = line.call(
        back_body,
        [*acc, resid, cotangent, w_t, v_t13, o_t, den, fq],
        [whole((rows, D))] * 4
        + [w_rows(D, lambda i, s: 3), vec_whole, whole((D, rows)), whole((16, rows)), whole((2 * D, rows))],
        [
            sds((rows, D), bf16),
            sds((rows, D), f32),
            sds((D, rows), bf16),
            sds((HEADS * AUG, rows), bf16),
            sds(st_shape, bf16),
            sds((4, D), f32),
        ],
        [whole((rows, D))] * 2
        + [whole((D, rows)), whole((HEADS * AUG, rows)), whole(st_shape), whole((4, D))],
        scratch=[pltpu.VMEM((D, rows), bf16)],
        vmem=10,
        out_far=(1, 2, 3),
        name="back",
    )
    back_states = [swap(ds_own, "seq", n_seq, k + 1) for k in range(n_peer)]
    if fast:
        second = mlp_grads(line, True, sels, acts[1], far=range(2, 6))
        (back_states,) = line.wait(back_states)
        second = Halves(
            line, *second, [("seq", 4, 2), ("grp", 8, 2), ("seq", 4, 1), ("grp", 8, 4)]
        )

    grads = [sds((4, D, rows), bf16), sds((D, HD), f32), sds((D, 3), f32)]
    got = []
    for start, count in ((0, N_QUAD),):

        def at(block, axis=0, start=start):
            return pl.BlockSpec(
                tuple(block), lambda i, s: tuple(start + i if d == axis else 0 for d in range(len(block)))
            )

        feat, head = at((2 * wide, rows)), at((wide, rows))
        state = at((QUAD * AUG, 2 * HD))
        args = [*back_states, fq, fk, v_t, rho, s_in, qt, kt, w_t, d_attn]
        got = line.call(
            partial(attend_back_body, n_peer),
            [*args, *got],
            [state] * n_peer
            + [feat, feat, head, at((QUAD * AUG, rows)), state, head, head]
            + [pl.BlockSpec((HD, wide), lambda i, s, start=start: ((4 * D + 2 * FF) // HD, start + i)), head]
            + [pl.BlockSpec(memory_space=pl.ANY)] * len(got),
            grads,
            [at((4, wide, rows), 1), at((wide, HD)), at((wide, 3))],
            grid=(count,),
            aliases={1 + len(args) + k: k for k in range(len(got))},
            hold=1,
            far=(n_peer + 3, n_peer + 8),
            vmem=16,
            name="attend_back",
        )
    dp, dm, db_qkv = got
    dp_both = both(dp)
    db_fc_rows = jnp.concatenate(db_fc, axis=1).reshape(FF // D, D)
    input_grad, *small = line.call(
        partial(input_body, fast),
        [dp, w_t, tokens, d_resid, v_t13, sums, db_fc_rows, db_qkv, dm],
        [
            along((1, D, rows)),
            w_rows(D, lambda i, s: i),
            whole((rows, D)),
            whole((rows, D)),
            vec_whole,
            whole((4, D)),
            whole((FF // D, D)),
            whole((D, 3)),
            whole((D, HD)),
        ],
        [sds((rows, D), bf16)] + [sds((1, r, 2 * HD), f32) for r in sel_rows],
        [whole((rows, D))] + [whole((1, r, 2 * HD)) for r in sel_rows],
        grid=(3,),
        scratch=[pltpu.VMEM((rows, D), f32)],
        vmem=14,
        name="input",
    )
    states_v = [v.T for v in (master_vecs, moment_vecs, square_vecs, average_vecs)]
    if fast:
        theirs, mine = small
        small = [mine, swap(theirs, "grp", 8, 1)]
        first.step(hold=14)
        second.step(hold=60)
        tail = tail_grads(line, sels, dp_both, small)
        tail_first, tail_second = tail_one(line, tail)
        first.step()
        second.step(hold=4)
        far = tail_first()
        first.step()
        second.step()
        mine = final_both(line, [first, second])
        part_x, part_y = swap(mine, "seq", 4, 1), swap(mine, "seq", 4, 2)
        last = tail_second(*far)
        (part_y,) = line.wait(part_y)
        both_mine = [mine, part_x, part_y, swap(part_x, "seq", 4, 2)]
        last_mine = tail_final(line, last)
        outs = adam_piece(
            line, both_mine, states_m, None,
            lambda i: jnp.where(jnp.bitwise_and(i, 2) == 0, 8, 4) + 2 * (i // 4) + jnp.bitwise_and(i, 1),
        )
        last_parts = gather_parts(last_mine)
        outs = adam_piece(
            line, last_parts, states_m, outs, lambda i: jnp.where(i < 4, i, (4 * D + 2 * FF) // D),
            vecs=states_v,
        )
        mats, vecs = outs[:6], [v.T for v in outs[6:]]
    else:
        h1t, obt, h2t = sels[0][1], sels[0][2], sels[0][3]
        joined = [jnp.transpose(a[0], (0, 2, 1, 3)).reshape(2, rows, piece) for a in acts]
        dn = [dot_tn(cotangent, v[0]) for v in joined]
        fc = [dot_nn(h2t, v[1]) for v in joined]
        qkvo = [dot_nt(h1t, dp[k]) for k in range(3)] + [dot_nt(obt, dp[3])]
        small = small[0][0]
        grad = jnp.concatenate([*qkvo, *fc, *dn, small[:, :HD]], axis=1).astype(bf16)
        own = lax.psum_scatter(grad, "grp", scatter_dimension=0, tiled=True)
        own = lax.psum(own, "seq").astype(f32)
        own_v = lax.psum(lax.psum_scatter(small, "grp", scatter_dimension=0, tiled=True), "seq")
        own_v = own_v[:, HD : HD + n_vec]
        results = adam_math(own, *states_m, learn_rate)
        mats = [own, *results, results[0].astype(bf16)]
        results = adam_math(own_v.T, *states_v, vector_rate)
        vecs = [own_v, *[v.T for v in (*results, results[0].astype(bf16))]]
    flat = [x for pair_ in zip(mats, vecs) for x in pair_]
    return (block_output, input_grad, *flat)


def solution(mesh):
    tok = P(("grp", "seq"), None)
    own = P("grp", None)
    in_specs = (tok, tok, P("grp"), P(), P()) + (own,) * 8
    out_specs = (tok, tok) + (own,) * 12
    body = partial(on_device, mesh.shape["seq"], mesh.shape["grp"])
    return jax.shard_map(body, mesh=mesh, in_specs=in_specs, out_specs=out_specs, check_vma=False)
```

```python
from functools import partial

import jax
import jax.numpy as jnp
from jax import lax
from jax.experimental import pallas as pl
from jax.experimental.pallas import tpu as pltpu
from jax.sharding import PartitionSpec as P

D = 768
HEADS = 12
HD = 64
FF = 3072
QUAD = 4
N_QUAD = HEADS // QUAD
AUG = 72

norm_eps = 1e-05
adam_eps = 1e-08
beta_first = 0.5
beta_second = 0.5
learn_rate = 0.01
vector_rate = 0.06
decay_rate = 0.1
average_keep = 0.9

f32 = jnp.float32
bf16 = jnp.bfloat16

S_SEQ, S_GRP, S_MASK, S_BACK = 0, 1, 4, 8

MIB = 1024 * 1024


def dot_nn(a, b):
    return lax.dot_general(a, b, (((1,), (0,)), ((), ())), preferred_element_type=f32)


def dot_nt(a, b):
    return lax.dot_general(a, b, (((1,), (1,)), ((), ())), preferred_element_type=f32)


def dot_tn(a, b):
    return lax.dot_general(a, b, (((0,), (0,)), ((), ())), preferred_element_type=f32)


def whole(shape):
    return pl.BlockSpec(tuple(shape), lambda *_: (0,) * len(shape))


def along(block, axis=0):
    return pl.BlockSpec(tuple(block), lambda i, s: tuple(i if d == axis else 0 for d in range(len(block))))


def sds(shape, dtype):
    return jax.ShapeDtypeStruct(tuple(shape), dtype)


class Line:
    def __init__(self, scal):
        self.scal = scal
        self.stay = set()

    def wait(self, *values):
        self.scal, values = lax.optimization_barrier((self.scal, values))
        return values

    def call(self, body, args, in_specs, outs, out_specs, grid=(1,), scratch=(), vmem=32,
             hold=0, far=(), out_far=(), aliases=None, name=None):
        args = [
            pltpu.with_memory_space_constraint(a, pltpu.HBM) if id(a) in self.stay or k in far else a
            for k, a in enumerate(args)
        ]
        got = pl.pallas_call(
            body,
            out_shape=tuple(pltpu.HBM(o.shape, o.dtype) if k in out_far else o for k, o in enumerate(outs)),
            grid_spec=pltpu.PrefetchScalarGridSpec(
                num_scalar_prefetch=1,
                grid=grid,
                in_specs=list(in_specs),
                out_specs=tuple(out_specs),
                scratch_shapes=list(scratch),
            ),
            compiler_params=pltpu.CompilerParams(
                dimension_semantics=("arbitrary",) * len(grid), vmem_limit_bytes=vmem * MIB
            ),
            cost_estimate=pl.CostEstimate(
                flops=hold * 10**9, bytes_accessed=1024, transcendentals=0
            ),
            input_output_aliases=aliases or {},
            name=name,
        )(self.scal, *args)
        self.scal, got = lax.optimization_barrier((self.scal, got))
        return got


def store_sel(refs, at, values, scal):
    if len(refs) == 1:
        refs[0][at] = values
        return
    block = D // 8
    for j in range(8):
        rel = jnp.bitwise_xor(scal[S_GRP], j)
        place = pl.multiple_of(jnp.right_shift(rel, 1) * block, block)
        odd = jnp.bitwise_and(rel, 1)
        part = values[j * block : (j + 1) * block, :]

        @pl.when(odd == 1)
        def _(part=part, place=place):
            refs[0][at, pl.ds(place, block), :] = part

        @pl.when(odd == 0)
        def _(part=part, place=place):
            refs[1][at, pl.ds(place, block), :] = part


def normalize(values):
    average = jnp.mean(values, axis=1, keepdims=True)
    centered = values - average
    variance = jnp.mean(centered * centered, axis=1, keepdims=True)
    inverse = lax.rsqrt(variance + norm_eps)
    return centered * inverse, inverse


def quad_maps(hedge_t):
    wide = QUAD * HD
    row = lax.broadcasted_iota(jnp.int32, (wide, HD), 0)
    col = lax.broadcasted_iota(jnp.int32, (wide, HD), 1)
    spread = (jnp.bitwise_and(row, HD - 1) == col).astype(bf16)
    tiled = dot_nn(spread, hedge_t)
    big_r = lax.broadcasted_iota(jnp.int32, (wide, wide), 0)
    big_c = lax.broadcasted_iota(jnp.int32, (wide, wide), 1)
    same = jnp.right_shift(big_r, 6) == jnp.right_shift(big_c, 6)
    return jnp.where(same, tiled, 0.0)


def ones_rows(count):
    return (lax.broadcasted_iota(jnp.int32, (AUG - HD, count), 0) == 0).astype(f32).astype(bf16)


def rows_up(values):
    return jnp.concatenate([values, jnp.zeros((3, values.shape[1]), f32)], axis=0).T


def features(pt, maps):
    high = pt.astype(bf16)
    rest = (pt - high.astype(f32)).astype(bf16)
    scores = dot_nn(jnp.concatenate([maps, maps], axis=1), jnp.concatenate([high, rest], axis=0))
    heads = []
    for h in range(QUAD):
        s = scores[h * HD : (h + 1) * HD, :]
        top = jnp.max(s, axis=0, keepdims=True)
        bottom = jnp.min(s, axis=0, keepdims=True)
        pos = jnp.exp(s - top)
        neg = jnp.exp(bottom - s)
        pos = pos * (1.0 / jnp.sum(pos, axis=0, keepdims=True))
        neg = neg * (1.0 / jnp.sum(neg, axis=0, keepdims=True))
        heads.append(jnp.concatenate([pos, neg], axis=0).astype(bf16))
    return high, heads


def keys_body(scal, x_ref, wk_ref, wv_ref, hedge_ref, vt_ref, vq_ref, h1_ref, kt_ref, fk_ref, vt_out, s_ref):
    rows = x_ref.shape[0]

    @pl.when(pl.program_id(0) == 0)
    def _():
        normed, _ = normalize(x_ref[...].astype(f32))
        vt = vt_ref[...].astype(f32)
        h1_ref[...] = (normed * vt[0:1] + vt[1:2]).astype(bf16)

    h1 = h1_ref[...]
    bias = rows_up(vq_ref[...].astype(f32))
    v_t = (dot_nt(wv_ref[...], h1) + bias[:, 8:9]).astype(bf16)
    vt_out[...] = v_t
    pt = dot_nt(wk_ref[...], h1) + bias[:, 7:8]
    kt_ref[...], heads = features(pt, quad_maps(hedge_ref[...]).astype(bf16))
    extra = ones_rows(rows)
    for h, both in enumerate(heads):
        fk_ref[h * 2 * HD : (h + 1) * 2 * HD, :] = both
        va = jnp.concatenate([v_t[h * HD : (h + 1) * HD, :], extra], axis=0)
        s_ref[h * AUG : (h + 1) * AUG, :] = dot_nt(va, both).astype(bf16)


def queries_body(n_sel, scal, h1_ref, g_ref, wq_ref, hedge_ref, vq_ref, *refs):
    sel = refs[:n_sel]
    qt_ref, fq_ref = refs[n_sel:]
    h1 = h1_ref[...]

    @pl.when(pl.program_id(0) == 0)
    def _():
        store_sel(sel, 0, g_ref[...].T, scal)
        store_sel(sel, 1, h1.T, scal)

    bias = rows_up(vq_ref[...].astype(f32))
    pt = dot_nt(wq_ref[...], h1) + bias[:, 6:7]
    qt_ref[...], heads = features(pt, quad_maps(hedge_ref[...]).astype(bf16))
    for h, both in enumerate(heads):
        fq_ref[h * 2 * HD : (h + 1) * 2 * HD, :] = both


def tri_mask(half):
    return lax.broadcasted_iota(jnp.int32, (half, half), 0) <= lax.broadcasted_iota(
        jnp.int32, (half, half), 1
    )


def masked_pair(left0, left1, right, keep):
    half = right.shape[1] // 2
    full = dot_tn(left0, right)
    low = dot_tn(left1, right[:, half:])
    diag0 = jnp.where(keep, full[:, :half], 0.0).astype(bf16)
    above = full[:, half:].astype(bf16)
    diag1 = jnp.where(keep, low, 0.0).astype(bf16)
    return diag0, above, diag1


def local_body(scal, fq_ref, fk_ref, vt_ref, num_ref):
    rows = fq_ref.shape[1]
    half = rows // 2
    keep = tri_mask(half)
    extra = ones_rows(rows)
    for h in range(QUAD):
        fq = fq_ref[h * 2 * HD : (h + 1) * 2 * HD, :]
        fk = fk_ref[h * 2 * HD : (h + 1) * 2 * HD, :]
        va = jnp.concatenate([vt_ref[h * HD : (h + 1) * HD, :], extra], axis=0)
        a00, a01, a11 = masked_pair(fk[:, :half], fk[:, half:], fq, keep)
        num_ref[h * AUG : (h + 1) * AUG, :half] = dot_nn(va[:, :half], a00)
        num_ref[h * AUG : (h + 1) * AUG, half:] = dot_nn(va[:, :half], a01) + dot_nn(va[:, half:], a11)


def weighted_state(scal, slot, parts):
    total = None
    for k, part in enumerate(parts):
        term = scal[slot + k].astype(f32) * part.astype(f32)
        total = term if total is None else total + term
    return total.astype(bf16)


def after_body(n_sel, n_parts, scal, *refs):
    parts = refs[:n_parts]
    num_ref, fq_ref, x_ref, w_ref, vt_ref = refs[n_parts : n_parts + 5]
    o_ref, den_ref, r_ref, h2_ref, sin_ref = refs[n_parts + 5 + n_sel : n_parts + 10 + n_sel]
    sel = refs[-1 - n_sel : -1]
    ob_ref = refs[-1]
    vt = vt_ref[...].astype(f32)
    state = weighted_state(scal, S_MASK, [p[...] for p in parts])
    sin_ref[...] = state
    for h in range(HEADS):
        num = num_ref[h * AUG : (h + 1) * AUG, :] + dot_nn(
            state[h * AUG : (h + 1) * AUG, :], fq_ref[h * 2 * HD : (h + 1) * 2 * HD, :]
        )
        den = num[HD : HD + 1, :]
        out = num[:HD, :] * (1.0 / den)
        o_ref[h * HD : (h + 1) * HD, :] = out
        den_ref[h : h + 1, :] = den
        ob_ref[h * HD : (h + 1) * HD, :] = out.astype(bf16)
    obt = ob_ref[...]
    store_sel(sel, 0, obt, scal)
    r = x_ref[...].astype(f32) + dot_nt(obt.T, w_ref[...]) + vt[4:5]
    r_ref[...] = r
    normed, _ = normalize(r)
    h2 = (normed * vt[2:3] + vt[3:4]).astype(bf16)
    h2_ref[...] = h2
    store_sel(sel, 1, h2.T, scal)


gelu_c = 0.7978845608028654
gelu_k = 0.044715


def mlp_body(first, scal, h2_ref, g_ref, wf_ref, wd_ref, bias_ref, *refs):
    if first:
        out_ref, dh_ref, act_ref, db_ref = refs
    else:
        out_in, dh_in, out_ref, dh_ref, act_ref, db_ref = refs
    u = dot_nt(h2_ref[...], wf_ref[...]) + bias_ref[...].astype(f32)
    de = dot_nt(g_ref[...], wd_ref[...])
    uu = u * u
    t = jnp.tanh(gelu_c * u * (1.0 + gelu_k * uu))
    half_t = 0.5 * (1.0 + t)
    e = (u * half_t).astype(bf16)
    slope = half_t + 0.5 * u * (1.0 - t * t) * (gelu_c * (1.0 + 3.0 * gelu_k * uu))
    du = (de * slope).astype(bf16)
    act_ref[0, 0] = e
    act_ref[1, 0] = du
    db_ref[...] = jnp.sum(du.astype(f32), axis=0, keepdims=True)
    add_out = dot_nn(e, wd_ref[...])
    add_dh = dot_nn(du, wf_ref[...])
    step = pl.program_id(0)

    @pl.when(step == 0)
    def _():
        if first:
            out_ref[...] = add_out
            dh_ref[...] = add_dh
        else:
            out_ref[...] = out_in[...] + add_out
            dh_ref[...] = dh_in[...] + add_dh

    @pl.when(step > 0)
    def _():
        out_ref[...] += add_out
        dh_ref[...] += add_dh


def back_body(scal, out_ref, dh_ref, r_ref, g_ref, w_ref, vt_ref, o_ref, den_ref, fq_ref, y_ref, dr_ref,
              da_ref, rho_ref, ds_ref, sums_ref, do_ref):
    vt = vt_ref[...].astype(f32)
    r = r_ref[...]
    y_ref[...] = (r + out_ref[...] + vt[5:6]).astype(bf16)
    grad_out = g_ref[...].astype(f32)
    normed, inverse = normalize(r)
    up = dh_ref[...]
    dn = up * vt[2:3]
    dr = grad_out + inverse * (
        dn - jnp.mean(dn, axis=1, keepdims=True) - normed * jnp.mean(dn * normed, axis=1, keepdims=True)
    )
    dr_ref[...] = dr
    da = dr.astype(bf16)
    da_ref[...] = da.T
    sums_ref[...] = jnp.concatenate(
        [
            jnp.sum(up * normed, axis=0, keepdims=True),
            jnp.sum(up, axis=0, keepdims=True),
            jnp.sum(da.astype(f32), axis=0, keepdims=True),
            jnp.sum(grad_out, axis=0, keepdims=True),
        ],
        axis=0,
    )
    do_ref[...] = dot_nn(da, w_ref[...]).astype(bf16).T
    rows = r.shape[0]
    zero_row = lax.broadcasted_iota(jnp.int32, (AUG - HD, rows), 0) == 0
    for h in range(HEADS):
        dout = do_ref[h * HD : (h + 1) * HD, :].astype(f32)
        inv = 1.0 / den_ref[h : h + 1, :]
        rho = (dout * inv).astype(bf16)
        c = -jnp.sum(dout * o_ref[h * HD : (h + 1) * HD, :], axis=0, keepdims=True) * inv
        extra = jnp.where(zero_row, jnp.broadcast_to(c, (AUG - HD, rows)), 0.0).astype(bf16)
        ra = jnp.concatenate([rho, extra], axis=0)
        rho_ref[h * AUG : (h + 1) * AUG, :] = ra
        ds_ref[h * AUG : (h + 1) * AUG, :] = dot_nt(ra, fq_ref[h * 2 * HD : (h + 1) * 2 * HD, :]).astype(bf16)


def feature_back(feat, upstream):
    pos, neg = feat[:HD].astype(f32), feat[HD:].astype(f32)
    up_pos, up_neg = upstream[:HD], upstream[HD:]
    return pos * (up_pos - jnp.sum(pos * up_pos, axis=0, keepdims=True)) - neg * (
        up_neg - jnp.sum(neg * up_neg, axis=0, keepdims=True)
    )


def attend_back_body(n_parts, scal, *refs):
    parts = refs[:n_parts]
    (fq_ref, fk_ref, vt_ref, rho_ref, sin_ref, qt_ref, kt_ref, hedge_ref, da_ref) = refs[n_parts : n_parts + 9]
    dp_ref, dm_ref, db_ref = refs[-3:]
    dp_ref[3] = da_ref[...]
    rows = fq_ref.shape[1]
    half = rows // 2
    keep = tri_mask(half)
    extra = ones_rows(rows)
    back_state = weighted_state(scal, S_BACK, [p[...] for p in parts])
    ds_q, ds_k = [], []
    for h in range(QUAD):
        fq = fq_ref[h * 2 * HD : (h + 1) * 2 * HD, :]
        fk = fk_ref[h * 2 * HD : (h + 1) * 2 * HD, :]
        head = slice(h * HD, (h + 1) * HD)
        aug = slice(h * AUG, (h + 1) * AUG)
        va = jnp.concatenate([vt_ref[head, :], extra], axis=0)
        ra = rho_ref[aug, :]
        state, back = sin_ref[aug, :], back_state[aug, :]
        a00, a01, a11 = masked_pair(fk[:, :half], fk[:, half:], fq, keep)
        g00, g01, g11 = masked_pair(va[:, :half], va[:, half:], ra, keep)
        far = dot_tn(state, ra)
        left = far[:, :half] + dot_nn(fk[:, :half], g00)
        right = far[:, half:] + dot_nn(fk[:, :half], g01) + dot_nn(fk[:, half:], g11)
        dfq = jnp.concatenate([left, right], axis=1)
        far_k = dot_tn(back, va)
        left = far_k[:, :half] + dot_nt(fq[:, :half], g00) + dot_nt(fq[:, half:], g01)
        right = far_k[:, half:] + dot_nt(fq[:, half:], g11)
        dfk = jnp.concatenate([left, right], axis=1)
        far_v = dot_nn(back, fk)[:HD]
        rv = ra[:HD]
        left = far_v[:, :half] + dot_nt(rv[:, :half], a00) + dot_nt(rv[:, half:], a01)
        right = far_v[:, half:] + dot_nt(rv[:, half:], a11)
        dp_ref[2, head, :] = jnp.concatenate([left, right], axis=1).astype(bf16)
        dsq = feature_back(fq, dfq).astype(bf16)
        dsk = feature_back(fk, dfk).astype(bf16)
        ds_q.append(dsq)
        ds_k.append(dsk)
    maps = quad_maps(hedge_ref[...]).T.astype(bf16)
    ds_q, ds_k = jnp.concatenate(ds_q, axis=0), jnp.concatenate(ds_k, axis=0)
    dm = dot_nt(qt_ref[...], ds_q) + dot_nt(kt_ref[...], ds_k)
    for h in range(QUAD):
        head = slice(h * HD, (h + 1) * HD)
        dm_ref[head, :] = dm[head, head]
    dq = dot_nn(maps, ds_q).astype(bf16)
    dk = dot_nn(maps, ds_k).astype(bf16)
    dp_ref[0] = dq
    dp_ref[1] = dk
    db_ref[...] = jnp.concatenate(
        [jnp.sum(v.astype(f32), axis=1, keepdims=True) for v in (dq, dk, dp_ref[2])], axis=1
    )


def input_body(fast, scal, dp_ref, w_ref, x_ref, dr_ref, vt_ref, sums_ref, dbfc_ref, db_ref, dm_ref, *refs):
    gin_ref, *small_refs, acc_ref = refs
    step = pl.program_id(0)
    part = dot_tn(dp_ref[0], w_ref[...])

    @pl.when(step == 0)
    def _():
        acc_ref[...] = part

    @pl.when(step == 1)
    def _():
        acc_ref[...] += part

    @pl.when(step == 2)
    def _():
        vt = vt_ref[...].astype(f32)
        up = acc_ref[...] + part
        normed, inverse = normalize(x_ref[...].astype(f32))
        dn = up * vt[0:1]
        gin = dr_ref[...] + inverse * (
            dn - jnp.mean(dn, axis=1, keepdims=True) - normed * jnp.mean(dn * normed, axis=1, keepdims=True)
        )
        gin_ref[...] = gin.astype(bf16)
        rows16 = jnp.concatenate(
            [
                jnp.sum(up * normed, axis=0, keepdims=True),
                jnp.sum(up, axis=0, keepdims=True),
                sums_ref[...],
                jnp.zeros((3, D), f32),
                dbfc_ref[...],
                jnp.zeros((3, D), f32),
            ],
            axis=0,
        )
        cols = rows16.T
        lane = lax.broadcasted_iota(jnp.int32, (D, HD), 1)
        tail = jnp.concatenate([cols, jnp.zeros((D, HD - 16), f32)], axis=1)
        for k in range(3):
            tail = jnp.where(lane == 6 + k, db_ref[:, k : k + 1], tail)
        small = jnp.concatenate([dm_ref[...], tail], axis=1)
        store_sel(small_refs, 0, small, scal)


def mlp_grads_body(by_y, scal, *refs):
    sels, acts_a, acts_b, sels_h = refs[0:2], refs[2:4], refs[4:6], refs[6:8]
    send, keep = refs[8:]
    block = D // 8
    wq = send.shape[2]
    y_last = 1 - pl.program_id(0)

    def total(lefts, rights):
        return (dot_nn(lefts[0][0], rights[0][0, 0]) + dot_nn(lefts[1][0], rights[1][0, 0])).astype(bf16)

    for path, value in enumerate((total(sels, acts_a), total(sels_h, acts_b))):
        rows = slice(path * block, (path + 1) * block)
        for half in range(2):
            x_last = 1 - jnp.bitwise_xor(half, jnp.bitwise_and(scal[S_SEQ], 1))
            cols = slice(half * wq, (half + 1) * wq)

            def part(z, value=value, cols=cols):
                return value[z * block : (z + 1) * block, cols]

            if by_y:
                for bit, ref in ((0, send), (1, keep)):

                    @pl.when(y_last == bit)
                    def _(ref=ref, part=part, rows=rows, x_last=x_last):
                        for at, z in enumerate((3, 1, 2, 0)):
                            ref[4 * (at // 2) + 2 * x_last + at % 2, rows, :] = part(z)
            else:
                base = 4 * y_last + 1 * x_last
                for ref, order in ((send, (3, 1)), (keep, (2, 0))):
                    for at, z in enumerate(order):
                        ref[2 * at + base, rows, :] = part(z)


def mlp_grads(line, by_y, sels, acts, far=(), out_far=()):
    _, depth, rows = sels[0].shape
    half = sds((8, 2 * (D // 8), D // 2), bf16)

    def act(path):
        return pl.BlockSpec((1, 1, rows, D), lambda i, s: (path, i, 0, 0))

    def sel(slot):
        return pl.BlockSpec((1, depth, rows), lambda i, s: (slot, 0, 0))

    return line.call(
        partial(mlp_grads_body, by_y),
        [*sels, *acts, *acts, *sels],
        [sel(0)] * 2 + [act(0)] * 2 + [act(1)] * 2 + [sel(3)] * 2,
        [half] * 2,
        [whole(half.shape)] * 2,
        grid=(2,),
        vmem=24,
        far=far,
        out_far=out_far,
        name="mlp_grads",
    )


def pack_rows(values, count):
    return jnp.concatenate([values[b * count : (b + 1) * count] for b in range(3)], axis=1)


def unpack_rows(values):
    return jnp.concatenate([values[:, b * 128 : (b + 1) * 128] for b in range(3)], axis=0)


def order_a(i):
    return jnp.where(i < 2, 2 * i + 1, 2 * i - 4)


def order_b(i):
    return jnp.where(i < 2, i + 2, i - 2)


def pick_rows(ref, half, count):
    rows = [ref[pl.ds(pl.multiple_of(z * 2 * count + half * count, 8), count), :] for z in range(4)]
    return jnp.concatenate(rows, axis=0)


def tail_grads_body(scal, *refs):
    h1, ob, dqk, dvo = refs[0:2], refs[2:4], refs[4:6], refs[6:8]
    small_own, small_other, send_a, keep_a, send_b, keep_b, small_ref, sum_ref = refs[8:]
    step = pl.program_id(0)
    wq = send_a.shape[1]
    qb = jnp.bitwise_xor(order_b(step), scal[S_SEQ])
    at = pl.multiple_of(jnp.bitwise_and(step, 1) * wq, wq)

    def total(lefts, rights):
        return (dot_nt(lefts[0][0], rights[0][0]) + dot_nt(lefts[1][0], rights[1][0])).astype(bf16)

    def put(send, keep, value):
        @pl.when(step < 2)
        def _():
            send[pl.ds(at, wq), :] = value

        @pl.when(step >= 2)
        def _():
            keep[pl.ds(at, wq), :] = value

    put(send_a, keep_a, total(h1, dqk))

    @pl.when(qb < 2)
    def _():
        put(send_b, keep_b, total(h1, dvo))

    @pl.when(qb >= 2)
    def _():
        put(send_b, keep_b, total(ob, dvo))

    @pl.when(step == 0)
    def _():
        sum_ref[...] = small_own[0] + small_other[0]
        x_abs = jnp.bitwise_and(scal[S_SEQ], 1)
        small_ref[...] = pack_rows(pick_rows(sum_ref, x_abs, 48), 64)
        send_a[2 * wq :, :] = pack_rows(pick_rows(sum_ref, 1 - x_abs, 48), 64).astype(bf16)


def tail_grads(line, sels, dp, small):
    _, depth, rows = sels[0].shape
    wq = D // 2
    dp = [v.reshape(8, wq, rows) for v in dp]

    def sel(slot):
        return pl.BlockSpec((1, depth, rows), lambda i, s: (slot, 0, 0))

    outs = [
        sds((2 * wq + 64, wq), bf16), sds((2 * wq, wq), bf16),
        sds((2 * wq, wq), bf16), sds((2 * wq, wq), bf16), sds((64, wq), f32),
    ]
    return line.call(
        tail_grads_body,
        [*sels, *sels, *dp, *dp, *small],
        [sel(1)] * 2
        + [sel(2)] * 2
        + [pl.BlockSpec((1, wq, rows), lambda i, s: (jnp.bitwise_xor(order_a(i), s[S_SEQ]), 0, 0))] * 2
        + [pl.BlockSpec((1, wq, rows), lambda i, s: (4 + jnp.bitwise_xor(order_b(i), s[S_SEQ]), 0, 0))] * 2
        + [whole(small[0].shape)] * 2,
        outs,
        [whole(o.shape) for o in outs],
        grid=(4,),
        scratch=[pltpu.VMEM((depth, 2 * HD), f32)],
        vmem=10,
        hold=9,
        name="tail_grads",
    )


def swap(value, axis, size, bit):
    return lax.ppermute(value, axis, [(i, i ^ bit) for i in range(size)])


def halve_body(scal, keep_ref, recv_ref, send_ref, left_ref):
    half = send_ref.shape[0]
    send_ref[...] = (keep_ref[:half].astype(f32) + recv_ref[:half].astype(f32)).astype(bf16)
    left_ref[...] = (keep_ref[half:].astype(f32) + recv_ref[half:].astype(f32)).astype(left_ref.dtype)


class Halves:
    def __init__(self, line, send, keep, stages):
        self.line, self.keep, self.stages = line, keep, list(stages)
        self.recv = swap(send, *self.stages.pop(0))

    def step(self, hold=0):
        count, rows, wq = self.keep.shape
        shape = (count // 2, rows, wq)
        send, self.keep = self.line.call(
            halve_body, [self.keep, self.recv], [whole(self.keep.shape)] * 2,
            [sds(shape, bf16), sds(shape, self.keep.dtype)], [whole(shape)] * 2,
            vmem=8, hold=hold, name="halve",
        )
        self.recv = swap(send, *self.stages.pop(0))


def final_body(scal, *refs):
    out = refs[-1]
    for j in range(2):
        out[j] = (refs[2 * j][0].astype(f32) + refs[2 * j + 1][0].astype(f32)).astype(bf16)


def final_both(line, pieces):
    shape = (2,) + pieces[0].keep.shape[1:]
    (mine,) = line.call(
        final_body, [v for p in pieces for v in (p.keep, p.recv)], [whole((1,) + shape[1:])] * 4,
        [sds(shape, bf16)], [whole(shape)], vmem=4, name="final",
    )
    return mine.reshape(4 * (D // 8), shape[2])


def tail_one_body(scal, keep_a, recv_a, keep_b, recv_b, small_ref, send_a, send_b, half_ref):
    wq = send_b.shape[0]
    send_a[:wq, :] = (keep_a[wq : 2 * wq].astype(f32) + recv_a[wq : 2 * wq].astype(f32)).astype(bf16)
    half_ref[...] = unpack_rows(small_ref[...] + recv_a[2 * wq :].astype(f32))
    y_abs = jnp.right_shift(scal[S_SEQ], 1)
    send_a[wq:, :] = pack_rows(pick_rows(half_ref, 1 - y_abs, 24), 32).astype(bf16)
    send_b[...] = (keep_b[wq:].astype(f32) + recv_b[wq:].astype(f32)).astype(bf16)


def tail_two_body(scal, keep_a, recv_a, keep_b, recv_b, small_ref, far_a, far_b, own_ref, *refs):
    out_refs, half_ref = refs[:-1], refs[-1]
    wq = far_b.shape[0]
    block = D // 8
    half_ref[...] = unpack_rows(small_ref[...] + recv_a[2 * wq :].astype(f32))
    small = pick_rows(half_ref, jnp.right_shift(scal[S_SEQ], 1), 24) + unpack_rows(far_a[wq:].astype(f32))
    first = keep_a[:wq].astype(f32) + recv_a[:wq].astype(f32) + far_a[:wq].astype(f32)
    second = keep_b[:wq].astype(f32) + recv_b[:wq].astype(f32) + far_b[...].astype(f32)
    for z, ref in enumerate((own_ref, *out_refs)):
        rows = slice(z * block, (z + 1) * block)
        ref[:block, :] = first[rows].astype(ref.dtype)
        ref[block : 2 * block, :] = second[rows].astype(ref.dtype)
        packed = pack_rows(small[z * 24 : (z + 1) * 24], 8)
        packed = jnp.concatenate([packed, jnp.zeros_like(packed)], axis=0)
        ref[2 * block :, :] = packed.astype(ref.dtype)


def tail_final_body(scal, *refs):
    total = refs[0][...]
    for ref in refs[1:-1]:
        total = total + ref[...].astype(f32)
    refs[-1][...] = total.astype(bf16)


def tail_one(line, tail):
    send_a, keep_a, send_b, keep_b, small = tail
    wq = D // 2
    recv_a, recv_b = swap(send_a, "seq", 4, 1), swap(send_b, "seq", 4, 2)
    shapes = [sds((wq + 32, wq), bf16), sds((wq, wq), bf16)]
    halves = [pltpu.VMEM((D // 4, 2 * HD), f32)]

    def first():
        args = [keep_a, recv_a, keep_b, recv_b, small]
        next_a, next_b = line.call(
            tail_one_body, args, [whole(v.shape) for v in args], shapes, [whole(v.shape) for v in shapes],
            scratch=halves, vmem=12, name="tail_one",
        )
        return swap(next_a, "seq", 4, 2), swap(next_b, "seq", 4, 1)

    def second(far_a, far_b):
        args = [keep_a, recv_a, keep_b, recv_b, small, far_a, far_b]
        shape = (2 * (D // 8) + 16, wq)
        own, *sends = line.call(
            tail_two_body, args, [whole(v.shape) for v in args], [sds(shape, f32)] + [sds(shape, bf16)] * 3,
            [whole(shape)] * 4, scratch=halves, vmem=10, hold=5, name="tail_two",
        )
        return [own, *(swap(v, "grp", 8, 2 * (k + 1)) for k, v in enumerate(sends))]

    return first, second


def tail_final(line, args):
    (mine,) = line.call(
        tail_final_body, args, [whole(v.shape) for v in args], [sds(args[0].shape, bf16)],
        [whole(args[0].shape)], vmem=6, hold=5, name="tail_final",
    )
    return mine


def gather_parts(mine):
    return [mine] + [swap(mine, "seq", 4, k) for k in (1, 2, 3)]


def adam_math(grad, master, first, second, average, rate):
    new_first = beta_first * first + (1.0 - beta_first) * grad
    new_second = beta_second * second + (1.0 - beta_second) * grad * grad
    new_master = master - rate * (
        new_first / (jnp.sqrt(new_second) + adam_eps) + decay_rate * master
    )
    new_average = average_keep * average + (1.0 - average_keep) * new_master
    return new_master, new_first, new_second, new_average


def adam_body(n_alias, has_small, scal, *refs):
    parts, refs = refs[:4], refs[4:]
    if has_small:
        vec_in, refs = refs[:4], refs[4:]
    states, refs = refs[:4], refs[4 + n_alias :]
    outs, refs = refs[:6], refs[6:]
    grad_ref = outs[0]
    block = D // 8
    count, wq = parts[0].shape[0] // block, parts[0].shape[1]
    step = pl.program_id(0)
    path, half = jnp.right_shift(step, 1), jnp.bitwise_and(step, 1)
    for k, ref in enumerate(parts):
        quarter = jnp.bitwise_xor(scal[S_SEQ], k)

        @pl.when((jnp.right_shift(quarter, 1) == half) & (step < 2 * count))
        def _(ref=ref, quarter=quarter):
            at = pl.multiple_of(jnp.bitwise_and(quarter, 1) * wq, 128)
            rows = pl.ds(pl.multiple_of(jnp.minimum(path, count - 1) * block, block), block)
            grad_ref[:, pl.ds(at, wq)] = ref[rows, :].astype(f32)

    if has_small:
        vec_outs, small_ref = refs[:6], refs[6]

        @pl.when(step == 2 * count)
        def _():
            for k, ref in enumerate(parts):
                quarter = jnp.bitwise_xor(scal[S_SEQ], k)
                first = jnp.bitwise_and(quarter, 1) * 48 + jnp.right_shift(quarter, 1) * 24
                packed = ref[2 * block :].astype(f32)
                for b in range(3):
                    small_ref[pl.ds(pl.multiple_of(first + 8 * b, 8), 8), :] = packed[:8, b * 128 : (b + 1) * 128]
            small = small_ref[...]
            grad_ref[...] = jnp.zeros_like(grad_ref)
            grad_ref[:, : 2 * HD] = small
            grad = small.T[HD : HD + vec_in[0].shape[0]]
            results = adam_math(grad, *[v[...] for v in vec_in], vector_rate)
            for ref, value in zip(vec_outs, (grad, *results, results[0])):
                ref[...] = value.astype(ref.dtype)

    results = adam_math(grad_ref[...], *[v[...] for v in states], learn_rate)
    for ref, value in zip(outs[1:], (*results, results[0])):
        ref[...] = value.astype(ref.dtype)


def adam_piece(line, parts, states, outs, block_of, vecs=()):
    block = D // 8
    count = parts[0].shape[0] // block
    rows, wide = states[0].shape
    spec = pl.BlockSpec((block, D), lambda i, s: (0, block_of(i)))
    anywhere = pl.BlockSpec(memory_space=pl.ANY)
    n_alias = 0 if outs is None else 6
    shapes = [sds((rows, wide), f32)] * 5 + [sds((rows, wide), bf16)]
    args = [*parts, *vecs, *states]
    n_before = len(args)
    out_specs = [spec] * 6
    if vecs:
        shapes += [sds(vecs[0].shape, f32)] * 5 + [sds(vecs[0].shape, bf16)]
        out_specs += [whole(vecs[0].shape)] * 6
    return line.call(
        partial(adam_body, n_alias, bool(vecs)),
        [*args, *(outs or [])],
        [whole(v.shape) for v in [*parts, *vecs]] + [spec] * 4 + [anywhere] * n_alias,
        shapes,
        out_specs,
        grid=(2 * count + (1 if vecs else 0),),
        scratch=[pltpu.VMEM((rows, 2 * HD), f32)] if vecs else [],
        aliases={1 + n_before + i: i for i in range(n_alias)},
        vmem=16,
        name="adam",
    )


def on_device(
    n_seq,
    n_grp,
    tokens,
    cotangent,
    seq_len,
    weight_mats,
    weight_vecs,
    master_mats,
    master_vecs,
    moment_mats,
    moment_vecs,
    square_mats,
    square_vecs,
    average_mats,
    average_vecs,
):
    rows = tokens.shape[0]
    fast = n_seq == 4 and n_grp == 8
    seq_at = lax.axis_index("seq")
    grp_at = lax.axis_index("grp")
    slot = jnp.arange(16, dtype=jnp.int32)
    seq_length = seq_len[0]
    peer = jnp.bitwise_xor(seq_at, jnp.bitwise_and(slot, 3) + 1)
    same = (peer * rows) // seq_length == (seq_at * rows) // seq_length
    before = (same & (peer < seq_at)).astype(jnp.int32)
    after = (same & (peer > seq_at)).astype(jnp.int32)
    scal = jnp.where(slot < 8, before, after)
    scal = jnp.where(slot == S_SEQ, seq_at if fast else 0, scal)
    scal = jnp.where(slot == S_GRP, grp_at, scal)
    line = Line(scal)

    w_t = weight_mats.T
    states_m = [master_mats, moment_mats, square_mats, average_mats]
    line.stay = {id(v) for v in (w_t, tokens, cotangent)}
    v_t13 = weight_vecs.T
    n_vec = v_t13.shape[0]
    bias_fc = v_t13[9:].reshape(1, FF)
    wide = QUAD * HD
    n_peer = n_seq - 1
    sel_rows = [D // 2, D // 2] if fast else [D]
    n_sel = len(sel_rows)
    sel_shapes = [sds((4, r, rows), bf16) for r in sel_rows]
    sel_low = [whole((2, r, rows)) for r in sel_rows]
    sel_high = [pl.BlockSpec((2, r, rows), lambda i, s: (1, 0, 0)) for r in sel_rows]

    def both(value):
        return [value, swap(value, "grp", 8, 1)] if fast else [value]

    def w_rows(count, at):
        return pl.BlockSpec((count, D), lambda i, s: (at(i, s), 0))

    hedge_spec = pl.BlockSpec((HD, wide), lambda i, s: ((4 * D + 2 * FF) // HD, i))
    vec_whole = whole(v_t13.shape)
    head_spec, feat_spec = along((wide, rows)), along((2 * wide, rows))
    aug_spec, quad_state = along((QUAD * AUG, rows)), along((QUAD * AUG, 2 * HD))
    st_shape = (HEADS * AUG, 2 * HD)
    vec_quad = pl.BlockSpec((n_vec, wide), lambda i, s: (0, i))
    h1, kt, fk, v_t, s_own = line.call(
        keys_body,
        [tokens, w_t, w_t, w_t, v_t13, v_t13],
        [
            whole((rows, D)),
            w_rows(wide, lambda i, s: N_QUAD + i),
            w_rows(wide, lambda i, s: 2 * N_QUAD + i),
            hedge_spec,
            vec_whole,
            vec_quad,
        ],
        [
            sds((rows, D), bf16),
            sds((D, rows), bf16),
            sds((2 * D, rows), bf16),
            sds((D, rows), bf16),
            sds(st_shape, bf16),
        ],
        [whole((rows, D)), head_spec, feat_spec, head_spec, quad_state],
        grid=(N_QUAD,),
        vmem=12,
        name="keys",
    )
    n_peer = n_seq - 1
    states = [swap(s_own, "seq", n_seq, k + 1) for k in range(n_peer)]
    got = line.call(
        partial(queries_body, n_sel),
        [h1, cotangent, w_t, w_t, v_t13],
        [whole((rows, D)), whole((rows, D)), w_rows(wide, lambda i, s: i), hedge_spec, vec_quad],
        sel_shapes + [sds((D, rows), bf16), sds((2 * D, rows), bf16)],
        sel_low + [head_spec, feat_spec],
        grid=(N_QUAD,),
        vmem=12,
        name="queries",
    )
    sels, (qt, fq) = got[:n_sel], got[n_sel:]

    (num,) = line.call(
        local_body,
        [fq, fk, v_t],
        [feat_spec, feat_spec, head_spec],
        [sds((HEADS * AUG, rows), f32)],
        [aug_spec],
        grid=(N_QUAD,),
        vmem=10,
        name="local",
    )
    got = line.call(
        partial(after_body, n_sel, n_peer),
        [*states, num, fq, tokens, w_t, v_t13, *sels],
        [whole(st_shape)] * n_peer
        + [whole(num.shape), whole(fq.shape), whole((rows, D)), w_rows(D, lambda i, s: 3), vec_whole]
        + [pl.BlockSpec(memory_space=pl.ANY)] * n_sel,
        [
            sds((D, rows), f32),
            sds((16, rows), f32),
            sds((rows, D), f32),
            sds((rows, D), bf16),
            sds(st_shape, bf16),
        ]
        + sel_shapes,
        [whole((D, rows)), whole((16, rows)), whole((rows, D)), whole((rows, D)), whole(st_shape)] + sel_high,
        aliases={n_peer + 6 + i: 5 + i for i in range(n_sel)},
        scratch=[pltpu.VMEM((D, rows), bf16)],
        vmem=10,
        name="after",
    )
    o_t, den, resid, h2, s_in = got[:5]
    sels = got[5:]
    if fast:
        sels = [sels[1], swap(sels[0], "grp", 8, 1)]

    n_piece = 2
    piece = FF // n_piece
    acc, acts, db_fc = [], [], []
    for j in range(n_piece):
        if j == 1:
            (sels,) = line.wait(sels)
        pair_of = lambda i, s, j=j: 2 * j + jnp.bitwise_xor(i, jnp.right_shift(s[S_SEQ], 1))
        out_y, out_dh, act, db = line.call(
            partial(mlp_body, j == 0),
            [h2, cotangent, w_t, w_t, bias_fc, *acc],
            [
                whole((rows, D)),
                whole((rows, D)),
                w_rows(D, lambda i, s: 4 + pair_of(i, s)),
                w_rows(D, lambda i, s: 8 + pair_of(i, s)),
                pl.BlockSpec((1, D), lambda i, s: (0, pair_of(i, s))),
            ]
            + [whole((rows, D))] * len(acc),
            [sds((rows, D), f32), sds((rows, D), f32), sds((2, 2, rows, D), bf16), sds((1, piece), f32)],
            [
                whole((rows, D)),
                whole((rows, D)),
                pl.BlockSpec((2, 1, rows, D), lambda i, s: (0, i, 0, 0)),
                pl.BlockSpec((1, D), lambda i, s: (0, jnp.bitwise_xor(i, jnp.right_shift(s[S_SEQ], 1)))),
            ],
            grid=(2,),
            vmem=14,
            name="mlp",
        )
        acc = [out_y, out_dh]
        db_fc.append(db)
        acts.append(both(act))

    if fast:
        first = Halves(
            line, *mlp_grads(line, False, sels, acts[0]),
            [("grp", 8, 2), ("seq", 4, 2), ("grp", 8, 4), ("seq", 4, 1)],
        )
        (acts[1],) = line.wait(acts[1])
    block_output, d_resid, d_attn, rho, ds_own, sums = line.call(
        back_body,
        [*acc, resid, cotangent, w_t, v_t13, o_t, den, fq],
        [whole((rows, D))] * 4
        + [w_rows(D, lambda i, s: 3), vec_whole, whole((D, rows)), whole((16, rows)), whole((2 * D, rows))],
        [
            sds((rows, D), bf16),
            sds((rows, D), f32),
            sds((D, rows), bf16),
            sds((HEADS * AUG, rows), bf16),
            sds(st_shape, bf16),
            sds((4, D), f32),
        ],
        [whole((rows, D))] * 2
        + [whole((D, rows)), whole((HEADS * AUG, rows)), whole(st_shape), whole((4, D))],
        scratch=[pltpu.VMEM((D, rows), bf16)],
        vmem=10,
        out_far=(1, 2, 3),
        name="back",
    )
    back_states = [swap(ds_own, "seq", n_seq, k + 1) for k in range(n_peer)]
    if fast:
        second = mlp_grads(line, True, sels, acts[1], far=range(2, 6))
        (back_states,) = line.wait(back_states)
        second = Halves(
            line, *second, [("seq", 4, 2), ("grp", 8, 2), ("seq", 4, 1), ("grp", 8, 4)]
        )

    grads = [sds((4, D, rows), bf16), sds((D, HD), f32), sds((D, 3), f32)]
    got = []
    for start, count in ((0, N_QUAD),):

        def at(block, axis=0, start=start):
            return pl.BlockSpec(
                tuple(block), lambda i, s: tuple(start + i if d == axis else 0 for d in range(len(block)))
            )

        feat, head = at((2 * wide, rows)), at((wide, rows))
        state = at((QUAD * AUG, 2 * HD))
        args = [*back_states, fq, fk, v_t, rho, s_in, qt, kt, w_t, d_attn]
        got = line.call(
            partial(attend_back_body, n_peer),
            [*args, *got],
            [state] * n_peer
            + [feat, feat, head, at((QUAD * AUG, rows)), state, head, head]
            + [pl.BlockSpec((HD, wide), lambda i, s, start=start: ((4 * D + 2 * FF) // HD, start + i)), head]
            + [pl.BlockSpec(memory_space=pl.ANY)] * len(got),
            grads,
            [at((4, wide, rows), 1), at((wide, HD)), at((wide, 3))],
            grid=(count,),
            aliases={1 + len(args) + k: k for k in range(len(got))},
            hold=1,
            far=(n_peer + 3, n_peer + 8),
            vmem=16,
            name="attend_back",
        )
    dp, dm, db_qkv = got
    dp_both = both(dp)
    db_fc_rows = jnp.concatenate(db_fc, axis=1).reshape(FF // D, D)
    input_grad, *small = line.call(
        partial(input_body, fast),
        [dp, w_t, tokens, d_resid, v_t13, sums, db_fc_rows, db_qkv, dm],
        [
            along((1, D, rows)),
            w_rows(D, lambda i, s: i),
            whole((rows, D)),
            whole((rows, D)),
            vec_whole,
            whole((4, D)),
            whole((FF // D, D)),
            whole((D, 3)),
            whole((D, HD)),
        ],
        [sds((rows, D), bf16)] + [sds((1, r, 2 * HD), f32) for r in sel_rows],
        [whole((rows, D))] + [whole((1, r, 2 * HD)) for r in sel_rows],
        grid=(3,),
        scratch=[pltpu.VMEM((rows, D), f32)],
        vmem=14,
        name="input",
    )
    states_v = [v.T for v in (master_vecs, moment_vecs, square_vecs, average_vecs)]
    if fast:
        theirs, mine = small
        small = [mine, swap(theirs, "grp", 8, 1)]
        first.step(hold=14)
        second.step(hold=60)
        tail = tail_grads(line, sels, dp_both, small)
        tail_first, tail_second = tail_one(line, tail)
        first.step()
        second.step(hold=4)
        far = tail_first()
        first.step()
        second.step()
        mine = final_both(line, [first, second])
        part_x, part_y = swap(mine, "seq", 4, 1), swap(mine, "seq", 4, 2)
        last = tail_second(*far)
        (part_y,) = line.wait(part_y)
        both_mine = [mine, part_x, part_y, swap(part_x, "seq", 4, 2)]
        last_mine = tail_final(line, last)
        outs = adam_piece(
            line, both_mine, states_m, None,
            lambda i: jnp.where(jnp.bitwise_and(i, 2) == 0, 8, 4) + 2 * (i // 4) + jnp.bitwise_and(i, 1),
        )
        last_parts = gather_parts(last_mine)
        outs = adam_piece(
            line, last_parts, states_m, outs, lambda i: jnp.where(i < 4, i, (4 * D + 2 * FF) // D),
            vecs=states_v,
        )
        mats, vecs = outs[:6], [v.T for v in outs[6:]]
    else:
        h1t, obt, h2t = sels[0][1], sels[0][2], sels[0][3]
        joined = [jnp.transpose(a[0], (0, 2, 1, 3)).reshape(2, rows, piece) for a in acts]
        dn = [dot_tn(cotangent, v[0]) for v in joined]
        fc = [dot_nn(h2t, v[1]) for v in joined]
        qkvo = [dot_nt(h1t, dp[k]) for k in range(3)] + [dot_nt(obt, dp[3])]
        small = small[0][0]
        grad = jnp.concatenate([*qkvo, *fc, *dn, small[:, :HD]], axis=1).astype(bf16)
        own = lax.psum_scatter(grad, "grp", scatter_dimension=0, tiled=True)
        own = lax.psum(own, "seq").astype(f32)
        own_v = lax.psum(lax.psum_scatter(small, "grp", scatter_dimension=0, tiled=True), "seq")
        own_v = own_v[:, HD : HD + n_vec]
        results = adam_math(own, *states_m, learn_rate)
        mats = [own, *results, results[0].astype(bf16)]
        results = adam_math(own_v.T, *states_v, vector_rate)
        vecs = [own_v, *[v.T for v in (*results, results[0].astype(bf16))]]
    flat = [x for pair_ in zip(mats, vecs) for x in pair_]
    return (block_output, input_grad, *flat)


def solution(mesh):
    tok = P(("grp", "seq"), None)
    own = P("grp", None)
    in_specs = (tok, tok, P("grp"), P(), P()) + (own,) * 8
    out_specs = (tok, tok) + (own,) * 12
    body = partial(on_device, mesh.shape["seq"], mesh.shape["grp"])
    return jax.shard_map(body, mesh=mesh, in_specs=in_specs, out_specs=out_specs, check_vma=False)
```

```python
from functools import partial

import jax
import jax.numpy as jnp
from jax import lax
from jax.experimental import pallas as pl
from jax.experimental.pallas import tpu as pltpu
from jax.sharding import PartitionSpec as P

D = 768
HEADS = 12
HD = 64
FF = 3072
QUAD = 4
N_QUAD = HEADS // QUAD
AUG = 72

norm_eps = 1e-05
adam_eps = 1e-08
beta_first = 0.5
beta_second = 0.5
learn_rate = 0.01
vector_rate = 0.06
decay_rate = 0.1
average_keep = 0.9

f32 = jnp.float32
bf16 = jnp.bfloat16

S_SEQ, S_GRP, S_MASK, S_BACK = 0, 1, 4, 8

MIB = 1024 * 1024


def dot_nn(a, b):
    return lax.dot_general(a, b, (((1,), (0,)), ((), ())), preferred_element_type=f32)


def dot_nt(a, b):
    return lax.dot_general(a, b, (((1,), (1,)), ((), ())), preferred_element_type=f32)


def dot_tn(a, b):
    return lax.dot_general(a, b, (((0,), (0,)), ((), ())), preferred_element_type=f32)


def whole(shape):
    return pl.BlockSpec(tuple(shape), lambda *_: (0,) * len(shape))


def along(block, axis=0):
    return pl.BlockSpec(tuple(block), lambda i, s: tuple(i if d == axis else 0 for d in range(len(block))))


def sds(shape, dtype):
    return jax.ShapeDtypeStruct(tuple(shape), dtype)


class Line:
    def __init__(self, scal):
        self.scal = scal
        self.stay = set()

    def wait(self, *values):
        self.scal, values = lax.optimization_barrier((self.scal, values))
        return values

    def call(self, body, args, in_specs, outs, out_specs, grid=(1,), scratch=(), vmem=32,
             hold=0, far=(), out_far=(), aliases=None, name=None):
        args = [
            pltpu.with_memory_space_constraint(a, pltpu.HBM) if id(a) in self.stay or k in far else a
            for k, a in enumerate(args)
        ]
        got = pl.pallas_call(
            body,
            out_shape=tuple(pltpu.HBM(o.shape, o.dtype) if k in out_far else o for k, o in enumerate(outs)),
            grid_spec=pltpu.PrefetchScalarGridSpec(
                num_scalar_prefetch=1,
                grid=grid,
                in_specs=list(in_specs),
                out_specs=tuple(out_specs),
                scratch_shapes=list(scratch),
            ),
            compiler_params=pltpu.CompilerParams(
                dimension_semantics=("arbitrary",) * len(grid), vmem_limit_bytes=vmem * MIB
            ),
            cost_estimate=pl.CostEstimate(
                flops=hold * 10**9, bytes_accessed=1024, transcendentals=0
            ),
            input_output_aliases=aliases or {},
            name=name,
        )(self.scal, *args)
        self.scal, got = lax.optimization_barrier((self.scal, got))
        return got


def store_sel(refs, at, values, scal):
    if len(refs) == 1:
        refs[0][at] = values
        return
    block = D // 8
    for j in range(8):
        rel = jnp.bitwise_xor(scal[S_GRP], j)
        place = pl.multiple_of(jnp.right_shift(rel, 1) * block, block)
        odd = jnp.bitwise_and(rel, 1)
        part = values[j * block : (j + 1) * block, :]

        @pl.when(odd == 1)
        def _(part=part, place=place):
            refs[0][at, pl.ds(place, block), :] = part

        @pl.when(odd == 0)
        def _(part=part, place=place):
            refs[1][at, pl.ds(place, block), :] = part


def normalize(values):
    average = jnp.mean(values, axis=1, keepdims=True)
    centered = values - average
    variance = jnp.mean(centered * centered, axis=1, keepdims=True)
    inverse = lax.rsqrt(variance + norm_eps)
    return centered * inverse, inverse


def quad_maps(hedge_t):
    wide = QUAD * HD
    row = lax.broadcasted_iota(jnp.int32, (wide, HD), 0)
    col = lax.broadcasted_iota(jnp.int32, (wide, HD), 1)
    spread = (jnp.bitwise_and(row, HD - 1) == col).astype(bf16)
    tiled = dot_nn(spread, hedge_t)
    big_r = lax.broadcasted_iota(jnp.int32, (wide, wide), 0)
    big_c = lax.broadcasted_iota(jnp.int32, (wide, wide), 1)
    same = jnp.right_shift(big_r, 6) == jnp.right_shift(big_c, 6)
    return jnp.where(same, tiled, 0.0)


def ones_rows(count):
    return (lax.broadcasted_iota(jnp.int32, (AUG - HD, count), 0) == 0).astype(f32).astype(bf16)


def rows_up(values):
    return jnp.concatenate([values, jnp.zeros((3, values.shape[1]), f32)], axis=0).T


def features(pt, maps):
    high = pt.astype(bf16)
    rest = (pt - high.astype(f32)).astype(bf16)
    scores = dot_nn(jnp.concatenate([maps, maps], axis=1), jnp.concatenate([high, rest], axis=0))
    heads = []
    for h in range(QUAD):
        s = scores[h * HD : (h + 1) * HD, :]
        top = jnp.max(s, axis=0, keepdims=True)
        bottom = jnp.min(s, axis=0, keepdims=True)
        pos = jnp.exp(s - top)
        neg = jnp.exp(bottom - s)
        pos = pos * (1.0 / jnp.sum(pos, axis=0, keepdims=True))
        neg = neg * (1.0 / jnp.sum(neg, axis=0, keepdims=True))
        heads.append(jnp.concatenate([pos, neg], axis=0).astype(bf16))
    return high, heads


def keys_body(scal, x_ref, wk_ref, wv_ref, hedge_ref, vt_ref, vq_ref, h1_ref, kt_ref, fk_ref, vt_out, s_ref):
    rows = x_ref.shape[0]

    @pl.when(pl.program_id(0) == 0)
    def _():
        normed, _ = normalize(x_ref[...].astype(f32))
        vt = vt_ref[...].astype(f32)
        h1_ref[...] = (normed * vt[0:1] + vt[1:2]).astype(bf16)

    h1 = h1_ref[...]
    bias = rows_up(vq_ref[...].astype(f32))
    v_t = (dot_nt(wv_ref[...], h1) + bias[:, 8:9]).astype(bf16)
    vt_out[...] = v_t
    pt = dot_nt(wk_ref[...], h1) + bias[:, 7:8]
    kt_ref[...], heads = features(pt, quad_maps(hedge_ref[...]).astype(bf16))
    extra = ones_rows(rows)
    for h, both in enumerate(heads):
        fk_ref[h * 2 * HD : (h + 1) * 2 * HD, :] = both
        va = jnp.concatenate([v_t[h * HD : (h + 1) * HD, :], extra], axis=0)
        s_ref[h * AUG : (h + 1) * AUG, :] = dot_nt(va, both).astype(bf16)


def queries_body(n_sel, scal, h1_ref, g_ref, wq_ref, hedge_ref, vq_ref, *refs):
    sel = refs[:n_sel]
    qt_ref, fq_ref = refs[n_sel:]
    h1 = h1_ref[...]

    @pl.when(pl.program_id(0) == 0)
    def _():
        store_sel(sel, 0, g_ref[...].T, scal)
        store_sel(sel, 1, h1.T, scal)

    bias = rows_up(vq_ref[...].astype(f32))
    pt = dot_nt(wq_ref[...], h1) + bias[:, 6:7]
    qt_ref[...], heads = features(pt, quad_maps(hedge_ref[...]).astype(bf16))
    for h, both in enumerate(heads):
        fq_ref[h * 2 * HD : (h + 1) * 2 * HD, :] = both


def tri_mask(half):
    return lax.broadcasted_iota(jnp.int32, (half, half), 0) <= lax.broadcasted_iota(
        jnp.int32, (half, half), 1
    )


def masked_pair(left0, left1, right, keep):
    half = right.shape[1] // 2
    full = dot_tn(left0, right)
    low = dot_tn(left1, right[:, half:])
    diag0 = jnp.where(keep, full[:, :half], 0.0).astype(bf16)
    above = full[:, half:].astype(bf16)
    diag1 = jnp.where(keep, low, 0.0).astype(bf16)
    return diag0, above, diag1


def local_body(scal, fq_ref, fk_ref, vt_ref, num_ref):
    rows = fq_ref.shape[1]
    half = rows // 2
    keep = tri_mask(half)
    extra = ones_rows(rows)
    for h in range(QUAD):
        fq = fq_ref[h * 2 * HD : (h + 1) * 2 * HD, :]
        fk = fk_ref[h * 2 * HD : (h + 1) * 2 * HD, :]
        va = jnp.concatenate([vt_ref[h * HD : (h + 1) * HD, :], extra], axis=0)
        a00, a01, a11 = masked_pair(fk[:, :half], fk[:, half:], fq, keep)
        num_ref[h * AUG : (h + 1) * AUG, :half] = dot_nn(va[:, :half], a00)
        num_ref[h * AUG : (h + 1) * AUG, half:] = dot_nn(va[:, :half], a01) + dot_nn(va[:, half:], a11)


def weighted_state(scal, slot, parts):
    total = None
    for k, part in enumerate(parts):
        term = scal[slot + k].astype(f32) * part.astype(f32)
        total = term if total is None else total + term
    return total.astype(bf16)


def after_body(n_sel, n_parts, scal, *refs):
    parts = refs[:n_parts]
    num_ref, fq_ref, x_ref, w_ref, vt_ref = refs[n_parts : n_parts + 5]
    o_ref, den_ref, r_ref, h2_ref, sin_ref = refs[n_parts + 5 + n_sel : n_parts + 10 + n_sel]
    sel = refs[-1 - n_sel : -1]
    ob_ref = refs[-1]
    vt = vt_ref[...].astype(f32)
    state = weighted_state(scal, S_MASK, [p[...] for p in parts])
    sin_ref[...] = state
    for h in range(HEADS):
        num = num_ref[h * AUG : (h + 1) * AUG, :] + dot_nn(
            state[h * AUG : (h + 1) * AUG, :], fq_ref[h * 2 * HD : (h + 1) * 2 * HD, :]
        )
        den = num[HD : HD + 1, :]
        out = num[:HD, :] * (1.0 / den)
        o_ref[h * HD : (h + 1) * HD, :] = out
        den_ref[h : h + 1, :] = den
        ob_ref[h * HD : (h + 1) * HD, :] = out.astype(bf16)
    obt = ob_ref[...]
    store_sel(sel, 0, obt, scal)
    r = x_ref[...].astype(f32) + dot_nt(obt.T, w_ref[...]) + vt[4:5]
    r_ref[...] = r
    normed, _ = normalize(r)
    h2 = (normed * vt[2:3] + vt[3:4]).astype(bf16)
    h2_ref[...] = h2
    store_sel(sel, 1, h2.T, scal)


gelu_c = 0.7978845608028654
gelu_k = 0.044715


def mlp_body(first, scal, h2_ref, g_ref, wf_ref, wd_ref, bias_ref, *refs):
    if first:
        out_ref, dh_ref, act_ref, db_ref = refs
    else:
        out_in, dh_in, out_ref, dh_ref, act_ref, db_ref = refs
    u = dot_nt(h2_ref[...], wf_ref[...]) + bias_ref[...].astype(f32)
    de = dot_nt(g_ref[...], wd_ref[...])
    uu = u * u
    t = jnp.tanh(gelu_c * u * (1.0 + gelu_k * uu))
    half_t = 0.5 * (1.0 + t)
    e = (u * half_t).astype(bf16)
    slope = half_t + 0.5 * u * (1.0 - t * t) * (gelu_c * (1.0 + 3.0 * gelu_k * uu))
    du = (de * slope).astype(bf16)
    act_ref[0, 0] = e
    act_ref[1, 0] = du
    db_ref[...] = jnp.sum(du.astype(f32), axis=0, keepdims=True)
    add_out = dot_nn(e, wd_ref[...])
    add_dh = dot_nn(du, wf_ref[...])
    step = pl.program_id(0)

    @pl.when(step == 0)
    def _():
        if first:
            out_ref[...] = add_out
            dh_ref[...] = add_dh
        else:
            out_ref[...] = out_in[...] + add_out
            dh_ref[...] = dh_in[...] + add_dh

    @pl.when(step > 0)
    def _():
        out_ref[...] += add_out
        dh_ref[...] += add_dh


def back_body(scal, out_ref, dh_ref, r_ref, g_ref, w_ref, vt_ref, o_ref, den_ref, fq_ref, y_ref, dr_ref,
              da_ref, rho_ref, ds_ref, sums_ref, do_ref):
    vt = vt_ref[...].astype(f32)
    r = r_ref[...]
    y_ref[...] = (r + out_ref[...] + vt[5:6]).astype(bf16)
    grad_out = g_ref[...].astype(f32)
    normed, inverse = normalize(r)
    up = dh_ref[...]
    dn = up * vt[2:3]
    dr = grad_out + inverse * (
        dn - jnp.mean(dn, axis=1, keepdims=True) - normed * jnp.mean(dn * normed, axis=1, keepdims=True)
    )
    dr_ref[...] = dr
    da = dr.astype(bf16)
    da_ref[...] = da.T
    sums_ref[...] = jnp.concatenate(
        [
            jnp.sum(up * normed, axis=0, keepdims=True),
            jnp.sum(up, axis=0, keepdims=True),
            jnp.sum(da.astype(f32), axis=0, keepdims=True),
            jnp.sum(grad_out, axis=0, keepdims=True),
        ],
        axis=0,
    )
    do_ref[...] = dot_nn(da, w_ref[...]).astype(bf16).T
    rows = r.shape[0]
    zero_row = lax.broadcasted_iota(jnp.int32, (AUG - HD, rows), 0) == 0
    for h in range(HEADS):
        dout = do_ref[h * HD : (h + 1) * HD, :].astype(f32)
        inv = 1.0 / den_ref[h : h + 1, :]
        rho = (dout * inv).astype(bf16)
        c = -jnp.sum(dout * o_ref[h * HD : (h + 1) * HD, :], axis=0, keepdims=True) * inv
        extra = jnp.where(zero_row, jnp.broadcast_to(c, (AUG - HD, rows)), 0.0).astype(bf16)
        ra = jnp.concatenate([rho, extra], axis=0)
        rho_ref[h * AUG : (h + 1) * AUG, :] = ra
        ds_ref[h * AUG : (h + 1) * AUG, :] = dot_nt(ra, fq_ref[h * 2 * HD : (h + 1) * 2 * HD, :]).astype(bf16)


def feature_back(feat, upstream):
    pos, neg = feat[:HD].astype(f32), feat[HD:].astype(f32)
    up_pos, up_neg = upstream[:HD], upstream[HD:]
    return pos * (up_pos - jnp.sum(pos * up_pos, axis=0, keepdims=True)) - neg * (
        up_neg - jnp.sum(neg * up_neg, axis=0, keepdims=True)
    )


def attend_back_body(n_parts, scal, *refs):
    parts = refs[:n_parts]
    (fq_ref, fk_ref, vt_ref, rho_ref, sin_ref, qt_ref, kt_ref, hedge_ref, da_ref) = refs[n_parts : n_parts + 9]
    dp_ref, dm_ref, db_ref = refs[-3:]
    dp_ref[3] = da_ref[...]
    rows = fq_ref.shape[1]
    half = rows // 2
    keep = tri_mask(half)
    extra = ones_rows(rows)
    back_state = weighted_state(scal, S_BACK, [p[...] for p in parts])
    ds_q, ds_k = [], []
    for h in range(QUAD):
        fq = fq_ref[h * 2 * HD : (h + 1) * 2 * HD, :]
        fk = fk_ref[h * 2 * HD : (h + 1) * 2 * HD, :]
        head = slice(h * HD, (h + 1) * HD)
        aug = slice(h * AUG, (h + 1) * AUG)
        va = jnp.concatenate([vt_ref[head, :], extra], axis=0)
        ra = rho_ref[aug, :]
        state, back = sin_ref[aug, :], back_state[aug, :]
        a00, a01, a11 = masked_pair(fk[:, :half], fk[:, half:], fq, keep)
        g00, g01, g11 = masked_pair(va[:, :half], va[:, half:], ra, keep)
        far = dot_tn(state, ra)
        left = far[:, :half] + dot_nn(fk[:, :half], g00)
        right = far[:, half:] + dot_nn(fk[:, :half], g01) + dot_nn(fk[:, half:], g11)
        dfq = jnp.concatenate([left, right], axis=1)
        far_k = dot_tn(back, va)
        left = far_k[:, :half] + dot_nt(fq[:, :half], g00) + dot_nt(fq[:, half:], g01)
        right = far_k[:, half:] + dot_nt(fq[:, half:], g11)
        dfk = jnp.concatenate([left, right], axis=1)
        far_v = dot_nn(back, fk)[:HD]
        rv = ra[:HD]
        left = far_v[:, :half] + dot_nt(rv[:, :half], a00) + dot_nt(rv[:, half:], a01)
        right = far_v[:, half:] + dot_nt(rv[:, half:], a11)
        dp_ref[2, head, :] = jnp.concatenate([left, right], axis=1).astype(bf16)
        dsq = feature_back(fq, dfq).astype(bf16)
        dsk = feature_back(fk, dfk).astype(bf16)
        ds_q.append(dsq)
        ds_k.append(dsk)
    maps = quad_maps(hedge_ref[...]).T.astype(bf16)
    ds_q, ds_k = jnp.concatenate(ds_q, axis=0), jnp.concatenate(ds_k, axis=0)
    dm = dot_nt(qt_ref[...], ds_q) + dot_nt(kt_ref[...], ds_k)
    for h in range(QUAD):
        head = slice(h * HD, (h + 1) * HD)
        dm_ref[head, :] = dm[head, head]
    dq = dot_nn(maps, ds_q).astype(bf16)
    dk = dot_nn(maps, ds_k).astype(bf16)
    dp_ref[0] = dq
    dp_ref[1] = dk
    db_ref[...] = jnp.concatenate(
        [jnp.sum(v.astype(f32), axis=1, keepdims=True) for v in (dq, dk, dp_ref[2])], axis=1
    )


def input_body(fast, scal, dp_ref, w_ref, x_ref, dr_ref, vt_ref, sums_ref, dbfc_ref, db_ref, dm_ref, *refs):
    gin_ref, *small_refs, acc_ref = refs
    step = pl.program_id(0)
    part = dot_tn(dp_ref[0], w_ref[...])

    @pl.when(step == 0)
    def _():
        acc_ref[...] = part

    @pl.when(step == 1)
    def _():
        acc_ref[...] += part

    @pl.when(step == 2)
    def _():
        vt = vt_ref[...].astype(f32)
        up = acc_ref[...] + part
        normed, inverse = normalize(x_ref[...].astype(f32))
        dn = up * vt[0:1]
        gin = dr_ref[...] + inverse * (
            dn - jnp.mean(dn, axis=1, keepdims=True) - normed * jnp.mean(dn * normed, axis=1, keepdims=True)
        )
        gin_ref[...] = gin.astype(bf16)
        rows16 = jnp.concatenate(
            [
                jnp.sum(up * normed, axis=0, keepdims=True),
                jnp.sum(up, axis=0, keepdims=True),
                sums_ref[...],
                jnp.zeros((3, D), f32),
                dbfc_ref[...],
                jnp.zeros((3, D), f32),
            ],
            axis=0,
        )
        cols = rows16.T
        lane = lax.broadcasted_iota(jnp.int32, (D, HD), 1)
        tail = jnp.concatenate([cols, jnp.zeros((D, HD - 16), f32)], axis=1)
        for k in range(3):
            tail = jnp.where(lane == 6 + k, db_ref[:, k : k + 1], tail)
        small = jnp.concatenate([dm_ref[...], tail], axis=1)
        store_sel(small_refs, 0, small, scal)


def mlp_grads_body(by_y, scal, *refs):
    sels, acts_a, acts_b, sels_h = refs[0:2], refs[2:4], refs[4:6], refs[6:8]
    send, keep = refs[8:]
    block = D // 8
    wq = send.shape[2]
    y_last = 1 - pl.program_id(0)

    def total(lefts, rights):
        return (dot_nn(lefts[0][0], rights[0][0, 0]) + dot_nn(lefts[1][0], rights[1][0, 0])).astype(bf16)

    for path, value in enumerate((total(sels, acts_a), total(sels_h, acts_b))):
        rows = slice(path * block, (path + 1) * block)
        for half in range(2):
            x_last = 1 - jnp.bitwise_xor(half, jnp.bitwise_and(scal[S_SEQ], 1))
            cols = slice(half * wq, (half + 1) * wq)

            def part(z, value=value, cols=cols):
                return value[z * block : (z + 1) * block, cols]

            if by_y:
                for bit, ref in ((0, send), (1, keep)):

                    @pl.when(y_last == bit)
                    def _(ref=ref, part=part, rows=rows, x_last=x_last):
                        for at, z in enumerate((3, 1, 2, 0)):
                            ref[4 * (at // 2) + 2 * x_last + at % 2, rows, :] = part(z)
            else:
                base = 4 * y_last + 1 * x_last
                for ref, order in ((send, (3, 1)), (keep, (2, 0))):
                    for at, z in enumerate(order):
                        ref[2 * at + base, rows, :] = part(z)


def mlp_grads(line, by_y, sels, acts, far=(), out_far=()):
    _, depth, rows = sels[0].shape
    half = sds((8, 2 * (D // 8), D // 2), bf16)

    def act(path):
        return pl.BlockSpec((1, 1, rows, D), lambda i, s: (path, i, 0, 0))

    def sel(slot):
        return pl.BlockSpec((1, depth, rows), lambda i, s: (slot, 0, 0))

    return line.call(
        partial(mlp_grads_body, by_y),
        [*sels, *acts, *acts, *sels],
        [sel(0)] * 2 + [act(0)] * 2 + [act(1)] * 2 + [sel(3)] * 2,
        [half] * 2,
        [whole(half.shape)] * 2,
        grid=(2,),
        vmem=24,
        far=far,
        out_far=out_far,
        name="mlp_grads",
    )


def pack_rows(values, count):
    return jnp.concatenate([values[b * count : (b + 1) * count] for b in range(3)], axis=1)


def unpack_rows(values):
    return jnp.concatenate([values[:, b * 128 : (b + 1) * 128] for b in range(3)], axis=0)


def order_a(i):
    return jnp.where(i < 2, 2 * i + 1, 2 * i - 4)


def order_b(i):
    return jnp.where(i < 2, i + 2, i - 2)


def pick_rows(ref, half, count):
    rows = [ref[pl.ds(pl.multiple_of(z * 2 * count + half * count, 8), count), :] for z in range(4)]
    return jnp.concatenate(rows, axis=0)


def tail_grads_body(scal, *refs):
    h1, ob, dqk, dvo = refs[0:2], refs[2:4], refs[4:6], refs[6:8]
    small_own, small_other, send_a, keep_a, send_b, keep_b, small_ref, sum_ref = refs[8:]
    step = pl.program_id(0)
    wq = send_a.shape[1]
    qb = jnp.bitwise_xor(order_b(step), scal[S_SEQ])
    at = pl.multiple_of(jnp.bitwise_and(step, 1) * wq, wq)

    def total(lefts, rights):
        return (dot_nt(lefts[0][0], rights[0][0]) + dot_nt(lefts[1][0], rights[1][0])).astype(bf16)

    def put(send, keep, value):
        @pl.when(step < 2)
        def _():
            send[pl.ds(at, wq), :] = value

        @pl.when(step >= 2)
        def _():
            keep[pl.ds(at, wq), :] = value

    put(send_a, keep_a, total(h1, dqk))

    @pl.when(qb < 2)
    def _():
        put(send_b, keep_b, total(h1, dvo))

    @pl.when(qb >= 2)
    def _():
        put(send_b, keep_b, total(ob, dvo))

    @pl.when(step == 0)
    def _():
        sum_ref[...] = small_own[0] + small_other[0]
        x_abs = jnp.bitwise_and(scal[S_SEQ], 1)
        small_ref[...] = pack_rows(pick_rows(sum_ref, x_abs, 48), 64)
        send_a[2 * wq :, :] = pack_rows(pick_rows(sum_ref, 1 - x_abs, 48), 64).astype(bf16)


def tail_grads(line, sels, dp, small):
    _, depth, rows = sels[0].shape
    wq = D // 2
    dp = [v.reshape(8, wq, rows) for v in dp]

    def sel(slot):
        return pl.BlockSpec((1, depth, rows), lambda i, s: (slot, 0, 0))

    outs = [
        sds((2 * wq + 64, wq), bf16), sds((2 * wq, wq), bf16),
        sds((2 * wq, wq), bf16), sds((2 * wq, wq), bf16), sds((64, wq), f32),
    ]
    return line.call(
        tail_grads_body,
        [*sels, *sels, *dp, *dp, *small],
        [sel(1)] * 2
        + [sel(2)] * 2
        + [pl.BlockSpec((1, wq, rows), lambda i, s: (jnp.bitwise_xor(order_a(i), s[S_SEQ]), 0, 0))] * 2
        + [pl.BlockSpec((1, wq, rows), lambda i, s: (4 + jnp.bitwise_xor(order_b(i), s[S_SEQ]), 0, 0))] * 2
        + [whole(small[0].shape)] * 2,
        outs,
        [whole(o.shape) for o in outs],
        grid=(4,),
        scratch=[pltpu.VMEM((depth, 2 * HD), f32)],
        vmem=10,
        hold=9,
        name="tail_grads",
    )


def swap(value, axis, size, bit):
    return lax.ppermute(value, axis, [(i, i ^ bit) for i in range(size)])


def halve_body(scal, keep_ref, recv_ref, send_ref, left_ref):
    half = send_ref.shape[0]
    send_ref[...] = (keep_ref[:half].astype(f32) + recv_ref[:half].astype(f32)).astype(bf16)
    left_ref[...] = (keep_ref[half:].astype(f32) + recv_ref[half:].astype(f32)).astype(left_ref.dtype)


class Halves:
    def __init__(self, line, send, keep, stages):
        self.line, self.keep, self.stages = line, keep, list(stages)
        self.recv = swap(send, *self.stages.pop(0))

    def step(self, hold=0):
        count, rows, wq = self.keep.shape
        shape = (count // 2, rows, wq)
        send, self.keep = self.line.call(
            halve_body, [self.keep, self.recv], [whole(self.keep.shape)] * 2,
            [sds(shape, bf16), sds(shape, self.keep.dtype)], [whole(shape)] * 2,
            vmem=8, hold=hold, name="halve",
        )
        self.recv = swap(send, *self.stages.pop(0))


def final_body(scal, *refs):
    out = refs[-1]
    for j in range(2):
        out[j] = (refs[2 * j][0].astype(f32) + refs[2 * j + 1][0].astype(f32)).astype(bf16)


def final_both(line, pieces):
    shape = (2,) + pieces[0].keep.shape[1:]
    (mine,) = line.call(
        final_body, [v for p in pieces for v in (p.keep, p.recv)], [whole((1,) + shape[1:])] * 4,
        [sds(shape, bf16)], [whole(shape)], vmem=4, name="final",
    )
    return mine.reshape(4 * (D // 8), shape[2])


def tail_one_body(scal, keep_a, recv_a, keep_b, recv_b, small_ref, send_a, send_b, half_ref):
    wq = send_b.shape[0]
    send_a[:wq, :] = (keep_a[wq : 2 * wq].astype(f32) + recv_a[wq : 2 * wq].astype(f32)).astype(bf16)
    half_ref[...] = unpack_rows(small_ref[...] + recv_a[2 * wq :].astype(f32))
    y_abs = jnp.right_shift(scal[S_SEQ], 1)
    send_a[wq:, :] = pack_rows(pick_rows(half_ref, 1 - y_abs, 24), 32).astype(bf16)
    send_b[...] = (keep_b[wq:].astype(f32) + recv_b[wq:].astype(f32)).astype(bf16)


def tail_two_body(scal, keep_a, recv_a, keep_b, recv_b, small_ref, far_a, far_b, own_ref, *refs):
    out_refs, half_ref = refs[:-1], refs[-1]
    wq = far_b.shape[0]
    block = D // 8
    half_ref[...] = unpack_rows(small_ref[...] + recv_a[2 * wq :].astype(f32))
    small = pick_rows(half_ref, jnp.right_shift(scal[S_SEQ], 1), 24) + unpack_rows(far_a[wq:].astype(f32))
    first = keep_a[:wq].astype(f32) + recv_a[:wq].astype(f32) + far_a[:wq].astype(f32)
    second = keep_b[:wq].astype(f32) + recv_b[:wq].astype(f32) + far_b[...].astype(f32)
    for z, ref in enumerate((own_ref, *out_refs)):
        rows = slice(z * block, (z + 1) * block)
        ref[:block, :] = first[rows].astype(ref.dtype)
        ref[block : 2 * block, :] = second[rows].astype(ref.dtype)
        packed = pack_rows(small[z * 24 : (z + 1) * 24], 8)
        packed = jnp.concatenate([packed, jnp.zeros_like(packed)], axis=0)
        ref[2 * block :, :] = packed.astype(ref.dtype)


def tail_final_body(scal, *refs):
    total = refs[0][...]
    for ref in refs[1:-1]:
        total = total + ref[...].astype(f32)
    refs[-1][...] = total.astype(bf16)


def tail_one(line, tail):
    send_a, keep_a, send_b, keep_b, small = tail
    wq = D // 2
    recv_a, recv_b = swap(send_a, "seq", 4, 1), swap(send_b, "seq", 4, 2)
    shapes = [sds((wq + 32, wq), bf16), sds((wq, wq), bf16)]
    halves = [pltpu.VMEM((D // 4, 2 * HD), f32)]

    def first():
        args = [keep_a, recv_a, keep_b, recv_b, small]
        next_a, next_b = line.call(
            tail_one_body, args, [whole(v.shape) for v in args], shapes, [whole(v.shape) for v in shapes],
            scratch=halves, vmem=12, name="tail_one",
        )
        return swap(next_a, "seq", 4, 2), swap(next_b, "seq", 4, 1)

    def second(far_a, far_b):
        args = [keep_a, recv_a, keep_b, recv_b, small, far_a, far_b]
        shape = (2 * (D // 8) + 16, wq)
        own, *sends = line.call(
            tail_two_body, args, [whole(v.shape) for v in args], [sds(shape, f32)] + [sds(shape, bf16)] * 3,
            [whole(shape)] * 4, scratch=halves, vmem=10, hold=5, name="tail_two",
        )
        return [own, *(swap(v, "grp", 8, 2 * (k + 1)) for k, v in enumerate(sends))]

    return first, second


def tail_final(line, args):
    (mine,) = line.call(
        tail_final_body, args, [whole(v.shape) for v in args], [sds(args[0].shape, bf16)],
        [whole(args[0].shape)], vmem=6, hold=5, name="tail_final",
    )
    return mine


def gather_parts(mine):
    return [mine] + [swap(mine, "seq", 4, k) for k in (1, 2, 3)]


def adam_math(grad, master, first, second, average, rate):
    new_first = beta_first * first + (1.0 - beta_first) * grad
    new_second = beta_second * second + (1.0 - beta_second) * grad * grad
    new_master = master - rate * (
        new_first / (jnp.sqrt(new_second) + adam_eps) + decay_rate * master
    )
    new_average = average_keep * average + (1.0 - average_keep) * new_master
    return new_master, new_first, new_second, new_average


def adam_body(n_alias, has_small, scal, *refs):
    parts, refs = refs[:4], refs[4:]
    if has_small:
        vec_in, refs = refs[:4], refs[4:]
    states, refs = refs[:4], refs[4 + n_alias :]
    outs, refs = refs[:6], refs[6:]
    grad_ref = outs[0]
    block = D // 8
    count, wq = parts[0].shape[0] // block, parts[0].shape[1]
    step = pl.program_id(0)
    for k, ref in enumerate(parts):
        quarter = jnp.bitwise_xor(scal[S_SEQ], k)

        @pl.when(step < count)
        def _(ref=ref, quarter=quarter):
            at = pl.multiple_of(quarter * wq, 128)
            rows = pl.ds(pl.multiple_of(jnp.minimum(step, count - 1) * block, block), block)
            grad_ref[:, pl.ds(at, wq)] = ref[rows, :].astype(f32)

    if has_small:
        vec_outs, small_ref = refs[:6], refs[6]

        @pl.when(step == count)
        def _():
            for k, ref in enumerate(parts):
                quarter = jnp.bitwise_xor(scal[S_SEQ], k)
                first = jnp.bitwise_and(quarter, 1) * 48 + jnp.right_shift(quarter, 1) * 24
                packed = ref[2 * block :].astype(f32)
                for b in range(3):
                    small_ref[pl.ds(pl.multiple_of(first + 8 * b, 8), 8), :] = packed[:8, b * 128 : (b + 1) * 128]
            small = small_ref[...]
            grad_ref[...] = jnp.zeros_like(grad_ref)
            grad_ref[:, : 2 * HD] = small
            grad = small.T[HD : HD + vec_in[0].shape[0]]
            results = adam_math(grad, *[v[...] for v in vec_in], vector_rate)
            for ref, value in zip(vec_outs, (grad, *results, results[0])):
                ref[...] = value.astype(ref.dtype)

    results = adam_math(grad_ref[...], *[v[...] for v in states], learn_rate)
    for ref, value in zip(outs[1:], (*results, results[0])):
        ref[...] = value.astype(ref.dtype)


def adam_piece(line, parts, states, outs, block_of, vecs=()):
    block = D // 8
    count = parts[0].shape[0] // block
    rows, wide = states[0].shape
    spec = pl.BlockSpec((block, 2 * D), lambda i, s: (0, block_of(i)))
    anywhere = pl.BlockSpec(memory_space=pl.ANY)
    n_alias = 0 if outs is None else 6
    shapes = [sds((rows, wide), f32)] * 5 + [sds((rows, wide), bf16)]
    args = [*parts, *vecs, *states]
    n_before = len(args)
    out_specs = [spec] * 6
    if vecs:
        shapes += [sds(vecs[0].shape, f32)] * 5 + [sds(vecs[0].shape, bf16)]
        out_specs += [whole(vecs[0].shape)] * 6
    return line.call(
        partial(adam_body, n_alias, bool(vecs)),
        [*args, *(outs or [])],
        [whole(v.shape) for v in [*parts, *vecs]] + [spec] * 4 + [anywhere] * n_alias,
        shapes,
        out_specs,
        grid=(count + (1 if vecs else 0),),
        scratch=[pltpu.VMEM((rows, 2 * HD), f32)] if vecs else [],
        aliases={1 + n_before + i: i for i in range(n_alias)},
        vmem=24,
        name="adam",
    )


def on_device(
    n_seq,
    n_grp,
    tokens,
    cotangent,
    seq_len,
    weight_mats,
    weight_vecs,
    master_mats,
    master_vecs,
    moment_mats,
    moment_vecs,
    square_mats,
    square_vecs,
    average_mats,
    average_vecs,
):
    rows = tokens.shape[0]
    fast = n_seq == 4 and n_grp == 8
    seq_at = lax.axis_index("seq")
    grp_at = lax.axis_index("grp")
    slot = jnp.arange(16, dtype=jnp.int32)
    seq_length = seq_len[0]
    peer = jnp.bitwise_xor(seq_at, jnp.bitwise_and(slot, 3) + 1)
    same = (peer * rows) // seq_length == (seq_at * rows) // seq_length
    before = (same & (peer < seq_at)).astype(jnp.int32)
    after = (same & (peer > seq_at)).astype(jnp.int32)
    scal = jnp.where(slot < 8, before, after)
    scal = jnp.where(slot == S_SEQ, seq_at if fast else 0, scal)
    scal = jnp.where(slot == S_GRP, grp_at, scal)
    line = Line(scal)

    w_t = weight_mats.T
    states_m = [master_mats, moment_mats, square_mats, average_mats]
    line.stay = {id(v) for v in (w_t, tokens, cotangent)}
    v_t13 = weight_vecs.T
    n_vec = v_t13.shape[0]
    bias_fc = v_t13[9:].reshape(1, FF)
    wide = QUAD * HD
    n_peer = n_seq - 1
    sel_rows = [D // 2, D // 2] if fast else [D]
    n_sel = len(sel_rows)
    sel_shapes = [sds((4, r, rows), bf16) for r in sel_rows]
    sel_low = [whole((2, r, rows)) for r in sel_rows]
    sel_high = [pl.BlockSpec((2, r, rows), lambda i, s: (1, 0, 0)) for r in sel_rows]

    def both(value):
        return [value, swap(value, "grp", 8, 1)] if fast else [value]

    def w_rows(count, at):
        return pl.BlockSpec((count, D), lambda i, s: (at(i, s), 0))

    hedge_spec = pl.BlockSpec((HD, wide), lambda i, s: ((4 * D + 2 * FF) // HD, i))
    vec_whole = whole(v_t13.shape)
    head_spec, feat_spec = along((wide, rows)), along((2 * wide, rows))
    aug_spec, quad_state = along((QUAD * AUG, rows)), along((QUAD * AUG, 2 * HD))
    st_shape = (HEADS * AUG, 2 * HD)
    vec_quad = pl.BlockSpec((n_vec, wide), lambda i, s: (0, i))
    h1, kt, fk, v_t, s_own = line.call(
        keys_body,
        [tokens, w_t, w_t, w_t, v_t13, v_t13],
        [
            whole((rows, D)),
            w_rows(wide, lambda i, s: N_QUAD + i),
            w_rows(wide, lambda i, s: 2 * N_QUAD + i),
            hedge_spec,
            vec_whole,
            vec_quad,
        ],
        [
            sds((rows, D), bf16),
            sds((D, rows), bf16),
            sds((2 * D, rows), bf16),
            sds((D, rows), bf16),
            sds(st_shape, bf16),
        ],
        [whole((rows, D)), head_spec, feat_spec, head_spec, quad_state],
        grid=(N_QUAD,),
        vmem=12,
        name="keys",
    )
    n_peer = n_seq - 1
    states = [swap(s_own, "seq", n_seq, k + 1) for k in range(n_peer)]
    got = line.call(
        partial(queries_body, n_sel),
        [h1, cotangent, w_t, w_t, v_t13],
        [whole((rows, D)), whole((rows, D)), w_rows(wide, lambda i, s: i), hedge_spec, vec_quad],
        sel_shapes + [sds((D, rows), bf16), sds((2 * D, rows), bf16)],
        sel_low + [head_spec, feat_spec],
        grid=(N_QUAD,),
        vmem=12,
        name="queries",
    )
    sels, (qt, fq) = got[:n_sel], got[n_sel:]

    (num,) = line.call(
        local_body,
        [fq, fk, v_t],
        [feat_spec, feat_spec, head_spec],
        [sds((HEADS * AUG, rows), f32)],
        [aug_spec],
        grid=(N_QUAD,),
        vmem=10,
        name="local",
    )
    got = line.call(
        partial(after_body, n_sel, n_peer),
        [*states, num, fq, tokens, w_t, v_t13, *sels],
        [whole(st_shape)] * n_peer
        + [whole(num.shape), whole(fq.shape), whole((rows, D)), w_rows(D, lambda i, s: 3), vec_whole]
        + [pl.BlockSpec(memory_space=pl.ANY)] * n_sel,
        [
            sds((D, rows), f32),
            sds((16, rows), f32),
            sds((rows, D), f32),
            sds((rows, D), bf16),
            sds(st_shape, bf16),
        ]
        + sel_shapes,
        [whole((D, rows)), whole((16, rows)), whole((rows, D)), whole((rows, D)), whole(st_shape)] + sel_high,
        aliases={n_peer + 6 + i: 5 + i for i in range(n_sel)},
        scratch=[pltpu.VMEM((D, rows), bf16)],
        vmem=10,
        name="after",
    )
    o_t, den, resid, h2, s_in = got[:5]
    sels = got[5:]
    if fast:
        sels = [sels[1], swap(sels[0], "grp", 8, 1)]

    n_piece = 2
    piece = FF // n_piece
    acc, acts, db_fc = [], [], []
    for j in range(n_piece):
        if j == 1:
            (sels,) = line.wait(sels)
        pair_of = lambda i, s, j=j: 2 * j + jnp.bitwise_xor(i, jnp.right_shift(s[S_SEQ], 1))
        out_y, out_dh, act, db = line.call(
            partial(mlp_body, j == 0),
            [h2, cotangent, w_t, w_t, bias_fc, *acc],
            [
                whole((rows, D)),
                whole((rows, D)),
                w_rows(D, lambda i, s: 4 + pair_of(i, s)),
                w_rows(D, lambda i, s: 8 + pair_of(i, s)),
                pl.BlockSpec((1, D), lambda i, s: (0, pair_of(i, s))),
            ]
            + [whole((rows, D))] * len(acc),
            [sds((rows, D), f32), sds((rows, D), f32), sds((2, 2, rows, D), bf16), sds((1, piece), f32)],
            [
                whole((rows, D)),
                whole((rows, D)),
                pl.BlockSpec((2, 1, rows, D), lambda i, s: (0, i, 0, 0)),
                pl.BlockSpec((1, D), lambda i, s: (0, jnp.bitwise_xor(i, jnp.right_shift(s[S_SEQ], 1)))),
            ],
            grid=(2,),
            vmem=14,
            name="mlp",
        )
        acc = [out_y, out_dh]
        db_fc.append(db)
        acts.append(both(act))

    if fast:
        first = Halves(
            line, *mlp_grads(line, False, sels, acts[0]),
            [("grp", 8, 2), ("seq", 4, 2), ("grp", 8, 4), ("seq", 4, 1)],
        )
        (acts[1],) = line.wait(acts[1])
    block_output, d_resid, d_attn, rho, ds_own, sums = line.call(
        back_body,
        [*acc, resid, cotangent, w_t, v_t13, o_t, den, fq],
        [whole((rows, D))] * 4
        + [w_rows(D, lambda i, s: 3), vec_whole, whole((D, rows)), whole((16, rows)), whole((2 * D, rows))],
        [
            sds((rows, D), bf16),
            sds((rows, D), f32),
            sds((D, rows), bf16),
            sds((HEADS * AUG, rows), bf16),
            sds(st_shape, bf16),
            sds((4, D), f32),
        ],
        [whole((rows, D))] * 2
        + [whole((D, rows)), whole((HEADS * AUG, rows)), whole(st_shape), whole((4, D))],
        scratch=[pltpu.VMEM((D, rows), bf16)],
        vmem=10,
        out_far=(1, 2, 3),
        name="back",
    )
    back_states = [swap(ds_own, "seq", n_seq, k + 1) for k in range(n_peer)]
    if fast:
        second = mlp_grads(line, True, sels, acts[1], far=range(2, 6))
        (back_states,) = line.wait(back_states)
        second = Halves(
            line, *second, [("seq", 4, 2), ("grp", 8, 2), ("seq", 4, 1), ("grp", 8, 4)]
        )

    grads = [sds((4, D, rows), bf16), sds((D, HD), f32), sds((D, 3), f32)]
    got = []
    for start, count in ((0, N_QUAD),):

        def at(block, axis=0, start=start):
            return pl.BlockSpec(
                tuple(block), lambda i, s: tuple(start + i if d == axis else 0 for d in range(len(block)))
            )

        feat, head = at((2 * wide, rows)), at((wide, rows))
        state = at((QUAD * AUG, 2 * HD))
        args = [*back_states, fq, fk, v_t, rho, s_in, qt, kt, w_t, d_attn]
        got = line.call(
            partial(attend_back_body, n_peer),
            [*args, *got],
            [state] * n_peer
            + [feat, feat, head, at((QUAD * AUG, rows)), state, head, head]
            + [pl.BlockSpec((HD, wide), lambda i, s, start=start: ((4 * D + 2 * FF) // HD, start + i)), head]
            + [pl.BlockSpec(memory_space=pl.ANY)] * len(got),
            grads,
            [at((4, wide, rows), 1), at((wide, HD)), at((wide, 3))],
            grid=(count,),
            aliases={1 + len(args) + k: k for k in range(len(got))},
            hold=1,
            far=(n_peer + 3, n_peer + 8),
            vmem=16,
            name="attend_back",
        )
    dp, dm, db_qkv = got
    dp_both = both(dp)
    db_fc_rows = jnp.concatenate(db_fc, axis=1).reshape(FF // D, D)
    input_grad, *small = line.call(
        partial(input_body, fast),
        [dp, w_t, tokens, d_resid, v_t13, sums, db_fc_rows, db_qkv, dm],
        [
            along((1, D, rows)),
            w_rows(D, lambda i, s: i),
            whole((rows, D)),
            whole((rows, D)),
            vec_whole,
            whole((4, D)),
            whole((FF // D, D)),
            whole((D, 3)),
            whole((D, HD)),
        ],
        [sds((rows, D), bf16)] + [sds((1, r, 2 * HD), f32) for r in sel_rows],
        [whole((rows, D))] + [whole((1, r, 2 * HD)) for r in sel_rows],
        grid=(3,),
        scratch=[pltpu.VMEM((rows, D), f32)],
        vmem=14,
        name="input",
    )
    states_v = [v.T for v in (master_vecs, moment_vecs, square_vecs, average_vecs)]
    if fast:
        theirs, mine = small
        small = [mine, swap(theirs, "grp", 8, 1)]
        first.step(hold=14)
        second.step(hold=60)
        tail = tail_grads(line, sels, dp_both, small)
        tail_first, tail_second = tail_one(line, tail)
        first.step()
        second.step(hold=4)
        far = tail_first()
        first.step()
        second.step()
        mine = final_both(line, [first, second])
        part_x, part_y = swap(mine, "seq", 4, 1), swap(mine, "seq", 4, 2)
        last = tail_second(*far)
        (part_y,) = line.wait(part_y)
        both_mine = [mine, part_x, part_y, swap(part_x, "seq", 4, 2)]
        last_mine = tail_final(line, last)
        outs = adam_piece(
            line, both_mine, states_m, None,
            lambda i: jnp.where(jnp.bitwise_and(i, 1) == 0, 4, 2) + i // 2,
        )
        last_parts = gather_parts(last_mine)
        outs = adam_piece(
            line, last_parts, states_m, outs, lambda i: jnp.where(i < 2, i, (4 * D + 2 * FF) // (2 * D)),
            vecs=states_v,
        )
        mats, vecs = outs[:6], [v.T for v in outs[6:]]
    else:
        h1t, obt, h2t = sels[0][1], sels[0][2], sels[0][3]
        joined = [jnp.transpose(a[0], (0, 2, 1, 3)).reshape(2, rows, piece) for a in acts]
        dn = [dot_tn(cotangent, v[0]) for v in joined]
        fc = [dot_nn(h2t, v[1]) for v in joined]
        qkvo = [dot_nt(h1t, dp[k]) for k in range(3)] + [dot_nt(obt, dp[3])]
        small = small[0][0]
        grad = jnp.concatenate([*qkvo, *fc, *dn, small[:, :HD]], axis=1).astype(bf16)
        own = lax.psum_scatter(grad, "grp", scatter_dimension=0, tiled=True)
        own = lax.psum(own, "seq").astype(f32)
        own_v = lax.psum(lax.psum_scatter(small, "grp", scatter_dimension=0, tiled=True), "seq")
        own_v = own_v[:, HD : HD + n_vec]
        results = adam_math(own, *states_m, learn_rate)
        mats = [own, *results, results[0].astype(bf16)]
        results = adam_math(own_v.T, *states_v, vector_rate)
        vecs = [own_v, *[v.T for v in (*results, results[0].astype(bf16))]]
    flat = [x for pair_ in zip(mats, vecs) for x in pair_]
    return (block_output, input_grad, *flat)


def solution(mesh):
    tok = P(("grp", "seq"), None)
    own = P("grp", None)
    in_specs = (tok, tok, P("grp"), P(), P()) + (own,) * 8
    out_specs = (tok, tok) + (own,) * 12
    body = partial(on_device, mesh.shape["seq"], mesh.shape["grp"])
    return jax.shard_map(body, mesh=mesh, in_specs=in_specs, out_specs=out_specs, check_vma=False)
```

```python
from functools import partial

import jax
import jax.numpy as jnp
from jax import lax
from jax.experimental import pallas as pl
from jax.experimental.pallas import tpu as pltpu
from jax.sharding import PartitionSpec as P

D = 768
HEADS = 12
HD = 64
FF = 3072
QUAD = 4
N_QUAD = HEADS // QUAD
AUG = 72

norm_eps = 1e-05
adam_eps = 1e-08
beta_first = 0.5
beta_second = 0.5
learn_rate = 0.01
vector_rate = 0.06
decay_rate = 0.1
average_keep = 0.9

f32 = jnp.float32
bf16 = jnp.bfloat16

S_SEQ, S_GRP, S_MASK, S_BACK = 0, 1, 4, 8

MIB = 1024 * 1024


def dot_nn(a, b):
    return lax.dot_general(a, b, (((1,), (0,)), ((), ())), preferred_element_type=f32)


def dot_nt(a, b):
    return lax.dot_general(a, b, (((1,), (1,)), ((), ())), preferred_element_type=f32)


def dot_tn(a, b):
    return lax.dot_general(a, b, (((0,), (0,)), ((), ())), preferred_element_type=f32)


def whole(shape):
    return pl.BlockSpec(tuple(shape), lambda *_: (0,) * len(shape))


def along(block, axis=0):
    return pl.BlockSpec(tuple(block), lambda i, s: tuple(i if d == axis else 0 for d in range(len(block))))


def sds(shape, dtype):
    return jax.ShapeDtypeStruct(tuple(shape), dtype)


class Line:
    def __init__(self, scal):
        self.scal = scal
        self.stay = set()

    def wait(self, *values):
        self.scal, values = lax.optimization_barrier((self.scal, values))
        return values

    def call(self, body, args, in_specs, outs, out_specs, grid=(1,), scratch=(), vmem=32,
             hold=0, far=(), out_far=(), aliases=None, name=None):
        args = [
            pltpu.with_memory_space_constraint(a, pltpu.HBM) if id(a) in self.stay or k in far else a
            for k, a in enumerate(args)
        ]
        got = pl.pallas_call(
            body,
            out_shape=tuple(pltpu.HBM(o.shape, o.dtype) if k in out_far else o for k, o in enumerate(outs)),
            grid_spec=pltpu.PrefetchScalarGridSpec(
                num_scalar_prefetch=1,
                grid=grid,
                in_specs=list(in_specs),
                out_specs=tuple(out_specs),
                scratch_shapes=list(scratch),
            ),
            compiler_params=pltpu.CompilerParams(
                dimension_semantics=("arbitrary",) * len(grid), vmem_limit_bytes=vmem * MIB
            ),
            cost_estimate=pl.CostEstimate(
                flops=hold * 10**9, bytes_accessed=1024, transcendentals=0
            ),
            input_output_aliases=aliases or {},
            name=name,
        )(self.scal, *args)
        self.scal, got = lax.optimization_barrier((self.scal, got))
        return got


def store_sel(refs, at, values, scal):
    if len(refs) == 1:
        refs[0][at] = values
        return
    block = D // 8
    for j in range(8):
        rel = jnp.bitwise_xor(scal[S_GRP], j)
        place = pl.multiple_of(jnp.right_shift(rel, 1) * block, block)
        odd = jnp.bitwise_and(rel, 1)
        part = values[j * block : (j + 1) * block, :]

        @pl.when(odd == 1)
        def _(part=part, place=place):
            refs[0][at, pl.ds(place, block), :] = part

        @pl.when(odd == 0)
        def _(part=part, place=place):
            refs[1][at, pl.ds(place, block), :] = part


def normalize(values):
    average = jnp.mean(values, axis=1, keepdims=True)
    centered = values - average
    variance = jnp.mean(centered * centered, axis=1, keepdims=True)
    inverse = lax.rsqrt(variance + norm_eps)
    return centered * inverse, inverse


def quad_maps(hedge_t):
    wide = QUAD * HD
    row = lax.broadcasted_iota(jnp.int32, (wide, HD), 0)
    col = lax.broadcasted_iota(jnp.int32, (wide, HD), 1)
    spread = (jnp.bitwise_and(row, HD - 1) == col).astype(bf16)
    tiled = dot_nn(spread, hedge_t)
    big_r = lax.broadcasted_iota(jnp.int32, (wide, wide), 0)
    big_c = lax.broadcasted_iota(jnp.int32, (wide, wide), 1)
    same = jnp.right_shift(big_r, 6) == jnp.right_shift(big_c, 6)
    return jnp.where(same, tiled, 0.0)


def ones_rows(count):
    return (lax.broadcasted_iota(jnp.int32, (AUG - HD, count), 0) == 0).astype(f32).astype(bf16)


def rows_up(values):
    return jnp.concatenate([values, jnp.zeros((3, values.shape[1]), f32)], axis=0).T


def features(pt, maps):
    high = pt.astype(bf16)
    rest = (pt - high.astype(f32)).astype(bf16)
    scores = dot_nn(jnp.concatenate([maps, maps], axis=1), jnp.concatenate([high, rest], axis=0))
    heads = []
    for h in range(QUAD):
        s = scores[h * HD : (h + 1) * HD, :]
        top = jnp.max(s, axis=0, keepdims=True)
        bottom = jnp.min(s, axis=0, keepdims=True)
        pos = jnp.exp(s - top)
        neg = jnp.exp(bottom - s)
        pos = pos * (1.0 / jnp.sum(pos, axis=0, keepdims=True))
        neg = neg * (1.0 / jnp.sum(neg, axis=0, keepdims=True))
        heads.append(jnp.concatenate([pos, neg], axis=0).astype(bf16))
    return high, heads


def keys_body(scal, x_ref, wk_ref, wv_ref, hedge_ref, vt_ref, vq_ref, h1_ref, kt_ref, fk_ref, vt_out, s_ref):
    rows = x_ref.shape[0]

    @pl.when(pl.program_id(0) == 0)
    def _():
        normed, _ = normalize(x_ref[...].astype(f32))
        vt = vt_ref[...].astype(f32)
        h1_ref[...] = (normed * vt[0:1] + vt[1:2]).astype(bf16)

    h1 = h1_ref[...]
    bias = rows_up(vq_ref[...].astype(f32))
    v_t = (dot_nt(wv_ref[...], h1) + bias[:, 8:9]).astype(bf16)
    vt_out[...] = v_t
    pt = dot_nt(wk_ref[...], h1) + bias[:, 7:8]
    kt_ref[...], heads = features(pt, quad_maps(hedge_ref[...]).astype(bf16))
    extra = ones_rows(rows)
    for h, both in enumerate(heads):
        fk_ref[h * 2 * HD : (h + 1) * 2 * HD, :] = both
        va = jnp.concatenate([v_t[h * HD : (h + 1) * HD, :], extra], axis=0)
        s_ref[h * AUG : (h + 1) * AUG, :] = dot_nt(va, both).astype(bf16)


def queries_body(n_sel, scal, h1_ref, g_ref, wq_ref, hedge_ref, vq_ref, *refs):
    sel = refs[:n_sel]
    qt_ref, fq_ref = refs[n_sel:]
    h1 = h1_ref[...]

    @pl.when(pl.program_id(0) == 0)
    def _():
        store_sel(sel, 0, g_ref[...].T, scal)
        store_sel(sel, 1, h1.T, scal)

    bias = rows_up(vq_ref[...].astype(f32))
    pt = dot_nt(wq_ref[...], h1) + bias[:, 6:7]
    qt_ref[...], heads = features(pt, quad_maps(hedge_ref[...]).astype(bf16))
    for h, both in enumerate(heads):
        fq_ref[h * 2 * HD : (h + 1) * 2 * HD, :] = both


def tri_mask(half):
    return lax.broadcasted_iota(jnp.int32, (half, half), 0) <= lax.broadcasted_iota(
        jnp.int32, (half, half), 1
    )


def masked_pair(left0, left1, right, keep):
    half = right.shape[1] // 2
    full = dot_tn(left0, right)
    low = dot_tn(left1, right[:, half:])
    diag0 = jnp.where(keep, full[:, :half], 0.0).astype(bf16)
    above = full[:, half:].astype(bf16)
    diag1 = jnp.where(keep, low, 0.0).astype(bf16)
    return diag0, above, diag1


def local_body(scal, fq_ref, fk_ref, vt_ref, num_ref):
    rows = fq_ref.shape[1]
    half = rows // 2
    keep = tri_mask(half)
    extra = ones_rows(rows)
    for h in range(QUAD):
        fq = fq_ref[h * 2 * HD : (h + 1) * 2 * HD, :]
        fk = fk_ref[h * 2 * HD : (h + 1) * 2 * HD, :]
        va = jnp.concatenate([vt_ref[h * HD : (h + 1) * HD, :], extra], axis=0)
        a00, a01, a11 = masked_pair(fk[:, :half], fk[:, half:], fq, keep)
        num_ref[h * AUG : (h + 1) * AUG, :half] = dot_nn(va[:, :half], a00)
        num_ref[h * AUG : (h + 1) * AUG, half:] = dot_nn(va[:, :half], a01) + dot_nn(va[:, half:], a11)


def weighted_state(scal, slot, parts):
    total = None
    for k, part in enumerate(parts):
        term = scal[slot + k].astype(f32) * part.astype(f32)
        total = term if total is None else total + term
    return total.astype(bf16)


def after_body(n_sel, n_parts, scal, *refs):
    parts = refs[:n_parts]
    num_ref, fq_ref, x_ref, w_ref, vt_ref = refs[n_parts : n_parts + 5]
    o_ref, den_ref, r_ref, h2_ref, sin_ref = refs[n_parts + 5 + n_sel : n_parts + 10 + n_sel]
    sel = refs[-1 - n_sel : -1]
    ob_ref = refs[-1]
    vt = vt_ref[...].astype(f32)
    state = weighted_state(scal, S_MASK, [p[...] for p in parts])
    sin_ref[...] = state
    for h in range(HEADS):
        num = num_ref[h * AUG : (h + 1) * AUG, :] + dot_nn(
            state[h * AUG : (h + 1) * AUG, :], fq_ref[h * 2 * HD : (h + 1) * 2 * HD, :]
        )
        den = num[HD : HD + 1, :]
        out = num[:HD, :] * (1.0 / den)
        o_ref[h * HD : (h + 1) * HD, :] = out
        den_ref[h : h + 1, :] = den
        ob_ref[h * HD : (h + 1) * HD, :] = out.astype(bf16)
    obt = ob_ref[...]
    store_sel(sel, 0, obt, scal)
    r = x_ref[...].astype(f32) + dot_nt(obt.T, w_ref[...]) + vt[4:5]
    r_ref[...] = r
    normed, _ = normalize(r)
    h2 = (normed * vt[2:3] + vt[3:4]).astype(bf16)
    h2_ref[...] = h2
    store_sel(sel, 1, h2.T, scal)


gelu_c = 0.7978845608028654
gelu_k = 0.044715


def mlp_body(first, scal, h2_ref, g_ref, wf_ref, wd_ref, bias_ref, *refs):
    if first:
        out_ref, dh_ref, act_ref, db_ref = refs
    else:
        out_in, dh_in, out_ref, dh_ref, act_ref, db_ref = refs
    u = dot_nt(h2_ref[...], wf_ref[...]) + bias_ref[...].astype(f32)
    de = dot_nt(g_ref[...], wd_ref[...])
    uu = u * u
    t = jnp.tanh(gelu_c * u * (1.0 + gelu_k * uu))
    half_t = 0.5 * (1.0 + t)
    e = (u * half_t).astype(bf16)
    slope = half_t + 0.5 * u * (1.0 - t * t) * (gelu_c * (1.0 + 3.0 * gelu_k * uu))
    du = (de * slope).astype(bf16)
    act_ref[0, 0] = e
    act_ref[1, 0] = du
    db_ref[...] = jnp.sum(du.astype(f32), axis=0, keepdims=True)
    add_out = dot_nn(e, wd_ref[...])
    add_dh = dot_nn(du, wf_ref[...])
    step = pl.program_id(0)

    @pl.when(step == 0)
    def _():
        if first:
            out_ref[...] = add_out
            dh_ref[...] = add_dh
        else:
            out_ref[...] = out_in[...] + add_out
            dh_ref[...] = dh_in[...] + add_dh

    @pl.when(step > 0)
    def _():
        out_ref[...] += add_out
        dh_ref[...] += add_dh


def back_body(scal, out_ref, dh_ref, r_ref, g_ref, w_ref, vt_ref, o_ref, den_ref, fq_ref, y_ref, dr_ref,
              da_ref, rho_ref, ds_ref, sums_ref, do_ref):
    vt = vt_ref[...].astype(f32)
    r = r_ref[...]
    y_ref[...] = (r + out_ref[...] + vt[5:6]).astype(bf16)
    grad_out = g_ref[...].astype(f32)
    normed, inverse = normalize(r)
    up = dh_ref[...]
    dn = up * vt[2:3]
    dr = grad_out + inverse * (
        dn - jnp.mean(dn, axis=1, keepdims=True) - normed * jnp.mean(dn * normed, axis=1, keepdims=True)
    )
    dr_ref[...] = dr
    da = dr.astype(bf16)
    da_ref[...] = da.T
    sums_ref[...] = jnp.concatenate(
        [
            jnp.sum(up * normed, axis=0, keepdims=True),
            jnp.sum(up, axis=0, keepdims=True),
            jnp.sum(da.astype(f32), axis=0, keepdims=True),
            jnp.sum(grad_out, axis=0, keepdims=True),
        ],
        axis=0,
    )
    do_ref[...] = dot_nn(da, w_ref[...]).astype(bf16).T
    rows = r.shape[0]
    zero_row = lax.broadcasted_iota(jnp.int32, (AUG - HD, rows), 0) == 0
    for h in range(HEADS):
        dout = do_ref[h * HD : (h + 1) * HD, :].astype(f32)
        inv = 1.0 / den_ref[h : h + 1, :]
        rho = (dout * inv).astype(bf16)
        c = -jnp.sum(dout * o_ref[h * HD : (h + 1) * HD, :], axis=0, keepdims=True) * inv
        extra = jnp.where(zero_row, jnp.broadcast_to(c, (AUG - HD, rows)), 0.0).astype(bf16)
        ra = jnp.concatenate([rho, extra], axis=0)
        rho_ref[h * AUG : (h + 1) * AUG, :] = ra
        ds_ref[h * AUG : (h + 1) * AUG, :] = dot_nt(ra, fq_ref[h * 2 * HD : (h + 1) * 2 * HD, :]).astype(bf16)


def feature_back(feat, upstream):
    pos, neg = feat[:HD].astype(f32), feat[HD:].astype(f32)
    up_pos, up_neg = upstream[:HD], upstream[HD:]
    return pos * (up_pos - jnp.sum(pos * up_pos, axis=0, keepdims=True)) - neg * (
        up_neg - jnp.sum(neg * up_neg, axis=0, keepdims=True)
    )


def attend_back_body(n_parts, scal, *refs):
    parts = refs[:n_parts]
    (fq_ref, fk_ref, vt_ref, rho_ref, sin_ref, qt_ref, kt_ref, hedge_ref, da_ref) = refs[n_parts : n_parts + 9]
    dp_ref, dm_ref, db_ref = refs[-3:]
    dp_ref[3] = da_ref[...]
    rows = fq_ref.shape[1]
    half = rows // 2
    keep = tri_mask(half)
    extra = ones_rows(rows)
    back_state = weighted_state(scal, S_BACK, [p[...] for p in parts])
    ds_q, ds_k = [], []
    for h in range(QUAD):
        fq = fq_ref[h * 2 * HD : (h + 1) * 2 * HD, :]
        fk = fk_ref[h * 2 * HD : (h + 1) * 2 * HD, :]
        head = slice(h * HD, (h + 1) * HD)
        aug = slice(h * AUG, (h + 1) * AUG)
        va = jnp.concatenate([vt_ref[head, :], extra], axis=0)
        ra = rho_ref[aug, :]
        state, back = sin_ref[aug, :], back_state[aug, :]
        a00, a01, a11 = masked_pair(fk[:, :half], fk[:, half:], fq, keep)
        g00, g01, g11 = masked_pair(va[:, :half], va[:, half:], ra, keep)
        far = dot_tn(state, ra)
        left = far[:, :half] + dot_nn(fk[:, :half], g00)
        right = far[:, half:] + dot_nn(fk[:, :half], g01) + dot_nn(fk[:, half:], g11)
        dfq = jnp.concatenate([left, right], axis=1)
        far_k = dot_tn(back, va)
        left = far_k[:, :half] + dot_nt(fq[:, :half], g00) + dot_nt(fq[:, half:], g01)
        right = far_k[:, half:] + dot_nt(fq[:, half:], g11)
        dfk = jnp.concatenate([left, right], axis=1)
        far_v = dot_nn(back, fk)[:HD]
        rv = ra[:HD]
        left = far_v[:, :half] + dot_nt(rv[:, :half], a00) + dot_nt(rv[:, half:], a01)
        right = far_v[:, half:] + dot_nt(rv[:, half:], a11)
        dp_ref[2, head, :] = jnp.concatenate([left, right], axis=1).astype(bf16)
        dsq = feature_back(fq, dfq).astype(bf16)
        dsk = feature_back(fk, dfk).astype(bf16)
        ds_q.append(dsq)
        ds_k.append(dsk)
    maps = quad_maps(hedge_ref[...]).T.astype(bf16)
    ds_q, ds_k = jnp.concatenate(ds_q, axis=0), jnp.concatenate(ds_k, axis=0)
    dm = dot_nt(qt_ref[...], ds_q) + dot_nt(kt_ref[...], ds_k)
    for h in range(QUAD):
        head = slice(h * HD, (h + 1) * HD)
        dm_ref[head, :] = dm[head, head]
    dq = dot_nn(maps, ds_q).astype(bf16)
    dk = dot_nn(maps, ds_k).astype(bf16)
    dp_ref[0] = dq
    dp_ref[1] = dk
    db_ref[...] = jnp.concatenate(
        [jnp.sum(v.astype(f32), axis=1, keepdims=True) for v in (dq, dk, dp_ref[2])], axis=1
    )


def input_body(fast, scal, dp_ref, w_ref, x_ref, dr_ref, vt_ref, sums_ref, dbfc_ref, db_ref, dm_ref, *refs):
    gin_ref, *small_refs, acc_ref = refs
    step = pl.program_id(0)
    part = dot_tn(dp_ref[0], w_ref[...])

    @pl.when(step == 0)
    def _():
        acc_ref[...] = part

    @pl.when(step == 1)
    def _():
        acc_ref[...] += part

    @pl.when(step == 2)
    def _():
        vt = vt_ref[...].astype(f32)
        up = acc_ref[...] + part
        normed, inverse = normalize(x_ref[...].astype(f32))
        dn = up * vt[0:1]
        gin = dr_ref[...] + inverse * (
            dn - jnp.mean(dn, axis=1, keepdims=True) - normed * jnp.mean(dn * normed, axis=1, keepdims=True)
        )
        gin_ref[...] = gin.astype(bf16)
        rows16 = jnp.concatenate(
            [
                jnp.sum(up * normed, axis=0, keepdims=True),
                jnp.sum(up, axis=0, keepdims=True),
                sums_ref[...],
                jnp.zeros((3, D), f32),
                dbfc_ref[...],
                jnp.zeros((3, D), f32),
            ],
            axis=0,
        )
        cols = rows16.T
        lane = lax.broadcasted_iota(jnp.int32, (D, HD), 1)
        tail = jnp.concatenate([cols, jnp.zeros((D, HD - 16), f32)], axis=1)
        for k in range(3):
            tail = jnp.where(lane == 6 + k, db_ref[:, k : k + 1], tail)
        small = jnp.concatenate([dm_ref[...], tail], axis=1)
        store_sel(small_refs, 0, small, scal)


def mlp_grads_body(by_y, scal, *refs):
    sels, acts_a, acts_b, sels_h = refs[0:2], refs[2:4], refs[4:6], refs[6:8]
    send, keep = refs[8:]
    block = D // 8
    wq = send.shape[2]
    y_last = 1 - pl.program_id(0)

    def total(lefts, rights):
        return (dot_nn(lefts[0][0], rights[0][0, 0]) + dot_nn(lefts[1][0], rights[1][0, 0])).astype(bf16)

    for path, value in enumerate((total(sels, acts_a), total(sels_h, acts_b))):
        rows = slice(path * block, (path + 1) * block)
        for half in range(2):
            x_last = 1 - jnp.bitwise_xor(half, jnp.bitwise_and(scal[S_SEQ], 1))
            cols = slice(half * wq, (half + 1) * wq)

            def part(z, value=value, cols=cols):
                return value[z * block : (z + 1) * block, cols]

            if by_y:
                for bit, ref in ((0, send), (1, keep)):

                    @pl.when(y_last == bit)
                    def _(ref=ref, part=part, rows=rows, x_last=x_last):
                        for at, z in enumerate((3, 1, 2, 0)):
                            ref[4 * (at // 2) + 2 * x_last + at % 2, rows, :] = part(z)
            else:
                base = 4 * y_last + 1 * x_last
                for ref, order in ((send, (3, 1)), (keep, (2, 0))):
                    for at, z in enumerate(order):
                        ref[2 * at + base, rows, :] = part(z)


def mlp_grads(line, by_y, sels, acts, far=(), out_far=()):
    _, depth, rows = sels[0].shape
    half = sds((8, 2 * (D // 8), D // 2), bf16)

    def act(path):
        return pl.BlockSpec((1, 1, rows, D), lambda i, s: (path, i, 0, 0))

    def sel(slot):
        return pl.BlockSpec((1, depth, rows), lambda i, s: (slot, 0, 0))

    return line.call(
        partial(mlp_grads_body, by_y),
        [*sels, *acts, *acts, *sels],
        [sel(0)] * 2 + [act(0)] * 2 + [act(1)] * 2 + [sel(3)] * 2,
        [half] * 2,
        [whole(half.shape)] * 2,
        grid=(2,),
        vmem=24,
        far=far,
        out_far=out_far,
        name="mlp_grads",
    )


def pack_rows(values, count):
    return jnp.concatenate([values[b * count : (b + 1) * count] for b in range(3)], axis=1)


def unpack_rows(values):
    return jnp.concatenate([values[:, b * 128 : (b + 1) * 128] for b in range(3)], axis=0)


def order_a(i):
    return jnp.where(i < 2, 2 * i + 1, 2 * i - 4)


def order_b(i):
    return jnp.where(i < 2, i + 2, i - 2)


def pick_rows(ref, half, count):
    rows = [ref[pl.ds(pl.multiple_of(z * 2 * count + half * count, 8), count), :] for z in range(4)]
    return jnp.concatenate(rows, axis=0)


def tail_grads_body(scal, *refs):
    h1, ob, dqk, dvo = refs[0:2], refs[2:4], refs[4:6], refs[6:8]
    small_own, small_other, send_a, keep_a, send_b, keep_b, small_ref, sum_ref = refs[8:]
    step = pl.program_id(0)
    wq = send_a.shape[1]
    qb = jnp.bitwise_xor(order_b(step), scal[S_SEQ])
    at = pl.multiple_of(jnp.bitwise_and(step, 1) * wq, wq)

    def total(lefts, rights):
        return (dot_nt(lefts[0][0], rights[0][0]) + dot_nt(lefts[1][0], rights[1][0])).astype(bf16)

    def put(send, keep, value):
        @pl.when(step < 2)
        def _():
            send[pl.ds(at, wq), :] = value

        @pl.when(step >= 2)
        def _():
            keep[pl.ds(at, wq), :] = value

    put(send_a, keep_a, total(h1, dqk))

    @pl.when(qb < 2)
    def _():
        put(send_b, keep_b, total(h1, dvo))

    @pl.when(qb >= 2)
    def _():
        put(send_b, keep_b, total(ob, dvo))

    @pl.when(step == 0)
    def _():
        sum_ref[...] = small_own[0] + small_other[0]
        x_abs = jnp.bitwise_and(scal[S_SEQ], 1)
        small_ref[...] = pack_rows(pick_rows(sum_ref, x_abs, 48), 64)
        send_a[2 * wq :, :] = pack_rows(pick_rows(sum_ref, 1 - x_abs, 48), 64).astype(bf16)


def tail_grads(line, sels, dp, small):
    _, depth, rows = sels[0].shape
    wq = D // 2
    dp = [v.reshape(8, wq, rows) for v in dp]

    def sel(slot):
        return pl.BlockSpec((1, depth, rows), lambda i, s: (slot, 0, 0))

    outs = [
        sds((2 * wq + 64, wq), bf16), sds((2 * wq, wq), bf16),
        sds((2 * wq, wq), bf16), sds((2 * wq, wq), bf16), sds((64, wq), f32),
    ]
    return line.call(
        tail_grads_body,
        [*sels, *sels, *dp, *dp, *small],
        [sel(1)] * 2
        + [sel(2)] * 2
        + [pl.BlockSpec((1, wq, rows), lambda i, s: (jnp.bitwise_xor(order_a(i), s[S_SEQ]), 0, 0))] * 2
        + [pl.BlockSpec((1, wq, rows), lambda i, s: (4 + jnp.bitwise_xor(order_b(i), s[S_SEQ]), 0, 0))] * 2
        + [whole(small[0].shape)] * 2,
        outs,
        [whole(o.shape) for o in outs],
        grid=(4,),
        scratch=[pltpu.VMEM((depth, 2 * HD), f32)],
        vmem=10,
        hold=9,
        name="tail_grads",
    )


def swap(value, axis, size, bit):
    return lax.ppermute(value, axis, [(i, i ^ bit) for i in range(size)])


def halve_body(scal, keep_ref, recv_ref, send_ref, left_ref):
    half = send_ref.shape[0]
    send_ref[...] = (keep_ref[:half].astype(f32) + recv_ref[:half].astype(f32)).astype(bf16)
    left_ref[...] = (keep_ref[half:].astype(f32) + recv_ref[half:].astype(f32)).astype(left_ref.dtype)


class Halves:
    def __init__(self, line, send, keep, stages):
        self.line, self.keep, self.stages = line, keep, list(stages)
        self.recv = swap(send, *self.stages.pop(0))

    def step(self, hold=0):
        count, rows, wq = self.keep.shape
        shape = (count // 2, rows, wq)
        send, self.keep = self.line.call(
            halve_body, [self.keep, self.recv], [whole(self.keep.shape)] * 2,
            [sds(shape, bf16), sds(shape, self.keep.dtype)], [whole(shape)] * 2,
            vmem=8, hold=hold, name="halve",
        )
        self.recv = swap(send, *self.stages.pop(0))


def final_body(scal, *refs):
    out = refs[-1]
    for j in range(2):
        out[j] = (refs[2 * j][0].astype(f32) + refs[2 * j + 1][0].astype(f32)).astype(bf16)


def final_both(line, pieces):
    shape = (2,) + pieces[0].keep.shape[1:]
    (mine,) = line.call(
        final_body, [v for p in pieces for v in (p.keep, p.recv)], [whole((1,) + shape[1:])] * 4,
        [sds(shape, bf16)], [whole(shape)], vmem=4, name="final",
    )
    return mine.reshape(4 * (D // 8), shape[2])


def tail_one_body(scal, keep_a, recv_a, keep_b, recv_b, small_ref, send_a, send_b, half_ref):
    wq = send_b.shape[0]
    send_a[:wq, :] = (keep_a[wq : 2 * wq].astype(f32) + recv_a[wq : 2 * wq].astype(f32)).astype(bf16)
    half_ref[...] = unpack_rows(small_ref[...] + recv_a[2 * wq :].astype(f32))
    y_abs = jnp.right_shift(scal[S_SEQ], 1)
    send_a[wq:, :] = pack_rows(pick_rows(half_ref, 1 - y_abs, 24), 32).astype(bf16)
    send_b[...] = (keep_b[wq:].astype(f32) + recv_b[wq:].astype(f32)).astype(bf16)


def tail_two_body(scal, keep_a, recv_a, keep_b, recv_b, small_ref, far_a, far_b, own_ref, *refs):
    out_refs, half_ref = refs[:-1], refs[-1]
    wq = far_b.shape[0]
    block = D // 8
    half_ref[...] = unpack_rows(small_ref[...] + recv_a[2 * wq :].astype(f32))
    small = pick_rows(half_ref, jnp.right_shift(scal[S_SEQ], 1), 24) + unpack_rows(far_a[wq:].astype(f32))
    first = keep_a[:wq].astype(f32) + recv_a[:wq].astype(f32) + far_a[:wq].astype(f32)
    second = keep_b[:wq].astype(f32) + recv_b[:wq].astype(f32) + far_b[...].astype(f32)
    for z, ref in enumerate((own_ref, *out_refs)):
        rows = slice(z * block, (z + 1) * block)
        ref[:block, :] = first[rows].astype(ref.dtype)
        ref[block : 2 * block, :] = second[rows].astype(ref.dtype)
        packed = pack_rows(small[z * 24 : (z + 1) * 24], 8)
        packed = jnp.concatenate([packed, jnp.zeros_like(packed)], axis=0)
        ref[2 * block :, :] = packed.astype(ref.dtype)


def tail_final_body(scal, *refs):
    total = refs[0][...]
    for ref in refs[1:-1]:
        total = total + ref[...].astype(f32)
    refs[-1][...] = total.astype(bf16)


def tail_one(line, tail):
    send_a, keep_a, send_b, keep_b, small = tail
    wq = D // 2
    recv_a, recv_b = swap(send_a, "seq", 4, 1), swap(send_b, "seq", 4, 2)
    shapes = [sds((wq + 32, wq), bf16), sds((wq, wq), bf16)]
    halves = [pltpu.VMEM((D // 4, 2 * HD), f32)]

    def first():
        args = [keep_a, recv_a, keep_b, recv_b, small]
        next_a, next_b = line.call(
            tail_one_body, args, [whole(v.shape) for v in args], shapes, [whole(v.shape) for v in shapes],
            scratch=halves, vmem=12, name="tail_one",
        )
        return swap(next_a, "seq", 4, 2), swap(next_b, "seq", 4, 1)

    def second(far_a, far_b):
        args = [keep_a, recv_a, keep_b, recv_b, small, far_a, far_b]
        shape = (2 * (D // 8) + 16, wq)
        own, *sends = line.call(
            tail_two_body, args, [whole(v.shape) for v in args], [sds(shape, f32)] + [sds(shape, bf16)] * 3,
            [whole(shape)] * 4, scratch=halves, vmem=10, hold=5, name="tail_two",
        )
        return [own, *(swap(v, "grp", 8, 2 * (k + 1)) for k, v in enumerate(sends))]

    return first, second


def tail_final(line, args):
    (mine,) = line.call(
        tail_final_body, args, [whole(v.shape) for v in args], [sds(args[0].shape, bf16)],
        [whole(args[0].shape)], vmem=6, hold=5, name="tail_final",
    )
    return mine


def gather_parts(mine):
    return [mine] + [swap(mine, "seq", 4, k) for k in (1, 2, 3)]


def adam_math(grad, master, first, second, average, rate):
    new_first = beta_first * first + (1.0 - beta_first) * grad
    new_second = beta_second * second + (1.0 - beta_second) * grad * grad
    new_master = master - rate * (
        new_first / (jnp.sqrt(new_second) + adam_eps) + decay_rate * master
    )
    new_average = average_keep * average + (1.0 - average_keep) * new_master
    return new_master, new_first, new_second, new_average


def adam_body(n_alias, has_small, scal, *refs):
    parts, refs = refs[:4], refs[4:]
    if has_small:
        vec_in, refs = refs[:4], refs[4:]
    states, refs = refs[:4], refs[4 + n_alias :]
    outs, refs = refs[:6], refs[6:]
    grad_ref = outs[0]
    block = D // 8
    count, wq = parts[0].shape[0] // block, parts[0].shape[1]
    step = pl.program_id(0)
    for k, ref in enumerate(parts):
        quarter = jnp.bitwise_xor(scal[S_SEQ], k)

        @pl.when(step < count)
        def _(ref=ref, quarter=quarter):
            at = pl.multiple_of(quarter * wq, 128)
            rows = pl.ds(pl.multiple_of(jnp.minimum(step, count - 1) * block, block), block)
            grad_ref[:, pl.ds(at, wq)] = ref[rows, :].astype(f32)

    if has_small:
        vec_outs, small_ref = refs[:6], refs[6]

        @pl.when(step == count)
        def _():
            for k, ref in enumerate(parts):
                quarter = jnp.bitwise_xor(scal[S_SEQ], k)
                first = jnp.bitwise_and(quarter, 1) * 48 + jnp.right_shift(quarter, 1) * 24
                packed = ref[2 * block :].astype(f32)
                for b in range(3):
                    small_ref[pl.ds(pl.multiple_of(first + 8 * b, 8), 8), :] = packed[:8, b * 128 : (b + 1) * 128]
            small = small_ref[...]
            grad_ref[...] = jnp.zeros_like(grad_ref)
            grad_ref[:, : 2 * HD] = small
            grad = small.T[HD : HD + vec_in[0].shape[0]]
            results = adam_math(grad, *[v[...] for v in vec_in], vector_rate)
            for ref, value in zip(vec_outs, (grad, *results, results[0])):
                ref[...] = value.astype(ref.dtype)

    results = adam_math(grad_ref[...], *[v[...] for v in states], learn_rate)
    for ref, value in zip(outs[1:], (*results, results[0])):
        ref[...] = value.astype(ref.dtype)


def adam_piece(line, parts, states, outs, block_of, vecs=()):
    block = D // 8
    count = parts[0].shape[0] // block
    rows, wide = states[0].shape
    spec = pl.BlockSpec((block, 2 * D), lambda i, s: (0, block_of(i)))
    anywhere = pl.BlockSpec(memory_space=pl.ANY)
    n_alias = 0 if outs is None else 6
    shapes = [sds((rows, wide), f32)] * 5 + [sds((rows, wide), bf16)]
    args = [*parts, *vecs, *states]
    n_before = len(args)
    out_specs = [spec] * 6
    if vecs:
        shapes += [sds(vecs[0].shape, f32)] * 5 + [sds(vecs[0].shape, bf16)]
        out_specs += [whole(vecs[0].shape)] * 6
    return line.call(
        partial(adam_body, n_alias, bool(vecs)),
        [*args, *(outs or [])],
        [whole(v.shape) for v in [*parts, *vecs]] + [spec] * 4 + [anywhere] * n_alias,
        shapes,
        out_specs,
        grid=(count + (1 if vecs else 0),),
        scratch=[pltpu.VMEM((rows, 2 * HD), f32)] if vecs else [],
        aliases={1 + n_before + i: i for i in range(n_alias)},
        vmem=24,
        name="adam",
    )


def on_device(
    n_seq,
    n_grp,
    tokens,
    cotangent,
    seq_len,
    weight_mats,
    weight_vecs,
    master_mats,
    master_vecs,
    moment_mats,
    moment_vecs,
    square_mats,
    square_vecs,
    average_mats,
    average_vecs,
):
    rows = tokens.shape[0]
    fast = n_seq == 4 and n_grp == 8
    seq_at = lax.axis_index("seq")
    grp_at = lax.axis_index("grp")
    slot = jnp.arange(16, dtype=jnp.int32)
    seq_length = seq_len[0]
    peer = jnp.bitwise_xor(seq_at, jnp.bitwise_and(slot, 3) + 1)
    same = (peer * rows) // seq_length == (seq_at * rows) // seq_length
    before = (same & (peer < seq_at)).astype(jnp.int32)
    after = (same & (peer > seq_at)).astype(jnp.int32)
    scal = jnp.where(slot < 8, before, after)
    scal = jnp.where(slot == S_SEQ, seq_at if fast else 0, scal)
    scal = jnp.where(slot == S_GRP, grp_at, scal)
    line = Line(scal)

    w_t = weight_mats.T
    states_m = [master_mats, moment_mats, square_mats, average_mats]
    line.stay = {id(v) for v in (w_t, tokens, cotangent)}
    v_t13 = weight_vecs.T
    n_vec = v_t13.shape[0]
    bias_fc = v_t13[9:].reshape(1, FF)
    wide = QUAD * HD
    n_peer = n_seq - 1
    sel_rows = [D // 2, D // 2] if fast else [D]
    n_sel = len(sel_rows)
    sel_shapes = [sds((4, r, rows), bf16) for r in sel_rows]
    sel_low = [whole((2, r, rows)) for r in sel_rows]
    sel_high = [pl.BlockSpec((2, r, rows), lambda i, s: (1, 0, 0)) for r in sel_rows]

    def both(value):
        return [value, swap(value, "grp", 8, 1)] if fast else [value]

    def w_rows(count, at):
        return pl.BlockSpec((count, D), lambda i, s: (at(i, s), 0))

    hedge_spec = pl.BlockSpec((HD, wide), lambda i, s: ((4 * D + 2 * FF) // HD, i))
    vec_whole = whole(v_t13.shape)
    head_spec, feat_spec = along((wide, rows)), along((2 * wide, rows))
    aug_spec, quad_state = along((QUAD * AUG, rows)), along((QUAD * AUG, 2 * HD))
    st_shape = (HEADS * AUG, 2 * HD)
    vec_quad = pl.BlockSpec((n_vec, wide), lambda i, s: (0, i))
    h1, kt, fk, v_t, s_own = line.call(
        keys_body,
        [tokens, w_t, w_t, w_t, v_t13, v_t13],
        [
            whole((rows, D)),
            w_rows(wide, lambda i, s: N_QUAD + i),
            w_rows(wide, lambda i, s: 2 * N_QUAD + i),
            hedge_spec,
            vec_whole,
            vec_quad,
        ],
        [
            sds((rows, D), bf16),
            sds((D, rows), bf16),
            sds((2 * D, rows), bf16),
            sds((D, rows), bf16),
            sds(st_shape, bf16),
        ],
        [whole((rows, D)), head_spec, feat_spec, head_spec, quad_state],
        grid=(N_QUAD,),
        vmem=12,
        name="keys",
    )
    n_peer = n_seq - 1
    states = [swap(s_own, "seq", n_seq, k + 1) for k in range(n_peer)]
    got = line.call(
        partial(queries_body, n_sel),
        [h1, cotangent, w_t, w_t, v_t13],
        [whole((rows, D)), whole((rows, D)), w_rows(wide, lambda i, s: i), hedge_spec, vec_quad],
        sel_shapes + [sds((D, rows), bf16), sds((2 * D, rows), bf16)],
        sel_low + [head_spec, feat_spec],
        grid=(N_QUAD,),
        vmem=12,
        name="queries",
    )
    sels, (qt, fq) = got[:n_sel], got[n_sel:]

    (num,) = line.call(
        local_body,
        [fq, fk, v_t],
        [feat_spec, feat_spec, head_spec],
        [sds((HEADS * AUG, rows), f32)],
        [aug_spec],
        grid=(N_QUAD,),
        vmem=10,
        name="local",
    )
    got = line.call(
        partial(after_body, n_sel, n_peer),
        [*states, num, fq, tokens, w_t, v_t13, *sels],
        [whole(st_shape)] * n_peer
        + [whole(num.shape), whole(fq.shape), whole((rows, D)), w_rows(D, lambda i, s: 3), vec_whole]
        + [pl.BlockSpec(memory_space=pl.ANY)] * n_sel,
        [
            sds((D, rows), f32),
            sds((16, rows), f32),
            sds((rows, D), f32),
            sds((rows, D), bf16),
            sds(st_shape, bf16),
        ]
        + sel_shapes,
        [whole((D, rows)), whole((16, rows)), whole((rows, D)), whole((rows, D)), whole(st_shape)] + sel_high,
        aliases={n_peer + 6 + i: 5 + i for i in range(n_sel)},
        scratch=[pltpu.VMEM((D, rows), bf16)],
        vmem=10,
        name="after",
    )
    o_t, den, resid, h2, s_in = got[:5]
    sels = got[5:]
    if fast:
        sels = [sels[1], swap(sels[0], "grp", 8, 1)]

    n_piece = 2
    piece = FF // n_piece
    acc, acts, db_fc = [], [], []
    for j in range(n_piece):
        if j == 1:
            (sels,) = line.wait(sels)
        pair_of = lambda i, s, j=j: 2 * j + jnp.bitwise_xor(i, jnp.right_shift(s[S_SEQ], 1))
        out_y, out_dh, act, db = line.call(
            partial(mlp_body, j == 0),
            [h2, cotangent, w_t, w_t, bias_fc, *acc],
            [
                whole((rows, D)),
                whole((rows, D)),
                w_rows(D, lambda i, s: 4 + pair_of(i, s)),
                w_rows(D, lambda i, s: 8 + pair_of(i, s)),
                pl.BlockSpec((1, D), lambda i, s: (0, pair_of(i, s))),
            ]
            + [whole((rows, D))] * len(acc),
            [sds((rows, D), f32), sds((rows, D), f32), sds((2, 2, rows, D), bf16), sds((1, piece), f32)],
            [
                whole((rows, D)),
                whole((rows, D)),
                pl.BlockSpec((2, 1, rows, D), lambda i, s: (0, i, 0, 0)),
                pl.BlockSpec((1, D), lambda i, s: (0, jnp.bitwise_xor(i, jnp.right_shift(s[S_SEQ], 1)))),
            ],
            grid=(2,),
            vmem=20,
            name="mlp",
        )
        acc = [out_y, out_dh]
        db_fc.append(db)
        acts.append(both(act))

    if fast:
        first = Halves(
            line, *mlp_grads(line, False, sels, acts[0]),
            [("grp", 8, 2), ("seq", 4, 2), ("grp", 8, 4), ("seq", 4, 1)],
        )
        (acts[1],) = line.wait(acts[1])
    block_output, d_resid, d_attn, rho, ds_own, sums = line.call(
        back_body,
        [*acc, resid, cotangent, w_t, v_t13, o_t, den, fq],
        [whole((rows, D))] * 4
        + [w_rows(D, lambda i, s: 3), vec_whole, whole((D, rows)), whole((16, rows)), whole((2 * D, rows))],
        [
            sds((rows, D), bf16),
            sds((rows, D), f32),
            sds((D, rows), bf16),
            sds((HEADS * AUG, rows), bf16),
            sds(st_shape, bf16),
            sds((4, D), f32),
        ],
        [whole((rows, D))] * 2
        + [whole((D, rows)), whole((HEADS * AUG, rows)), whole(st_shape), whole((4, D))],
        scratch=[pltpu.VMEM((D, rows), bf16)],
        vmem=10,
        out_far=(1, 2, 3),
        name="back",
    )
    back_states = [swap(ds_own, "seq", n_seq, k + 1) for k in range(n_peer)]
    if fast:
        second = mlp_grads(line, True, sels, acts[1], far=range(2, 6))
        (back_states,) = line.wait(back_states)
        second = Halves(
            line, *second, [("seq", 4, 2), ("grp", 8, 2), ("seq", 4, 1), ("grp", 8, 4)]
        )

    grads = [sds((4, D, rows), bf16), sds((D, HD), f32), sds((D, 3), f32)]
    got = []
    for start, count in ((0, N_QUAD),):

        def at(block, axis=0, start=start):
            return pl.BlockSpec(
                tuple(block), lambda i, s: tuple(start + i if d == axis else 0 for d in range(len(block)))
            )

        feat, head = at((2 * wide, rows)), at((wide, rows))
        state = at((QUAD * AUG, 2 * HD))
        args = [*back_states, fq, fk, v_t, rho, s_in, qt, kt, w_t, d_attn]
        got = line.call(
            partial(attend_back_body, n_peer),
            [*args, *got],
            [state] * n_peer
            + [feat, feat, head, at((QUAD * AUG, rows)), state, head, head]
            + [pl.BlockSpec((HD, wide), lambda i, s, start=start: ((4 * D + 2 * FF) // HD, start + i)), head]
            + [pl.BlockSpec(memory_space=pl.ANY)] * len(got),
            grads,
            [at((4, wide, rows), 1), at((wide, HD)), at((wide, 3))],
            grid=(count,),
            aliases={1 + len(args) + k: k for k in range(len(got))},
            hold=1,
            far=(n_peer + 3, n_peer + 8),
            vmem=16,
            name="attend_back",
        )
    dp, dm, db_qkv = got
    dp_both = both(dp)
    db_fc_rows = jnp.concatenate(db_fc, axis=1).reshape(FF // D, D)
    input_grad, *small = line.call(
        partial(input_body, fast),
        [dp, w_t, tokens, d_resid, v_t13, sums, db_fc_rows, db_qkv, dm],
        [
            along((1, D, rows)),
            w_rows(D, lambda i, s: i),
            whole((rows, D)),
            whole((rows, D)),
            vec_whole,
            whole((4, D)),
            whole((FF // D, D)),
            whole((D, 3)),
            whole((D, HD)),
        ],
        [sds((rows, D), bf16)] + [sds((1, r, 2 * HD), f32) for r in sel_rows],
        [whole((rows, D))] + [whole((1, r, 2 * HD)) for r in sel_rows],
        grid=(3,),
        scratch=[pltpu.VMEM((rows, D), f32)],
        vmem=14,
        name="input",
    )
    states_v = [v.T for v in (master_vecs, moment_vecs, square_vecs, average_vecs)]
    if fast:
        theirs, mine = small
        small = [mine, swap(theirs, "grp", 8, 1)]
        first.step(hold=14)
        second.step(hold=60)
        tail = tail_grads(line, sels, dp_both, small)
        tail_first, tail_second = tail_one(line, tail)
        first.step()
        second.step(hold=4)
        far = tail_first()
        first.step()
        second.step()
        mine = final_both(line, [first, second])
        part_x, part_y = swap(mine, "seq", 4, 1), swap(mine, "seq", 4, 2)
        last = tail_second(*far)
        (part_y,) = line.wait(part_y)
        both_mine = [mine, part_x, part_y, swap(part_x, "seq", 4, 2)]
        last_mine = tail_final(line, last)
        outs = adam_piece(
            line, both_mine, states_m, None,
            lambda i: jnp.where(jnp.bitwise_and(i, 1) == 0, 4, 2) + i // 2,
        )
        last_parts = gather_parts(last_mine)
        outs = adam_piece(
            line, last_parts, states_m, outs, lambda i: jnp.where(i < 2, i, (4 * D + 2 * FF) // (2 * D)),
            vecs=states_v,
        )
        mats, vecs = outs[:6], [v.T for v in outs[6:]]
    else:
        h1t, obt, h2t = sels[0][1], sels[0][2], sels[0][3]
        joined = [jnp.transpose(a[0], (0, 2, 1, 3)).reshape(2, rows, piece) for a in acts]
        dn = [dot_tn(cotangent, v[0]) for v in joined]
        fc = [dot_nn(h2t, v[1]) for v in joined]
        qkvo = [dot_nt(h1t, dp[k]) for k in range(3)] + [dot_nt(obt, dp[3])]
        small = small[0][0]
        grad = jnp.concatenate([*qkvo, *fc, *dn, small[:, :HD]], axis=1).astype(bf16)
        own = lax.psum_scatter(grad, "grp", scatter_dimension=0, tiled=True)
        own = lax.psum(own, "seq").astype(f32)
        own_v = lax.psum(lax.psum_scatter(small, "grp", scatter_dimension=0, tiled=True), "seq")
        own_v = own_v[:, HD : HD + n_vec]
        results = adam_math(own, *states_m, learn_rate)
        mats = [own, *results, results[0].astype(bf16)]
        results = adam_math(own_v.T, *states_v, vector_rate)
        vecs = [own_v, *[v.T for v in (*results, results[0].astype(bf16))]]
    flat = [x for pair_ in zip(mats, vecs) for x in pair_]
    return (block_output, input_grad, *flat)


def solution(mesh):
    tok = P(("grp", "seq"), None)
    own = P("grp", None)
    in_specs = (tok, tok, P("grp"), P(), P()) + (own,) * 8
    out_specs = (tok, tok) + (own,) * 12
    body = partial(on_device, mesh.shape["seq"], mesh.shape["grp"])
    return jax.shard_map(body, mesh=mesh, in_specs=in_specs, out_specs=out_specs, check_vma=False)
```
